32 devices in a mesh: dp: 4 (over y, core), seq: 2 (over x), tensor: 4 (over z).
Axes of the slice: x: 2, y: 2, z: 4, core: 2. Of those that a mesh axis runs over, the one named last changes fastest.
Arguments:
- latents: bfloat16 [4, 16, 256, 1152], P('dp', 'seq', 'tensor'), may hold values from -6 to 6
- condition: bfloat16 [4, 1152], P('dp'), may hold values from -6 to 6
- teacher: bfloat16 [4, 16, 256, 1152], P('dp', 'seq', 'tensor'), may hold values from -6 to 6
- valid_mask: int32 [4, 256], P('dp', 'tensor'), may hold values from 0 to 1, as said below
- qkv_weight: bfloat16 [2, 1152, 3, 1152], P(None, ('dp', 'seq'), None, 'tensor'), may hold values from -0.1875 to 0.1875
- out_weight: bfloat16 [2, 1152, 1152], P(None, 'tensor', ('dp', 'seq')), may hold values from -0.5 to 0.5
- up_weight: bfloat16 [2, 1152, 4608], P(None, ('dp', 'seq'), 'tensor'), may hold values from -0.1875 to 0.1875
- down_weight: bfloat16 [2, 4608, 1152], P(None, 'tensor', ('dp', 'seq')), may hold values from -0.09375 to 0.09375
- ada_weight: bfloat16 [2, 1152, 6, 1152], P(None, ('dp', 'seq'), None, 'tensor'), may hold values from -0.1875 to 0.1875
Outputs:
- block_out: bfloat16 [4, 16, 256, 1152], P('dp', 'seq', 'tensor')
- loss_value: float32 [], replicated
- grad_latents: float32 [4, 16, 256, 1152], P('dp', 'seq', 'tensor')
- grad_condition: float32 [4, 1152], P('dp')
- grad_qkv_weight: float32 [2, 1152, 3, 1152], P(None, ('dp', 'seq'), None, 'tensor')
- grad_out_weight: float32 [2, 1152, 1152], P(None, 'tensor', ('dp', 'seq'))
- grad_up_weight: float32 [2, 1152, 4608], P(None, ('dp', 'seq'), 'tensor')
- grad_down_weight: float32 [2, 4608, 1152], P(None, 'tensor', ('dp', 'seq'))
- grad_ada_weight: float32 [2, 1152, 6, 1152], P(None, ('dp', 'seq'), None, 'tensor')
The draws below stay inside these ranges and needn't reach their ends.
Inputs may be any that keep to these rules, and one draw needn't show every extreme that they name: `valid_mask`: 1 marks a patch of a clip that counts in the loss; the last patch of the last clip always counts.
All inputs are finite; a program needn't handle non-finite values.
Results may differ from the reference program's by a relative error of at most 0.022.
Values may be sent and summed in bfloat16 or wider, within the bound.
A program may use at most 320 MiB of HBM per device.

```python
import jax
import jax.numpy as jnp
from jax import lax

D = 1152
HEADS = 16
HEAD_DIM = 72
FF = 4608
FRAMES = 16
PATCHES = 256
CLIPS = 4
TOKENS = 16384


def draw_valid_mask(key, part):
    cells = CLIPS * PATCHES
    samples = jax.random.randint(key, (CLIPS, PATCHES), 0, 4 * cells)
    position = jnp.arange(cells, dtype=jnp.int32).reshape(CLIPS, PATCHES)
    threshold = cells + 3 * cells * position // (cells - 1)
    return (samples < threshold).astype(jnp.int32)


def level_of(key, extent, pieces, low, high):
    def one(axis_at, parts):
        draws = jax.random.uniform(jax.random.fold_in(jax.random.fold_in(key, 6), axis_at), (parts,), jnp.float32, low / len(pieces), high / len(pieces))
        return jnp.repeat(jnp.exp(draws), extent[axis_at] // parts).reshape((-1,) + (1,) * (len(extent) - axis_at - 1))

    factor_of = one(*pieces[0])
    for cut in pieces[1:]:
        factor_of = factor_of * one(*cut)
    return factor_of


def scatter_about(rng, shape, spread, most, pieces=(), kind=jnp.bfloat16):
    array = jax.random.normal(rng, shape, jnp.float32) * spread
    if len(pieces) > 0:
        array = level_of(rng, shape, pieces, -0.22, 0.18) * array
    return jnp.clip(array, min=-most, max=most).astype(kind)


def setup_inputs(seed: int = 0) -> dict:
    seeds = jax.random.split(jax.random.key(seed), 10)
    return {
        "latents": scatter_about(seeds[0], (CLIPS, FRAMES, PATCHES, D), 1.0, 6.0, ((0, 4), (1, 2), (2, 4))),
        "condition": scatter_about(seeds[1], (CLIPS, D), 1.0, 6.0, ((0, 4),)),
        "teacher": scatter_about(seeds[2], (CLIPS, FRAMES, PATCHES, D), 1.0, 6.0, ((0, 4), (1, 2), (2, 4))),
        "valid_mask": draw_valid_mask(jax.random.fold_in(seeds[9], 71), 0),
        "qkv_weight": scatter_about(seeds[4], (2, D, 3, D), D ** -0.5, 0.1875, ((1, 8), (3, 4))),
        "out_weight": scatter_about(seeds[5], (2, D, D), (D // 8) ** -0.5, 0.5, ((1, 4), (2, 8))),
        "up_weight": scatter_about(seeds[6], (2, D, FF), D ** -0.5, 0.1875, ((1, 8), (2, 4))),
        "down_weight": scatter_about(seeds[7], (2, FF, D), FF ** -0.5, 0.09375, ((1, 4), (2, 8))),
        "ada_weight": scatter_about(seeds[8], (2, D, 6, D), D ** -0.5, 0.1875, ((1, 8), (3, 4))),
    }


@jax.custom_vjp
def low(v):
    return lax.optimization_barrier(v.astype(jnp.bfloat16)).astype(jnp.float32)

@jax.custom_vjp
def low_back(v):
    return v

def low_keep(v):
    return (low(v), None)

def low_pass(kept, grad):
    return (grad,)

def back_keep(v):
    return (v, None)

def back_low(kept, grad):
    return (low(grad),)
low.defvjp(low_keep, low_pass)
low_back.defvjp(back_keep, back_low)
EPSILON = 1e-06
HIGHEST = lax.Precision.HIGHEST
SPATIAL = ('flhe,fmhe->fhlm', 'fhlm,fmhe->flhe')
TEMPORAL = ('lphe,mphe->phlm', 'phlm,mphe->lphe')

def layer_norm(stream):
    center = stream - lax.optimization_barrier(jnp.mean(stream, axis=-1, keepdims=True))
    return center * lax.rsqrt(lax.optimization_barrier(jnp.mean(center * center, axis=-1, keepdims=True)) + EPSILON)

def attention(queries, key_heads, values, einsum_forms):
    scores = jnp.einsum(einsum_forms[0], queries, key_heads, precision=HIGHEST) * HEAD_DIM ** (-0.5)
    scores = low_back(scores)
    probability = low(jax.nn.softmax(scores, axis=-1))
    return jnp.einsum(einsum_forms[1], probability, values, precision=HIGHEST)

def run_clip(stream, silu_low, weights):
    qkv_all, out_all, up_all, down_all, ada_all = weights
    for block_index in range(2):
        einsum_forms = SPATIAL if block_index == 0 else TEMPORAL
        modulation = jnp.dot(silu_low, ada_all[block_index].reshape(D, 6 * D), precision=HIGHEST).reshape(6, D)
        normed = low(layer_norm(stream) * (1.0 + modulation[1]) + modulation[0])
        triple = jnp.dot(normed.reshape(-1, D), qkv_all[block_index].reshape(D, 3 * D), precision=HIGHEST)
        triple = low(low_back(triple)).reshape(FRAMES, PATCHES, 3, HEADS, HEAD_DIM)
        mixed_heads = attention(triple[:, :, 0], triple[:, :, 1], triple[:, :, 2], einsum_forms)
        mixed_heads = low(low_back(mixed_heads.reshape(-1, D)))
        branch = low_back(jnp.dot(mixed_heads, out_all[block_index], precision=HIGHEST)).reshape(FRAMES, PATCHES, D)
        stream = stream + modulation[2] * branch
        normed = low(layer_norm(stream) * (1.0 + modulation[4]) + modulation[3])
        hidden = low_back(jnp.dot(normed.reshape(-1, D), up_all[block_index], precision=HIGHEST))
        hidden = low(jax.nn.gelu(hidden, approximate=True))
        branch = low_back(jnp.dot(hidden, down_all[block_index], precision=HIGHEST)).reshape(FRAMES, PATCHES, D)
        stream = stream + modulation[5] * branch
    return stream

def reference(latents, condition, teacher, valid_mask, qkv_weight, out_weight, up_weight, down_weight, ada_weight):
    weights = tuple((matrix.astype(jnp.float32) for matrix in (qkv_weight, out_weight, up_weight, down_weight, ada_weight)))
    start_rows = latents.astype(jnp.float32)
    cond_rows = condition.astype(jnp.float32)
    target = teacher.astype(jnp.float32)
    mask_rows = valid_mask.astype(jnp.float32)
    valid_count = FRAMES * jnp.sum(mask_rows)

    def objective(start_rows, cond_rows, weights):

        def per_clip(clip_items):
            stream, cond_row, target_clip, mask_row = clip_items
            silu_low = low(jax.nn.silu(cond_row))
            final_rows = run_clip(stream, silu_low, weights)
            error_rows = final_rows - target_clip
            return (jnp.sum(mask_row[None, :, None] * error_rows * error_rows), final_rows)
        clip_sums, final_rows = lax.map(jax.checkpoint(per_clip), (start_rows, cond_rows, target, mask_rows))
        return (jnp.sum(clip_sums) / (D * valid_count), final_rows)
    loss_value, backward, final_rows = jax.vjp(objective, start_rows, cond_rows, weights, has_aux=True)
    grad_latents, grad_condition, weight_grads = backward(jnp.asarray(D * TOKENS, dtype=jnp.float32))
    return (final_rows.astype(jnp.bfloat16), loss_value, grad_latents, grad_condition, weight_grads[0], weight_grads[1], weight_grads[2], weight_grads[3], weight_grads[4])
```

```python
import functools

import jax
import jax.numpy as jnp
from jax import lax
from jax.experimental import pallas as pl
from jax.experimental.pallas import tpu as pltpu
from jax.sharding import PartitionSpec as P

HEAD_DIM = 72
EPSILON = 1e-06
HIGHEST = lax.Precision.HIGHEST
MESH = pl.DeviceIdType.MESH
DMA = pltpu.SemaphoreType.DMA
BF16 = jnp.bfloat16
F32 = jnp.float32
ANY = pl.BlockSpec(memory_space=pl.ANY)


def position():
    dp = lax.axis_index("dp")
    return dp // 2, dp % 2, lax.axis_index("seq"), lax.axis_index("tensor")


def device(y, c, x, z):
    return (y * 2 + c, x, z)


def neighbours(nz):
    y, c, x, z = position()
    return (
        device(y, c, 1 - x, z),
        device(1 - y, c, x, z),
        device(y, 1 - c, x, z),
        device(y, c, x, jnp.maximum(z - 1, 0)),
        device(y, c, x, jnp.minimum(z + 1, nz - 1)),
    )


def remote(src, dst, send_sem, recv_sem, target):
    return pltpu.make_async_remote_copy(
        src_ref=src,
        dst_ref=dst,
        send_sem=send_sem,
        recv_sem=recv_sem,
        device_id=target,
        device_id_type=MESH,
    )


def greet(nz):
    z = lax.axis_index("tensor")
    x_dev, y_dev, core_dev, below, above = neighbours(nz)
    barrier = pltpu.get_barrier_semaphore()
    for target in (x_dev, y_dev, core_dev):
        pl.semaphore_signal(barrier, inc=1, device_id=target, device_id_type=MESH)

    @pl.when(z > 0)
    def _():
        pl.semaphore_signal(barrier, inc=1, device_id=below, device_id_type=MESH)

    @pl.when(z < nz - 1)
    def _():
        pl.semaphore_signal(barrier, inc=1, device_id=above, device_id_type=MESH)

    inside = ((z > 0) & (z < nz - 1)).astype(jnp.int32)
    pl.semaphore_wait(barrier, 4 + inside)


def gather_kernel(
    w_ref, g_ref, lsem, s_zab, r_zab, s_xy, r_xy, s_zcd, r_zcd, s_c, r_c, *, nz, ahead
):
    layers, rows, _ = w_ref.shape
    unit = rows // 9
    ab = 7 * unit
    y, c, x, z = position()
    x_dev, y_dev, core_dev, below, above = neighbours(nz)
    greet(nz)
    own = []
    for l in range(layers):
        copy = pltpu.make_async_copy(w_ref.at[l], g_ref.at[l, z, y, c, x], lsem.at[l])
        copy.start()
        own.append(copy)

    def split(l):
        a = (4 if l % 2 == 0 else 3) * unit
        return pl.ds(0, a), pl.ds(a, ab - a), pl.ds(ab, unit), pl.ds(ab + unit, unit)

    def region_ab(l, t):
        return g_ref.at[l, t, y, c, x, pl.ds(0, ab)]

    def region_cd(l, t):
        return g_ref.at[l, t, :, c, :, pl.ds(ab, 2 * unit)]

    def along_z(l, hop, region, ssem, rsem, mode, first=None):
        up, down = z - hop, z + hop

        if mode == "recv":

            @pl.when(z - 1 - hop >= 0)
            def _():
                r = region(l, jnp.maximum(z - 1 - hop, 0))
                remote(r, r, ssem.at[l, hop, 1], rsem.at[l, hop, 1], above).wait_recv()

            @pl.when(z + 1 + hop < nz)
            def _():
                r = region(l, jnp.minimum(z + 1 + hop, nz - 1))
                remote(r, r, ssem.at[l, hop, 0], rsem.at[l, hop, 0], below).wait_recv()

            return

        @pl.when((up >= 0) & (z < nz - 1))
        def _():
            r = region(l, jnp.maximum(up, 0))
            src = first if first is not None and hop == 0 else r
            copy = remote(src, r, ssem.at[l, hop, 1], rsem.at[l, hop, 1], above)
            copy.start() if mode == "start" else copy.wait_send()

        @pl.when((down < nz) & (z > 0))
        def _():
            r = region(l, jnp.minimum(down, nz - 1))
            src = first if first is not None and hop == 0 else r
            copy = remote(src, r, ssem.at[l, hop, 0], rsem.at[l, hop, 0], below)
            copy.start() if mode == "start" else copy.wait_send()

    def region_xy(l, kind, yy, xx):
        a, b, cc, d = split(l)
        return (
            lambda: g_ref.at[l, :, yy, c, xx, a],
            lambda: g_ref.at[l, :, yy, c, xx, b],
            lambda: g_ref.at[l, :, yy, c, :, a],
            lambda: g_ref.at[l, :, :, c, xx, b],
            lambda: g_ref.at[l, z, yy, c, xx, cc],
            lambda: g_ref.at[l, z, yy, c, xx, d],
            lambda: g_ref.at[l, z, yy, c, :, cc],
            lambda: g_ref.at[l, z, :, c, xx, d],
        )[kind]()

    along_x = (True, False, False, True, True, False, False, True)

    def along_xy(l, kind, mode):
        target = x_dev if along_x[kind] else y_dev
        if mode == "recv":
            r = region_xy(l, kind, y, 1 - x) if along_x[kind] else region_xy(l, kind, 1 - y, x)
            remote(r, r, s_xy.at[l, kind], r_xy.at[l, kind], target).wait_recv()
            return
        r = region_xy(l, kind, y, x)
        src = r
        if kind == 4:
            src = w_ref.at[l, pl.ds(ab, unit)]
        if kind == 5:
            src = w_ref.at[l, pl.ds(ab + unit, unit)]
        copy = remote(src, r, s_xy.at[l, kind], r_xy.at[l, kind], target)
        copy.start() if mode == "start" else copy.wait_send()

    def to_core(l, mode):
        r = g_ref.at[l, :, :, c if mode != "recv" else 1 - c]
        copy = remote(r, r, s_c.at[l], r_c.at[l], core_dev)
        if mode == "start":
            copy.start()
        elif mode == "send":
            copy.wait_send()
        else:
            copy.wait_recv()

    def z_ab(l, hop, mode):
        along_z(l, hop, region_ab, s_zab, r_zab, mode, first=w_ref.at[l, pl.ds(0, ab)])

    def z_cd(l, hop, mode):
        along_z(l, hop, region_cd, s_zcd, r_zcd, mode)

    def stage(l, s):
        if s == 0:
            z_ab(l, 0, "start")
            along_xy(l, 4, "start")
            along_xy(l, 5, "start")
        if s == 1:
            z_ab(l, 0, "recv")
            z_ab(l, 1, "start")
            own[l].wait()
            along_xy(l, 4, "recv")
            along_xy(l, 6, "start")
            along_xy(l, 5, "recv")
            along_xy(l, 7, "start")
        if s == 2:
            z_ab(l, 1, "recv")
            z_ab(l, 2, "start")
            along_xy(l, 6, "recv")
            along_xy(l, 7, "recv")
            z_cd(l, 0, "start")
        if s == 3:
            z_ab(l, 2, "recv")
            along_xy(l, 0, "start")
            along_xy(l, 1, "start")
            z_cd(l, 0, "recv")
            z_cd(l, 1, "start")
        if s == 4:
            along_xy(l, 0, "recv")
            along_xy(l, 2, "start")
            along_xy(l, 1, "recv")
            along_xy(l, 3, "start")
            z_cd(l, 1, "recv")
            z_cd(l, 2, "start")
        if s == 5:
            along_xy(l, 2, "recv")
            along_xy(l, 3, "recv")
            z_cd(l, 2, "recv")
            to_core(l, "start")

    for l in range(min(ahead, layers)):
        stage(l, 0)
    for slot in range(layers + 5):
        for l in range(layers):
            s = slot - l
            if s == 0 and l + ahead < layers:
                stage(l + ahead, 0)
            if 1 <= s <= 5:
                stage(l, s)
    for l in range(layers):
        to_core(l, "recv")
        to_core(l, "send")
        for kind in range(8):
            along_xy(l, kind, "send")
        for hop in range(nz - 1):
            z_ab(l, hop, "send")
            z_cd(l, hop, "send")


def gather_weights(shards, nz):
    layers, rows, cols = shards.shape
    hops = nz - 1
    return pl.pallas_call(
        functools.partial(gather_kernel, nz=nz, ahead=2),
        out_shape=jax.ShapeDtypeStruct((layers, nz, 2, 2, 2, rows, cols), BF16),
        in_specs=[ANY],
        out_specs=ANY,
        scratch_shapes=[
            DMA((layers,)),
            DMA((layers, hops, 2)),
            DMA((layers, hops, 2)),
            DMA((layers, 8)),
            DMA((layers, 8)),
            DMA((layers, hops, 2)),
            DMA((layers, hops, 2)),
            DMA((layers,)),
            DMA((layers,)),
        ],
        compiler_params=pltpu.CompilerParams(collective_id=0, has_side_effects=True),
        name="gather_weights",
    )(shards)


STAGES = 7
SLOTS = 3
KINDS = ("yA", "xA", "xB", "yB", "yC", "xC", "xD", "yD")


def reduce_kernel(*refs, chunks, n_x, n_g, split_at, nz, rows, width):
    x_refs, g_refs = refs[:n_x], refs[n_x : n_x + n_g]
    (
        o_ref, acc, stg, prb, gbuf, xraw, xt, ya, xa, xb, yb, yc, xc, xd, yd, zab, zcd,
        gsem, xsem, osem, s_p, r_p, s_xy, r_xy, s_z, r_z,
    ) = refs[n_x + n_g :]
    unit = rows // 9
    ab = 7 * unit
    count = len(chunks)
    y, c, x, z = position()
    x_dev, y_dev, core_dev, below, above = neighbours(nz)
    greet(nz)

    def add_in(dst, src):
        lead = dst.shape[:-2]
        total = 1
        for v in lead:
            total *= v
        if total == 1:
            dst[...] = dst[...] + src[...]
            return

        def body(i, carry):
            index = []
            rest = i
            for v in reversed(lead):
                index.append(rest % v)
                rest = rest // v
            index = tuple(reversed(index))
            dst[index] = dst[index] + src[index]
            return carry

        lax.fori_loop(0, total, body, 0)

    def exchange(k, kind, mode):
        a = (4 if k % 2 == 0 else 3) * unit
        b = ab - a
        ra, rb, rc, rd = pl.ds(0, a), pl.ds(a, b), pl.ds(ab, unit), pl.ds(ab + unit, unit)
        m = k % SLOTS
        part = acc.at[k % STAGES]
        src, buf, target, dst = {
            "yA": lambda: (part.at[:, 1 - y, :, ra], ya.at[m, :, :, pl.ds(0, a)], y_dev, part.at[:, y, :, ra]),
            "xA": lambda: (part.at[:, y, 1 - x, ra], xa.at[m, :, pl.ds(0, a)], x_dev, part.at[:, y, x, ra]),
            "xB": lambda: (part.at[:, :, 1 - x, rb], xb.at[m, :, :, pl.ds(0, b)], x_dev, part.at[:, :, x, rb]),
            "yB": lambda: (part.at[:, 1 - y, x, rb], yb.at[m, :, pl.ds(0, b)], y_dev, part.at[:, y, x, rb]),
            "yC": lambda: (part.at[z, 1 - y, :, rc], yc.at[m], y_dev, part.at[z, y, :, rc]),
            "xC": lambda: (part.at[z, y, 1 - x, rc], xc.at[m], x_dev, part.at[z, y, x, rc]),
            "xD": lambda: (part.at[z, :, 1 - x, rd], xd.at[m], x_dev, part.at[z, :, x, rd]),
            "yD": lambda: (part.at[z, 1 - y, x, rd], yd.at[m], y_dev, part.at[z, y, x, rd]),
        }[kind]()
        i = KINDS.index(kind)
        copy = remote(src, buf, s_xy.at[k % STAGES, i], r_xy.at[m, i], target)
        if mode == "start":
            copy.start()
        elif mode == "send":
            copy.wait_send()
        else:
            copy.wait_recv()
            add_in(dst, buf)

    def region_z(k, t, which):
        part = acc.at[k % STAGES, t]
        return part.at[y, x, pl.ds(0, ab)] if which == 0 else part.at[:, :, pl.ds(ab, 2 * unit)]

    def along_z(k, hop, which, mode):
        m, n = k % SLOTS, k % STAGES
        landing = (zab, zcd)[which]
        t_down, t_up = hop - (nz - 1 - z), nz - 1 - (hop - z)
        if mode != "recv":

            @pl.when((t_down >= 0) & (z > 0))
            def _():
                copy = remote(
                    region_z(k, jnp.maximum(t_down, 0), which), landing.at[m, hop, 0],
                    s_z.at[n, which, hop, 0], r_z.at[m, which, hop, 0], below,
                )
                copy.start() if mode == "start" else copy.wait_send()

            @pl.when((hop >= z) & (z < nz - 1))
            def _():
                copy = remote(
                    region_z(k, jnp.minimum(t_up, nz - 1), which), landing.at[m, hop, 1],
                    s_z.at[n, which, hop, 1], r_z.at[m, which, hop, 1], above,
                )
                copy.start() if mode == "start" else copy.wait_send()

            return
        from_above, from_below = t_down + 1, t_up - 1

        @pl.when((from_above >= 0) & (z < nz - 1))
        def _():
            buf = landing.at[m, hop, 0]
            remote(buf, buf, s_z.at[n, which, hop, 0], r_z.at[m, which, hop, 0], below).wait_recv()
            add_in(region_z(k, jnp.maximum(from_above, 0), which), buf)

        @pl.when((hop >= z - 1) & (z > 0))
        def _():
            buf = landing.at[m, hop, 1]
            remote(buf, buf, s_z.at[n, which, hop, 1], r_z.at[m, which, hop, 1], above).wait_recv()
            add_in(region_z(k, jnp.minimum(from_below, nz - 1), which), buf)

    def pair(k, mode):
        m = k % 2
        copy = remote(stg.at[m], prb.at[m], s_p.at[m], r_p.at[m], core_dev)
        if mode == "start":
            copy.start()
        elif mode == "send":
            copy.wait_send()
        else:
            copy.wait_recv()
            add_in(acc.at[k % STAGES], prb.at[m])

    def load_g(k):
        layer, col, _ = chunks[k]
        return pltpu.make_async_copy(
            g_refs[layer].at[:, :, pl.ds(col * width, width)], gbuf.at[k % 2], gsem.at[k % 2]
        )

    order = []
    for _, _, used in chunks:
        for q in used:
            if q not in order:
                order.append(q)

    def load_x(i):
        return pltpu.make_async_copy(x_refs[order[i]], xraw.at[i % 2], xsem.at[i % 2])

    ready = [0]

    def turned(q):
        i = order.index(q)
        if i >= ready[0]:
            load_x(i).wait()
            for j in range(xraw.shape[2] // 128):
                xt[i % 3, pl.ds(j * 128, 128), :] = xraw[i % 2, :, pl.ds(j * 128, 128)].T
            ready[0] += 1
            if i + 2 < len(order):
                load_x(i + 2).start()
        return i % 3

    def multiply(k):
        _, _, used = chunks[k]
        slots = [turned(q) for q in used]
        if k + 1 < count:
            load_g(k + 1).start()
        load_g(k).wait()

        def fill(dst, core):
            def body(i, carry):
                t, yy = i // 2, i % 2
                at = pl.ds(pl.multiple_of((yy * 4 + core * 2) * rows, 16), 2 * rows)
                g = gbuf[k % 2, t]
                r = jnp.dot(xt[slots[0], at, :], g, preferred_element_type=F32)
                if len(slots) == 2:
                    second = jnp.dot(xt[slots[1], at, :], g, preferred_element_type=F32)
                    col = lax.broadcasted_iota(jnp.int32, r.shape, 1)
                    r = jnp.where(col < split_at, r, second)
                r = r.astype(BF16)
                dst[t, yy, 0] = r[:rows]
                dst[t, yy, 1] = r[rows:]
                return carry

            lax.fori_loop(0, nz * 2, body, 0)

        fill(stg.at[k % 2], 1 - c)
        pair(k, "start")
        fill(acc.at[k % STAGES], c)

    def hand_out(k):
        layer, col, _ = chunks[k]
        return pltpu.make_async_copy(
            acc.at[k % STAGES, z, y, x],
            o_ref.at[layer, :, pl.ds(col * width, width)],
            osem.at[k % STAGES],
        )

    def stage(k, s):
        if s == 0:
            if k >= STAGES:
                hand_out(k - STAGES).wait()
            multiply(k)
        if s == 1:
            pair(k, "send")
            pair(k, "recv")
            exchange(k, "yA", "start")
            exchange(k, "xB", "start")
            along_z(k, 0, 1, "start")
        if s == 2:
            along_z(k, 0, 1, "recv")
            along_z(k, 1, 1, "start")
            exchange(k, "yA", "recv")
            exchange(k, "xA", "start")
            exchange(k, "xB", "recv")
            exchange(k, "yB", "start")
        if s == 3:
            along_z(k, 1, 1, "recv")
            along_z(k, 2, 1, "start")
            exchange(k, "xA", "recv")
            exchange(k, "yB", "recv")
            along_z(k, 0, 0, "start")
        if s == 4:
            along_z(k, 0, 0, "recv")
            along_z(k, 1, 0, "start")
            along_z(k, 2, 1, "recv")
            exchange(k, "yC", "start")
            exchange(k, "xD", "start")
        if s == 5:
            along_z(k, 1, 0, "recv")
            along_z(k, 2, 0, "start")
            exchange(k, "yC", "recv")
            exchange(k, "xC", "start")
            exchange(k, "xD", "recv")
            exchange(k, "yD", "start")
        if s == 6:
            along_z(k, 2, 0, "recv")
            exchange(k, "xC", "recv")
            exchange(k, "yD", "recv")
            for kind in KINDS:
                exchange(k, kind, "send")
            for hop in range(nz - 1):
                along_z(k, hop, 0, "send")
                along_z(k, hop, 1, "send")
            hand_out(k).start()

    load_x(0).start()
    load_x(1).start()
    load_g(0).start()
    for slot in range(count + STAGES - 1):
        for s in range(STAGES - 1, -1, -1):
            if 0 <= slot - s < count:
                stage(slot - s, s)
    for k in range(max(0, count - STAGES), count):
        hand_out(k).wait()


def reduce_weights(x_list, g_list, rows, nz, split_at):
    tokens, cols = x_list[0].shape
    width = cols // 3
    unit = rows // 9
    chunks = []
    for block in (1, 0):
        for layer, used in ((2, (3,)), (1, (2,)), (0, (0, 1))):
            for col in range(3):
                ids = tuple(4 * block + q for q in used)
                if layer == 0 and (col + 1) * width <= split_at:
                    ids = ids[:1]
                chunks.append((3 * block + layer, col, ids))
    vmem = pltpu.VMEM
    hops = nz - 1
    scratch = [
        vmem((STAGES, nz, 2, 2, rows, width), BF16),
        vmem((2, nz, 2, 2, rows, width), BF16),
        vmem((2, nz, 2, 2, rows, width), BF16),
        vmem((2, nz, tokens, width), BF16),
        vmem((2, tokens, cols), BF16),
        vmem((3, cols, tokens), BF16),
        vmem((SLOTS, nz, 2, 4 * unit, width), BF16),
        vmem((SLOTS, nz, 4 * unit, width), BF16),
        vmem((SLOTS, nz, 2, 4 * unit, width), BF16),
        vmem((SLOTS, nz, 4 * unit, width), BF16),
        vmem((SLOTS, 2, unit, width), BF16),
        vmem((SLOTS, unit, width), BF16),
        vmem((SLOTS, 2, unit, width), BF16),
        vmem((SLOTS, unit, width), BF16),
        vmem((SLOTS, hops, 2, 7 * unit, width), BF16),
        vmem((SLOTS, hops, 2, 2, 2, 2 * unit, width), BF16),
        DMA((2,)),
        DMA((2,)),
        DMA((STAGES,)),
        DMA((2,)),
        DMA((2,)),
        DMA((STAGES, 8)),
        DMA((SLOTS, 8)),
        DMA((STAGES, 2, hops, 2)),
        DMA((SLOTS, 2, hops, 2)),
    ]
    return pl.pallas_call(
        functools.partial(
            reduce_kernel,
            chunks=chunks,
            n_x=len(x_list),
            n_g=len(g_list),
            split_at=split_at - 2 * width,
            nz=nz,
            rows=rows,
            width=width,
        ),
        out_shape=jax.ShapeDtypeStruct((len(g_list), rows, cols), BF16),
        in_specs=[ANY] * (len(x_list) + len(g_list)),
        out_specs=ANY,
        scratch_shapes=scratch,
        compiler_params=pltpu.CompilerParams(
            collective_id=1, has_side_effects=True, vmem_limit_bytes=60 << 20
        ),
        name="reduce_weights",
    )(*x_list, *g_list)


def normalize(stream):
    center = stream - jnp.mean(stream, axis=-1, keepdims=True)
    inverse = lax.rsqrt(jnp.mean(center * center, axis=-1, keepdims=True) + EPSILON)
    return center * inverse, inverse


def norm_backward(grad_normed, normed, inverse):
    mean_grad = jnp.mean(grad_normed, axis=-1, keepdims=True)
    mean_along = jnp.mean(grad_normed * normed, axis=-1, keepdims=True)
    return inverse * (grad_normed - mean_grad - normed * mean_along)


def gelu_tanh(values):
    return jax.nn.gelu(values, approximate=True)


def dot(a, b):
    return jnp.dot(a, b, preferred_element_type=F32)


def dot_t(a, b):
    return lax.dot_general(a, b, (((1,), (1,)), ((), ())), preferred_element_type=F32)


def attend_forward(heads, factor):
    q, k, v = heads[:, :, :, 0], heads[:, :, :, 1], heads[:, :, :, 2]
    scores = jnp.einsum("tglhe,tgmhe->tghlm", q, k, preferred_element_type=F32) * factor
    peak = jnp.max(scores, axis=-1, keepdims=True)
    expanded = jnp.exp(scores - peak)
    total = jnp.sum(expanded, axis=-1, keepdims=True)
    probs = (expanded / total).astype(BF16)
    mixed = jnp.einsum("tghlm,tgmhe->tglhe", probs, v, preferred_element_type=F32)
    return mixed.astype(BF16), peak + jnp.log(total)


def attend_backward(heads, log_total, grad_mixed, factor):
    q, k, v = heads[:, :, :, 0], heads[:, :, :, 1], heads[:, :, :, 2]
    scores = jnp.einsum("tglhe,tgmhe->tghlm", q, k, preferred_element_type=F32) * factor
    probs = jnp.exp(scores - log_total)
    grad_v = jnp.einsum(
        "tghlm,tglhe->tgmhe", probs.astype(BF16), grad_mixed, preferred_element_type=F32
    )
    grad_probs = jnp.einsum("tglhe,tgmhe->tghlm", grad_mixed, v, preferred_element_type=F32)
    inner = jnp.sum(grad_probs * probs, axis=-1, keepdims=True)
    grad_scores = (probs * (grad_probs - inner)).astype(BF16)
    grad_q = jnp.einsum("tghlm,tgmhe->tglhe", grad_scores, k, preferred_element_type=F32) * factor
    grad_k = jnp.einsum("tghlm,tglhe->tgmhe", grad_scores, q, preferred_element_type=F32) * factor
    return jnp.stack([grad_q, grad_k, grad_v], axis=3).astype(BF16)


def block_forward(stream, modulation, weights, group):
    attn, up, down = weights
    blocks, width, cols = attn.shape
    inner = cols // 4 * 3
    head_count = cols // 4 // HEAD_DIM
    clips, per_clip, _ = stream.shape
    tokens = clips * per_clip
    factor = HEAD_DIM**-0.5

    def column(i):
        return modulation[:, i][:, None, :]

    normed_a, inverse_a = normalize(stream)
    hidden_a = (normed_a * (1.0 + column(1)) + column(0)).astype(BF16).reshape(tokens, width)
    triple = jnp.stack([dot(hidden_a, attn[t, :, :inner]).astype(BF16) for t in range(blocks)])
    heads = triple.reshape(blocks, tokens // group, group, 3, head_count, HEAD_DIM)
    mixed, log_total = attend_forward(heads, factor)
    mixed = mixed.reshape(blocks, tokens, cols // 4)
    branch_a = sum(dot_t(mixed[t], attn[t, :, inner:]) for t in range(blocks)).reshape(stream.shape)
    middle = stream + column(2) * branch_a
    normed_b, inverse_b = normalize(middle)
    hidden_b = (normed_b * (1.0 + column(4)) + column(3)).astype(BF16).reshape(tokens, width)
    pre_act = jnp.stack([dot(hidden_b, up[t]) for t in range(blocks)])
    activated = gelu_tanh(pre_act).astype(BF16)
    branch_b = sum(dot_t(activated[t], down[t]) for t in range(blocks)).reshape(stream.shape)
    output = middle + column(5) * branch_b
    saved = (
        normed_a, inverse_a, hidden_a, heads, log_total, mixed, branch_a,
        normed_b, inverse_b, hidden_b, pre_act, activated, branch_b,
    )
    return output, saved


def block_backward(grad, modulation, weights, saved, group):
    attn, up, down = weights
    blocks, width, cols = attn.shape
    inner = cols // 4 * 3
    head_count = cols // 4 // HEAD_DIM
    (
        normed_a, inverse_a, hidden_a, heads, log_total, mixed, branch_a,
        normed_b, inverse_b, hidden_b, pre_act, activated, branch_b,
    ) = saved
    tokens = hidden_a.shape[0]
    factor = HEAD_DIM**-0.5

    def column(i):
        return modulation[:, i][:, None, :]

    def clip_sum(values):
        return jnp.sum(values, axis=1)

    gate_b = clip_sum(grad * branch_b)
    branch_grad_b = (grad * column(5)).astype(BF16).reshape(tokens, width)
    grad_act = jnp.stack([dot(branch_grad_b, down[t]) for t in range(blocks)])
    grad_pre = jax.vjp(gelu_tanh, pre_act)[1](grad_act)[0].astype(BF16)
    grad_hidden_b = sum(dot_t(grad_pre[t], up[t]) for t in range(blocks)).reshape(grad.shape)
    shift_b = clip_sum(grad_hidden_b)
    scale_b = clip_sum(grad_hidden_b * normed_b)
    grad_middle = grad + norm_backward(grad_hidden_b * (1.0 + column(4)), normed_b, inverse_b)
    gate_a = clip_sum(grad_middle * branch_a)
    branch_grad_a = (grad_middle * column(2)).astype(BF16).reshape(tokens, width)
    grad_mixed = jnp.stack(
        [dot(branch_grad_a, attn[t, :, inner:]).astype(BF16) for t in range(blocks)]
    )
    grad_mixed = grad_mixed.reshape(blocks, tokens // group, group, head_count, HEAD_DIM)
    grad_heads = attend_backward(heads, log_total, grad_mixed, factor)
    grad_triple = grad_heads.reshape(blocks, tokens, inner)
    grad_hidden_a = sum(
        dot_t(grad_triple[t], attn[t, :, :inner]) for t in range(blocks)
    ).reshape(grad.shape)
    shift_a = clip_sum(grad_hidden_a)
    scale_a = clip_sum(grad_hidden_a * normed_a)
    grad_input = grad_middle + norm_backward(
        grad_hidden_a * (1.0 + column(1)), normed_a, inverse_a
    )
    grad_modulation = jnp.stack([shift_a, scale_a, gate_a, shift_b, scale_b, gate_b], axis=1)
    x_list = [hidden_a, branch_grad_a, hidden_b, branch_grad_b]
    g_list = [jnp.concatenate([grad_triple, mixed], axis=2), grad_pre, activated]
    return grad_input, grad_modulation, x_list, g_list


def local(
    latents, condition, teacher, valid_mask,
    qkv_weight, out_weight, up_weight, down_weight, ada_weight,
):
    n_dp, n_seq, n_tensor = (lax.axis_size(a) for a in ("dp", "seq", "tensor"))
    fast = n_dp == 4 and n_seq == 2 and n_tensor == 4
    clips, frames, patches, width = latents.shape
    rows = ada_weight.shape[1]
    blocks = qkv_weight.shape[0]
    heads_width = qkv_weight.shape[3]
    inner = 3 * heads_width
    dp, seq, tensor = (lax.axis_index(a) for a in ("dp", "seq", "tensor"))
    row_block = dp * n_seq + seq

    shards = []
    for b in range(blocks):
        shards.append(jnp.concatenate([qkv_weight[b].reshape(rows, inner), out_weight[b].T], axis=1))
        shards.append(up_weight[b])
        shards.append(down_weight[b].T)
    shards = jnp.stack(shards)
    if fast:
        full = gather_weights(shards, n_tensor)
        full = full.reshape(shards.shape[0], n_tensor, width, shards.shape[2])
    else:
        full = lax.all_gather(shards, ("dp", "seq"), axis=1, tiled=True)
        full = lax.all_gather(full, "tensor", axis=1)
    weights = [(full[3 * b], full[3 * b + 1], full[3 * b + 2]) for b in range(blocks)]

    cond_float = condition.astype(F32)
    all_cond = lax.all_gather(condition, "dp", axis=0, tiled=True).astype(F32)
    all_silu = jax.nn.silu(all_cond).astype(BF16)
    silu_rows = lax.dynamic_slice_in_dim(all_silu, row_block * rows, rows, axis=1)
    partial_mod = jnp.einsum("cd,bdke->cbke", silu_rows, ada_weight, preferred_element_type=F32)
    partial_mod = lax.psum_scatter(partial_mod, "dp", scatter_dimension=0, tiled=True)
    partial_mod = lax.psum(partial_mod, "seq")
    modulation = lax.all_gather(partial_mod, "tensor", axis=3, tiled=True)

    by_frame = frames % n_tensor == 0
    split_axis = 1 if by_frame else 0

    def to_spatial(v):
        return lax.all_to_all(v, "tensor", split_axis=split_axis, concat_axis=2, tiled=True)

    def from_spatial(v):
        return lax.all_to_all(v, "tensor", split_axis=2, concat_axis=split_axis, tiled=True)

    def to_temporal(v):
        return lax.all_to_all(v, "seq", split_axis=2, concat_axis=1, tiled=True)

    def from_temporal(v):
        return lax.all_to_all(v, "seq", split_axis=1, concat_axis=2, tiled=True)

    own_clips = clips if by_frame else clips // n_tensor
    first_clip = 0 if by_frame else tensor * own_clips
    spatial_mod = lax.dynamic_slice_in_dim(modulation[:, 0], first_clip, own_clips, axis=0)
    temporal_mod = modulation[:, 1]

    def patch_major(v):
        return v.transpose(0, 2, 1, 3)

    spatial = to_spatial(latents)
    spatial_shape = spatial.shape
    stream = spatial.astype(F32).reshape(own_clips, -1, width)
    stream, saved_0 = block_forward(stream, spatial_mod, weights[0], spatial_shape[2])
    moved = to_temporal(from_spatial(stream.astype(BF16).reshape(spatial_shape)))
    temporal_shape = moved.shape
    stream = patch_major(moved).astype(F32).reshape(clips, -1, width)
    stream, saved_1 = block_forward(stream, temporal_mod, weights[1], temporal_shape[1])

    def to_frames(v):
        return patch_major(
            v.reshape(clips, temporal_shape[2], temporal_shape[1], width)
        )

    block_out = from_temporal(to_frames(stream.astype(BF16)))

    teacher_rows = patch_major(to_temporal(teacher)).astype(F32).reshape(clips, -1, width)
    mask_float = valid_mask.astype(F32)
    own_mask = lax.dynamic_slice_in_dim(
        mask_float, seq * temporal_shape[2], temporal_shape[2], axis=1
    )
    mask_rows = jnp.repeat(own_mask, temporal_shape[1], axis=1)[:, :, None]
    error = stream - teacher_rows
    error_sum = lax.psum(jnp.sum(mask_rows * error * error), ("dp", "seq", "tensor"))
    total_frames = frames * n_seq
    valid_count = lax.psum(jnp.sum(mask_float), ("dp", "tensor")) * total_frames
    loss_value = error_sum / (width * valid_count)
    token_total = clips * frames * patches * n_dp * n_seq * n_tensor
    grad = mask_rows * error * (2.0 * token_total / valid_count)

    grad, mod_grad_1, x_1, g_1 = block_backward(
        grad, temporal_mod, weights[1], saved_1, temporal_shape[1]
    )
    moved = to_spatial(from_temporal(to_frames(grad.astype(BF16))))
    grad = moved.astype(F32).reshape(own_clips, -1, width)
    grad, mod_grad_0, x_0, g_0 = block_backward(
        grad, spatial_mod, weights[0], saved_0, spatial_shape[2]
    )
    grad_latents = from_spatial(grad.astype(BF16).reshape(spatial_shape)).astype(F32)

    x_list, g_list = x_0 + x_1, g_0 + g_1
    if fast:
        summed = reduce_weights(x_list, g_list, rows, n_tensor, inner)
    else:
        terms = []
        for b in range(blocks):
            for layer, q in ((0, 0), (1, 2), (2, 3)):
                term = jnp.einsum(
                    "nd,tnk->tdk", x_list[4 * b + q], g_list[3 * b + layer], preferred_element_type=F32
                )
                if layer == 0:
                    other = jnp.einsum(
                        "nd,tnk->tdk", x_list[4 * b + 1], g_list[3 * b], preferred_element_type=F32
                    )
                    term = jnp.where(jnp.arange(term.shape[2]) < inner, term, other)
                term = lax.psum_scatter(
                    term.astype(BF16), ("dp", "seq"), scatter_dimension=1, tiled=True
                )
                terms.append(lax.psum_scatter(term, "tensor", scatter_dimension=0, tiled=True)[0])
        summed = jnp.stack(terms)
    summed = summed.reshape(blocks, 3, rows, -1).astype(F32)
    grad_qkv = summed[:, 0, :, :inner].reshape(blocks, rows, 3, heads_width)
    grad_out = summed[:, 0, :, inner:].transpose(0, 2, 1)
    grad_up = summed[:, 1]
    grad_down = summed[:, 2].transpose(0, 2, 1)

    placed_0 = lax.dynamic_update_slice_in_dim(
        jnp.zeros((clips,) + mod_grad_0.shape[1:], F32), mod_grad_0, first_clip, axis=0
    )
    mod_grad = jnp.stack([placed_0, mod_grad_1], axis=1)
    mod_grad = lax.psum_scatter(mod_grad, "tensor", scatter_dimension=3, tiled=True)
    mod_grad = lax.psum(mod_grad, "seq")
    mod_grad = lax.all_gather(mod_grad, "dp", axis=0, tiled=True)
    grad_ada = jnp.einsum("cd,cbke->bdke", silu_rows.astype(F32), mod_grad, precision=HIGHEST)
    grad_silu = jnp.einsum("cbke,bdke->cd", mod_grad, ada_weight.astype(F32), precision=HIGHEST)
    grad_silu = lax.psum(grad_silu, "tensor")
    grad_silu = lax.all_gather(grad_silu, ("dp", "seq"), axis=1, tiled=True)
    grad_silu = lax.dynamic_slice_in_dim(grad_silu, dp * clips, clips, axis=0)
    grad_condition = jax.vjp(jax.nn.silu, cond_float)[1](grad_silu)[0]
    return (
        block_out, loss_value, grad_latents, grad_condition,
        grad_qkv, grad_out, grad_up, grad_down, grad_ada,
    )


def solution(mesh):
    return jax.shard_map(
        local,
        mesh=mesh,
        in_specs=(
            P("dp", "seq", "tensor", None),
            P("dp", None),
            P("dp", "seq", "tensor", None),
            P("dp", "tensor"),
            P(None, ("dp", "seq"), None, "tensor"),
            P(None, "tensor", ("dp", "seq")),
            P(None, ("dp", "seq"), "tensor"),
            P(None, "tensor", ("dp", "seq")),
            P(None, ("dp", "seq"), None, "tensor"),
        ),
        out_specs=(
            P("dp", "seq", "tensor", None),
            P(),
            P("dp", "seq", "tensor", None),
            P("dp", None),
            P(None, ("dp", "seq"), None, "tensor"),
            P(None, "tensor", ("dp", "seq")),
            P(None, ("dp", "seq"), "tensor"),
            P(None, "tensor", ("dp", "seq")),
            P(None, ("dp", "seq"), None, "tensor"),
        ),
        check_vma=False,
    )
```

```python
import functools

import jax
import jax.numpy as jnp
from jax import lax
from jax.experimental import pallas as pl
from jax.experimental.pallas import tpu as pltpu
from jax.sharding import PartitionSpec as P

DP, SEQ, TENSOR = "dp", "seq", "tensor"
START, SEND, RECV = range(3)
HEAD_DIM = 72
EPSILON = 1e-06
HIGHEST = lax.Precision.HIGHEST
MESH = pl.DeviceIdType.MESH
DMA = pltpu.SemaphoreType.DMA
BF16 = jnp.bfloat16
F32 = jnp.float32
ANY = pl.BlockSpec(memory_space=pl.ANY)
VM = pl.BlockSpec(memory_space=pltpu.VMEM)
LANES = 128
NEGATIVE = -1e30
GELU_C = 0.7978845608028654
GELU_K = 0.044715


def position():
    dp = lax.axis_index(DP)
    return dp // 2, dp % 2, lax.axis_index(SEQ), lax.axis_index(TENSOR)


def device(y, c, x, z):
    return (y * 2 + c, x, z)


def neighbours(nz):
    y, c, x, z = position()
    return (
        device(y, c, 1 - x, z),
        device(1 - y, c, x, z),
        device(y, 1 - c, x, z),
        device(y, c, x, jnp.maximum(z - 1, 0)),
        device(y, c, x, jnp.minimum(z + 1, nz - 1)),
    )


def remote(src, dst, send_sem, recv_sem, target):
    return pltpu.make_async_remote_copy(
        src_ref=src,
        dst_ref=dst,
        send_sem=send_sem,
        recv_sem=recv_sem,
        device_id=target,
        device_id_type=MESH,
    )


def in_plane(d):
    y, c, x, z = position()
    q = (y * 4 + c * 2 + x + d) % 8
    return (q // 2, q % 2, z), q


def across(d, nz):
    y, c, x, z = position()
    q = (x * nz + z + d) % (2 * nz)
    return (y * 2 + c, q // nz, q % nz), q


def over_z(d, nz):
    y, c, x, z = position()
    q = (z + d) % nz
    return device(y, c, x, q), q


def over_dp(d):
    y, c, x, z = position()
    q = (y * 2 + c + d) % 4
    return (q, x, z), q


def greet(peers):
    barrier = pltpu.get_barrier_semaphore()
    for target in peers:
        pl.semaphore_signal(barrier, inc=1, device_id=target, device_id_type=MESH)
    pl.semaphore_wait(barrier, len(peers))


def send_all(copies):
    for copy in copies:
        copy.start()


def finish_all(copies):
    for copy in copies:
        copy.wait_send()
        copy.wait_recv()


def gather_kernel(
    w_ref, lat_ref, teach_ref, cond_ref, count_ref, ada_ref,
    g_ref, spat_ref, teach_o, mod_o, silu_o,
    lsem, s_zab, r_zab, s_xy, r_xy, s_zcd, r_zcd, s_c, r_c,
    s_lat, r_lat, s_tea, r_tea, s_m, r_m, local_sem,
    ada, cond_all, parts, landed, mod_all, *, nz, ahead
):
    layers, rows, _ = w_ref.shape
    unit = rows // 9
    ab = 7 * unit
    y, c, x, z = position()
    x_dev, y_dev, core_dev, below, above = neighbours(nz)
    greet([in_plane(d)[0] for d in range(1, 8)] + [over_z(d, nz)[0] for d in range(1, nz)])
    own = []
    for l in range(layers):
        copy = pltpu.make_async_copy(w_ref.at[l], g_ref.at[l, z, y, c, x], lsem.at[l])
        copy.start()
        own.append(copy)

    def split(l):
        a = (4 if l % 2 == 0 else 3) * unit
        return pl.ds(0, a), pl.ds(a, ab - a), pl.ds(ab, unit), pl.ds(ab + unit, unit)

    def region_ab(l, t):
        return g_ref.at[l, t, y, c, x, pl.ds(0, ab)]

    def region_cd(l, t):
        return g_ref.at[l, t, :, c, :, pl.ds(ab, 2 * unit)]

    def along_z(l, hop, region, ssem, rsem, mode, first=None):
        up, down = z - hop, z + hop

        if mode == RECV:

            @pl.when(z - 1 - hop >= 0)
            def _():
                r = region(l, jnp.maximum(z - 1 - hop, 0))
                remote(r, r, ssem.at[l, hop, 1], rsem.at[l, hop, 1], above).wait_recv()

            @pl.when(z + 1 + hop < nz)
            def _():
                r = region(l, jnp.minimum(z + 1 + hop, nz - 1))
                remote(r, r, ssem.at[l, hop, 0], rsem.at[l, hop, 0], below).wait_recv()

            return

        @pl.when((up >= 0) & (z < nz - 1))
        def _():
            r = region(l, jnp.maximum(up, 0))
            src = first if first is not None and hop == 0 else r
            copy = remote(src, r, ssem.at[l, hop, 1], rsem.at[l, hop, 1], above)
            copy.start() if mode == START else copy.wait_send()

        @pl.when((down < nz) & (z > 0))
        def _():
            r = region(l, jnp.minimum(down, nz - 1))
            src = first if first is not None and hop == 0 else r
            copy = remote(src, r, ssem.at[l, hop, 0], rsem.at[l, hop, 0], below)
            copy.start() if mode == START else copy.wait_send()

    def region_xy(l, kind, yy, xx):
        a, b, cc, d = split(l)
        return (
            lambda: g_ref.at[l, :, yy, c, xx, a],
            lambda: g_ref.at[l, :, yy, c, xx, b],
            lambda: g_ref.at[l, :, yy, c, :, a],
            lambda: g_ref.at[l, :, :, c, xx, b],
            lambda: g_ref.at[l, z, yy, c, xx, cc],
            lambda: g_ref.at[l, z, yy, c, xx, d],
            lambda: g_ref.at[l, z, yy, c, :, cc],
            lambda: g_ref.at[l, z, :, c, xx, d],
        )[kind]()

    along_x = (True, False, False, True, True, False, False, True)

    def along_xy(l, kind, mode):
        target = x_dev if along_x[kind] else y_dev
        if mode == RECV:
            r = region_xy(l, kind, y, 1 - x) if along_x[kind] else region_xy(l, kind, 1 - y, x)
            remote(r, r, s_xy.at[l, kind], r_xy.at[l, kind], target).wait_recv()
            return
        r = region_xy(l, kind, y, x)
        src = r
        if kind == 4:
            src = w_ref.at[l, pl.ds(ab, unit)]
        if kind == 5:
            src = w_ref.at[l, pl.ds(ab + unit, unit)]
        copy = remote(src, r, s_xy.at[l, kind], r_xy.at[l, kind], target)
        copy.start() if mode == START else copy.wait_send()

    def to_core(l, mode):
        r = g_ref.at[l, :, :, c if mode != RECV else 1 - c]
        copy = remote(r, r, s_c.at[l], r_c.at[l], core_dev)
        if mode == START:
            copy.start()
        elif mode == SEND:
            copy.wait_send()
        else:
            copy.wait_recv()

    def z_ab(l, hop, mode):
        along_z(l, hop, region_ab, s_zab, r_zab, mode, first=w_ref.at[l, pl.ds(0, ab)])

    def z_cd(l, hop, mode):
        along_z(l, hop, region_cd, s_zcd, r_zcd, mode)

    def stage(l, s):
        if s == 0:
            z_ab(l, 0, START)
            along_xy(l, 4, START)
            along_xy(l, 5, START)
        if s == 1:
            z_ab(l, 0, RECV)
            z_ab(l, 1, START)
            own[l].wait()
            along_xy(l, 4, RECV)
            along_xy(l, 6, START)
            along_xy(l, 5, RECV)
            along_xy(l, 7, START)
        if s == 2:
            z_ab(l, 1, RECV)
            z_ab(l, 2, START)
            along_xy(l, 6, RECV)
            along_xy(l, 7, RECV)
            z_cd(l, 0, START)
        if s == 3:
            z_ab(l, 2, RECV)
            along_xy(l, 0, START)
            along_xy(l, 1, START)
            z_cd(l, 0, RECV)
            z_cd(l, 1, START)
        if s == 4:
            along_xy(l, 0, RECV)
            along_xy(l, 2, START)
            along_xy(l, 1, RECV)
            along_xy(l, 3, START)
            z_cd(l, 1, RECV)
            z_cd(l, 2, START)
        if s == 5:
            along_xy(l, 2, RECV)
            along_xy(l, 3, RECV)
            z_cd(l, 2, RECV)
            to_core(l, START)

    dp, block = y * 2 + c, (y * 2 + c) * 2 + x
    side = [
        pltpu.make_async_copy(lat_ref.at[z], spat_ref.at[:, z], local_sem.at[0]),
        pltpu.make_async_copy(teach_ref.at[:, x], teach_o.at[x], local_sem.at[1]),
        pltpu.make_async_copy(ada_ref, ada, local_sem.at[2]),
    ]
    moves = []
    for d in range(1, nz):
        target, q = over_z(d, nz)
        moves.append(remote(lat_ref.at[q], spat_ref.at[:, z], s_lat.at[d], r_lat.at[d], target))
    moves.append(remote(teach_ref.at[:, 1 - x], teach_o.at[x], s_tea, r_tea, x_dev))
    conds, sums, spread = [], [], []
    for d in range(1, 4):
        target, q = over_dp(d)
        conds.append(remote(cond_ref, cond_all.at[dp], s_m.at[0, d], r_m.at[0, d], target))
    for d in range(1, 8):
        target, q = in_plane(d)
        sums.append(remote(parts.at[q // 2], landed.at[d], s_m.at[1, d], r_m.at[1, d], target))
    for d in range(1, nz):
        target, q = over_z(d, nz)
        spread.append(remote(mod_all.at[z], mod_all.at[z], s_m.at[2, d], r_m.at[2, d], target))

    def modulate(step):
        if step == 0:
            send_all(conds)
            cond_all[dp] = cond_ref[...]
        if step == 1:
            finish_all(conds)
            side[2].wait()
            silu_o[...] = jnp.zeros_like(silu_o)
            for i in range(4):
                row = cond_all[i, pl.ds(block, 1), :]
                silu_o[i : i + 1, :] = (row / (1.0 + jnp.exp(-row))).astype(BF16).astype(F32)
            parts[...] = jnp.zeros_like(parts)
            for b in range(ada.shape[0]):
                for k in range(6):
                    got = kdot(silu_o[...].astype(BF16), ada[b, k])
                    for i in range(4):
                        parts[i, 6 * b + k : 6 * b + k + 1, :] = got[i : i + 1]
            for i in range(4):
                parts[i, 12:13, :] = count_ref[...]
            send_all(sums)
        if step == 2:
            finish_all(sums)
            total = parts[dp]
            for d in range(1, 8):
                total = total + landed[d]
            mod_all[z] = total
            send_all(spread)
        if step == 3:
            finish_all(spread)
            mod_o[...] = mod_all[...]

    for l in range(min(ahead, layers)):
        stage(l, 0)
    modulate(0)
    send_all(side)
    send_all(moves)
    for slot in range(layers + 5):
        if 1 <= slot <= 3:
            modulate(slot)
        for l in range(layers):
            s = slot - l
            if s == 0 and l + ahead < layers:
                stage(l + ahead, 0)
            if 1 <= s <= 5:
                stage(l, s)
    for l in range(layers):
        to_core(l, RECV)
        to_core(l, SEND)
        for kind in range(8):
            along_xy(l, kind, SEND)
        for hop in range(nz - 1):
            z_ab(l, hop, SEND)
            z_cd(l, hop, SEND)
    side[0].wait()
    side[1].wait()
    finish_all(moves)


def gather_weights(shards, latents, teacher, cond, count, ada, nz):
    layers, rows, cols = shards.shape
    hops = nz - 1
    sds = jax.ShapeDtypeStruct
    frames, patches, width = latents.shape[1:]
    _, halves, own_patches, _ = teacher.shape
    vmem = pltpu.VMEM
    mod_shape = (16, ada.shape[3])
    return pl.pallas_call(
        functools.partial(gather_kernel, nz=nz, ahead=2),
        out_shape=[
            sds((layers, nz, 2, 2, 2, rows, cols), BF16),
            sds((frames, nz, patches, width), BF16),
            sds((halves, teacher.shape[0], own_patches, width), BF16),
            sds((nz,) + mod_shape, F32),
            sds((8, cond.shape[1]), F32),
        ],
        in_specs=[ANY, ANY, ANY, VM, VM, ANY],
        out_specs=[ANY, ANY, ANY, VM, VM],
        scratch_shapes=[
            DMA((layers,)),
            DMA((layers, hops, 2)),
            DMA((layers, hops, 2)),
            DMA((layers, 8)),
            DMA((layers, 8)),
            DMA((layers, hops, 2)),
            DMA((layers, hops, 2)),
            DMA((layers,)),
            DMA((layers,)),
            DMA((nz,)),
            DMA((nz,)),
            DMA(()),
            DMA(()),
            DMA((3, 8)),
            DMA((3, 8)),
            DMA((3,)),
            vmem(ada.shape, BF16),
            vmem((4,) + cond.shape, F32),
            vmem((4,) + mod_shape, F32),
            vmem((8,) + mod_shape, F32),
            vmem((nz,) + mod_shape, F32),
        ],
        compiler_params=pltpu.CompilerParams(
            collective_id=0, has_side_effects=True, vmem_limit_bytes=16 << 20
        ),
        name="gather_weights",
    )(shards, latents, teacher, cond, count, ada)


STAGES = 7
SLOTS = 3
Y_A, X_A, X_B, Y_B, Y_C, X_C, X_D, Y_D = KINDS = tuple(range(8))


def reduce_kernel(*refs, chunks, n_x, n_g, split_at, nz, rows, width):
    x_refs, g_refs = refs[:n_x], refs[n_x : n_x + n_g]
    lat_ref, mod_ref, ada_ref = refs[n_x + n_g : n_x + n_g + 3]
    (
        o_ref, lat_o, mod_o, silu_o, acc, stg, prb, gbuf, xraw, xt, ya, xa, xb, yb, yc, xc, xd, yd, zab, zcd,
        gsem, xsem, osem, s_p, r_p, s_xy, r_xy, s_z, r_z,
        s_lat, r_lat, s_m, r_m, local_sem, ada, first, every, along, back, silus,
    ) = refs[n_x + n_g + 3 :]
    unit = rows // 9
    ab = 7 * unit
    count = len(chunks)
    y, c, x, z = position()
    x_dev, y_dev, core_dev, below, above = neighbours(nz)
    greet(
        [in_plane(d)[0] for d in range(1, 8)]
        + [
            (y * 2 + c, xx, (z + d) % nz)
            for d in range(1, nz)
            for xx in (x, 1 - x)
        ]
    )

    dp, block = y * 2 + c, (y * 2 + c) * 2 + x
    side = [
        pltpu.make_async_copy(lat_ref.at[:, z], lat_o.at[z], local_sem.at[0]),
        pltpu.make_async_copy(ada_ref, ada, local_sem.at[1]),
    ]
    moves, sums, spread, slices, rows_out = [], [], [], [], []
    for d in range(1, nz):
        target, q = over_z(d, nz)
        moves.append(remote(lat_ref.at[:, q], lat_o.at[z], s_lat.at[d], r_lat.at[d], target))
        slices.append(remote(along, back.at[d], s_m.at[2, d], r_m.at[2, d], target))
    for d in range(1, 2 * nz):
        target, q = across(d, nz)
        sums.append(remote(mod_ref.at[q % nz], first.at[d], s_m.at[0, d], r_m.at[0, d], target))
    for d in range(1, 4):
        target, q = over_dp(d)
        spread.append(remote(every.at[dp], every.at[dp], s_m.at[1, d], r_m.at[1, d], target))
    for d in range(1, 8):
        target, q = in_plane(d)
        rows_out.append(remote(silus.at[block], silus.at[block], s_m.at[3, d], r_m.at[3, d], target))

    def modulation(step):
        if step == 0:
            send_all(sums)
            send_all(side)
            send_all(moves)
        if step == 2:
            finish_all(sums)
            total = mod_ref[z]
            for d in range(1, 2 * nz):
                total = total + first[d]
            every[dp] = total
            send_all(spread)
        if step == 4:
            finish_all(spread)
            side[1].wait()
            mod_o[...] = every[...]
            total = jnp.zeros(along.shape, F32)
            for b in range(ada.shape[0]):
                for k in range(6):
                    i = 6 * b + k
                    got = jnp.concatenate([every[q, i : i + 1, :] for q in range(4)] * 2, axis=0)
                    high = got.astype(BF16)
                    rest = got - high.astype(F32)
                    middle = rest.astype(BF16)
                    lowest = (rest - middle.astype(F32)).astype(BF16)
                    for part in (high, middle, lowest):
                        total = total + kdot_t(part, ada[b, k])
            along[...] = total
            send_all(slices)
        if step == 7:
            finish_all(slices)
            total = along[...]
            for d in range(1, nz):
                total = total + back[d]
            silus[block] = total
            send_all(rows_out)
        if step == 10:
            finish_all(rows_out)
            for q in range(8):
                silu_o[q : q + 1, :] = silus[q, pl.ds(dp, 1), :]

    def add_in(dst, src):
        lead = dst.shape[:-2]
        total = 1
        for v in lead:
            total *= v
        if total == 1:
            dst[...] = dst[...] + src[...]
            return

        def body(i, carry):
            index = []
            rest = i
            for v in reversed(lead):
                index.append(rest % v)
                rest = rest // v
            index = tuple(reversed(index))
            dst[index] = dst[index] + src[index]
            return carry

        lax.fori_loop(0, total, body, 0)

    def exchange(k, kind, mode):
        a = (4 if k % 2 == 0 else 3) * unit
        b = ab - a
        ra, rb, rc, rd = pl.ds(0, a), pl.ds(a, b), pl.ds(ab, unit), pl.ds(ab + unit, unit)
        m = k % SLOTS
        part = acc.at[k % STAGES]
        src, buf, target, dst = {
            Y_A: lambda: (part.at[:, 1 - y, :, ra], ya.at[m, :, :, pl.ds(0, a)], y_dev, part.at[:, y, :, ra]),
            X_A: lambda: (part.at[:, y, 1 - x, ra], xa.at[m, :, pl.ds(0, a)], x_dev, part.at[:, y, x, ra]),
            X_B: lambda: (part.at[:, :, 1 - x, rb], xb.at[m, :, :, pl.ds(0, b)], x_dev, part.at[:, :, x, rb]),
            Y_B: lambda: (part.at[:, 1 - y, x, rb], yb.at[m, :, pl.ds(0, b)], y_dev, part.at[:, y, x, rb]),
            Y_C: lambda: (part.at[z, 1 - y, :, rc], yc.at[m], y_dev, part.at[z, y, :, rc]),
            X_C: lambda: (part.at[z, y, 1 - x, rc], xc.at[m], x_dev, part.at[z, y, x, rc]),
            X_D: lambda: (part.at[z, :, 1 - x, rd], xd.at[m], x_dev, part.at[z, :, x, rd]),
            Y_D: lambda: (part.at[z, 1 - y, x, rd], yd.at[m], y_dev, part.at[z, y, x, rd]),
        }[kind]()
        i = kind
        copy = remote(src, buf, s_xy.at[k % STAGES, i], r_xy.at[m, i], target)
        if mode == START:
            copy.start()
        elif mode == SEND:
            copy.wait_send()
        else:
            copy.wait_recv()
            add_in(dst, buf)

    def region_z(k, t, which):
        part = acc.at[k % STAGES, t]
        return part.at[y, x, pl.ds(0, ab)] if which == 0 else part.at[:, :, pl.ds(ab, 2 * unit)]

    def along_z(k, hop, which, mode):
        m, n = k % SLOTS, k % STAGES
        landing = (zab, zcd)[which]
        t_down, t_up = hop - (nz - 1 - z), nz - 1 - (hop - z)
        if mode != RECV:

            @pl.when((t_down >= 0) & (z > 0))
            def _():
                copy = remote(
                    region_z(k, jnp.maximum(t_down, 0), which), landing.at[m, hop, 0],
                    s_z.at[n, which, hop, 0], r_z.at[m, which, hop, 0], below,
                )
                copy.start() if mode == START else copy.wait_send()

            @pl.when((hop >= z) & (z < nz - 1))
            def _():
                copy = remote(
                    region_z(k, jnp.minimum(t_up, nz - 1), which), landing.at[m, hop, 1],
                    s_z.at[n, which, hop, 1], r_z.at[m, which, hop, 1], above,
                )
                copy.start() if mode == START else copy.wait_send()

            return
        from_above, from_below = t_down + 1, t_up - 1

        @pl.when((from_above >= 0) & (z < nz - 1))
        def _():
            buf = landing.at[m, hop, 0]
            remote(buf, buf, s_z.at[n, which, hop, 0], r_z.at[m, which, hop, 0], below).wait_recv()
            add_in(region_z(k, jnp.maximum(from_above, 0), which), buf)

        @pl.when((hop >= z - 1) & (z > 0))
        def _():
            buf = landing.at[m, hop, 1]
            remote(buf, buf, s_z.at[n, which, hop, 1], r_z.at[m, which, hop, 1], above).wait_recv()
            add_in(region_z(k, jnp.minimum(from_below, nz - 1), which), buf)

    def pair(k, mode):
        m = k % 2
        copy = remote(stg.at[m], prb.at[m], s_p.at[m], r_p.at[m], core_dev)
        if mode == START:
            copy.start()
        elif mode == SEND:
            copy.wait_send()
        else:
            copy.wait_recv()
            add_in(acc.at[k % STAGES], prb.at[m])

    def load_g(k):
        layer, col, _ = chunks[k]
        return pltpu.make_async_copy(
            g_refs[layer].at[:, :, pl.ds(col * width, width)], gbuf.at[k % 2], gsem.at[k % 2]
        )

    order = []
    for _, _, used in chunks:
        for q in used:
            if q not in order:
                order.append(q)

    def load_x(i):
        return pltpu.make_async_copy(x_refs[order[i]], xraw.at[i % 2], xsem.at[i % 2])

    ready = [0]

    def turned(q):
        i = order.index(q)
        if i >= ready[0]:
            load_x(i).wait()
            for j in range(xraw.shape[2] // 128):
                xt[i % 3, pl.ds(j * 128, 128), :] = xraw[i % 2, :, pl.ds(j * 128, 128)].T
            ready[0] += 1
            if i + 2 < len(order):
                load_x(i + 2).start()
        return i % 3

    def multiply(k):
        _, _, used = chunks[k]
        slots = [turned(q) for q in used]
        if k + 1 < count:
            load_g(k + 1).start()
        load_g(k).wait()

        def fill(dst, core):
            def body(i, carry):
                t, yy = i // 2, i % 2
                at = pl.ds(pl.multiple_of((yy * 4 + core * 2) * rows, 16), 2 * rows)
                g = gbuf[k % 2, t]
                r = jnp.dot(xt[slots[0], at, :], g, preferred_element_type=F32)
                if len(slots) == 2:
                    second = jnp.dot(xt[slots[1], at, :], g, preferred_element_type=F32)
                    col = lax.broadcasted_iota(jnp.int32, r.shape, 1)
                    r = jnp.where(col < split_at, r, second)
                r = r.astype(BF16)
                dst[t, yy, 0] = r[:rows]
                dst[t, yy, 1] = r[rows:]
                return carry

            lax.fori_loop(0, nz * 2, body, 0)

        fill(stg.at[k % 2], 1 - c)
        pair(k, START)
        fill(acc.at[k % STAGES], c)

    def hand_out(k):
        layer, col, _ = chunks[k]
        return pltpu.make_async_copy(
            acc.at[k % STAGES, z, y, x],
            o_ref.at[layer, :, pl.ds(col * width, width)],
            osem.at[k % STAGES],
        )

    def stage(k, s):
        if s == 0:
            if k >= STAGES:
                hand_out(k - STAGES).wait()
            multiply(k)
        if s == 1:
            pair(k, SEND)
            pair(k, RECV)
            exchange(k, Y_A, START)
            exchange(k, X_B, START)
            along_z(k, 0, 1, START)
        if s == 2:
            along_z(k, 0, 1, RECV)
            along_z(k, 1, 1, START)
            exchange(k, Y_A, RECV)
            exchange(k, X_A, START)
            exchange(k, X_B, RECV)
            exchange(k, Y_B, START)
        if s == 3:
            along_z(k, 1, 1, RECV)
            along_z(k, 2, 1, START)
            exchange(k, X_A, RECV)
            exchange(k, Y_B, RECV)
            along_z(k, 0, 0, START)
        if s == 4:
            along_z(k, 0, 0, RECV)
            along_z(k, 1, 0, START)
            along_z(k, 2, 1, RECV)
            exchange(k, Y_C, START)
            exchange(k, X_D, START)
        if s == 5:
            along_z(k, 1, 0, RECV)
            along_z(k, 2, 0, START)
            exchange(k, Y_C, RECV)
            exchange(k, X_C, START)
            exchange(k, X_D, RECV)
            exchange(k, Y_D, START)
        if s == 6:
            along_z(k, 2, 0, RECV)
            exchange(k, X_C, RECV)
            exchange(k, Y_D, RECV)
            for kind in KINDS:
                exchange(k, kind, SEND)
            for hop in range(nz - 1):
                along_z(k, hop, 0, SEND)
                along_z(k, hop, 1, SEND)
            hand_out(k).start()

    load_x(0).start()
    load_x(1).start()
    load_g(0).start()
    for slot in range(count + STAGES - 1):
        modulation(slot)
        for s in range(STAGES - 1, -1, -1):
            if 0 <= slot - s < count:
                stage(slot - s, s)
    for k in range(max(0, count - STAGES), count):
        hand_out(k).wait()
    side[0].wait()
    finish_all(moves)


def reduce_weights(x_list, g_list, grad_latents, mod_grad, ada, rows, nz, split_at):
    tokens, cols = x_list[0].shape
    width = cols // 3
    unit = rows // 9
    chunks = []
    for block in (1, 0):
        for layer, used in ((2, (3,)), (1, (2,)), (0, (0, 1))):
            for col in range(3):
                ids = tuple(4 * block + q for q in used)
                if layer == 0 and (col + 1) * width <= split_at:
                    ids = ids[:1]
                chunks.append((3 * block + layer, col, ids))
    vmem = pltpu.VMEM
    hops = nz - 1
    scratch = [
        vmem((STAGES, nz, 2, 2, rows, width), BF16),
        vmem((2, nz, 2, 2, rows, width), BF16),
        vmem((2, nz, 2, 2, rows, width), BF16),
        vmem((2, nz, tokens, width), BF16),
        vmem((2, tokens, cols), BF16),
        vmem((3, cols, tokens), BF16),
        vmem((SLOTS, nz, 2, 4 * unit, width), BF16),
        vmem((SLOTS, nz, 4 * unit, width), BF16),
        vmem((SLOTS, nz, 2, 4 * unit, width), BF16),
        vmem((SLOTS, nz, 4 * unit, width), BF16),
        vmem((SLOTS, 2, unit, width), BF16),
        vmem((SLOTS, unit, width), BF16),
        vmem((SLOTS, 2, unit, width), BF16),
        vmem((SLOTS, unit, width), BF16),
        vmem((SLOTS, hops, 2, 7 * unit, width), BF16),
        vmem((SLOTS, hops, 2, 2, 2, 2 * unit, width), BF16),
        DMA((2,)),
        DMA((2,)),
        DMA((STAGES,)),
        DMA((2,)),
        DMA((2,)),
        DMA((STAGES, 8)),
        DMA((SLOTS, 8)),
        DMA((STAGES, 2, hops, 2)),
        DMA((SLOTS, 2, hops, 2)),
        DMA((nz,)),
        DMA((nz,)),
        DMA((4, 8)),
        DMA((4, 8)),
        DMA((2,)),
        vmem(ada.shape, BF16),
        vmem((2 * nz,) + mod_grad.shape[1:], F32),
        vmem((4,) + mod_grad.shape[1:], F32),
        vmem((8, rows), F32),
        vmem((nz, 8, rows), F32),
        vmem((8, 8, rows), F32),
    ]
    sds = jax.ShapeDtypeStruct
    frames, _, patches, lat_width = grad_latents.shape
    return pl.pallas_call(
        functools.partial(
            reduce_kernel,
            chunks=chunks,
            n_x=len(x_list),
            n_g=len(g_list),
            split_at=split_at - 2 * width,
            nz=nz,
            rows=rows,
            width=width,
        ),
        out_shape=[
            sds((len(g_list), rows, cols), BF16),
            sds((nz, frames, patches, lat_width), BF16),
            sds((4,) + mod_grad.shape[1:], F32),
            sds((8, rows), F32),
        ],
        in_specs=[ANY] * (len(x_list) + len(g_list)) + [ANY, VM, ANY],
        out_specs=[ANY, ANY, VM, VM],
        scratch_shapes=scratch,
        compiler_params=pltpu.CompilerParams(
            collective_id=1, has_side_effects=True, vmem_limit_bytes=60 << 20
        ),
        name="reduce_weights",
    )(*x_list, *g_list, grad_latents, mod_grad, ada)


def kdot(a, b):
    return jnp.dot(a, b, preferred_element_type=F32)
def kdot_t(a, b):
    return lax.dot_general(a, b, (((1,), (1,)), ((), ())), preferred_element_type=F32)
def kdot_l(a, b):
    return lax.dot_general(a, b, (((0,), (0,)), ((), ())), preferred_element_type=F32)

class Windows:
    def __init__(self, hw):
        self.hw = hw
        self.start = [i * hw // LANES * LANES for i in range(4)]
        self.off = [i * hw - s for i, s in enumerate(self.start)]
        self.width = -(-(max(self.off) + hw) // LANES) * LANES
        self.qkv = self.start[2] + self.width
        self.heads = hw // HEAD_DIM
    def head_mask(self, which, h):
        lane = lax.broadcasted_iota(jnp.int32, (1, self.width), 1) - self.off[which] - h * HEAD_DIM
        return (lane >= 0) & (lane < HEAD_DIM)
    def span_mask(self, which):
        lane = lax.broadcasted_iota(jnp.int32, (1, self.width), 1) - self.off[which]
        return (lane >= 0) & (lane < self.hw)

def column_loop(total, body, tile=256):
    full = total // tile
    if full:
        def step(j, carry):
            body(pl.multiple_of(j * tile, tile), tile)
            return carry
        lax.fori_loop(0, full, step, 0)
    if total % tile:
        body(full * tile, total % tile)

def row_loop(total, step, body):
    def go(i, carry):
        body(pl.ds(pl.multiple_of(i * step, step), step))
        return carry
    lax.fori_loop(0, total // step, go, 0)

def normed_of(v):
    center = v - jnp.mean(v, axis=-1, keepdims=True)
    inverse = lax.rsqrt(jnp.mean(center * center, axis=-1, keepdims=True) + EPSILON)
    return center * inverse, inverse

def gelu_parts(u):
    inner = GELU_C * (u + GELU_K * u * u * u)
    return jnp.tanh(inner)

def order_matrix(tokens, group, back):
    per = tokens // group
    row = lax.broadcasted_iota(jnp.int32, (tokens, tokens), 1 if back else 0)
    col = lax.broadcasted_iota(jnp.int32, (tokens, tokens), 0 if back else 1)
    return (col == row % group * per + row // group).astype(F32).astype(BF16)

def reorder(dst, src, order):
    def tile(c0, n):
        dst[:, pl.ds(c0, n)] = kdot(order[...], src[:, pl.ds(c0, n)]).astype(BF16)
    column_loop(src.shape[1], tile)

def forward_kernel(xin_ref, mod_ref, w_ref, out_ref, x_o, hida_o, qkv_o, prob_o, mix_o, bra_o, mid_o, hidb_o, pre_o, act_o, brb_o,
                   wbuf, xbuf, perm, acc, qkv, kst, vst, sc, wsem, osem, hida, prob, mix, hidb, pre, act, mid, bra, brb, *, layer, group, sub, win):
    nt = w_ref.shape[1]; tokens, width = xin_ref.shape
    depth = wbuf.shape[0]
    order = [(0, t) for t in range(nt)] + [(l, t) for t in range(nt) for l in (1, 2)]
    n_w = len(order)
    def wcopy(i):
        l, t = order[i]
        return pltpu.make_async_copy(w_ref.at[layer + l, t], wbuf.at[i % depth], wsem.at[i % depth])
    for i in range(depth): wcopy(i).start()
    outs = []
    def emit(src, dst, n):
        c = pltpu.make_async_copy(src, dst, osem.at[n]); c.start(); outs.append(c)
    mod = lambda i: mod_ref[i:i+1, :]
    factor = HEAD_DIM ** -0.5
    x_ref = xin_ref
    if sub is not None:
        perm[...] = order_matrix(tokens, sub, False)
        reorder(xbuf, xin_ref, perm)
        x_ref = xbuf
        emit(xbuf, x_o, 10)
    def ln_a(r):
        v = x_ref[r, :].astype(F32)
        n, _ = normed_of(v)
        hida[r, :] = (n * (1.0 + mod(1)) + mod(0)).astype(BF16)
        acc[r, :] = jnp.zeros_like(v)
    row_loop(tokens, 32, ln_a)
    emit(hida, hida_o, 0)
    kmask = [win.head_mask(1, h).astype(BF16) for h in range(win.heads)]
    vmask = [win.head_mask(2, h).astype(BF16) for h in range(win.heads)]
    for t in range(nt):
        wcopy(t).wait()
        w = wbuf.at[t % depth]
        def qkv_tile(c0, n):
            qkv[t, :, pl.ds(c0, n)] = kdot(hida[...], w[:, pl.ds(c0, n)]).astype(BF16)
        column_loop(win.qkv, qkv_tile)
        def one_group(g, carry):
            r = pl.ds(pl.multiple_of(g * group, group), group)
            q = pltpu.roll(qkv[t, r, pl.ds(0, win.width)].astype(F32), win.off[1], 1).astype(BF16)
            k = qkv[t, r, pl.ds(win.start[1], win.width)]
            v = qkv[t, r, pl.ds(win.start[2], win.width)]
            for h in range(win.heads):
                kst[pl.ds(h * group, group), :] = k * kmask[h]
                vst[pl.ds(h * group, group), :] = v * vmask[h]
            sc[...] = kdot_t(q, kst[...])
            def soft(i, c2):
                rr = pl.ds(pl.multiple_of(i * 32, 32), 32)
                for h in range(win.heads):
                    hs = pl.ds(h * group, group)
                    s = sc[rr, hs] * factor
                    if sub is not None:
                        ra = (lax.broadcasted_iota(jnp.int32, s.shape, 0) + i * 32) // sub
                        ca = lax.broadcasted_iota(jnp.int32, s.shape, 1) // sub
                        s = jnp.where(ra == ca, s, NEGATIVE)
                    e = jnp.exp(s - jnp.max(s, axis=-1, keepdims=True))
                    p = e * (1.0 / jnp.sum(e, axis=-1, keepdims=True))
                    prob[t, g, rr, hs] = p.astype(BF16)
                return c2
            lax.fori_loop(0, group // 32, soft, 0)
            m = kdot(prob[t, g], vst[...])
            mix[t, r, :] = pltpu.roll(m, win.off[3] - win.off[2], 1).astype(BF16)
            return carry
        lax.fori_loop(0, tokens // group, one_group, 0)
        def out_tile(c0, n):
            acc[:, pl.ds(c0, n)] += kdot_t(mix[t], w[pl.ds(c0, n), pl.ds(win.start[3], win.width)])
        column_loop(width, out_tile)
        if t + depth < n_w: wcopy(t + depth).start()
    emit(qkv, qkv_o, 1); emit(prob, prob_o, 2); emit(mix, mix_o, 3)
    def ln_b(r):
        b = acc[r, :]
        m = x_ref[r, :].astype(F32) + mod(2) * b
        mid[r, :] = m
        bra[r, :] = b.astype(BF16)
        n, _ = normed_of(m)
        hidb[r, :] = (n * (1.0 + mod(4)) + mod(3)).astype(BF16)
        acc[r, :] = jnp.zeros_like(m)
    row_loop(tokens, 32, ln_b)
    emit(bra, bra_o, 4); emit(mid, mid_o, 5); emit(hidb, hidb_o, 6)
    for t in range(nt):
        i = nt + 2 * t
        wcopy(i).wait()
        w = wbuf.at[i % depth]
        def up_tile(c0, n):
            u = kdot(hidb[...], w[:, pl.ds(c0, n)])
            pre[t, :, pl.ds(c0, n)] = u.astype(BF16)
            act[t, :, pl.ds(c0, n)] = (0.5 * u * (1.0 + gelu_parts(u))).astype(BF16)
        column_loop(width, up_tile)
        if i + depth < n_w: wcopy(i + depth).start()
        i += 1
        wcopy(i).wait()
        w2 = wbuf.at[i % depth]
        def down_tile(c0, n):
            acc[:, pl.ds(c0, n)] += kdot_t(act[t], w2[pl.ds(c0, n), :])
        column_loop(width, down_tile)
        if i + depth < n_w: wcopy(i + depth).start()
    emit(pre, pre_o, 7); emit(act, act_o, 8)
    def last(r):
        b = acc[r, :]
        brb[r, :] = b.astype(BF16)
        out_ref[r, :] = (mid[r, :] + mod(5) * b).astype(out_ref.dtype)
    row_loop(tokens, 32, last)
    emit(brb, brb_o, 9)
    if sub is None:
        xbuf[...] = jnp.zeros_like(xbuf)
        emit(xbuf, x_o, 10)
    for c in outs: c.wait()

def forward_call(x, mod, w, layer, group, sub, out_dtype, name):
    tokens, width = x.shape
    nt, cols = w.shape[1], w.shape[3]
    win = Windows(cols // 4)
    ng = tokens // group
    V = pltpu.VMEM
    sds = jax.ShapeDtypeStruct
    side = tokens if sub is not None else 16
    saved = [sds((side, width), BF16), sds((tokens, width), BF16), sds((nt, tokens, win.qkv), BF16), sds((nt, ng, group, win.heads * group), BF16),
             sds((nt, tokens, win.width), BF16), sds((tokens, width), BF16), sds((tokens, width), F32), sds((tokens, width), BF16),
             sds((nt, tokens, cols), BF16), sds((nt, tokens, cols), BF16), sds((tokens, width), BF16)]
    scratch = [V((3, width, cols), BF16), V((side, width), BF16), V((side, side), BF16), V((tokens, width), F32), V((nt, tokens, win.qkv), BF16),
               V((win.heads * group, win.width), BF16), V((win.heads * group, win.width), BF16), V((group, win.heads * group), F32),
               DMA((3,)), DMA((11,)),
               V((tokens, width), BF16), V((nt, ng, group, win.heads * group), BF16), V((nt, tokens, win.width), BF16), V((tokens, width), BF16),
               V((nt, tokens, cols), BF16), V((nt, tokens, cols), BF16), V((tokens, width), F32), V((tokens, width), BF16), V((tokens, width), BF16)]
    return pl.pallas_call(functools.partial(forward_kernel, layer=layer, group=group, sub=sub, win=win),
        out_shape=[sds((tokens, width), out_dtype)] + saved,
        in_specs=[VM, VM, ANY], out_specs=[VM] + [ANY] * 11, scratch_shapes=scratch,
        compiler_params=pltpu.CompilerParams(vmem_limit_bytes=62 << 20), name=name,
        cost_estimate=pl.CostEstimate(flops=2*tokens*width*cols*12, bytes_accessed=60<<20, transcendentals=0))(x, mod, w)

def backward_kernel(*refs, layer, group, sub, win, loss):
    refs = list(refs)
    if loss:
        final_ref, teach_ref, mask_ref, coef_ref = refs[:4]; del refs[:4]
    else:
        gin_ref = refs.pop(0)
    (x_ref, mod_ref, w_ref, qkv_ref, prob_ref, mix_ref, bra_ref, mid_ref, pre_ref, brb_ref) = refs[:10]
    del refs[:10]
    if loss:
        bout_ref, err_ref = refs[:2]; del refs[:2]
    (gout_ref, mg_ref, gba_o, gbb_o, gat_o, gpre_o,
     wbuf, wsem, gr, acc, gbb, gba, gpre, gat, dmx, dqkv, kst, vst, sc, ds, pbuf, preb, lsem, osem, tbuf, perm) = refs
    nt = w_ref.shape[1]; tokens, width = x_ref.shape
    depth = wbuf.shape[0]
    order = [(l, t) for t in range(nt) for l in (2, 1)] + [(0, t) for t in range(nt)]
    n_w = len(order)
    def wcopy(i):
        l, t = order[i]
        return pltpu.make_async_copy(w_ref.at[layer + l, t], wbuf.at[i % depth], wsem.at[i % depth])
    for i in range(depth): wcopy(i).start()
    def precopy(t): return pltpu.make_async_copy(pre_ref.at[t], preb.at[t % 2], lsem.at[t % 2])
    precopy(0).start(); precopy(1).start()
    qc = pltpu.make_async_copy(qkv_ref, dqkv, lsem.at[2]); qc.start()
    pc = pltpu.make_async_copy(prob_ref, pbuf, lsem.at[3]); pc.start()
    outs = []
    def emit(src, dst, n):
        c = pltpu.make_async_copy(src, dst, osem.at[n]); c.start(); outs.append(c)
    mod = lambda i: mod_ref[i:i+1, :]
    factor = HEAD_DIM ** -0.5
    mg_ref[...] = jnp.zeros_like(mg_ref)
    if loss:
        err_ref[...] = jnp.zeros_like(err_ref)
        perm[...] = order_matrix(tokens, sub, False)
        reorder(tbuf, teach_ref, perm)
    def rsum(v): return jnp.sum(v, axis=0, keepdims=True)
    def first(r):
        if loss:
            f = final_ref[r, :]
            e = f - tbuf[r, :].astype(F32)
            me = mask_ref[r, :] * e
            err_ref[...] += rsum(me * e)
            gba[r, :] = f.astype(BF16)
            g = me * coef_ref[0, 0]
        else:
            g = gin_ref[r, :].astype(F32)
        gr[r, :] = g
        mg_ref[5:6, :] += rsum(g * brb_ref[r, :].astype(F32))
        gbb[r, :] = (g * mod(5)).astype(BF16)
        acc[r, :] = jnp.zeros_like(g)
    row_loop(tokens, 32, first)
    emit(gbb, gbb_o, 0)
    if loss:
        perm[...] = order_matrix(tokens, sub, True)
        reorder(bout_ref, gba, perm)
    for t in range(nt):
        i = 2 * t
        wcopy(i).wait(); precopy(t).wait()
        w = wbuf.at[i % depth]
        def act_tile(c0, n):
            ga = kdot(gbb[...], w[:, pl.ds(c0, n)])
            u = preb[t % 2, :, pl.ds(c0, n)].astype(F32)
            th = gelu_parts(u)
            d = 0.5 * (1.0 + th) + 0.5 * u * (1.0 - th * th) * (GELU_C * (1.0 + 3.0 * GELU_K * u * u))
            gpre[t, :, pl.ds(c0, n)] = (ga * d).astype(BF16)
        column_loop(width, act_tile)
        if i + depth < n_w: wcopy(i + depth).start()
        if t + 2 < nt: precopy(t + 2).start()
        i += 1
        wcopy(i).wait()
        w2 = wbuf.at[i % depth]
        def hid_tile(c0, n):
            acc[:, pl.ds(c0, n)] += kdot_t(gpre[t], w2[pl.ds(c0, n), :])
        column_loop(width, hid_tile)
        if i + depth < n_w: wcopy(i + depth).start()
    emit(gpre, gpre_o, 1)
    def norm_back(gh, base, shift_row, scale_row, scale_i):
        n, inv = normed_of(base)
        mg_ref[shift_row:shift_row+1, :] += rsum(gh)
        mg_ref[scale_row:scale_row+1, :] += rsum(gh * n)
        dn = gh * (1.0 + mod(scale_i))
        return inv * (dn - jnp.mean(dn, axis=-1, keepdims=True) - n * jnp.mean(dn * n, axis=-1, keepdims=True))
    def mid_step(r):
        g = gr[r, :] + norm_back(acc[r, :], mid_ref[r, :], 3, 4, 4)
        gr[r, :] = g
        mg_ref[2:3, :] += rsum(g * bra_ref[r, :].astype(F32))
        gba[r, :] = (g * mod(2)).astype(BF16)
        acc[r, :] = jnp.zeros_like(g)
    row_loop(tokens, 32, mid_step)
    emit(gba, gba_o, 2)
    qc.wait(); pc.wait()
    kmask = [win.head_mask(1, h).astype(BF16) for h in range(win.heads)]
    vmask = [win.head_mask(2, h).astype(BF16) for h in range(win.heads)]
    kmask_f = [win.head_mask(1, h).astype(F32) for h in range(win.heads)]
    vmask_f = [win.head_mask(2, h).astype(F32) for h in range(win.heads)]
    W = win.width
    for t in range(nt):
        i = 2 * nt + t
        wcopy(i).wait()
        w = wbuf.at[i % depth]
        d = kdot(gba[...], w[:, pl.ds(win.start[3], W)])
        dmx[...] = pltpu.roll(d, W - (win.off[3] - win.off[2]), 1).astype(BF16)
        def one_group(g, carry):
            r = pl.ds(pl.multiple_of(g * group, group), group)
            q = pltpu.roll(dqkv[t, r, pl.ds(0, W)].astype(F32), win.off[1], 1).astype(BF16)
            k = dqkv[t, r, pl.ds(win.start[1], W)]
            v = dqkv[t, r, pl.ds(win.start[2], W)]
            dm = dmx[r, :]
            for h in range(win.heads):
                kst[pl.ds(h * group, group), :] = k * kmask[h]
                vst[pl.ds(h * group, group), :] = v * vmask[h]
            sc[...] = kdot_t(dm, vst[...])
            def back(i2, c2):
                rr = pl.ds(pl.multiple_of(i2 * 32, 32), 32)
                for h in range(win.heads):
                    hs = pl.ds(h * group, group)
                    p = pbuf[t, g, rr, hs].astype(F32)
                    gp = sc[rr, hs]
                    inner = jnp.sum(gp * p, axis=-1, keepdims=True)
                    ds[rr, hs] = (p * (gp - inner)).astype(BF16)
                return c2
            lax.fori_loop(0, group // 32, back, 0)
            dq = pltpu.roll(kdot(ds[...], kst[...]) * factor, W - win.off[1], 1)
            dk = jnp.zeros((group, W), F32)
            dv = jnp.zeros((group, W), F32)
            for h in range(win.heads):
                hs = pl.ds(h * group, group)
                dk = dk + kdot_l(ds[:, hs], q) * kmask_f[h]
                dv = dv + kdot_l(pbuf[t, g, :, hs], dm) * vmask_f[h]
            dk = dk * factor
            a, b = win.start[1], win.start[2]
            o = W - a
            o2 = a + W - b
            gat[t, r, pl.ds(0, a)] = dq[:, :a].astype(BF16)
            gat[t, r, pl.ds(a, o)] = (dq[:, a:] + dk[:, :o]).astype(BF16)
            gat[t, r, pl.ds(W, b - W)] = dk[:, o:W - o2].astype(BF16)
            gat[t, r, pl.ds(b, o2)] = (dk[:, W - o2:] + dv[:, :o2]).astype(BF16)
            gat[t, r, pl.ds(a + W, b - a)] = dv[:, o2:].astype(BF16)
            return carry
        lax.fori_loop(0, tokens // group, one_group, 0)
        def hid_tile(c0, n):
            acc[:, pl.ds(c0, n)] += kdot_t(gat[t, :, pl.ds(0, win.qkv)], w[pl.ds(c0, n), pl.ds(0, win.qkv)])
        column_loop(width, hid_tile)
        if i + depth < n_w: wcopy(i + depth).start()
        s3 = win.start[3]
        ov = win.qkv - s3
        gat[t, :, pl.ds(s3, ov)] = gat[t, :, pl.ds(s3, ov)] + mix_ref[t, :, pl.ds(0, ov)]
        gat[t, :, pl.ds(win.qkv, W - ov)] = mix_ref[t, :, pl.ds(ov, W - ov)]
    emit(gat, gat_o, 3)
    def last(r):
        g = gr[r, :] + norm_back(acc[r, :], x_ref[r, :].astype(F32), 0, 1, 1)
        if loss:
            tbuf[r, :] = g.astype(BF16)
        else:
            gout_ref[r, :] = g.astype(BF16)
    row_loop(tokens, 32, last)
    if loss:
        reorder(gout_ref, tbuf, perm)
    for c in outs: c.wait()

def backward_call(head_args, x, mod, w, saved, layer, group, sub, name):
    _, hida, qkv, prob, mix, bra, mid, hidb, pre, act, brb = saved
    loss = len(head_args) == 4
    tokens, width = x.shape
    nt, cols = w.shape[1], w.shape[3]
    win = Windows(cols // 4)
    ng = tokens // group
    V = pltpu.VMEM
    sds = jax.ShapeDtypeStruct
    scratch = [V((3, width, cols), BF16), DMA((3,)), V((tokens, width), F32), V((tokens, width), F32), V((tokens, width), BF16), V((tokens, width), BF16),
               V((nt, tokens, cols), BF16), V((nt, tokens, cols), BF16), V((tokens, win.width), BF16), V((nt, tokens, win.qkv), BF16),
               V((win.heads * group, win.width), BF16), V((win.heads * group, win.width), BF16), V((group, win.heads * group), F32), V((group, win.heads * group), BF16),
               V((nt, ng, group, win.heads * group), BF16), V((2, tokens, cols), BF16), DMA((4,)), DMA((4,)),
               V((tokens, width) if loss else (16, 128), BF16), V((tokens, tokens) if loss else (16, 128), BF16)]
    out = ([sds((tokens, width), BF16), sds((1, width), F32)] if loss else []) + [sds((tokens, width), BF16), sds((6, width), F32),
           sds((tokens, width), BF16), sds((tokens, width), BF16), sds((nt, tokens, cols), BF16), sds((nt, tokens, cols), BF16)]
    SM = pl.BlockSpec(memory_space=pltpu.SMEM)
    in_specs = ([VM, VM, VM, SM] if loss else [VM]) + [VM, VM, ANY, ANY, ANY, VM, VM, VM, ANY, VM]
    out_specs = ([VM, VM] if loss else []) + [VM, VM, ANY, ANY, ANY, ANY]
    return pl.pallas_call(functools.partial(backward_kernel, layer=layer, group=group, sub=sub, win=win, loss=loss),
        out_shape=out, in_specs=in_specs, out_specs=out_specs, scratch_shapes=scratch,
        compiler_params=pltpu.CompilerParams(vmem_limit_bytes=62 << 20), name=name,
        cost_estimate=pl.CostEstimate(flops=2*tokens*width*cols*12, bytes_accessed=60<<20, transcendentals=0))(*head_args, x, mod, w, qkv, prob, mix, bra, mid, pre, brb)


def transit_kernel(in_ref, out_ref, s_sem, r_sem, local_sem, *, nz):
    y, c, x, z = position()
    me = x * nz + z
    greet([across(d, nz)[0] for d in range(1, 2 * nz)])
    copies = []
    for d in range(1, 2 * nz):
        target, q = across(d, nz)
        copies.append(
            remote(in_ref.at[:, q % nz, q // nz], out_ref.at[me], s_sem.at[d], r_sem.at[d], target)
        )
    send_all(copies)
    own = pltpu.make_async_copy(in_ref.at[:, z, x], out_ref.at[me], local_sem)
    own.start()
    own.wait()
    finish_all(copies)


def to_patches(rows, nz):
    frames, _, halves, patches, width = rows.shape
    return pl.pallas_call(
        functools.partial(transit_kernel, nz=nz),
        out_shape=jax.ShapeDtypeStruct((halves * nz, frames, patches, width), BF16),
        in_specs=[ANY],
        out_specs=ANY,
        scratch_shapes=[DMA((2 * nz,)), DMA((2 * nz,)), DMA(())],
        compiler_params=pltpu.CompilerParams(collective_id=2, has_side_effects=True),
        name="to_patches",
    )(rows)


def transit_back_kernel(in_ref, res_ref, out_ref, res_o, s_sem, r_sem, local_sem, *, nz):
    y, c, x, z = position()
    greet([across(d, nz)[0] for d in range(1, 2 * nz)])
    copies = []
    for d in range(1, 2 * nz):
        target, q = across(d, nz)
        copies.append(
            remote(in_ref.at[q], out_ref.at[:, z, x], s_sem.at[d], r_sem.at[d], target)
        )
    copies.append(
        remote(res_ref.at[1 - x], res_o.at[:, x], s_sem.at[0], r_sem.at[0], device(y, c, 1 - x, z))
    )
    send_all(copies)
    own = [
        pltpu.make_async_copy(in_ref.at[x * nz + z], out_ref.at[:, z, x], local_sem.at[0]),
        pltpu.make_async_copy(res_ref.at[x], res_o.at[:, x], local_sem.at[1]),
    ]
    send_all(own)
    for copy in own:
        copy.wait()
    finish_all(copies)


def to_frames(rows, result, nz):
    _, frames, patches, width = rows.shape
    halves, all_frames, _, _ = result.shape
    sds = jax.ShapeDtypeStruct
    return pl.pallas_call(
        functools.partial(transit_back_kernel, nz=nz),
        out_shape=[
            sds((frames, nz, halves, patches, width), BF16),
            sds((all_frames, halves, patches, width), BF16),
        ],
        in_specs=[ANY, ANY],
        out_specs=[ANY, ANY],
        scratch_shapes=[DMA((2 * nz,)), DMA((2 * nz,)), DMA((2,))],
        compiler_params=pltpu.CompilerParams(collective_id=3, has_side_effects=True),
        name="to_frames",
    )(rows, result)


def normalize(stream):
    center = stream - jnp.mean(stream, axis=-1, keepdims=True)
    inverse = lax.rsqrt(jnp.mean(center * center, axis=-1, keepdims=True) + EPSILON)
    return center * inverse, inverse


def norm_backward(grad_normed, normed, inverse):
    mean_grad = jnp.mean(grad_normed, axis=-1, keepdims=True)
    mean_along = jnp.mean(grad_normed * normed, axis=-1, keepdims=True)
    return inverse * (grad_normed - mean_grad - normed * mean_along)


def gelu_tanh(values):
    return jax.nn.gelu(values, approximate=True)


def dot(a, b):
    return jnp.dot(a, b, preferred_element_type=F32)


def dot_t(a, b):
    return lax.dot_general(a, b, (((1,), (1,)), ((), ())), preferred_element_type=F32)


def attend_forward(heads, factor):
    q, k, v = heads[:, :, :, 0], heads[:, :, :, 1], heads[:, :, :, 2]
    scores = jnp.einsum("tglhe,tgmhe->tghlm", q, k, preferred_element_type=F32) * factor
    peak = jnp.max(scores, axis=-1, keepdims=True)
    expanded = jnp.exp(scores - peak)
    total = jnp.sum(expanded, axis=-1, keepdims=True)
    probs = (expanded / total).astype(BF16)
    mixed = jnp.einsum("tghlm,tgmhe->tglhe", probs, v, preferred_element_type=F32)
    return mixed.astype(BF16), peak + jnp.log(total)


def attend_backward(heads, log_total, grad_mixed, factor):
    q, k, v = heads[:, :, :, 0], heads[:, :, :, 1], heads[:, :, :, 2]
    scores = jnp.einsum("tglhe,tgmhe->tghlm", q, k, preferred_element_type=F32) * factor
    probs = jnp.exp(scores - log_total)
    grad_v = jnp.einsum(
        "tghlm,tglhe->tgmhe", probs.astype(BF16), grad_mixed, preferred_element_type=F32
    )
    grad_probs = jnp.einsum("tglhe,tgmhe->tghlm", grad_mixed, v, preferred_element_type=F32)
    inner = jnp.sum(grad_probs * probs, axis=-1, keepdims=True)
    grad_scores = (probs * (grad_probs - inner)).astype(BF16)
    grad_q = jnp.einsum("tghlm,tgmhe->tglhe", grad_scores, k, preferred_element_type=F32) * factor
    grad_k = jnp.einsum("tghlm,tglhe->tgmhe", grad_scores, q, preferred_element_type=F32) * factor
    return jnp.stack([grad_q, grad_k, grad_v], axis=3).astype(BF16)


def block_forward(stream, modulation, weights, group):
    attn, up, down = weights
    blocks, width, cols = attn.shape
    inner = cols // 4 * 3
    head_count = cols // 4 // HEAD_DIM
    clips, per_clip, _ = stream.shape
    tokens = clips * per_clip
    factor = HEAD_DIM**-0.5

    def column(i):
        return modulation[:, i][:, None, :]

    normed_a, inverse_a = normalize(stream)
    hidden_a = (normed_a * (1.0 + column(1)) + column(0)).astype(BF16).reshape(tokens, width)
    triple = jnp.stack([dot(hidden_a, attn[t, :, :inner]).astype(BF16) for t in range(blocks)])
    heads = triple.reshape(blocks, tokens // group, group, 3, head_count, HEAD_DIM)
    mixed, log_total = attend_forward(heads, factor)
    mixed = mixed.reshape(blocks, tokens, cols // 4)
    branch_a = sum(dot_t(mixed[t], attn[t, :, inner:]) for t in range(blocks)).reshape(stream.shape)
    middle = stream + column(2) * branch_a
    normed_b, inverse_b = normalize(middle)
    hidden_b = (normed_b * (1.0 + column(4)) + column(3)).astype(BF16).reshape(tokens, width)
    pre_act = jnp.stack([dot(hidden_b, up[t]) for t in range(blocks)])
    activated = gelu_tanh(pre_act).astype(BF16)
    branch_b = sum(dot_t(activated[t], down[t]) for t in range(blocks)).reshape(stream.shape)
    output = middle + column(5) * branch_b
    saved = (
        normed_a, inverse_a, hidden_a, heads, log_total, mixed, branch_a,
        normed_b, inverse_b, hidden_b, pre_act, activated, branch_b,
    )
    return output, saved


def block_backward(grad, modulation, weights, saved, group):
    attn, up, down = weights
    blocks, width, cols = attn.shape
    inner = cols // 4 * 3
    head_count = cols // 4 // HEAD_DIM
    (
        normed_a, inverse_a, hidden_a, heads, log_total, mixed, branch_a,
        normed_b, inverse_b, hidden_b, pre_act, activated, branch_b,
    ) = saved
    tokens = hidden_a.shape[0]
    factor = HEAD_DIM**-0.5

    def column(i):
        return modulation[:, i][:, None, :]

    def clip_sum(values):
        return jnp.sum(values, axis=1)

    gate_b = clip_sum(grad * branch_b)
    branch_grad_b = (grad * column(5)).astype(BF16).reshape(tokens, width)
    grad_act = jnp.stack([dot(branch_grad_b, down[t]) for t in range(blocks)])
    grad_pre = jax.vjp(gelu_tanh, pre_act)[1](grad_act)[0].astype(BF16)
    grad_hidden_b = sum(dot_t(grad_pre[t], up[t]) for t in range(blocks)).reshape(grad.shape)
    shift_b = clip_sum(grad_hidden_b)
    scale_b = clip_sum(grad_hidden_b * normed_b)
    grad_middle = grad + norm_backward(grad_hidden_b * (1.0 + column(4)), normed_b, inverse_b)
    gate_a = clip_sum(grad_middle * branch_a)
    branch_grad_a = (grad_middle * column(2)).astype(BF16).reshape(tokens, width)
    grad_mixed = jnp.stack(
        [dot(branch_grad_a, attn[t, :, inner:]).astype(BF16) for t in range(blocks)]
    )
    grad_mixed = grad_mixed.reshape(blocks, tokens // group, group, head_count, HEAD_DIM)
    grad_heads = attend_backward(heads, log_total, grad_mixed, factor)
    grad_triple = grad_heads.reshape(blocks, tokens, inner)
    grad_hidden_a = sum(
        dot_t(grad_triple[t], attn[t, :, :inner]) for t in range(blocks)
    ).reshape(grad.shape)
    shift_a = clip_sum(grad_hidden_a)
    scale_a = clip_sum(grad_hidden_a * normed_a)
    grad_input = grad_middle + norm_backward(
        grad_hidden_a * (1.0 + column(1)), normed_a, inverse_a
    )
    grad_modulation = jnp.stack([shift_a, scale_a, gate_a, shift_b, scale_b, gate_b], axis=1)
    x_list = [hidden_a, branch_grad_a, hidden_b, branch_grad_b]
    g_list = [jnp.concatenate([grad_triple, mixed], axis=2), grad_pre, activated]
    return grad_input, grad_modulation, x_list, g_list


def local_anywhere(
    latents, condition, teacher, valid_mask,
    qkv_weight, out_weight, up_weight, down_weight, ada_weight,
):
    n_dp, n_seq, n_tensor = (lax.axis_size(a) for a in (DP, SEQ, TENSOR))
    clips, frames, patches, width = latents.shape
    rows = ada_weight.shape[1]
    blocks = qkv_weight.shape[0]
    heads_width = qkv_weight.shape[3]
    inner = 3 * heads_width
    dp, seq, tensor = (lax.axis_index(a) for a in (DP, SEQ, TENSOR))
    row_block = dp * n_seq + seq

    shards = pack_shards(qkv_weight, out_weight, up_weight, down_weight)
    full = lax.all_gather(shards, (DP, SEQ), axis=1, tiled=True)
    full = lax.all_gather(full, TENSOR, axis=1)
    weights = [(full[3 * b], full[3 * b + 1], full[3 * b + 2]) for b in range(blocks)]

    cond_float = condition.astype(F32)
    all_cond = lax.all_gather(condition, DP, axis=0, tiled=True).astype(F32)
    all_silu = jax.nn.silu(all_cond).astype(BF16)
    silu_rows = lax.dynamic_slice_in_dim(all_silu, row_block * rows, rows, axis=1)
    partial_mod = jnp.einsum("cd,bdke->cbke", silu_rows, ada_weight, preferred_element_type=F32)
    partial_mod = lax.psum_scatter(partial_mod, DP, scatter_dimension=0, tiled=True)
    partial_mod = lax.psum(partial_mod, SEQ)
    modulation = lax.all_gather(partial_mod, TENSOR, axis=3, tiled=True)

    by_frame = frames % n_tensor == 0
    split_axis = 1 if by_frame else 0

    def to_spatial(v):
        return lax.all_to_all(v, TENSOR, split_axis=split_axis, concat_axis=2, tiled=True)

    def from_spatial(v):
        return lax.all_to_all(v, TENSOR, split_axis=2, concat_axis=split_axis, tiled=True)

    def to_temporal(v):
        return lax.all_to_all(v, SEQ, split_axis=2, concat_axis=1, tiled=True)

    def from_temporal(v):
        return lax.all_to_all(v, SEQ, split_axis=1, concat_axis=2, tiled=True)

    own_clips = clips if by_frame else clips // n_tensor
    first_clip = 0 if by_frame else tensor * own_clips
    spatial_mod = lax.dynamic_slice_in_dim(modulation[:, 0], first_clip, own_clips, axis=0)
    temporal_mod = modulation[:, 1]

    def patch_major(v):
        return v.transpose(0, 2, 1, 3)

    spatial = to_spatial(latents)
    spatial_shape = spatial.shape
    stream = spatial.astype(F32).reshape(own_clips, -1, width)
    stream, saved_0 = block_forward(stream, spatial_mod, weights[0], spatial_shape[2])
    moved = to_temporal(from_spatial(stream.astype(BF16).reshape(spatial_shape)))
    temporal_shape = moved.shape
    stream = patch_major(moved).astype(F32).reshape(clips, -1, width)
    stream, saved_1 = block_forward(stream, temporal_mod, weights[1], temporal_shape[1])

    def to_frames(v):
        return patch_major(
            v.reshape(clips, temporal_shape[2], temporal_shape[1], width)
        )

    block_out = from_temporal(to_frames(stream.astype(BF16)))

    teacher_rows = patch_major(to_temporal(teacher)).astype(F32).reshape(clips, -1, width)
    mask_float = valid_mask.astype(F32)
    own_mask = lax.dynamic_slice_in_dim(
        mask_float, seq * temporal_shape[2], temporal_shape[2], axis=1
    )
    mask_rows = jnp.repeat(own_mask, temporal_shape[1], axis=1)[:, :, None]
    error = stream - teacher_rows
    error_sum = lax.psum(jnp.sum(mask_rows * error * error), (DP, SEQ, TENSOR))
    total_frames = frames * n_seq
    valid_count = lax.psum(jnp.sum(mask_float), (DP, TENSOR)) * total_frames
    loss_value = error_sum / (width * valid_count)
    token_total = clips * frames * patches * n_dp * n_seq * n_tensor
    grad = mask_rows * error * (2.0 * token_total / valid_count)

    grad, mod_grad_1, x_1, g_1 = block_backward(
        grad, temporal_mod, weights[1], saved_1, temporal_shape[1]
    )
    moved = to_spatial(from_temporal(to_frames(grad.astype(BF16))))
    grad = moved.astype(F32).reshape(own_clips, -1, width)
    grad, mod_grad_0, x_0, g_0 = block_backward(
        grad, spatial_mod, weights[0], saved_0, spatial_shape[2]
    )
    grad_latents = from_spatial(grad.astype(BF16).reshape(spatial_shape)).astype(F32)

    x_list, g_list = x_0 + x_1, g_0 + g_1
    terms = []
    for b in range(blocks):
        for layer, q in ((0, 0), (1, 2), (2, 3)):
            term = jnp.einsum(
                "nd,tnk->tdk", x_list[4 * b + q], g_list[3 * b + layer], preferred_element_type=F32
            )
            if layer == 0:
                other = jnp.einsum(
                    "nd,tnk->tdk", x_list[4 * b + 1], g_list[3 * b], preferred_element_type=F32
                )
                term = jnp.where(jnp.arange(term.shape[2]) < inner, term, other)
            term = lax.psum_scatter(
                term.astype(BF16), (DP, SEQ), scatter_dimension=1, tiled=True
            )
            terms.append(lax.psum_scatter(term, TENSOR, scatter_dimension=0, tiled=True)[0])
    summed = jnp.stack(terms)
    grad_qkv, grad_out, grad_up, grad_down = unpack_shards(summed, blocks, heads_width)

    placed_0 = lax.dynamic_update_slice_in_dim(
        jnp.zeros((clips,) + mod_grad_0.shape[1:], F32), mod_grad_0, first_clip, axis=0
    )
    mod_grad = jnp.stack([placed_0, mod_grad_1], axis=1)
    mod_grad = lax.psum_scatter(mod_grad, TENSOR, scatter_dimension=3, tiled=True)
    mod_grad = lax.psum(mod_grad, SEQ)
    mod_grad = lax.all_gather(mod_grad, DP, axis=0, tiled=True)
    grad_ada = jnp.einsum("cd,cbke->bdke", silu_rows.astype(F32), mod_grad, precision=HIGHEST)
    grad_silu = jnp.einsum("cbke,bdke->cd", mod_grad, ada_weight.astype(F32), precision=HIGHEST)
    grad_silu = lax.psum(grad_silu, TENSOR)
    grad_silu = lax.all_gather(grad_silu, (DP, SEQ), axis=1, tiled=True)
    grad_silu = lax.dynamic_slice_in_dim(grad_silu, dp * clips, clips, axis=0)
    grad_condition = jax.vjp(jax.nn.silu, cond_float)[1](grad_silu)[0]
    return (
        block_out, loss_value, grad_latents, grad_condition,
        grad_qkv, grad_out, grad_up, grad_down, grad_ada,
    )


def pack_shards(qkv_weight, out_weight, up_weight, down_weight):
    blocks, rows = qkv_weight.shape[:2]
    shards = []
    for b in range(blocks):
        shards.append(jnp.concatenate([qkv_weight[b].reshape(rows, -1), out_weight[b].T], axis=1))
        shards.append(up_weight[b])
        shards.append(down_weight[b].T)
    return jnp.stack(shards)


def unpack_shards(summed, blocks, heads_width):
    rows = summed.shape[1]
    inner = 3 * heads_width
    summed = summed.reshape(blocks, 3, rows, -1).astype(F32)
    return (
        summed[:, 0, :, :inner].reshape(blocks, rows, 3, heads_width),
        summed[:, 0, :, inner:].transpose(0, 2, 1),
        summed[:, 1],
        summed[:, 2].transpose(0, 2, 1),
    )


def local_grid(
    latents, condition, teacher, valid_mask,
    qkv_weight, out_weight, up_weight, down_weight, ada_weight,
):
    n_dp, n_seq, nz = (lax.axis_size(a) for a in (DP, SEQ, TENSOR))
    _, frames, patches, width = latents.shape
    blocks, rows = ada_weight.shape[:2]
    heads_width = qkv_weight.shape[3]
    seq = lax.axis_index(SEQ)
    all_frames, own_patches, own_frames = frames * n_seq, patches // n_seq, frames // nz
    tokens = frames * patches

    shards = pack_shards(qkv_weight, out_weight, up_weight, down_weight)
    cond_float = condition.astype(F32)
    mask_float = valid_mask.astype(F32)
    count = jnp.broadcast_to(jnp.sum(mask_float), (1, ada_weight.shape[3]))
    ada = ada_weight.transpose(0, 2, 1, 3)
    full, spatial, teacher_rows, mod_parts, silu_rows = gather_weights(
        shards,
        latents.reshape(nz, own_frames, patches, width),
        teacher.reshape(frames, n_seq, own_patches, width),
        cond_float.reshape(-1, rows),
        count,
        ada,
        nz,
    )
    full = full.reshape(shards.shape[0], nz, width, shards.shape[2])
    modulation = mod_parts[:, : 6 * blocks].reshape(nz, blocks, 6, -1)
    modulation = modulation.transpose(1, 2, 0, 3).reshape(blocks, 6, width)
    valid_count = jnp.sum(mod_parts[:, 12, 0]) / n_seq * all_frames
    token_total = tokens * n_dp * n_seq * nz
    scale = (2.0 * token_total / valid_count).reshape(1, 1)
    own_mask = lax.dynamic_slice_in_dim(mask_float, seq * own_patches, own_patches, axis=1)
    mask_rows = jnp.repeat(own_mask.reshape(-1), all_frames).reshape(tokens, 1)

    x_0 = spatial.reshape(tokens, width)
    frame = tokens // own_frames
    out_0, *saved_0 = forward_call(x_0, modulation[0], full, 0, frame, None, BF16, "spatial_forward")
    moved = to_patches(out_0.reshape(own_frames, nz, n_seq, own_patches, width), nz)
    group = 8 * all_frames
    final, *saved_1 = forward_call(
        moved.reshape(tokens, width), modulation[1], full, 3, group, all_frames, F32, "temporal_forward"
    )

    result, error, grad, mod_grad_1, a_1, b_1, g_1, p_1 = backward_call(
        (final, teacher_rows.reshape(tokens, width), mask_rows, scale),
        saved_1[0], modulation[1], full, saved_1, 3, group, all_frames, "temporal_backward",
    )
    grad, block_out = to_frames(
        grad.reshape(n_seq * nz, own_frames, own_patches, width),
        result.reshape(n_seq, frames, own_patches, width),
        nz,
    )
    grad, mod_grad_0, a_0, b_0, g_0, p_0 = backward_call(
        (grad.reshape(tokens, width),), x_0, modulation[0], full, saved_0, 0, frame, None, "spatial_backward"
    )

    mod_grad = jnp.concatenate(
        [mod_grad_0, mod_grad_1, jnp.broadcast_to(jnp.sum(error), (4, width))], axis=0
    )
    mod_grad = mod_grad.reshape(16, nz, -1).transpose(1, 0, 2)
    summed, grad_latents, mod_all, silu_grad = reduce_weights(
        [saved_0[1], a_0, saved_0[7], b_0, saved_1[1], a_1, saved_1[7], b_1],
        [g_0, p_0, saved_0[9], g_1, p_1, saved_1[9]],
        grad.reshape(own_frames, nz, patches, width),
        mod_grad,
        ada,
        rows,
        nz,
        3 * heads_width,
    )
    loss_value = jnp.sum(mod_all[:, 12, 0]) / (width * valid_count)
    grad_ada = jnp.einsum(
        "cd,cbke->bdke",
        silu_rows[:n_dp],
        mod_all[:, : 6 * blocks].reshape(n_dp, blocks, 6, -1),
        precision=HIGHEST,
    )
    grad_condition = jax.vjp(jax.nn.silu, cond_float)[1](silu_grad.reshape(1, width))[0]
    return (
        block_out.reshape(latents.shape),
        loss_value,
        grad_latents.reshape(latents.shape).astype(F32),
        grad_condition,
        *unpack_shards(summed, blocks, heads_width),
        grad_ada,
    )


def local(latents, *rest):
    sizes = tuple(lax.axis_size(a) for a in (DP, SEQ, TENSOR))
    if sizes == (4, 2, 4) and latents.shape[0] == 1:
        return local_grid(latents, *rest)
    return local_anywhere(latents, *rest)


def solution(mesh):
    return jax.shard_map(
        local,
        mesh=mesh,
        in_specs=(
            P(DP, SEQ, TENSOR, None),
            P(DP, None),
            P(DP, SEQ, TENSOR, None),
            P(DP, TENSOR),
            P(None, (DP, SEQ), None, TENSOR),
            P(None, TENSOR, (DP, SEQ)),
            P(None, (DP, SEQ), TENSOR),
            P(None, TENSOR, (DP, SEQ)),
            P(None, (DP, SEQ), None, TENSOR),
        ),
        out_specs=(
            P(DP, SEQ, TENSOR, None),
            P(),
            P(DP, SEQ, TENSOR, None),
            P(DP, None),
            P(None, (DP, SEQ), None, TENSOR),
            P(None, TENSOR, (DP, SEQ)),
            P(None, (DP, SEQ), TENSOR),
            P(None, TENSOR, (DP, SEQ)),
            P(None, (DP, SEQ), None, TENSOR),
        ),
        check_vma=False,
    )
```

```python
import functools

import jax
import jax.numpy as jnp
from jax import lax
from jax.experimental import pallas as pl
from jax.experimental.pallas import tpu as pltpu
from jax.sharding import PartitionSpec as P

DP, SEQ, TENSOR = "dp", "seq", "tensor"
START, SEND, RECV = range(3)
HEAD_DIM = 72
EPSILON = 1e-06
HIGHEST = lax.Precision.HIGHEST
MESH = pl.DeviceIdType.MESH
DMA = pltpu.SemaphoreType.DMA
BF16 = jnp.bfloat16
F32 = jnp.float32
ANY = pl.BlockSpec(memory_space=pl.ANY)
VM = pl.BlockSpec(memory_space=pltpu.VMEM)
LANES = 128
NEGATIVE = -1e30
GELU_C = 0.7978845608028654
GELU_K = 0.044715


def position():
    dp = lax.axis_index(DP)
    return dp // 2, dp % 2, lax.axis_index(SEQ), lax.axis_index(TENSOR)


def device(y, c, x, z):
    return (y * 2 + c, x, z)


def neighbours(nz):
    y, c, x, z = position()
    return (
        device(y, c, 1 - x, z),
        device(1 - y, c, x, z),
        device(y, 1 - c, x, z),
        device(y, c, x, jnp.maximum(z - 1, 0)),
        device(y, c, x, jnp.minimum(z + 1, nz - 1)),
    )


def remote(src, dst, send_sem, recv_sem, target):
    return pltpu.make_async_remote_copy(
        src_ref=src,
        dst_ref=dst,
        send_sem=send_sem,
        recv_sem=recv_sem,
        device_id=target,
        device_id_type=MESH,
    )


def in_plane(d):
    y, c, x, z = position()
    q = (y * 4 + c * 2 + x + d) % 8
    return (q // 2, q % 2, z), q


def across(d, nz):
    y, c, x, z = position()
    q = (x * nz + z + d) % (2 * nz)
    return (y * 2 + c, q // nz, q % nz), q


def over_z(d, nz):
    y, c, x, z = position()
    q = (z + d) % nz
    return device(y, c, x, q), q


def over_dp(d):
    y, c, x, z = position()
    q = (y * 2 + c + d) % 4
    return (q, x, z), q


def greet(peers):
    barrier = pltpu.get_barrier_semaphore()
    for target in peers:
        pl.semaphore_signal(barrier, inc=1, device_id=target, device_id_type=MESH)
    pl.semaphore_wait(barrier, len(peers))


def send_all(copies):
    for copy in copies:
        copy.start()


def finish_all(copies):
    for copy in copies:
        copy.wait_send()
        copy.wait_recv()


def kdot(a, b):
    return jnp.dot(a, b, preferred_element_type=F32)


def kdot_t(a, b):
    return lax.dot_general(a, b, (((1,), (1,)), ((), ())), preferred_element_type=F32)


class Lanes:
    def __init__(self, span):
        self.span = span
        self.heads = span // HEAD_DIM
        self.starts = [i * span // LANES * LANES for i in range(4)]
        self.offsets = [i * span - s for i, s in enumerate(self.starts)]
        self.width = 3 * LANES
        self.qkv = self.starts[2] + self.width

    def place(self, which, h):
        return self.offsets[which] + h * HEAD_DIM - (h // 2) * LANES

    def mask(self, which, h):
        lane = lax.broadcasted_iota(jnp.int32, (1, 2 * LANES), 1) - self.place(which, h)
        return ((lane >= 0) & (lane < HEAD_DIM)).astype(F32).astype(BF16)


def row_loop(total, step, body, unroll=2):
    def go(i, carry):
        body(pl.ds(pl.multiple_of(i * step, step), step))
        return carry

    lax.fori_loop(0, total // step, go, 0, unroll=unroll)


def tiles(total):
    first = -(-total // 2 // LANES) * LANES
    return ((0, first), (first, total - first))


def normed_of(v):
    center = v - jnp.mean(v, axis=-1, keepdims=True)
    inverse = lax.rsqrt(jnp.mean(center * center, axis=-1, keepdims=True) + EPSILON)
    return center * inverse, inverse


def gelu_inner(u):
    return jnp.tanh(GELU_C * (u + GELU_K * u * u * u))


def order_matrix(tokens, group, back):
    per = tokens // group
    row = lax.broadcasted_iota(jnp.int32, (tokens, tokens), 1 if back else 0)
    col = lax.broadcasted_iota(jnp.int32, (tokens, tokens), 0 if back else 1)
    return (col == row % group * per + row // group).astype(F32).astype(BF16)


def reorder(dst, src, order):
    for c0, n in tiles(src.shape[1]):
        dst[:, pl.ds(c0, n)] = kdot(order[...], src[:, pl.ds(c0, n)]).astype(BF16)


class Blocks:
    def __init__(self, w_ref, ring, sem, order, ready):
        self.w_ref, self.ring, self.sem, self.order = w_ref, ring, sem, order
        self.ready = ready
        self.loaded = self.done = 0
        self.depth = ring.shape[0]

    def copy(self, i):
        layer, t = self.order[i]
        s = i % self.depth
        dst = self.ring.at[s]
        if len(self.w_ref.shape) == 7:
            dst = dst.reshape(self.w_ref.shape[2:])
        return pltpu.make_async_copy(self.w_ref.at[layer, t], dst, self.sem.at[s])

    def pump(self):
        while (
            self.loaded < len(self.order)
            and self.loaded < self.done + self.depth
            and self.order[self.loaded][0] in self.ready
        ):
            self.copy(self.loaded).start()
            self.loaded += 1

    def take(self):
        i = self.done
        self.pump()
        self.copy(i).wait()
        return self.ring.at[i % self.depth]

    def drop(self):
        self.done += 1
        self.pump()


class Saves:
    def __init__(self, sem):
        self.sem, self.copies, self.used = sem, [], 0

    def put(self, src, dst):
        copy = pltpu.make_async_copy(src, dst, self.sem.at[self.used])
        copy.start()
        self.copies.append(copy)
        self.used += 1
        return copy

    def wait(self, copy):
        copy.wait()
        self.copies = [other for other in self.copies if other is not copy]

    def finish(self):
        for copy in self.copies:
            copy.wait()
        self.copies = []


def stack_heads(dst, value, masks, group):
    for h, mask in enumerate(masks):
        lane = (h // 2) * LANES
        dst[h // 2, pl.ds(h % 2 * group, group), :] = value[:, lane : lane + 2 * LANES] * mask


FORWARD_SAVES = 24


def forward_steps(x_in, mod_ref, out_ref, saved, scratch, blocks, saves, *, sub, group, lanes):
    x_o, hida_o, qkv_o, prob_o, mix_o, bra_o, mid_o, hidb_o, pre_o, act_o, brb_o = saved
    xbuf, perm, acc, qkv, qst, sc, hida, prob, mix, hidb, pre, act, mid, bra, brb = scratch
    tokens, width = x_in.shape
    nt = act.shape[0]
    cols = act.shape[2]
    heads = lanes.heads
    scale = HEAD_DIM**-0.5 * 1.4426950408889634
    x_ref = x_in if sub is None else xbuf
    steps = []

    def mod(i):
        return mod_ref[i : i + 1, :]

    def begin():
        if sub is not None:
            perm[...] = order_matrix(tokens, sub, False)
            reorder(xbuf, x_in, perm)
            saves.put(xbuf, x_o)

        def rows(r):
            n, _ = normed_of(x_ref[r, :].astype(F32))
            hida[r, :] = (n * (1.0 + mod(1)) + mod(0)).astype(BF16)

        row_loop(tokens, 32, rows)
        saves.put(hida, hida_o)

    steps.append((None, begin))

    kept = {}

    def project(t):
        if t >= 2:
            saves.wait(kept[0, t - 2])
        w = blocks.take()
        for c0, n in tiles(lanes.qkv):
            qkv[t % 2, :, pl.ds(c0, n)] = kdot(hida[...], w[:, pl.ds(c0, n)]).astype(BF16)
        kept[0, t] = saves.put(qkv.at[t % 2], qkv_o.at[t])

    def attend(t):
        now = qkv.at[t % 2]
        masks = [lanes.mask(1, h) for h in range(heads)]

        def one(g, carry):
            r = pl.ds(pl.multiple_of(g * group, group), group)
            q = pltpu.roll(now[r, pl.ds(0, lanes.width)].astype(F32), lanes.offsets[1], 1).astype(BF16)
            stack_heads(qst, q, masks, group)
            for p in range(heads // 2):
                k = now[r, pl.ds(lanes.starts[1] + p * LANES, 2 * LANES)]
                sc[:, pl.ds(p * 2 * group, 2 * group)] = kdot_t(k, qst[p])

            def soft(j, c2):
                at = pl.ds(pl.multiple_of(j * LANES, LANES), LANES)
                s = sc[:, at] * scale
                if sub is not None:
                    row = lax.broadcasted_iota(jnp.int32, s.shape, 0) // sub
                    col = lax.broadcasted_iota(jnp.int32, s.shape, 1) // sub
                    s = jnp.where(row == col, s, NEGATIVE)
                e = jnp.exp2(s - jnp.max(s, axis=0, keepdims=True))
                prob[t, g, :, at] = (e * (1.0 / jnp.sum(e, axis=0, keepdims=True))).astype(BF16)
                return c2

            lax.fori_loop(0, heads * group // LANES, soft, 0, unroll=2)
            pieces = [jnp.zeros((lanes.offsets[3], group), F32)]
            for p in range(heads // 2):
                v = now[r, pl.ds(lanes.starts[2] + p * LANES, 2 * LANES)].T
                for h in (2 * p, 2 * p + 1):
                    got = kdot(v, prob[t, g, :, pl.ds(h * group, group)])
                    at = lanes.place(2, h)
                    pieces.append(got[at : at + HEAD_DIM])
            rest = lanes.width - lanes.offsets[3] - heads * HEAD_DIM
            if rest:
                pieces.append(jnp.zeros((rest, group), F32))
            mix[t, r, :] = jnp.concatenate(pieces, axis=0).T.astype(BF16)
            return carry

        lax.fori_loop(0, tokens // group, one, 0)
        saves.put(prob.at[t], prob_o.at[t])
        saves.put(mix.at[t], mix_o.at[t])

    def bring_out(t):
        w = blocks.ring.at[blocks.done % blocks.depth]
        got = kdot_t(mix[t], w[:, pl.ds(lanes.starts[3], lanes.width)])
        if t == 0:
            acc[...] = got
        else:
            acc[...] += got
        blocks.drop()

    for t in range(nt):
        steps.append((0, functools.partial(project, t)))
        steps.append((0, functools.partial(attend, t)))
        steps.append((0, functools.partial(bring_out, t)))

    def between():
        def rows(r):
            b = acc[r, :]
            m = x_ref[r, :].astype(F32) + mod(2) * b
            mid[r, :] = m
            bra[r, :] = b.astype(BF16)
            n, _ = normed_of(m)
            hidb[r, :] = (n * (1.0 + mod(4)) + mod(3)).astype(BF16)

        row_loop(tokens, 32, rows)
        saves.put(bra, bra_o)
        saves.put(mid, mid_o)
        saves.put(hidb, hidb_o)

    steps.append((0, between))

    def go_up(t):
        if t >= 2:
            saves.wait(kept[1, t - 2])
        w = blocks.take()
        for c0, n in tiles(cols):
            u = kdot(hidb[...], w[:, pl.ds(c0, n)])
            pre[t % 2, :, pl.ds(c0, n)] = u.astype(BF16)
            act[t, :, pl.ds(c0, n)] = (0.5 * u * (1.0 + gelu_inner(u))).astype(BF16)
        kept[1, t] = saves.put(pre.at[t % 2], pre_o.at[t])
        saves.put(act.at[t], act_o.at[t])
        blocks.drop()

    def go_down(t):
        w = blocks.take()
        got = kdot_t(act[t], w[...])
        if t == 0:
            acc[...] = got
        else:
            acc[...] += got
        blocks.drop()

    for t in range(nt):
        steps.append((1, functools.partial(go_up, t)))
    for t in range(nt):
        steps.append((2, functools.partial(go_down, t)))

    def end():
        def rows(r):
            b = acc[r, :]
            brb[r, :] = b.astype(BF16)
            out_ref[r, :] = (mid[r, :] + mod(5) * b).astype(out_ref.dtype)

        row_loop(tokens, 32, rows)
        saves.put(brb, brb_o)

    steps.append((2, end))
    return steps


def forward_scratch(tokens, width, nt, cols, group, sub, lanes):
    side = tokens if sub is not None else 16
    vmem = pltpu.VMEM
    return [
        vmem((side, width), BF16),
        vmem((side, side), BF16),
        vmem((tokens, width), F32),
        vmem((2, tokens, lanes.qkv), BF16),
        vmem((lanes.heads // 2, 2 * group, 2 * LANES), BF16),
        vmem((group, lanes.heads * group), F32),
        vmem((tokens, width), BF16),
        vmem((nt, tokens // group, group, lanes.heads * group), BF16),
        vmem((nt, tokens, lanes.width), BF16),
        vmem((tokens, width), BF16),
        vmem((2, tokens, cols), BF16),
        vmem((nt, tokens, cols), BF16),
        vmem((tokens, width), F32),
        vmem((tokens, width), BF16),
        vmem((tokens, width), BF16),
    ]


def forward_saved(tokens, width, nt, cols, group, sub, lanes):
    sds = jax.ShapeDtypeStruct
    return [
        sds((tokens if sub is not None else 16, width), BF16),
        sds((tokens, width), BF16),
        sds((nt, tokens, lanes.qkv), BF16),
        sds((nt, tokens // group, group, lanes.heads * group), BF16),
        sds((nt, tokens, lanes.width), BF16),
        sds((tokens, width), BF16),
        sds((tokens, width), F32),
        sds((tokens, width), BF16),
        sds((nt, tokens, cols), BF16),
        sds((nt, tokens, cols), BF16),
        sds((tokens, width), BF16),
    ]


def backward_steps(head, ins, outs, scratch, blocks, saves, *, sub, group, lanes):
    loss = len(head) == 4
    x_hbm, mod_ref, qkv_hbm, prob_hbm, mix_hbm, bra_hbm, mid_hbm, pre_hbm, brb_hbm = ins
    gout_ref, mg_ref, gba_o, gbb_o, gat_o, gpre_o = outs[:6]
    (
        gr, acc, gbb, gba, gpre, gat, dmx, qkv, qst, dst, sc, ds, prob, preb, mix,
        x_ref, bra, mid, brb, lsem, tbuf, perm,
    ) = scratch
    tokens, width = gr.shape
    nt, _, cols = gpre.shape
    heads = lanes.heads
    factor = HEAD_DIM**-0.5
    steps = []

    def mod(i):
        return mod_ref[i : i + 1, :]

    def load(src, dst, n):
        return pltpu.make_async_copy(src, dst, lsem.at[n])

    whole = [
        load(brb_hbm, brb, 0),
        load(mid_hbm, mid, 1),
        load(bra_hbm, bra, 2),
        load(x_hbm, x_ref, 3),
        load(mix_hbm, mix, 4),
    ]

    def load_pre(t):
        return load(pre_hbm.at[t], preb.at[t % 2], 5 + t % 2)

    def load_heads(t):
        return (
            load(qkv_hbm.at[t], qkv.at[t % 2], 7 + t % 2),
            load(prob_hbm.at[t], prob.at[t % 2], 9 + t % 2),
        )

    def row_sum(v):
        return jnp.sum(v, axis=0, keepdims=True)

    def begin():
        for copy in whole:
            copy.start()
        for t in range(2):
            load_pre(t).start()
            send_all(load_heads(t))
        mg_ref[...] = jnp.zeros_like(mg_ref)
        if loss:
            final_ref, teach_ref, mask_ref, coef_ref = head
            bout_ref, err_ref = outs[6:]
            err_ref[...] = jnp.zeros_like(err_ref)
            perm[...] = order_matrix(tokens, sub, False)
            reorder(tbuf, teach_ref, perm)
        whole[0].wait()

        def rows(r):
            if loss:
                f = final_ref[r, :]
                e = f - tbuf[r, :].astype(F32)
                me = mask_ref[r, :] * e
                err_ref[...] += row_sum(me * e)
                gba[r, :] = f.astype(BF16)
                g = me * coef_ref[0, 0]
            else:
                g = head[0][r, :].astype(F32)
            gr[r, :] = g
            mg_ref[5:6, :] += row_sum(g * brb[r, :].astype(F32))
            gbb[r, :] = (g * mod(5)).astype(BF16)

        row_loop(tokens, 32, rows)
        saves.put(gbb, gbb_o)
        if loss:
            perm[...] = order_matrix(tokens, sub, True)
            reorder(bout_ref, gba, perm)

    steps.append((None, begin))

    def through_gelu(t):
        w = blocks.take()
        load_pre(t).wait()
        for c0, n in tiles(cols):
            ga = kdot(gbb[...], w[:, pl.ds(c0, n)])
            u = preb[t % 2, :, pl.ds(c0, n)].astype(F32)
            th = gelu_inner(u)
            slope = 0.5 * (1.0 + th) + 0.5 * u * (1.0 - th * th) * (
                GELU_C * (1.0 + 3.0 * GELU_K * u * u)
            )
            gpre[t, :, pl.ds(c0, n)] = (ga * slope).astype(BF16)
        saves.put(gpre.at[t], gpre_o.at[t])
        blocks.drop()
        if t + 2 < nt:
            load_pre(t + 2).start()

    def under_up(t):
        w = blocks.take()
        got = kdot_t(gpre[t], w[...])
        if t == 0:
            acc[...] = got
        else:
            acc[...] += got
        blocks.drop()

    for t in range(nt):
        steps.append((2, functools.partial(through_gelu, t)))
    for t in range(nt):
        steps.append((1, functools.partial(under_up, t)))

    def norm_back(gh, base, shift_row, scale_row, scale_i):
        n, inv = normed_of(base)
        mg_ref[shift_row : shift_row + 1, :] += row_sum(gh)
        mg_ref[scale_row : scale_row + 1, :] += row_sum(gh * n)
        dn = gh * (1.0 + mod(scale_i))
        along = jnp.mean(dn * n, axis=-1, keepdims=True)
        return inv * (dn - jnp.mean(dn, axis=-1, keepdims=True) - n * along)

    def between():
        whole[1].wait()
        whole[2].wait()

        def rows(r):
            g = gr[r, :] + norm_back(acc[r, :], mid[r, :], 3, 4, 4)
            gr[r, :] = g
            mg_ref[2:3, :] += row_sum(g * bra[r, :].astype(F32))
            gba[r, :] = (g * mod(2)).astype(BF16)

        row_loop(tokens, 32, rows)
        saves.put(gba, gba_o)
        whole[4].wait()

    steps.append((1, between))

    kept = {}

    def attend(t):
        if t >= 2:
            saves.wait(kept[t - 2])
        w = blocks.take()
        d = kdot(gba[...], w[:, pl.ds(lanes.starts[3], lanes.width)])
        back = lanes.width - (lanes.offsets[3] - lanes.offsets[2])
        dmx[...] = pltpu.roll(d, back, 1).astype(BF16)
        for copy in load_heads(t):
            copy.wait()
        now, probs = qkv.at[t % 2], prob.at[t % 2]
        kmasks = [lanes.mask(1, h) for h in range(heads)]
        vmasks = [lanes.mask(2, h) for h in range(heads)]
        out = gat.at[t % 2]

        def one(g, carry):
            r = pl.ds(pl.multiple_of(g * group, group), group)
            q = pltpu.roll(now[r, pl.ds(0, lanes.width)].astype(F32), lanes.offsets[1], 1).astype(BF16)
            stack_heads(qst, q, kmasks, group)
            stack_heads(dst, dmx[r, :], vmasks, group)
            for p in range(heads // 2):
                v = now[r, pl.ds(lanes.starts[2] + p * LANES, 2 * LANES)]
                sc[:, pl.ds(p * 2 * group, 2 * group)] = kdot_t(v, dst[p])

            def soft(j, c2):
                at = pl.ds(pl.multiple_of(j * LANES, LANES), LANES)
                p = probs[g, :, at].astype(F32)
                gp = sc[:, at]
                inner = jnp.sum(gp * p, axis=0, keepdims=True)
                ds[:, at] = (p * (gp - inner)).astype(BF16)
                return c2

            lax.fori_loop(0, heads * group // LANES, soft, 0, unroll=2)
            pieces, dk, dv = [], [], []
            for p in range(heads // 2):
                pair = pl.ds(p * 2 * group, 2 * group)
                dk.append(kdot(ds[:, pair], qst[p]) * factor)
                dv.append(kdot(probs[g, :, pair], dst[p]))
                k = now[r, pl.ds(lanes.starts[1] + p * LANES, 2 * LANES)].T
                for h in (2 * p, 2 * p + 1):
                    got = kdot(k, ds[:, pl.ds(h * group, group)])
                    at = lanes.place(1, h)
                    pieces.append(got[at : at + HEAD_DIM])
            pieces.append(jnp.zeros((lanes.width - heads * HEAD_DIM, group), F32))
            dq = jnp.concatenate(pieces, axis=0).T * factor
            parts = [dq[:, i * LANES : (i + 1) * LANES] for i in range(3)]
            low, high = slice(0, LANES), slice(LANES, 2 * LANES)
            parts[2] = parts[2] + dk[0][:, low]
            parts.append(dk[0][:, high] + dk[1][:, low])
            parts.append(dk[1][:, high] + dv[0][:, low])
            parts.append(dv[0][:, high] + dv[1][:, low])
            parts.append(dv[1][:, high])
            for i, part in enumerate(parts):
                out[r, pl.ds(i * LANES, LANES)] = part.astype(BF16)
            return carry

        lax.fori_loop(0, tokens // group, one, 0)
        if t + 2 < nt:
            send_all(load_heads(t + 2))

    def under_qkv(t):
        w = blocks.ring.at[blocks.done % blocks.depth]
        out = gat.at[t % 2]
        got = kdot_t(out[:, pl.ds(0, lanes.qkv)], w[:, pl.ds(0, lanes.qkv)])
        if t == 0:
            acc[...] = got
        else:
            acc[...] += got
        blocks.drop()
        s3 = lanes.starts[3]
        out[:, pl.ds(s3, LANES)] = out[:, pl.ds(s3, LANES)] + mix[t, :, pl.ds(0, LANES)]
        out[:, pl.ds(s3 + LANES, 2 * LANES)] = mix[t, :, pl.ds(LANES, 2 * LANES)]
        kept[t] = saves.put(out, gat_o.at[t])

    for t in range(nt):
        steps.append((0, functools.partial(attend, t)))
        steps.append((0, functools.partial(under_qkv, t)))

    def end():
        whole[3].wait()

        def rows(r):
            g = gr[r, :] + norm_back(acc[r, :], x_ref[r, :].astype(F32), 0, 1, 1)
            if loss:
                tbuf[r, :] = g.astype(BF16)
            else:
                gout_ref[r, :] = g.astype(BF16)

        row_loop(tokens, 32, rows)
        if loss:
            reorder(gout_ref, tbuf, perm)

    steps.append((0, end))
    return steps


def backward_scratch(tokens, width, nt, cols, group, loss, lanes):
    vmem = pltpu.VMEM
    return [
        vmem((tokens, width), F32),
        vmem((tokens, width), F32),
        vmem((tokens, width), BF16),
        vmem((tokens, width), BF16),
        vmem((nt, tokens, cols), BF16),
        vmem((2, tokens, cols), BF16),
        vmem((tokens, lanes.width), BF16),
        vmem((2, tokens, lanes.qkv), BF16),
        vmem((lanes.heads // 2, 2 * group, 2 * LANES), BF16),
        vmem((lanes.heads // 2, 2 * group, 2 * LANES), BF16),
        vmem((group, lanes.heads * group), F32),
        vmem((group, lanes.heads * group), BF16),
        vmem((2, tokens // group, group, lanes.heads * group), BF16),
        vmem((2, tokens, cols), BF16),
        vmem((nt, tokens, lanes.width), BF16),
        vmem((tokens, width), BF16),
        vmem((tokens, width), BF16),
        vmem((tokens, width), F32),
        vmem((tokens, width), BF16),
        DMA((11,)),
        vmem((tokens, width) if loss else (16, LANES), BF16),
        vmem((tokens, tokens) if loss else (16, LANES), BF16),
    ]


def backward_kernel(*refs, layer, group, sub, lanes, loss):
    n_head = 4 if loss else 1
    head, refs = refs[:n_head], refs[n_head:]
    ins, w_ref = refs[:9], refs[9]
    n_out = 8 if loss else 6
    outs, scratch = refs[10 : 10 + n_out], refs[10 + n_out :]
    ring, wsem, osem = scratch[:3]
    nt = w_ref.shape[1]
    order = [(layer + i, t) for i in (2, 1, 0) for t in range(nt)]
    blocks = Blocks(w_ref, ring, wsem, order, {layer, layer + 1, layer + 2})
    blocks.pump()
    saves = Saves(osem)
    for _, step in backward_steps(
        head, ins, outs, scratch[3:], blocks, saves, sub=sub, group=group, lanes=lanes
    ):
        step()
    saves.finish()


def backward_call(head, x, mod, w, saved, layer, group, sub, name):
    _, hida, qkv, prob, mix, bra, mid, hidb, pre, act, brb = saved
    loss = len(head) == 4
    tokens, width = x.shape
    nt, cols = w.shape[1], w.shape[3]
    lanes = Lanes(cols // 4)
    sds = jax.ShapeDtypeStruct
    rows = sds((tokens, width), BF16)
    tall = sds((nt, tokens, cols), BF16)
    smem = pl.BlockSpec(memory_space=pltpu.SMEM)
    return pl.pallas_call(
        functools.partial(backward_kernel, layer=layer, group=group, sub=sub, lanes=lanes, loss=loss),
        out_shape=[rows, sds((6, width), F32), rows, rows, tall, tall]
        + ([rows, sds((1, width), F32)] if loss else []),
        in_specs=([VM, VM, VM, smem] if loss else [VM]) + [ANY, VM] + [ANY] * 8,
        out_specs=[VM, VM, ANY, ANY, ANY, ANY] + ([VM, VM] if loss else []),
        scratch_shapes=[pltpu.VMEM((3, width, cols), BF16), DMA((3,)), DMA((16,))]
        + backward_scratch(tokens, width, nt, cols, group, loss, lanes),
        compiler_params=pltpu.CompilerParams(vmem_limit_bytes=62 << 20),
        name=name,
        cost_estimate=pl.CostEstimate(
            flops=24 * tokens * width * cols, bytes_accessed=60 << 20, transcendentals=0
        ),
    )(*head, x, mod, qkv, prob, mix, bra, mid, pre, brb, w)


THIRDS = 3
GATHER_STAGES = 6


class Gather:
    def __init__(self, w_ref, g_ref, sems, nz):
        self.w, self.g, self.nz = w_ref, g_ref, nz
        (
            self.lsem, self.s_zab, self.r_zab, self.s_xy, self.r_xy,
            self.s_zcd, self.r_zcd, self.s_c, self.r_c,
        ) = sems
        self.layers, self.rows, self.cols = w_ref.shape
        self.unit = self.rows // 9
        self.ab = 7 * self.unit
        self.count = self.layers * THIRDS
        self.at = position()
        self.peers = neighbours(nz)

    def columns(self, k):
        width = self.cols // THIRDS
        return k // THIRDS, pl.ds(k % THIRDS * width, width)

    def own(self, l):
        y, c, x, z = self.at
        return pltpu.make_async_copy(self.w.at[l], self.g.at[l, z, y, c, x], self.lsem.at[l])

    def region_ab(self, k, t):
        y, c, x, z = self.at
        l, cs = self.columns(k)
        return self.g.at[l, t, y, c, x, pl.ds(0, self.ab), cs]

    def region_cd(self, k, t):
        y, c, x, z = self.at
        l, cs = self.columns(k)
        return self.g.at[l, t, :, c, :, pl.ds(self.ab, 2 * self.unit), cs]

    def along_z(self, k, hop, which, mode):
        z, nz = self.at[3], self.nz
        below, above = self.peers[3:]
        region = (self.region_ab, self.region_cd)[which]
        ssem, rsem = ((self.s_zab, self.r_zab), (self.s_zcd, self.r_zcd))[which]
        up, down = z - hop, z + hop
        if mode == RECV:

            @pl.when(z - 1 - hop >= 0)
            def _():
                r = region(k, jnp.maximum(z - 1 - hop, 0))
                remote(r, r, ssem.at[k, hop, 1], rsem.at[k, hop, 1], above).wait_recv()

            @pl.when(z + 1 + hop < nz)
            def _():
                r = region(k, jnp.minimum(z + 1 + hop, nz - 1))
                remote(r, r, ssem.at[k, hop, 0], rsem.at[k, hop, 0], below).wait_recv()

            return
        l, cs = self.columns(k)
        first = self.w.at[l, pl.ds(0, self.ab), cs] if which == 0 and hop == 0 else None

        @pl.when((up >= 0) & (z < nz - 1))
        def _():
            r = region(k, jnp.maximum(up, 0))
            copy = remote(r if first is None else first, r, ssem.at[k, hop, 1], rsem.at[k, hop, 1], above)
            copy.start() if mode == START else copy.wait_send()

        @pl.when((down < nz) & (z > 0))
        def _():
            r = region(k, jnp.minimum(down, nz - 1))
            copy = remote(r if first is None else first, r, ssem.at[k, hop, 0], rsem.at[k, hop, 0], below)
            copy.start() if mode == START else copy.wait_send()

    def region_xy(self, k, kind, yy, xx):
        y, c, x, z = self.at
        l, cs = self.columns(k)
        a = (4 if k % 2 == 0 else 3) * self.unit
        ra, rb = pl.ds(0, a), pl.ds(a, self.ab - a)
        rc, rd = pl.ds(self.ab, self.unit), pl.ds(self.ab + self.unit, self.unit)
        g = self.g
        return (
            lambda: g.at[l, :, yy, c, xx, ra, cs],
            lambda: g.at[l, :, yy, c, xx, rb, cs],
            lambda: g.at[l, :, yy, c, :, ra, cs],
            lambda: g.at[l, :, :, c, xx, rb, cs],
            lambda: g.at[l, z, yy, c, xx, rc, cs],
            lambda: g.at[l, z, yy, c, xx, rd, cs],
            lambda: g.at[l, z, yy, c, :, rc, cs],
            lambda: g.at[l, z, :, c, xx, rd, cs],
        )[kind]()

    def along_xy(self, k, kind, mode):
        y, c, x, z = self.at
        on_x = (True, False, False, True, True, False, False, True)[kind]
        target = self.peers[0 if on_x else 1]
        s, r = self.s_xy.at[k, kind], self.r_xy.at[k, kind]
        if mode == RECV:
            there = self.region_xy(k, kind, y, 1 - x) if on_x else self.region_xy(k, kind, 1 - y, x)
            remote(there, there, s, r, target).wait_recv()
            return
        here = self.region_xy(k, kind, y, x)
        l, cs = self.columns(k)
        src = here
        if kind == 4:
            src = self.w.at[l, pl.ds(self.ab, self.unit), cs]
        if kind == 5:
            src = self.w.at[l, pl.ds(self.ab + self.unit, self.unit), cs]
        copy = remote(src, here, s, r, target)
        copy.start() if mode == START else copy.wait_send()

    def to_core(self, k, mode):
        c = self.at[1]
        l, cs = self.columns(k)
        r = self.g.at[l, :, :, 1 - c if mode == RECV else c, :, :, cs]
        copy = remote(r, r, self.s_c.at[k], self.r_c.at[k], self.peers[2])
        if mode == START:
            copy.start()
        elif mode == SEND:
            copy.wait_send()
        else:
            copy.wait_recv()

    def stage(self, k, s):
        z, xy = self.along_z, self.along_xy
        if s == 0:
            z(k, 0, 0, START)
            xy(k, 4, START)
            xy(k, 5, START)
        if s == 1:
            z(k, 0, 0, RECV)
            z(k, 1, 0, START)
            if k % THIRDS == 0:
                self.own(k // THIRDS).wait()
            xy(k, 4, RECV)
            xy(k, 6, START)
            xy(k, 5, RECV)
            xy(k, 7, START)
        if s == 2:
            z(k, 1, 0, RECV)
            z(k, 2, 0, START)
            xy(k, 6, RECV)
            xy(k, 7, RECV)
            z(k, 0, 1, START)
        if s == 3:
            z(k, 2, 0, RECV)
            xy(k, 0, START)
            xy(k, 1, START)
            z(k, 0, 1, RECV)
            z(k, 1, 1, START)
        if s == 4:
            xy(k, 0, RECV)
            xy(k, 2, START)
            xy(k, 1, RECV)
            xy(k, 3, START)
            z(k, 1, 1, RECV)
            z(k, 2, 1, START)
        if s == 5:
            xy(k, 2, RECV)
            xy(k, 3, RECV)
            z(k, 2, 1, RECV)
            self.to_core(k, START)

    def begin(self, ahead):
        self.ahead = ahead
        for l in range(self.layers):
            self.own(l).start()
        for k in range(min(ahead, self.count)):
            self.stage(k, 0)

    def slots(self):
        return self.count + GATHER_STAGES - 1

    def slot(self, i):
        for k in range(self.count):
            s = i - k
            if s == 0 and k + self.ahead < self.count:
                self.stage(k + self.ahead, 0)
            if 1 <= s < GATHER_STAGES:
                self.stage(k, s)

    def arrive(self, layer):
        for k in range(layer * THIRDS, (layer + 1) * THIRDS):
            self.to_core(k, RECV)

    def end(self):
        for k in range(self.count):
            self.to_core(k, SEND)
            for kind in range(8):
                self.along_xy(k, kind, SEND)
            for hop in range(self.nz - 1):
                self.along_z(k, hop, 0, SEND)
                self.along_z(k, hop, 1, SEND)


def forward_pass_kernel(*refs, nz, n_seq, group_0, group_1, sub, lanes):
    w_ref, lat_ref, teach_ref, cond_ref, count_ref, ada_ref = refs[:6]
    g_ref, x0_o, teach_o, mod_o, silu_o, count_o, final_ref = refs[6:13]
    saved_0, saved_1 = refs[13:24], refs[24:35]
    rest = refs[35:]
    sems, rest = rest[:9], rest[9:]
    (
        s_lat, r_lat, s_tea, r_tea, s_m, r_m, local_sem, s_t, r_t,
        ada, cond_all, parts, landed, mod_all, x0, x1, out_0, ring, wsem, osem_0, osem_1,
        qst_0, sc_0, prob_0,
    ) = rest[:24]
    shared = rest[24:]
    y, c, x, z = position()
    x_dev = neighbours(nz)[0]
    layers = w_ref.shape[0]
    tokens, width = x0.shape
    _, own_frames, patches, _ = lat_ref.shape
    frame = nz * patches
    part = patches // n_seq
    greet(
        [in_plane(d)[0] for d in range(1, 8)]
        + [(y * 2 + c, xx, (z + d) % nz) for d in range(1, nz) for xx in (x, 1 - x)]
    )
    gather = Gather(w_ref, g_ref, sems, nz)

    dp, block = y * 2 + c, (y * 2 + c) * 2 + x
    me = x * nz + z
    side = [
        pltpu.make_async_copy(teach_ref.at[:, x], teach_o.at[x], local_sem.at[0]),
        pltpu.make_async_copy(ada_ref, ada, local_sem.at[1]),
    ]
    lat_in, own_rows, teach_in = [], [], []
    for i in range(own_frames):
        rows = pl.ds(pl.multiple_of(i * frame + z * patches, 16), patches)
        own_rows.append(pltpu.make_async_copy(lat_ref.at[z, i], x0.at[rows], local_sem.at[2 + i]))
        for d in range(1, nz):
            target, q = over_z(d, nz)
            lat_in.append(remote(lat_ref.at[q, i], x0.at[rows], s_lat.at[i, d], r_lat.at[i, d], target))
    teach_in.append(remote(teach_ref.at[:, 1 - x], teach_o.at[x], s_tea, r_tea, x_dev))

    conds, sums, spread = [], [], []
    for d in range(1, 4):
        target, q = over_dp(d)
        conds.append(remote(cond_ref, cond_all.at[dp], s_m.at[0, d], r_m.at[0, d], target))
    for d in range(1, 8):
        target, q = in_plane(d)
        sums.append(remote(parts.at[q // 2], landed.at[d], s_m.at[1, d], r_m.at[1, d], target))
    for d in range(1, nz):
        target, q = over_z(d, nz)
        spread.append(remote(mod_all.at[z], mod_all.at[z], s_m.at[2, d], r_m.at[2, d], target))

    def modulate(step):
        if step == 0:
            send_all(conds)
            cond_all[dp] = cond_ref[...]
        if step == 1:
            finish_all(conds)
            side[1].wait()
            silu_o[...] = jnp.zeros_like(silu_o)
            for i in range(4):
                row = cond_all[i, pl.ds(block, 1), :]
                silu_o[i : i + 1, :] = (row / (1.0 + jnp.exp(-row))).astype(BF16).astype(F32)
            parts[...] = jnp.zeros_like(parts)
            for b in range(ada.shape[0]):
                for k in range(6):
                    got = kdot(silu_o[...].astype(BF16), ada[b, k])
                    for i in range(4):
                        parts[i, 6 * b + k : 6 * b + k + 1, :] = got[i : i + 1]
            for i in range(4):
                parts[i, 12:13, :] = count_ref[...]
            send_all(sums)
        if step == 2:
            finish_all(sums)
            total = parts[dp]
            for d in range(1, 8):
                total = total + landed[d]
            mod_all[z] = total
            send_all(spread)
        if step == 3:
            finish_all(spread)
            count = mod_all[0, 12:13, :]
            for q in range(1, nz):
                count = count + mod_all[q, 12:13, :]
            count_o[...] = count
            for b in range(ada.shape[0]):
                mod_o[b] = jnp.concatenate(
                    [mod_all[q, 6 * b : 6 * b + 6, :] for q in range(nz)], axis=1
                )

    moved, kept = [], []
    for i in range(own_frames):
        dst = x1.at[pl.ds(pl.multiple_of((me * own_frames + i) * part, 16), part)]
        for d in range(1, 2 * nz):
            target, q = across(d, nz)
            src = out_0.at[
                pl.ds(pl.multiple_of(i * frame + q % nz * patches + q // nz * part, 16), part)
            ]
            moved.append(remote(src, dst, s_t.at[i, d], r_t.at[i, d], target))
        src = out_0.at[pl.ds(pl.multiple_of(i * frame + z * patches + x * part, 16), part)]
        kept.append(pltpu.make_async_copy(src, dst, local_sem.at[2 + own_frames + i]))

    ready = set()
    order = [(l, t) for l in range(layers) for t in range(nz)]
    blocks = Blocks(g_ref, ring, wsem, order, ready)
    saves_0, saves_1 = Saves(osem_0), Saves(osem_1)
    per_block = layers // 2
    common = list(shared)
    scratch_1 = common
    scratch_0 = common[:4] + [qst_0, sc_0] + common[6:7] + [prob_0] + common[8:]

    def start_spatial():
        for copy in own_rows:
            copy.wait()
        finish_all(lat_in)
        saves_0.put(x0, x0_o)

    def leave_spatial():
        send_all(moved)
        send_all(kept)

    def start_temporal():
        for copy in kept:
            copy.wait()
        finish_all(moved)
        saves_0.finish()

    work = [(None, start_spatial)]
    for need, step in forward_steps(
        x0, mod_o.at[0], out_0, (None,) + saved_0[1:], scratch_0, blocks, saves_0,
        sub=None, group=group_0, lanes=lanes,
    ):
        work.append((need, step))
    work.append((None, leave_spatial))
    pause = len(work)
    work.append((None, start_temporal))
    for need, step in forward_steps(
        x1, mod_o.at[1], final_ref, saved_1, scratch_1, blocks, saves_1,
        sub=sub, group=group_1, lanes=lanes,
    ):
        work.append((None if need is None else need + per_block, step))

    send_all(own_rows)
    send_all(lat_in)
    modulate(0)
    gather.begin(2)
    send_all(side)
    send_all(teach_in)
    done, waited = 0, 0
    for slot in range(gather.slots() + 1):
        if slot < gather.slots():
            gather.slot(slot)
        if slot % 2 == 1 and slot < 6:
            modulate((slot + 1) // 2)
        if slot >= GATHER_STAGES + THIRDS - 1 and (slot - GATHER_STAGES - THIRDS + 1) % THIRDS == 0:
            layer = (slot - GATHER_STAGES - THIRDS + 1) // THIRDS
            gather.arrive(layer)
            ready.add(layer)
            blocks.pump()
        quota = 5
        while done < len(work) and quota and slot >= 6:
            need = work[done][0]
            if need is not None and need not in ready:
                break
            if done == pause:
                waited += 1
                if waited < 3 and slot < gather.slots():
                    break
            work[done][1]()
            done += 1
            quota -= 1
    while done < len(work):
        work[done][1]()
        done += 1
    gather.end()
    side[0].wait()
    finish_all(teach_in)
    saves_1.finish()


def forward_pass(shards, latents, teacher, cond, count, ada, nz, n_seq, sub):
    layers, rows, cols = shards.shape
    hops = nz - 1
    chunks = layers * THIRDS
    sds = jax.ShapeDtypeStruct
    _, own_frames, patches, width = latents.shape
    tokens = nz * own_frames * patches
    frames, halves, own_patches, _ = teacher.shape
    vmem = pltpu.VMEM
    mod_shape = (16, ada.shape[3])
    lanes = Lanes(cols // 4)
    group_0, group_1 = nz * patches, 8 * sub
    sizes_0 = (tokens, width, nz, cols, group_0, None, lanes)
    sizes_1 = (tokens, width, nz, cols, group_1, sub, lanes)
    scratch_0, scratch_1 = forward_scratch(*sizes_0), forward_scratch(*sizes_1)
    rowsb = vmem((tokens, width), BF16)
    outs = pl.pallas_call(
        functools.partial(
            forward_pass_kernel, nz=nz, n_seq=n_seq, group_0=group_0, group_1=group_1, sub=sub, lanes=lanes
        ),
        out_shape=[
            sds((layers, nz, 2, 2, 2, rows, cols), BF16),
            sds((tokens, width), BF16),
            sds((halves, frames, own_patches, width), BF16),
            sds((2, 6, width), F32),
            sds((8, cond.shape[1]), F32),
            sds((1, ada.shape[3]), F32),
            sds((tokens, width), F32),
        ]
        + forward_saved(*sizes_0)
        + forward_saved(*sizes_1),
        in_specs=[ANY, ANY, ANY, VM, VM, ANY],
        out_specs=[ANY, ANY, ANY, VM, VM, VM, VM] + [ANY] * 22,
        scratch_shapes=[
            DMA((layers,)),
            DMA((chunks, hops, 2)),
            DMA((chunks, hops, 2)),
            DMA((chunks, 8)),
            DMA((chunks, 8)),
            DMA((chunks, hops, 2)),
            DMA((chunks, hops, 2)),
            DMA((chunks,)),
            DMA((chunks,)),
            DMA((own_frames, nz)),
            DMA((own_frames, nz)),
            DMA(()),
            DMA(()),
            DMA((3, 8)),
            DMA((3, 8)),
            DMA((2 + 2 * own_frames,)),
            DMA((own_frames, 2 * nz)),
            DMA((own_frames, 2 * nz)),
            vmem(ada.shape, BF16),
            vmem((4,) + cond.shape, F32),
            vmem((4,) + mod_shape, F32),
            vmem((8,) + mod_shape, F32),
            vmem((nz,) + mod_shape, F32),
            rowsb,
            rowsb,
            rowsb,
            vmem((3, width, cols), BF16),
            DMA((3,)),
            DMA((32,)),
            DMA((32,)),
            scratch_0[4],
            scratch_0[5],
            scratch_0[7],
        ]
        + scratch_1,
        compiler_params=pltpu.CompilerParams(
            collective_id=0, has_side_effects=True, vmem_limit_bytes=62 << 20
        ),
        name="forward_pass",
    )(shards, latents, teacher, cond, count, ada)
    full, x_0, teach, mod, silu, count, final = outs[:7]
    full = full.reshape(layers, nz, -1, cols)
    return full, x_0, teach, mod, silu, count, final, outs[7:18], outs[18:29]


STAGES = 7
SLOTS = 3
Y_A, X_A, X_B, Y_B, Y_C, X_C, X_D, Y_D = KINDS = tuple(range(8))


def reduce_kernel(*refs, chunks, n_x, n_g, split_at, nz, rows, width):
    x_refs, g_refs = refs[:n_x], refs[n_x : n_x + n_g]
    lat_ref, mod_ref, ada_ref = refs[n_x + n_g : n_x + n_g + 3]
    (
        o_ref, lat_o, mod_o, silu_o, acc, stg, prb, gbuf, xraw, xt, ya, xa, xb, yb, yc, xc, xd, yd, zab, zcd,
        gsem, xsem, osem, s_p, r_p, s_xy, r_xy, s_z, r_z,
        s_lat, r_lat, s_m, r_m, local_sem, ada, first, every, along, back, silus,
    ) = refs[n_x + n_g + 3 :]
    unit = rows // 9
    ab = 7 * unit
    count = len(chunks)
    y, c, x, z = position()
    x_dev, y_dev, core_dev, below, above = neighbours(nz)
    greet(
        [in_plane(d)[0] for d in range(1, 8)]
        + [
            (y * 2 + c, xx, (z + d) % nz)
            for d in range(1, nz)
            for xx in (x, 1 - x)
        ]
    )

    dp, block = y * 2 + c, (y * 2 + c) * 2 + x
    side = [
        pltpu.make_async_copy(lat_ref.at[:, z], lat_o.at[z], local_sem.at[0]),
        pltpu.make_async_copy(ada_ref, ada, local_sem.at[1]),
    ]
    moves, sums, spread, slices, rows_out = [], [], [], [], []
    for d in range(1, nz):
        target, q = over_z(d, nz)
        moves.append(remote(lat_ref.at[:, q], lat_o.at[z], s_lat.at[d], r_lat.at[d], target))
        slices.append(remote(along, back.at[d], s_m.at[2, d], r_m.at[2, d], target))
    for d in range(1, 2 * nz):
        target, q = across(d, nz)
        sums.append(remote(mod_ref.at[q % nz], first.at[d], s_m.at[0, d], r_m.at[0, d], target))
    for d in range(1, 4):
        target, q = over_dp(d)
        spread.append(remote(every.at[dp], every.at[dp], s_m.at[1, d], r_m.at[1, d], target))
    for d in range(1, 8):
        target, q = in_plane(d)
        rows_out.append(remote(silus.at[block], silus.at[block], s_m.at[3, d], r_m.at[3, d], target))

    def modulation(step):
        if step == 0:
            send_all(sums)
            send_all(side)
            send_all(moves)
        if step == 2:
            finish_all(sums)
            total = mod_ref[z]
            for d in range(1, 2 * nz):
                total = total + first[d]
            every[dp] = total
            send_all(spread)
        if step == 4:
            finish_all(spread)
            side[1].wait()
            mod_o[...] = every[...]
            total = jnp.zeros(along.shape, F32)
            for b in range(ada.shape[0]):
                for k in range(6):
                    i = 6 * b + k
                    got = jnp.concatenate([every[q, i : i + 1, :] for q in range(4)] * 2, axis=0)
                    high = got.astype(BF16)
                    rest = got - high.astype(F32)
                    middle = rest.astype(BF16)
                    lowest = (rest - middle.astype(F32)).astype(BF16)
                    for part in (high, middle, lowest):
                        total = total + kdot_t(part, ada[b, k])
            along[...] = total
            send_all(slices)
        if step == 7:
            finish_all(slices)
            total = along[...]
            for d in range(1, nz):
                total = total + back[d]
            silus[block] = total
            send_all(rows_out)
        if step == 10:
            finish_all(rows_out)
            for q in range(8):
                silu_o[q : q + 1, :] = silus[q, pl.ds(dp, 1), :]

    def add_in(dst, src):
        lead = dst.shape[:-2]
        total = 1
        for v in lead:
            total *= v
        if total == 1:
            dst[...] = dst[...] + src[...]
            return

        def body(i, carry):
            index = []
            rest = i
            for v in reversed(lead):
                index.append(rest % v)
                rest = rest // v
            index = tuple(reversed(index))
            dst[index] = dst[index] + src[index]
            return carry

        lax.fori_loop(0, total, body, 0)

    def exchange(k, kind, mode):
        a = (4 if k % 2 == 0 else 3) * unit
        b = ab - a
        ra, rb, rc, rd = pl.ds(0, a), pl.ds(a, b), pl.ds(ab, unit), pl.ds(ab + unit, unit)
        m = k % SLOTS
        part = acc.at[k % STAGES]
        src, buf, target, dst = {
            Y_A: lambda: (part.at[:, 1 - y, :, ra], ya.at[m, :, :, pl.ds(0, a)], y_dev, part.at[:, y, :, ra]),
            X_A: lambda: (part.at[:, y, 1 - x, ra], xa.at[m, :, pl.ds(0, a)], x_dev, part.at[:, y, x, ra]),
            X_B: lambda: (part.at[:, :, 1 - x, rb], xb.at[m, :, :, pl.ds(0, b)], x_dev, part.at[:, :, x, rb]),
            Y_B: lambda: (part.at[:, 1 - y, x, rb], yb.at[m, :, pl.ds(0, b)], y_dev, part.at[:, y, x, rb]),
            Y_C: lambda: (part.at[z, 1 - y, :, rc], yc.at[m], y_dev, part.at[z, y, :, rc]),
            X_C: lambda: (part.at[z, y, 1 - x, rc], xc.at[m], x_dev, part.at[z, y, x, rc]),
            X_D: lambda: (part.at[z, :, 1 - x, rd], xd.at[m], x_dev, part.at[z, :, x, rd]),
            Y_D: lambda: (part.at[z, 1 - y, x, rd], yd.at[m], y_dev, part.at[z, y, x, rd]),
        }[kind]()
        i = kind
        copy = remote(src, buf, s_xy.at[k % STAGES, i], r_xy.at[m, i], target)
        if mode == START:
            copy.start()
        elif mode == SEND:
            copy.wait_send()
        else:
            copy.wait_recv()
            add_in(dst, buf)

    def region_z(k, t, which):
        part = acc.at[k % STAGES, t]
        return part.at[y, x, pl.ds(0, ab)] if which == 0 else part.at[:, :, pl.ds(ab, 2 * unit)]

    def along_z(k, hop, which, mode):
        m, n = k % SLOTS, k % STAGES
        landing = (zab, zcd)[which]
        t_down, t_up = hop - (nz - 1 - z), nz - 1 - (hop - z)
        if mode != RECV:

            @pl.when((t_down >= 0) & (z > 0))
            def _():
                copy = remote(
                    region_z(k, jnp.maximum(t_down, 0), which), landing.at[m, hop, 0],
                    s_z.at[n, which, hop, 0], r_z.at[m, which, hop, 0], below,
                )
                copy.start() if mode == START else copy.wait_send()

            @pl.when((hop >= z) & (z < nz - 1))
            def _():
                copy = remote(
                    region_z(k, jnp.minimum(t_up, nz - 1), which), landing.at[m, hop, 1],
                    s_z.at[n, which, hop, 1], r_z.at[m, which, hop, 1], above,
                )
                copy.start() if mode == START else copy.wait_send()

            return
        from_above, from_below = t_down + 1, t_up - 1

        @pl.when((from_above >= 0) & (z < nz - 1))
        def _():
            buf = landing.at[m, hop, 0]
            remote(buf, buf, s_z.at[n, which, hop, 0], r_z.at[m, which, hop, 0], below).wait_recv()
            add_in(region_z(k, jnp.maximum(from_above, 0), which), buf)

        @pl.when((hop >= z - 1) & (z > 0))
        def _():
            buf = landing.at[m, hop, 1]
            remote(buf, buf, s_z.at[n, which, hop, 1], r_z.at[m, which, hop, 1], above).wait_recv()
            add_in(region_z(k, jnp.minimum(from_below, nz - 1), which), buf)

    def pair(k, mode):
        m = k % 2
        copy = remote(stg.at[m], prb.at[m], s_p.at[m], r_p.at[m], core_dev)
        if mode == START:
            copy.start()
        elif mode == SEND:
            copy.wait_send()
        else:
            copy.wait_recv()
            add_in(acc.at[k % STAGES], prb.at[m])

    def load_g(k):
        layer, col, _ = chunks[k]
        return pltpu.make_async_copy(
            g_refs[layer].at[:, :, pl.ds(col * width, width)], gbuf.at[k % 2], gsem.at[k % 2]
        )

    order = []
    for _, _, used in chunks:
        for q in used:
            if q not in order:
                order.append(q)

    def load_x(i):
        return pltpu.make_async_copy(x_refs[order[i]], xraw.at[i % 2], xsem.at[i % 2])

    ready = [0]

    def turned(q):
        i = order.index(q)
        if i >= ready[0]:
            load_x(i).wait()
            for j in range(xraw.shape[2] // 128):
                xt[i % 3, pl.ds(j * 128, 128), :] = xraw[i % 2, :, pl.ds(j * 128, 128)].T
            ready[0] += 1
            if i + 2 < len(order):
                load_x(i + 2).start()
        return i % 3

    def multiply(k):
        _, _, used = chunks[k]
        slots = [turned(q) for q in used]
        if k + 1 < count:
            load_g(k + 1).start()
        load_g(k).wait()

        def fill(dst, core):
            def body(i, carry):
                t, yy = i // 2, i % 2
                at = pl.ds(pl.multiple_of((yy * 4 + core * 2) * rows, 16), 2 * rows)
                g = gbuf[k % 2, t]
                r = jnp.dot(xt[slots[0], at, :], g, preferred_element_type=F32)
                if len(slots) == 2:
                    second = jnp.dot(xt[slots[1], at, :], g, preferred_element_type=F32)
                    col = lax.broadcasted_iota(jnp.int32, r.shape, 1)
                    r = jnp.where(col < split_at, r, second)
                r = r.astype(BF16)
                dst[t, yy, 0] = r[:rows]
                dst[t, yy, 1] = r[rows:]
                return carry

            lax.fori_loop(0, nz * 2, body, 0)

        fill(stg.at[k % 2], 1 - c)
        pair(k, START)
        fill(acc.at[k % STAGES], c)

    def hand_out(k):
        layer, col, _ = chunks[k]
        return pltpu.make_async_copy(
            acc.at[k % STAGES, z, y, x],
            o_ref.at[layer, :, pl.ds(col * width, width)],
            osem.at[k % STAGES],
        )

    def stage(k, s):
        if s == 0:
            if k >= STAGES:
                hand_out(k - STAGES).wait()
            multiply(k)
        if s == 1:
            pair(k, SEND)
            pair(k, RECV)
            exchange(k, Y_A, START)
            exchange(k, X_B, START)
            along_z(k, 0, 1, START)
        if s == 2:
            along_z(k, 0, 1, RECV)
            along_z(k, 1, 1, START)
            exchange(k, Y_A, RECV)
            exchange(k, X_A, START)
            exchange(k, X_B, RECV)
            exchange(k, Y_B, START)
        if s == 3:
            along_z(k, 1, 1, RECV)
            along_z(k, 2, 1, START)
            exchange(k, X_A, RECV)
            exchange(k, Y_B, RECV)
            along_z(k, 0, 0, START)
        if s == 4:
            along_z(k, 0, 0, RECV)
            along_z(k, 1, 0, START)
            along_z(k, 2, 1, RECV)
            exchange(k, Y_C, START)
            exchange(k, X_D, START)
        if s == 5:
            along_z(k, 1, 0, RECV)
            along_z(k, 2, 0, START)
            exchange(k, Y_C, RECV)
            exchange(k, X_C, START)
            exchange(k, X_D, RECV)
            exchange(k, Y_D, START)
        if s == 6:
            along_z(k, 2, 0, RECV)
            exchange(k, X_C, RECV)
            exchange(k, Y_D, RECV)
            for kind in KINDS:
                exchange(k, kind, SEND)
            for hop in range(nz - 1):
                along_z(k, hop, 0, SEND)
                along_z(k, hop, 1, SEND)
            hand_out(k).start()

    load_x(0).start()
    load_x(1).start()
    load_g(0).start()
    for slot in range(count + STAGES - 1):
        modulation(slot)
        for s in range(STAGES - 1, -1, -1):
            if 0 <= slot - s < count:
                stage(slot - s, s)
    for k in range(max(0, count - STAGES), count):
        hand_out(k).wait()
    side[0].wait()
    finish_all(moves)


def reduce_weights(x_list, g_list, grad_latents, mod_grad, ada, rows, nz, split_at):
    tokens, cols = x_list[0].shape
    width = cols // 3
    unit = rows // 9
    chunks = []
    for block in (1, 0):
        for layer, used in ((2, (3,)), (1, (2,)), (0, (0, 1))):
            for col in range(3):
                ids = tuple(4 * block + q for q in used)
                if layer == 0 and (col + 1) * width <= split_at:
                    ids = ids[:1]
                chunks.append((3 * block + layer, col, ids))
    vmem = pltpu.VMEM
    hops = nz - 1
    scratch = [
        vmem((STAGES, nz, 2, 2, rows, width), BF16),
        vmem((2, nz, 2, 2, rows, width), BF16),
        vmem((2, nz, 2, 2, rows, width), BF16),
        vmem((2, nz, tokens, width), BF16),
        vmem((2, tokens, cols), BF16),
        vmem((3, cols, tokens), BF16),
        vmem((SLOTS, nz, 2, 4 * unit, width), BF16),
        vmem((SLOTS, nz, 4 * unit, width), BF16),
        vmem((SLOTS, nz, 2, 4 * unit, width), BF16),
        vmem((SLOTS, nz, 4 * unit, width), BF16),
        vmem((SLOTS, 2, unit, width), BF16),
        vmem((SLOTS, unit, width), BF16),
        vmem((SLOTS, 2, unit, width), BF16),
        vmem((SLOTS, unit, width), BF16),
        vmem((SLOTS, hops, 2, 7 * unit, width), BF16),
        vmem((SLOTS, hops, 2, 2, 2, 2 * unit, width), BF16),
        DMA((2,)),
        DMA((2,)),
        DMA((STAGES,)),
        DMA((2,)),
        DMA((2,)),
        DMA((STAGES, 8)),
        DMA((SLOTS, 8)),
        DMA((STAGES, 2, hops, 2)),
        DMA((SLOTS, 2, hops, 2)),
        DMA((nz,)),
        DMA((nz,)),
        DMA((4, 8)),
        DMA((4, 8)),
        DMA((2,)),
        vmem(ada.shape, BF16),
        vmem((2 * nz,) + mod_grad.shape[1:], F32),
        vmem((4,) + mod_grad.shape[1:], F32),
        vmem((8, rows), F32),
        vmem((nz, 8, rows), F32),
        vmem((8, 8, rows), F32),
    ]
    sds = jax.ShapeDtypeStruct
    frames, _, patches, lat_width = grad_latents.shape
    return pl.pallas_call(
        functools.partial(
            reduce_kernel,
            chunks=chunks,
            n_x=len(x_list),
            n_g=len(g_list),
            split_at=split_at - 2 * width,
            nz=nz,
            rows=rows,
            width=width,
        ),
        out_shape=[
            sds((len(g_list), rows, cols), BF16),
            sds((nz, frames, patches, lat_width), BF16),
            sds((4,) + mod_grad.shape[1:], F32),
            sds((8, rows), F32),
        ],
        in_specs=[ANY] * (len(x_list) + len(g_list)) + [ANY, VM, ANY],
        out_specs=[ANY, ANY, VM, VM],
        scratch_shapes=scratch,
        compiler_params=pltpu.CompilerParams(
            collective_id=1, has_side_effects=True, vmem_limit_bytes=60 << 20
        ),
        name="reduce_weights",
    )(*x_list, *g_list, grad_latents, mod_grad, ada)


def transit_back_kernel(in_ref, res_ref, out_ref, res_o, s_sem, r_sem, local_sem, *, nz):
    y, c, x, z = position()
    greet([across(d, nz)[0] for d in range(1, 2 * nz)])
    copies = []
    for d in range(1, 2 * nz):
        target, q = across(d, nz)
        copies.append(
            remote(in_ref.at[q], out_ref.at[:, z, x], s_sem.at[d], r_sem.at[d], target)
        )
    copies.append(
        remote(res_ref.at[1 - x], res_o.at[:, x], s_sem.at[0], r_sem.at[0], device(y, c, 1 - x, z))
    )
    send_all(copies)
    own = [
        pltpu.make_async_copy(in_ref.at[x * nz + z], out_ref.at[:, z, x], local_sem.at[0]),
        pltpu.make_async_copy(res_ref.at[x], res_o.at[:, x], local_sem.at[1]),
    ]
    send_all(own)
    for copy in own:
        copy.wait()
    finish_all(copies)


def to_frames(rows, result, nz):
    _, frames, patches, width = rows.shape
    halves, all_frames, _, _ = result.shape
    sds = jax.ShapeDtypeStruct
    return pl.pallas_call(
        functools.partial(transit_back_kernel, nz=nz),
        out_shape=[
            sds((frames, nz, halves, patches, width), BF16),
            sds((all_frames, halves, patches, width), BF16),
        ],
        in_specs=[ANY, ANY],
        out_specs=[ANY, ANY],
        scratch_shapes=[DMA((2 * nz,)), DMA((2 * nz,)), DMA((2,))],
        compiler_params=pltpu.CompilerParams(collective_id=3, has_side_effects=True),
        name="to_frames",
    )(rows, result)


def normalize(stream):
    center = stream - jnp.mean(stream, axis=-1, keepdims=True)
    inverse = lax.rsqrt(jnp.mean(center * center, axis=-1, keepdims=True) + EPSILON)
    return center * inverse, inverse


def norm_backward(grad_normed, normed, inverse):
    mean_grad = jnp.mean(grad_normed, axis=-1, keepdims=True)
    mean_along = jnp.mean(grad_normed * normed, axis=-1, keepdims=True)
    return inverse * (grad_normed - mean_grad - normed * mean_along)


def gelu_tanh(values):
    return jax.nn.gelu(values, approximate=True)


def dot(a, b):
    return jnp.dot(a, b, preferred_element_type=F32)


def dot_t(a, b):
    return lax.dot_general(a, b, (((1,), (1,)), ((), ())), preferred_element_type=F32)


def attend_forward(heads, factor):
    q, k, v = heads[:, :, :, 0], heads[:, :, :, 1], heads[:, :, :, 2]
    scores = jnp.einsum("tglhe,tgmhe->tghlm", q, k, preferred_element_type=F32) * factor
    peak = jnp.max(scores, axis=-1, keepdims=True)
    expanded = jnp.exp(scores - peak)
    total = jnp.sum(expanded, axis=-1, keepdims=True)
    probs = (expanded / total).astype(BF16)
    mixed = jnp.einsum("tghlm,tgmhe->tglhe", probs, v, preferred_element_type=F32)
    return mixed.astype(BF16), peak + jnp.log(total)


def attend_backward(heads, log_total, grad_mixed, factor):
    q, k, v = heads[:, :, :, 0], heads[:, :, :, 1], heads[:, :, :, 2]
    scores = jnp.einsum("tglhe,tgmhe->tghlm", q, k, preferred_element_type=F32) * factor
    probs = jnp.exp(scores - log_total)
    grad_v = jnp.einsum(
        "tghlm,tglhe->tgmhe", probs.astype(BF16), grad_mixed, preferred_element_type=F32
    )
    grad_probs = jnp.einsum("tglhe,tgmhe->tghlm", grad_mixed, v, preferred_element_type=F32)
    inner = jnp.sum(grad_probs * probs, axis=-1, keepdims=True)
    grad_scores = (probs * (grad_probs - inner)).astype(BF16)
    grad_q = jnp.einsum("tghlm,tgmhe->tglhe", grad_scores, k, preferred_element_type=F32) * factor
    grad_k = jnp.einsum("tghlm,tglhe->tgmhe", grad_scores, q, preferred_element_type=F32) * factor
    return jnp.stack([grad_q, grad_k, grad_v], axis=3).astype(BF16)


def block_forward(stream, modulation, weights, group):
    attn, up, down = weights
    blocks, width, cols = attn.shape
    inner = cols // 4 * 3
    head_count = cols // 4 // HEAD_DIM
    clips, per_clip, _ = stream.shape
    tokens = clips * per_clip
    factor = HEAD_DIM**-0.5

    def column(i):
        return modulation[:, i][:, None, :]

    normed_a, inverse_a = normalize(stream)
    hidden_a = (normed_a * (1.0 + column(1)) + column(0)).astype(BF16).reshape(tokens, width)
    triple = jnp.stack([dot(hidden_a, attn[t, :, :inner]).astype(BF16) for t in range(blocks)])
    heads = triple.reshape(blocks, tokens // group, group, 3, head_count, HEAD_DIM)
    mixed, log_total = attend_forward(heads, factor)
    mixed = mixed.reshape(blocks, tokens, cols // 4)
    branch_a = sum(dot_t(mixed[t], attn[t, :, inner:]) for t in range(blocks)).reshape(stream.shape)
    middle = stream + column(2) * branch_a
    normed_b, inverse_b = normalize(middle)
    hidden_b = (normed_b * (1.0 + column(4)) + column(3)).astype(BF16).reshape(tokens, width)
    pre_act = jnp.stack([dot(hidden_b, up[t]) for t in range(blocks)])
    activated = gelu_tanh(pre_act).astype(BF16)
    branch_b = sum(dot_t(activated[t], down[t]) for t in range(blocks)).reshape(stream.shape)
    output = middle + column(5) * branch_b
    saved = (
        normed_a, inverse_a, hidden_a, heads, log_total, mixed, branch_a,
        normed_b, inverse_b, hidden_b, pre_act, activated, branch_b,
    )
    return output, saved


def block_backward(grad, modulation, weights, saved, group):
    attn, up, down = weights
    blocks, width, cols = attn.shape
    inner = cols // 4 * 3
    head_count = cols // 4 // HEAD_DIM
    (
        normed_a, inverse_a, hidden_a, heads, log_total, mixed, branch_a,
        normed_b, inverse_b, hidden_b, pre_act, activated, branch_b,
    ) = saved
    tokens = hidden_a.shape[0]
    factor = HEAD_DIM**-0.5

    def column(i):
        return modulation[:, i][:, None, :]

    def clip_sum(values):
        return jnp.sum(values, axis=1)

    gate_b = clip_sum(grad * branch_b)
    branch_grad_b = (grad * column(5)).astype(BF16).reshape(tokens, width)
    grad_act = jnp.stack([dot(branch_grad_b, down[t]) for t in range(blocks)])
    grad_pre = jax.vjp(gelu_tanh, pre_act)[1](grad_act)[0].astype(BF16)
    grad_hidden_b = sum(dot_t(grad_pre[t], up[t]) for t in range(blocks)).reshape(grad.shape)
    shift_b = clip_sum(grad_hidden_b)
    scale_b = clip_sum(grad_hidden_b * normed_b)
    grad_middle = grad + norm_backward(grad_hidden_b * (1.0 + column(4)), normed_b, inverse_b)
    gate_a = clip_sum(grad_middle * branch_a)
    branch_grad_a = (grad_middle * column(2)).astype(BF16).reshape(tokens, width)
    grad_mixed = jnp.stack(
        [dot(branch_grad_a, attn[t, :, inner:]).astype(BF16) for t in range(blocks)]
    )
    grad_mixed = grad_mixed.reshape(blocks, tokens // group, group, head_count, HEAD_DIM)
    grad_heads = attend_backward(heads, log_total, grad_mixed, factor)
    grad_triple = grad_heads.reshape(blocks, tokens, inner)
    grad_hidden_a = sum(
        dot_t(grad_triple[t], attn[t, :, :inner]) for t in range(blocks)
    ).reshape(grad.shape)
    shift_a = clip_sum(grad_hidden_a)
    scale_a = clip_sum(grad_hidden_a * normed_a)
    grad_input = grad_middle + norm_backward(
        grad_hidden_a * (1.0 + column(1)), normed_a, inverse_a
    )
    grad_modulation = jnp.stack([shift_a, scale_a, gate_a, shift_b, scale_b, gate_b], axis=1)
    x_list = [hidden_a, branch_grad_a, hidden_b, branch_grad_b]
    g_list = [jnp.concatenate([grad_triple, mixed], axis=2), grad_pre, activated]
    return grad_input, grad_modulation, x_list, g_list


def local_anywhere(
    latents, condition, teacher, valid_mask,
    qkv_weight, out_weight, up_weight, down_weight, ada_weight,
):
    n_dp, n_seq, n_tensor = (lax.axis_size(a) for a in (DP, SEQ, TENSOR))
    clips, frames, patches, width = latents.shape
    rows = ada_weight.shape[1]
    blocks = qkv_weight.shape[0]
    heads_width = qkv_weight.shape[3]
    inner = 3 * heads_width
    dp, seq, tensor = (lax.axis_index(a) for a in (DP, SEQ, TENSOR))
    row_block = dp * n_seq + seq

    shards = pack_shards(qkv_weight, out_weight, up_weight, down_weight)
    full = lax.all_gather(shards, (DP, SEQ), axis=1, tiled=True)
    full = lax.all_gather(full, TENSOR, axis=1)
    weights = [(full[3 * b], full[3 * b + 1], full[3 * b + 2]) for b in range(blocks)]

    cond_float = condition.astype(F32)
    all_cond = lax.all_gather(condition, DP, axis=0, tiled=True).astype(F32)
    all_silu = jax.nn.silu(all_cond).astype(BF16)
    silu_rows = lax.dynamic_slice_in_dim(all_silu, row_block * rows, rows, axis=1)
    partial_mod = jnp.einsum("cd,bdke->cbke", silu_rows, ada_weight, preferred_element_type=F32)
    partial_mod = lax.psum_scatter(partial_mod, DP, scatter_dimension=0, tiled=True)
    partial_mod = lax.psum(partial_mod, SEQ)
    modulation = lax.all_gather(partial_mod, TENSOR, axis=3, tiled=True)

    by_frame = frames % n_tensor == 0
    split_axis = 1 if by_frame else 0

    def to_spatial(v):
        return lax.all_to_all(v, TENSOR, split_axis=split_axis, concat_axis=2, tiled=True)

    def from_spatial(v):
        return lax.all_to_all(v, TENSOR, split_axis=2, concat_axis=split_axis, tiled=True)

    def to_temporal(v):
        return lax.all_to_all(v, SEQ, split_axis=2, concat_axis=1, tiled=True)

    def from_temporal(v):
        return lax.all_to_all(v, SEQ, split_axis=1, concat_axis=2, tiled=True)

    own_clips = clips if by_frame else clips // n_tensor
    first_clip = 0 if by_frame else tensor * own_clips
    spatial_mod = lax.dynamic_slice_in_dim(modulation[:, 0], first_clip, own_clips, axis=0)
    temporal_mod = modulation[:, 1]

    def patch_major(v):
        return v.transpose(0, 2, 1, 3)

    spatial = to_spatial(latents)
    spatial_shape = spatial.shape
    stream = spatial.astype(F32).reshape(own_clips, -1, width)
    stream, saved_0 = block_forward(stream, spatial_mod, weights[0], spatial_shape[2])
    moved = to_temporal(from_spatial(stream.astype(BF16).reshape(spatial_shape)))
    temporal_shape = moved.shape
    stream = patch_major(moved).astype(F32).reshape(clips, -1, width)
    stream, saved_1 = block_forward(stream, temporal_mod, weights[1], temporal_shape[1])

    def to_frames(v):
        return patch_major(
            v.reshape(clips, temporal_shape[2], temporal_shape[1], width)
        )

    block_out = from_temporal(to_frames(stream.astype(BF16)))

    teacher_rows = patch_major(to_temporal(teacher)).astype(F32).reshape(clips, -1, width)
    mask_float = valid_mask.astype(F32)
    own_mask = lax.dynamic_slice_in_dim(
        mask_float, seq * temporal_shape[2], temporal_shape[2], axis=1
    )
    mask_rows = jnp.repeat(own_mask, temporal_shape[1], axis=1)[:, :, None]
    error = stream - teacher_rows
    error_sum = lax.psum(jnp.sum(mask_rows * error * error), (DP, SEQ, TENSOR))
    total_frames = frames * n_seq
    valid_count = lax.psum(jnp.sum(mask_float), (DP, TENSOR)) * total_frames
    loss_value = error_sum / (width * valid_count)
    token_total = clips * frames * patches * n_dp * n_seq * n_tensor
    grad = mask_rows * error * (2.0 * token_total / valid_count)

    grad, mod_grad_1, x_1, g_1 = block_backward(
        grad, temporal_mod, weights[1], saved_1, temporal_shape[1]
    )
    moved = to_spatial(from_temporal(to_frames(grad.astype(BF16))))
    grad = moved.astype(F32).reshape(own_clips, -1, width)
    grad, mod_grad_0, x_0, g_0 = block_backward(
        grad, spatial_mod, weights[0], saved_0, spatial_shape[2]
    )
    grad_latents = from_spatial(grad.astype(BF16).reshape(spatial_shape)).astype(F32)

    x_list, g_list = x_0 + x_1, g_0 + g_1
    terms = []
    for b in range(blocks):
        for layer, q in ((0, 0), (1, 2), (2, 3)):
            term = jnp.einsum(
                "nd,tnk->tdk", x_list[4 * b + q], g_list[3 * b + layer], preferred_element_type=F32
            )
            if layer == 0:
                other = jnp.einsum(
                    "nd,tnk->tdk", x_list[4 * b + 1], g_list[3 * b], preferred_element_type=F32
                )
                term = jnp.where(jnp.arange(term.shape[2]) < inner, term, other)
            term = lax.psum_scatter(
                term.astype(BF16), (DP, SEQ), scatter_dimension=1, tiled=True
            )
            terms.append(lax.psum_scatter(term, TENSOR, scatter_dimension=0, tiled=True)[0])
    summed = jnp.stack(terms)
    grad_qkv, grad_out, grad_up, grad_down = unpack_shards(summed, blocks, heads_width)

    placed_0 = lax.dynamic_update_slice_in_dim(
        jnp.zeros((clips,) + mod_grad_0.shape[1:], F32), mod_grad_0, first_clip, axis=0
    )
    mod_grad = jnp.stack([placed_0, mod_grad_1], axis=1)
    mod_grad = lax.psum_scatter(mod_grad, TENSOR, scatter_dimension=3, tiled=True)
    mod_grad = lax.psum(mod_grad, SEQ)
    mod_grad = lax.all_gather(mod_grad, DP, axis=0, tiled=True)
    grad_ada = jnp.einsum("cd,cbke->bdke", silu_rows.astype(F32), mod_grad, precision=HIGHEST)
    grad_silu = jnp.einsum("cbke,bdke->cd", mod_grad, ada_weight.astype(F32), precision=HIGHEST)
    grad_silu = lax.psum(grad_silu, TENSOR)
    grad_silu = lax.all_gather(grad_silu, (DP, SEQ), axis=1, tiled=True)
    grad_silu = lax.dynamic_slice_in_dim(grad_silu, dp * clips, clips, axis=0)
    grad_condition = jax.vjp(jax.nn.silu, cond_float)[1](grad_silu)[0]
    return (
        block_out, loss_value, grad_latents, grad_condition,
        grad_qkv, grad_out, grad_up, grad_down, grad_ada,
    )


def pack_shards(qkv_weight, out_weight, up_weight, down_weight):
    blocks, rows = qkv_weight.shape[:2]
    shards = []
    for b in range(blocks):
        shards.append(jnp.concatenate([qkv_weight[b].reshape(rows, -1), out_weight[b].T], axis=1))
        shards.append(up_weight[b])
        shards.append(down_weight[b].T)
    return jnp.stack(shards)


def unpack_shards(summed, blocks, heads_width):
    rows = summed.shape[1]
    inner = 3 * heads_width
    summed = summed.reshape(blocks, 3, rows, -1).astype(F32)
    return (
        summed[:, 0, :, :inner].reshape(blocks, rows, 3, heads_width),
        summed[:, 0, :, inner:].transpose(0, 2, 1),
        summed[:, 1],
        summed[:, 2].transpose(0, 2, 1),
    )


def local_grid(
    latents, condition, teacher, valid_mask,
    qkv_weight, out_weight, up_weight, down_weight, ada_weight,
):
    n_dp, n_seq, nz = (lax.axis_size(a) for a in (DP, SEQ, TENSOR))
    _, frames, patches, width = latents.shape
    blocks, rows = ada_weight.shape[:2]
    heads_width = qkv_weight.shape[3]
    seq = lax.axis_index(SEQ)
    all_frames, own_patches, own_frames = frames * n_seq, patches // n_seq, frames // nz
    tokens = frames * patches

    shards = pack_shards(qkv_weight, out_weight, up_weight, down_weight)
    cond_float = condition.astype(F32)
    mask_float = valid_mask.astype(F32)
    count = jnp.broadcast_to(jnp.sum(mask_float), (1, ada_weight.shape[3]))
    ada = ada_weight.transpose(0, 2, 1, 3)
    full, x_0, teacher_rows, modulation, silu_rows, counted, final, saved_0, saved_1 = forward_pass(
        shards,
        latents.reshape(nz, own_frames, patches, width),
        teacher.reshape(frames, n_seq, own_patches, width),
        cond_float.reshape(-1, rows),
        count,
        ada,
        nz,
        n_seq,
        all_frames,
    )
    valid_count = counted[0, 0] / n_seq * all_frames
    token_total = tokens * n_dp * n_seq * nz
    scale = (2.0 * token_total / valid_count).reshape(1, 1)
    own_mask = lax.dynamic_slice_in_dim(mask_float, seq * own_patches, own_patches, axis=1)
    mask_rows = jnp.repeat(own_mask.reshape(-1), all_frames).reshape(tokens, 1)

    frame, group = tokens // own_frames, 8 * all_frames

    grad, mod_grad_1, a_1, b_1, g_1, p_1, result, error = backward_call(
        (final, teacher_rows.reshape(tokens, width), mask_rows, scale),
        saved_1[0], modulation[1], full, saved_1, 3, group, all_frames, "temporal_backward",
    )
    grad, block_out = to_frames(
        grad.reshape(n_seq * nz, own_frames, own_patches, width),
        result.reshape(n_seq, frames, own_patches, width),
        nz,
    )
    grad, mod_grad_0, a_0, b_0, g_0, p_0 = backward_call(
        (grad.reshape(tokens, width),), x_0, modulation[0], full, saved_0, 0, frame, None, "spatial_backward"
    )

    mod_grad = jnp.concatenate(
        [mod_grad_0, mod_grad_1, jnp.broadcast_to(jnp.sum(error), (4, width))], axis=0
    )
    mod_grad = mod_grad.reshape(16, nz, -1).transpose(1, 0, 2)
    summed, grad_latents, mod_all, silu_grad = reduce_weights(
        [saved_0[1], a_0, saved_0[7], b_0, saved_1[1], a_1, saved_1[7], b_1],
        [g_0, p_0, saved_0[9], g_1, p_1, saved_1[9]],
        grad.reshape(own_frames, nz, patches, width),
        mod_grad,
        ada,
        rows,
        nz,
        3 * heads_width,
    )
    loss_value = jnp.sum(mod_all[:, 12, 0]) / (width * valid_count)
    grad_ada = jnp.einsum(
        "cd,cbke->bdke",
        silu_rows[:n_dp],
        mod_all[:, : 6 * blocks].reshape(n_dp, blocks, 6, -1),
        precision=HIGHEST,
    )
    grad_condition = jax.vjp(jax.nn.silu, cond_float)[1](silu_grad.reshape(1, width))[0]
    return (
        block_out.reshape(latents.shape),
        loss_value,
        grad_latents.reshape(latents.shape).astype(F32),
        grad_condition,
        *unpack_shards(summed, blocks, heads_width),
        grad_ada,
    )


def local(latents, *rest):
    sizes = tuple(lax.axis_size(a) for a in (DP, SEQ, TENSOR))
    if sizes == (4, 2, 4) and latents.shape[0] == 1:
        return local_grid(latents, *rest)
    return local_anywhere(latents, *rest)


def solution(mesh):
    return jax.shard_map(
        local,
        mesh=mesh,
        in_specs=(
            P(DP, SEQ, TENSOR, None),
            P(DP, None),
            P(DP, SEQ, TENSOR, None),
            P(DP, TENSOR),
            P(None, (DP, SEQ), None, TENSOR),
            P(None, TENSOR, (DP, SEQ)),
            P(None, (DP, SEQ), TENSOR),
            P(None, TENSOR, (DP, SEQ)),
            P(None, (DP, SEQ), None, TENSOR),
        ),
        out_specs=(
            P(DP, SEQ, TENSOR, None),
            P(),
            P(DP, SEQ, TENSOR, None),
            P(DP, None),
            P(None, (DP, SEQ), None, TENSOR),
            P(None, TENSOR, (DP, SEQ)),
            P(None, (DP, SEQ), TENSOR),
            P(None, TENSOR, (DP, SEQ)),
            P(None, (DP, SEQ), None, TENSOR),
        ),
        check_vma=False,
    )
```

```python
import functools

import jax
import jax.numpy as jnp
from jax import lax
from jax.experimental import pallas as pl
from jax.experimental.pallas import tpu as pltpu
from jax.sharding import PartitionSpec as P

DP, SEQ, TENSOR = "dp", "seq", "tensor"
START, SEND, RECV = range(3)
HEAD_DIM = 72
EPSILON = 1e-06
HIGHEST = lax.Precision.HIGHEST
MESH = pl.DeviceIdType.MESH
DMA = pltpu.SemaphoreType.DMA
BF16 = jnp.bfloat16
F32 = jnp.float32
ANY = pl.BlockSpec(memory_space=pl.ANY)
VM = pl.BlockSpec(memory_space=pltpu.VMEM)
LANES = 128
NEGATIVE = -1e30
GELU_C = 0.7978845608028654
GELU_K = 0.044715


def position():
    dp = lax.axis_index(DP)
    return dp // 2, dp % 2, lax.axis_index(SEQ), lax.axis_index(TENSOR)


def device(y, c, x, z):
    return (y * 2 + c, x, z)


def neighbours(nz):
    y, c, x, z = position()
    return (
        device(y, c, 1 - x, z),
        device(1 - y, c, x, z),
        device(y, 1 - c, x, z),
        device(y, c, x, jnp.maximum(z - 1, 0)),
        device(y, c, x, jnp.minimum(z + 1, nz - 1)),
    )


def remote(src, dst, send_sem, recv_sem, target):
    return pltpu.make_async_remote_copy(
        src_ref=src,
        dst_ref=dst,
        send_sem=send_sem,
        recv_sem=recv_sem,
        device_id=target,
        device_id_type=MESH,
    )


def in_plane(d):
    y, c, x, z = position()
    q = (y * 4 + c * 2 + x + d) % 8
    return (q // 2, q % 2, z), q


def across(d, nz):
    y, c, x, z = position()
    q = (x * nz + z + d) % (2 * nz)
    return (y * 2 + c, q // nz, q % nz), q


def over_z(d, nz):
    y, c, x, z = position()
    q = (z + d) % nz
    return device(y, c, x, q), q


def over_dp(d):
    y, c, x, z = position()
    q = (y * 2 + c + d) % 4
    return (q, x, z), q


def greet(peers):
    barrier = pltpu.get_barrier_semaphore()
    for target in peers:
        pl.semaphore_signal(barrier, inc=1, device_id=target, device_id_type=MESH)
    pl.semaphore_wait(barrier, len(peers))


def send_all(copies):
    for copy in copies:
        copy.start()


def finish_all(copies):
    for copy in copies:
        copy.wait_send()
        copy.wait_recv()


def kdot(a, b):
    return jnp.dot(a, b, preferred_element_type=F32)


def kdot_t(a, b):
    return lax.dot_general(a, b, (((1,), (1,)), ((), ())), preferred_element_type=F32)


class Lanes:
    def __init__(self, span):
        self.span = span
        self.heads = span // HEAD_DIM
        self.starts = [i * span // LANES * LANES for i in range(4)]
        self.offsets = [i * span - s for i, s in enumerate(self.starts)]
        self.width = 3 * LANES
        self.qkv = self.starts[2] + self.width

    def place(self, which, h):
        return self.offsets[which] + h * HEAD_DIM - (h // 2) * LANES

    def mask(self, which, h):
        lane = lax.broadcasted_iota(jnp.int32, (1, 2 * LANES), 1) - self.place(which, h)
        return ((lane >= 0) & (lane < HEAD_DIM)).astype(F32).astype(BF16)


def row_loop(total, step, body, unroll=2):
    def go(i, carry):
        body(pl.ds(pl.multiple_of(i * step, step), step))
        return carry

    lax.fori_loop(0, total // step, go, 0, unroll=unroll)


def tiles(total):
    first = -(-total // 2 // LANES) * LANES
    return ((0, first), (first, total - first))


def normed_of(v):
    center = v - jnp.mean(v, axis=-1, keepdims=True)
    inverse = lax.rsqrt(jnp.mean(center * center, axis=-1, keepdims=True) + EPSILON)
    return center * inverse, inverse


def gelu_inner(u):
    return jnp.tanh(GELU_C * (u + GELU_K * u * u * u))


def order_matrix(tokens, group, back):
    per = tokens // group
    row = lax.broadcasted_iota(jnp.int32, (tokens, tokens), 1 if back else 0)
    col = lax.broadcasted_iota(jnp.int32, (tokens, tokens), 0 if back else 1)
    return (col == row % group * per + row // group).astype(F32).astype(BF16)


def reorder(dst, src, order):
    for c0, n in tiles(src.shape[1]):
        dst[:, pl.ds(c0, n)] = kdot(order[...], src[:, pl.ds(c0, n)]).astype(BF16)


class Blocks:
    def __init__(self, w_ref, ring, sem, order, ready):
        self.w_ref, self.ring, self.sem, self.order = w_ref, ring, sem, order
        self.ready = ready
        self.loaded = self.done = 0
        self.depth = ring.shape[0]

    def copy(self, i):
        layer, t = self.order[i]
        s = i % self.depth
        dst = self.ring.at[s]
        if len(self.w_ref.shape) == 7:
            dst = dst.reshape(self.w_ref.shape[2:])
        return pltpu.make_async_copy(self.w_ref.at[layer, t], dst, self.sem.at[s])

    def pump(self):
        while (
            self.loaded < len(self.order)
            and self.loaded < self.done + self.depth
            and self.order[self.loaded][0] in self.ready
        ):
            self.copy(self.loaded).start()
            self.loaded += 1

    def take(self):
        i = self.done
        self.pump()
        self.copy(i).wait()
        return self.ring.at[i % self.depth]

    def drop(self):
        self.done += 1
        self.pump()


class Saves:
    def __init__(self, sem):
        self.sem, self.copies, self.used = sem, [], 0

    def put(self, src, dst):
        copy = pltpu.make_async_copy(src, dst, self.sem.at[self.used])
        copy.start()
        self.copies.append(copy)
        self.used += 1
        return copy

    def wait(self, copy):
        if any(other is copy for other in self.copies):
            copy.wait()
            self.copies = [other for other in self.copies if other is not copy]

    def finish(self):
        for copy in self.copies:
            copy.wait()
        self.copies = []


def stack_heads(dst, value, masks, group):
    for h, mask in enumerate(masks):
        lane = (h // 2) * LANES
        dst[h // 2, pl.ds(h % 2 * group, group), :] = value[:, lane : lane + 2 * LANES] * mask


FORWARD_SAVES = 24


def forward_steps(x_in, mod_ref, out_ref, saved, scratch, blocks, saves, *, sub, group, lanes):
    x_o, hida_o, qkv_o, prob_o, mix_o, bra_o, hidb_o, pre_o, act_o, brb_o = saved
    xbuf, perm, acc, qkv, qst, sc, hida, prob, mix, hidb, pre, act, mid, bra, brb = scratch
    tokens, width = x_in.shape
    nt = act.shape[0]
    cols = act.shape[2]
    heads = lanes.heads
    scale = HEAD_DIM**-0.5 * 1.4426950408889634
    x_ref = x_in if sub is None else xbuf
    steps = []

    def mod(i):
        return mod_ref[i : i + 1, :]

    def begin():
        if sub is not None:
            perm[...] = order_matrix(tokens, sub, False)
            reorder(xbuf, x_in, perm)
            saves.put(xbuf, x_o)

        def rows(r):
            n, _ = normed_of(x_ref[r, :].astype(F32))
            hida[r, :] = (n * (1.0 + mod(1)) + mod(0)).astype(BF16)

        row_loop(tokens, 32, rows)
        saves.put(hida, hida_o)

    steps.append((None, begin))

    kept = {}

    def project(t):
        if t >= 2:
            saves.wait(kept[0, t - 2])
        w = blocks.take()
        for c0, n in tiles(lanes.qkv):
            qkv[t % 2, :, pl.ds(c0, n)] = kdot(hida[...], w[:, pl.ds(c0, n)]).astype(BF16)
        kept[0, t] = saves.put(qkv.at[t % 2], qkv_o.at[t])

    def attend(t):
        now = qkv.at[t % 2]
        masks = [lanes.mask(1, h) for h in range(heads)]

        def one(g, carry):
            r = pl.ds(pl.multiple_of(g * group, group), group)
            q = pltpu.roll(now[r, pl.ds(0, lanes.width)].astype(F32), lanes.offsets[1], 1).astype(BF16)
            stack_heads(qst, q, masks, group)
            for p in range(heads // 2):
                k = now[r, pl.ds(lanes.starts[1] + p * LANES, 2 * LANES)]
                sc[:, pl.ds(p * 2 * group, 2 * group)] = kdot_t(k, qst[p])

            def soft(j, c2):
                at = pl.ds(pl.multiple_of(j * LANES, LANES), LANES)
                s = sc[:, at] * scale
                if sub is not None:
                    row = lax.broadcasted_iota(jnp.int32, s.shape, 0) // sub
                    col = lax.broadcasted_iota(jnp.int32, s.shape, 1) // sub
                    s = jnp.where(row == col, s, NEGATIVE)
                e = jnp.exp2(s - jnp.max(s, axis=0, keepdims=True))
                prob[t, g, :, at] = (e * (1.0 / jnp.sum(e, axis=0, keepdims=True))).astype(BF16)
                return c2

            lax.fori_loop(0, heads * group // LANES, soft, 0, unroll=2)
            pieces = [jnp.zeros((lanes.offsets[3], group), F32)]
            for p in range(heads // 2):
                v = now[r, pl.ds(lanes.starts[2] + p * LANES, 2 * LANES)].T
                for h in (2 * p, 2 * p + 1):
                    got = kdot(v, prob[t, g, :, pl.ds(h * group, group)])
                    at = lanes.place(2, h)
                    pieces.append(got[at : at + HEAD_DIM])
            rest = lanes.width - lanes.offsets[3] - heads * HEAD_DIM
            if rest:
                pieces.append(jnp.zeros((rest, group), F32))
            mix[t, r, :] = jnp.concatenate(pieces, axis=0).T.astype(BF16)
            return carry

        lax.fori_loop(0, tokens // group, one, 0)
        saves.put(prob.at[t], prob_o.at[t])
        saves.put(mix.at[t], mix_o.at[t])

    def bring_out(t):
        w = blocks.ring.at[blocks.done % blocks.depth]
        got = kdot_t(mix[t], w[:, pl.ds(lanes.starts[3], lanes.width)])
        if t == 0:
            acc[...] = got
        else:
            acc[...] += got
        blocks.drop()

    for t in range(nt):
        steps.append((0, functools.partial(project, t)))
        steps.append((0, functools.partial(attend, t)))
        steps.append((0, functools.partial(bring_out, t)))

    def between():
        def rows(r):
            b = acc[r, :]
            m = x_ref[r, :].astype(F32) + mod(2) * b
            mid[r, :] = m
            bra[r, :] = b.astype(BF16)
            n, _ = normed_of(m)
            hidb[r, :] = (n * (1.0 + mod(4)) + mod(3)).astype(BF16)

        row_loop(tokens, 32, rows)
        saves.put(bra, bra_o)
        saves.put(hidb, hidb_o)

    steps.append((0, between))

    def go_up(t):
        if t >= 2:
            saves.wait(kept[1, t - 2])
        w = blocks.take()
        for c0, n in tiles(cols):
            u = kdot(hidb[...], w[:, pl.ds(c0, n)])
            pre[t % 2, :, pl.ds(c0, n)] = u.astype(BF16)
            act[t, :, pl.ds(c0, n)] = (0.5 * u * (1.0 + gelu_inner(u))).astype(BF16)
        kept[1, t] = saves.put(pre.at[t % 2], pre_o.at[t])
        saves.put(act.at[t], act_o.at[t])
        blocks.drop()

    def go_down(t):
        w = blocks.take()
        got = kdot_t(act[t], w[...])
        if t == 0:
            acc[...] = got
        else:
            acc[...] += got
        blocks.drop()

    for t in range(nt):
        steps.append((1, functools.partial(go_up, t)))
    for t in range(nt):
        steps.append((2, functools.partial(go_down, t)))

    def end():
        def rows(r):
            b = acc[r, :]
            brb[r, :] = b.astype(BF16)
            out_ref[r, :] = (mid[r, :] + mod(5) * b).astype(out_ref.dtype)

        row_loop(tokens, 32, rows)
        saves.put(brb, brb_o)

    steps.append((2, end))
    return steps


def forward_scratch(tokens, width, nt, cols, group, sub, lanes):
    side = tokens if sub is not None else 16
    vmem = pltpu.VMEM
    return [
        vmem((side, width), BF16),
        vmem((side, side), BF16),
        vmem((tokens, width), F32),
        vmem((2, tokens, lanes.qkv), BF16),
        vmem((lanes.heads // 2, 2 * group, 2 * LANES), BF16),
        vmem((group, lanes.heads * group), F32),
        vmem((tokens, width), BF16),
        vmem((nt, tokens // group, group, lanes.heads * group), BF16),
        vmem((nt, tokens, lanes.width), BF16),
        vmem((tokens, width), BF16),
        vmem((2, tokens, cols), BF16),
        vmem((nt, tokens, cols), BF16),
        vmem((tokens, width), F32),
        vmem((tokens, width), BF16),
        vmem((tokens, width), BF16),
    ]


def forward_saved(tokens, width, nt, cols, group, sub, lanes):
    sds = jax.ShapeDtypeStruct
    return [
        sds((tokens, width), BF16),
        sds((tokens, width), BF16),
        sds((nt, tokens, lanes.qkv), BF16),
        sds((nt, tokens // group, group, lanes.heads * group), BF16),
        sds((nt, tokens, lanes.width), BF16),
        sds((tokens, width), BF16),
        sds((tokens, width), BF16),
        sds((nt, tokens, cols), BF16),
        sds((nt, tokens, cols), BF16),
        sds((tokens, width), BF16),
    ]


THIRDS = 3
GATHER_STAGES = 6


class Gather:
    def __init__(self, w_ref, g_ref, sems, nz):
        self.w, self.g, self.nz = w_ref, g_ref, nz
        (
            self.lsem, self.s_zab, self.r_zab, self.s_xy, self.r_xy,
            self.s_zcd, self.r_zcd, self.s_c, self.r_c,
        ) = sems
        self.layers, self.rows, self.cols = w_ref.shape
        self.unit = self.rows // 9
        self.ab = 7 * self.unit
        self.count = self.layers * THIRDS
        self.at = position()
        self.peers = neighbours(nz)

    def columns(self, k):
        width = self.cols // THIRDS
        return k // THIRDS, pl.ds(k % THIRDS * width, width)

    def own(self, l):
        y, c, x, z = self.at
        return pltpu.make_async_copy(self.w.at[l], self.g.at[l, z, y, c, x], self.lsem.at[l])

    def region_ab(self, k, t):
        y, c, x, z = self.at
        l, cs = self.columns(k)
        return self.g.at[l, t, y, c, x, pl.ds(0, self.ab), cs]

    def region_cd(self, k, t):
        y, c, x, z = self.at
        l, cs = self.columns(k)
        return self.g.at[l, t, :, c, :, pl.ds(self.ab, 2 * self.unit), cs]

    def along_z(self, k, hop, which, mode):
        z, nz = self.at[3], self.nz
        below, above = self.peers[3:]
        region = (self.region_ab, self.region_cd)[which]
        ssem, rsem = ((self.s_zab, self.r_zab), (self.s_zcd, self.r_zcd))[which]
        up, down = z - hop, z + hop
        if mode == RECV:

            @pl.when(z - 1 - hop >= 0)
            def _():
                r = region(k, jnp.maximum(z - 1 - hop, 0))
                remote(r, r, ssem.at[k, hop, 1], rsem.at[k, hop, 1], above).wait_recv()

            @pl.when(z + 1 + hop < nz)
            def _():
                r = region(k, jnp.minimum(z + 1 + hop, nz - 1))
                remote(r, r, ssem.at[k, hop, 0], rsem.at[k, hop, 0], below).wait_recv()

            return
        l, cs = self.columns(k)
        first = self.w.at[l, pl.ds(0, self.ab), cs] if which == 0 and hop == 0 else None

        @pl.when((up >= 0) & (z < nz - 1))
        def _():
            r = region(k, jnp.maximum(up, 0))
            copy = remote(r if first is None else first, r, ssem.at[k, hop, 1], rsem.at[k, hop, 1], above)
            copy.start() if mode == START else copy.wait_send()

        @pl.when((down < nz) & (z > 0))
        def _():
            r = region(k, jnp.minimum(down, nz - 1))
            copy = remote(r if first is None else first, r, ssem.at[k, hop, 0], rsem.at[k, hop, 0], below)
            copy.start() if mode == START else copy.wait_send()

    def region_xy(self, k, kind, yy, xx):
        y, c, x, z = self.at
        l, cs = self.columns(k)
        a = (4 if k % 2 == 0 else 3) * self.unit
        ra, rb = pl.ds(0, a), pl.ds(a, self.ab - a)
        rc, rd = pl.ds(self.ab, self.unit), pl.ds(self.ab + self.unit, self.unit)
        g = self.g
        return (
            lambda: g.at[l, :, yy, c, xx, ra, cs],
            lambda: g.at[l, :, yy, c, xx, rb, cs],
            lambda: g.at[l, :, yy, c, :, ra, cs],
            lambda: g.at[l, :, :, c, xx, rb, cs],
            lambda: g.at[l, z, yy, c, xx, rc, cs],
            lambda: g.at[l, z, yy, c, xx, rd, cs],
            lambda: g.at[l, z, yy, c, :, rc, cs],
            lambda: g.at[l, z, :, c, xx, rd, cs],
        )[kind]()

    def along_xy(self, k, kind, mode):
        y, c, x, z = self.at
        on_x = (True, False, False, True, True, False, False, True)[kind]
        target = self.peers[0 if on_x else 1]
        s, r = self.s_xy.at[k, kind], self.r_xy.at[k, kind]
        if mode == RECV:
            there = self.region_xy(k, kind, y, 1 - x) if on_x else self.region_xy(k, kind, 1 - y, x)
            remote(there, there, s, r, target).wait_recv()
            return
        here = self.region_xy(k, kind, y, x)
        l, cs = self.columns(k)
        src = here
        if kind == 4:
            src = self.w.at[l, pl.ds(self.ab, self.unit), cs]
        if kind == 5:
            src = self.w.at[l, pl.ds(self.ab + self.unit, self.unit), cs]
        copy = remote(src, here, s, r, target)
        copy.start() if mode == START else copy.wait_send()

    def to_core(self, k, mode):
        c = self.at[1]
        l, cs = self.columns(k)
        r = self.g.at[l, :, :, 1 - c if mode == RECV else c, :, :, cs]
        copy = remote(r, r, self.s_c.at[k], self.r_c.at[k], self.peers[2])
        if mode == START:
            copy.start()
        elif mode == SEND:
            copy.wait_send()
        else:
            copy.wait_recv()

    def stage(self, k, s):
        z, xy = self.along_z, self.along_xy
        if s == 0:
            z(k, 0, 0, START)
            xy(k, 4, START)
            xy(k, 5, START)
        if s == 1:
            z(k, 0, 0, RECV)
            z(k, 1, 0, START)
            if k % THIRDS == 0:
                self.own(k // THIRDS).wait()
            xy(k, 4, RECV)
            xy(k, 6, START)
            xy(k, 5, RECV)
            xy(k, 7, START)
        if s == 2:
            z(k, 1, 0, RECV)
            z(k, 2, 0, START)
            xy(k, 6, RECV)
            xy(k, 7, RECV)
            z(k, 0, 1, START)
        if s == 3:
            z(k, 2, 0, RECV)
            xy(k, 0, START)
            xy(k, 1, START)
            z(k, 0, 1, RECV)
            z(k, 1, 1, START)
        if s == 4:
            xy(k, 0, RECV)
            xy(k, 2, START)
            xy(k, 1, RECV)
            xy(k, 3, START)
            z(k, 1, 1, RECV)
            z(k, 2, 1, START)
        if s == 5:
            xy(k, 2, RECV)
            xy(k, 3, RECV)
            z(k, 2, 1, RECV)
            self.to_core(k, START)

    def begin(self, ahead):
        self.ahead = ahead
        for l in range(self.layers):
            self.own(l).start()
        for k in range(min(ahead, self.count)):
            self.stage(k, 0)

    def slots(self):
        return self.count + GATHER_STAGES - 1

    def slot(self, i):
        for k in range(self.count):
            s = i - k
            if s == 0 and k + self.ahead < self.count:
                self.stage(k + self.ahead, 0)
            if 1 <= s < GATHER_STAGES:
                self.stage(k, s)

    def arrive(self, layer):
        for k in range(layer * THIRDS, (layer + 1) * THIRDS):
            self.to_core(k, RECV)

    def end(self):
        for k in range(self.count):
            self.to_core(k, SEND)
            for kind in range(8):
                self.along_xy(k, kind, SEND)
            for hop in range(self.nz - 1):
                self.along_z(k, hop, 0, SEND)
                self.along_z(k, hop, 1, SEND)


def forward_pass_kernel(*refs, nz, n_seq, group_0, group_1, sub, lanes):
    w_ref, lat_ref, teach_ref, cond_ref, count_ref, ada_ref = refs[:6]
    g_ref, teach_o, mod_o, silu_o, count_o, final_ref = refs[6:12]
    saved_0, saved_1 = refs[12:22], refs[22:32]
    rest = refs[32:]
    sems, rest = rest[:9], rest[9:]
    (
        s_lat, r_lat, s_tea, r_tea, s_m, r_m, local_sem, s_t, r_t,
        ada, cond_all, parts, landed, mod_all, x0, x1, out_0, ring, wsem, osem_0, osem_1,
        qst_0, sc_0, prob_0,
    ) = rest[:24]
    shared = rest[24:]
    y, c, x, z = position()
    x_dev = neighbours(nz)[0]
    layers = w_ref.shape[0]
    tokens, width = x0.shape
    _, own_frames, patches, _ = lat_ref.shape
    frame = nz * patches
    part = patches // n_seq
    greet(
        [in_plane(d)[0] for d in range(1, 8)]
        + [(y * 2 + c, xx, (z + d) % nz) for d in range(1, nz) for xx in (x, 1 - x)]
    )
    gather = Gather(w_ref, g_ref, sems, nz)

    dp, block = y * 2 + c, (y * 2 + c) * 2 + x
    me = x * nz + z
    side = [
        pltpu.make_async_copy(teach_ref.at[:, x], teach_o.at[x], local_sem.at[0]),
        pltpu.make_async_copy(ada_ref, ada, local_sem.at[1]),
    ]
    lat_in, own_rows, teach_in = [], [], []
    for i in range(own_frames):
        rows = pl.ds(pl.multiple_of(i * frame + z * patches, 16), patches)
        own_rows.append(pltpu.make_async_copy(lat_ref.at[z, i], x0.at[rows], local_sem.at[2 + i]))
        for d in range(1, nz):
            target, q = over_z(d, nz)
            lat_in.append(remote(lat_ref.at[q, i], x0.at[rows], s_lat.at[i, d], r_lat.at[i, d], target))
    teach_in.append(remote(teach_ref.at[:, 1 - x], teach_o.at[x], s_tea, r_tea, x_dev))

    conds, sums, spread = [], [], []
    for d in range(1, 4):
        target, q = over_dp(d)
        conds.append(remote(cond_ref, cond_all.at[dp], s_m.at[0, d], r_m.at[0, d], target))
    for d in range(1, 8):
        target, q = in_plane(d)
        sums.append(remote(parts.at[q // 2], landed.at[d], s_m.at[1, d], r_m.at[1, d], target))
    for d in range(1, nz):
        target, q = over_z(d, nz)
        spread.append(remote(mod_all.at[z], mod_all.at[z], s_m.at[2, d], r_m.at[2, d], target))

    def modulate(step):
        if step == 0:
            send_all(conds)
            cond_all[dp] = cond_ref[...]
        if step == 1:
            finish_all(conds)
            side[1].wait()
            silu_o[...] = jnp.zeros_like(silu_o)
            for i in range(4):
                row = cond_all[i, pl.ds(block, 1), :]
                silu_o[i : i + 1, :] = (row / (1.0 + jnp.exp(-row))).astype(BF16).astype(F32)
            parts[...] = jnp.zeros_like(parts)
            for b in range(ada.shape[0]):
                for k in range(6):
                    got = kdot(silu_o[...].astype(BF16), ada[b, k])
                    for i in range(4):
                        parts[i, 6 * b + k : 6 * b + k + 1, :] = got[i : i + 1]
            for i in range(4):
                parts[i, 12:13, :] = count_ref[...]
            send_all(sums)
        if step == 2:
            finish_all(sums)
            total = parts[dp]
            for d in range(1, 8):
                total = total + landed[d]
            mod_all[z] = total
            send_all(spread)
        if step == 3:
            finish_all(spread)
            count = mod_all[0, 12:13, :]
            for q in range(1, nz):
                count = count + mod_all[q, 12:13, :]
            count_o[...] = count
            for b in range(ada.shape[0]):
                mod_o[b] = jnp.concatenate(
                    [mod_all[q, 6 * b : 6 * b + 6, :] for q in range(nz)], axis=1
                )

    moved, kept = [], []
    for i in range(own_frames):
        dst = x1.at[pl.ds(pl.multiple_of((me * own_frames + i) * part, 16), part)]
        for d in range(1, 2 * nz):
            target, q = across(d, nz)
            src = out_0.at[
                pl.ds(pl.multiple_of(i * frame + q % nz * patches + q // nz * part, 16), part)
            ]
            moved.append(remote(src, dst, s_t.at[i, d], r_t.at[i, d], target))
        src = out_0.at[pl.ds(pl.multiple_of(i * frame + z * patches + x * part, 16), part)]
        kept.append(pltpu.make_async_copy(src, dst, local_sem.at[2 + own_frames + i]))

    ready = set()
    order = [(l, t) for l in range(layers) for t in range(nz)]
    blocks = Blocks(g_ref, ring, wsem, order, ready)
    saves_0, saves_1 = Saves(osem_0), Saves(osem_1)
    per_block = layers // 2
    common = list(shared)
    scratch_1 = common
    scratch_0 = common[:4] + [qst_0, sc_0] + common[6:7] + [prob_0] + common[8:]

    def start_spatial():
        for copy in own_rows:
            copy.wait()
        finish_all(lat_in)
        saves_0.put(x0, saved_0[0])

    def leave_spatial():
        send_all(moved)
        send_all(kept)

    def start_temporal():
        for copy in kept:
            copy.wait()
        finish_all(moved)
        saves_0.finish()

    work = [(None, start_spatial)]
    for need, step in forward_steps(
        x0, mod_o.at[0], out_0, saved_0, scratch_0, blocks, saves_0,
        sub=None, group=group_0, lanes=lanes,
    ):
        work.append((need, step))
    work.append((None, leave_spatial))
    pause = len(work)
    work.append((None, start_temporal))
    for need, step in forward_steps(
        x1, mod_o.at[1], final_ref, saved_1, scratch_1, blocks, saves_1,
        sub=sub, group=group_1, lanes=lanes,
    ):
        work.append((None if need is None else need + per_block, step))

    send_all(own_rows)
    send_all(lat_in)
    modulate(0)
    gather.begin(2)
    send_all(side)
    send_all(teach_in)
    done, waited = 0, 0
    for slot in range(gather.slots() + 1):
        if slot < gather.slots():
            gather.slot(slot)
        if slot % 2 == 1 and slot < 6:
            modulate((slot + 1) // 2)
        if slot >= GATHER_STAGES + THIRDS - 1 and (slot - GATHER_STAGES - THIRDS + 1) % THIRDS == 0:
            layer = (slot - GATHER_STAGES - THIRDS + 1) // THIRDS
            gather.arrive(layer)
            ready.add(layer)
            blocks.pump()
        quota = 5
        while done < len(work) and quota and slot >= 6:
            need = work[done][0]
            if need is not None and need not in ready:
                break
            if done == pause:
                waited += 1
                if waited < 3 and slot < gather.slots():
                    break
            work[done][1]()
            done += 1
            quota -= 1
    while done < len(work):
        work[done][1]()
        done += 1
    gather.end()
    side[0].wait()
    finish_all(teach_in)
    saves_1.finish()


def forward_pass(shards, latents, teacher, cond, count, ada, nz, n_seq, sub):
    layers, rows, cols = shards.shape
    hops = nz - 1
    chunks = layers * THIRDS
    sds = jax.ShapeDtypeStruct
    _, own_frames, patches, width = latents.shape
    tokens = nz * own_frames * patches
    frames, halves, own_patches, _ = teacher.shape
    vmem = pltpu.VMEM
    mod_shape = (16, ada.shape[3])
    lanes = Lanes(cols // 4)
    group_0, group_1 = nz * patches, 8 * sub
    sizes_0 = (tokens, width, nz, cols, group_0, None, lanes)
    sizes_1 = (tokens, width, nz, cols, group_1, sub, lanes)
    scratch_0, scratch_1 = forward_scratch(*sizes_0), forward_scratch(*sizes_1)
    rowsb = vmem((tokens, width), BF16)
    outs = pl.pallas_call(
        functools.partial(
            forward_pass_kernel, nz=nz, n_seq=n_seq, group_0=group_0, group_1=group_1, sub=sub, lanes=lanes
        ),
        out_shape=[
            sds((layers, nz, 2, 2, 2, rows, cols), BF16),
            sds((halves, frames, own_patches, width), BF16),
            sds((2, 6, width), F32),
            sds((8, cond.shape[1]), F32),
            sds((1, ada.shape[3]), F32),
            sds((tokens, width), F32),
        ]
        + forward_saved(*sizes_0)
        + forward_saved(*sizes_1),
        in_specs=[ANY, ANY, ANY, VM, VM, ANY],
        out_specs=[ANY, ANY, VM, VM, VM, VM] + [ANY] * 20,
        scratch_shapes=[
            DMA((layers,)),
            DMA((chunks, hops, 2)),
            DMA((chunks, hops, 2)),
            DMA((chunks, 8)),
            DMA((chunks, 8)),
            DMA((chunks, hops, 2)),
            DMA((chunks, hops, 2)),
            DMA((chunks,)),
            DMA((chunks,)),
            DMA((own_frames, nz)),
            DMA((own_frames, nz)),
            DMA(()),
            DMA(()),
            DMA((3, 8)),
            DMA((3, 8)),
            DMA((2 + 2 * own_frames,)),
            DMA((own_frames, 2 * nz)),
            DMA((own_frames, 2 * nz)),
            vmem(ada.shape, BF16),
            vmem((4,) + cond.shape, F32),
            vmem((4,) + mod_shape, F32),
            vmem((8,) + mod_shape, F32),
            vmem((nz,) + mod_shape, F32),
            rowsb,
            rowsb,
            rowsb,
            vmem((3, width, cols), BF16),
            DMA((3,)),
            DMA((32,)),
            DMA((32,)),
            scratch_0[4],
            scratch_0[5],
            scratch_0[7],
        ]
        + scratch_1,
        compiler_params=pltpu.CompilerParams(
            collective_id=0, has_side_effects=True, vmem_limit_bytes=62 << 20
        ),
        name="forward_pass",
    )(shards, latents, teacher, cond, count, ada)
    full, teach, mod, silu, count, final = outs[:6]
    full = full.reshape(layers, nz, -1, cols)
    return full, teach, mod, silu, count, final, outs[6:16], outs[16:26]


def backward_steps(head, ins, outs, scratch, blocks, saves, marks, *, sub, group, lanes):
    loss = len(head) > 1
    x_hbm, mod_ref, qkv_hbm, prob_hbm, mix_hbm, bra_hbm, pre_hbm, brb_hbm = ins
    gout_ref, mg_ref, gba_o, gbb_o, gat_o, gpre_o = outs[:6]
    (
        gr, acc, gbb, gba, gpre, gat, dmx, qkv, qst, dst, sc, ds, prob, preb, mix,
        x_ref, branch, lsem, tbuf, perm,
    ) = scratch
    tokens, width = gr.shape
    nt, _, cols = pre_hbm.shape
    heads = lanes.heads
    factor = HEAD_DIM**-0.5
    steps = []

    def mod(i):
        return mod_ref[i : i + 1, :]

    def load(src, dst, n):
        return pltpu.make_async_copy(src, dst, lsem.at[n])

    load_x = load(x_hbm, x_ref, 0)
    load_brb = load(brb_hbm, branch, 1)
    load_bra = load(bra_hbm, branch, 2)

    def load_pre(t):
        return load(pre_hbm.at[t], preb, 3)

    def load_heads(t):
        return load(qkv_hbm.at[t], qkv, 4), load(prob_hbm.at[t], prob, 5), load(mix_hbm.at[t], mix, 6)

    def row_sum(v):
        return jnp.sum(v, axis=0, keepdims=True)

    def begin():
        load_brb.start()
        load_pre(0).start()
        send_all(load_heads(0))
        mg_ref[...] = jnp.zeros_like(mg_ref)
        if loss:
            final_hbm, teach_hbm, mask_ref, coef_ref = head
            bout_ref, err_ref = outs[6:]
            load_teach = load(teach_hbm, x_ref, 7)
            load_final = load(final_hbm, gr, 8)
            load_teach.start()
            load_final.start()
            err_ref[...] = jnp.zeros_like(err_ref)
            perm[...] = order_matrix(tokens, sub, False)
            load_teach.wait()
            reorder(tbuf, x_ref, perm)
            load_final.wait()
        load_x.start()
        load_brb.wait()

        def rows(r):
            if loss:
                f = gr[r, :]
                e = f - tbuf[r, :].astype(F32)
                me = mask_ref[r, :] * e
                err_ref[...] += row_sum(me * e)
                gba[r, :] = f.astype(BF16)
                g = me * coef_ref[0, 0]
            else:
                g = head[0][r, :].astype(F32)
            gr[r, :] = g
            mg_ref[5:6, :] += row_sum(g * branch[r, :].astype(F32))
            gbb[r, :] = (g * mod(5)).astype(BF16)

        row_loop(tokens, 32, rows)
        load_bra.start()
        marks[2] = [saves.put(gbb, gbb_o)]
        marks[1], marks[0] = [], []
        if loss:
            perm[...] = order_matrix(tokens, sub, True)
            reorder(bout_ref, gba, perm)

    steps.append(begin)
    kept = {}

    def through_gelu(t):
        if t:
            saves.wait(kept[t - 1])
        w = blocks.take()
        load_pre(t).wait()
        for c0, n in tiles(cols):
            ga = kdot(gbb[...], w[:, pl.ds(c0, n)])
            u = preb[:, pl.ds(c0, n)].astype(F32)
            th = gelu_inner(u)
            slope = 0.5 * (1.0 + th) + 0.5 * u * (1.0 - th * th) * (
                GELU_C * (1.0 + 3.0 * GELU_K * u * u)
            )
            gpre[:, pl.ds(c0, n)] = (ga * slope).astype(BF16)
        kept[t] = saves.put(gpre, gpre_o.at[t])
        if t == nt - 1:
            marks[1].append(kept[t])
        blocks.drop()
        if t + 1 < nt:
            load_pre(t + 1).start()

    def add_up(t, got):
        if t == 0:
            acc[...] = got
        else:
            acc[...] += got

    def under_up(t):
        w = blocks.take()
        add_up(t, kdot_t(gpre[...], w[...]))
        blocks.drop()

    for t in range(nt):
        steps.append(functools.partial(through_gelu, t))
        steps.append(functools.partial(under_up, t))

    def norm_back(gh, base, shift_row, scale_row, scale_i):
        n, inv = normed_of(base)
        mg_ref[shift_row : shift_row + 1, :] += row_sum(gh)
        mg_ref[scale_row : scale_row + 1, :] += row_sum(gh * n)
        dn = gh * (1.0 + mod(scale_i))
        along = jnp.mean(dn * n, axis=-1, keepdims=True)
        return inv * (dn - jnp.mean(dn, axis=-1, keepdims=True) - n * along)

    def between():
        load_x.wait()
        load_bra.wait()

        def rows(r):
            b = branch[r, :].astype(F32)
            middle = x_ref[r, :].astype(F32) + mod(2) * b
            g = gr[r, :] + norm_back(acc[r, :], middle, 3, 4, 4)
            gr[r, :] = g
            mg_ref[2:3, :] += row_sum(g * b)
            gba[r, :] = (g * mod(2)).astype(BF16)

        row_loop(tokens, 32, rows)
        marks[0].append(saves.put(gba, gba_o))

    steps.append(between)
    sent = {}

    def attend(t):
        if t:
            saves.wait(sent[t - 1])
        w = blocks.take()
        d = kdot(gba[...], w[:, pl.ds(lanes.starts[3], lanes.width)])
        back = lanes.width - (lanes.offsets[3] - lanes.offsets[2])
        dmx[...] = pltpu.roll(d, back, 1).astype(BF16)
        for copy in load_heads(t):
            copy.wait()
        kmasks = [lanes.mask(1, h) for h in range(heads)]
        vmasks = [lanes.mask(2, h) for h in range(heads)]

        def one(g, carry):
            r = pl.ds(pl.multiple_of(g * group, group), group)
            q = pltpu.roll(qkv[r, pl.ds(0, lanes.width)].astype(F32), lanes.offsets[1], 1).astype(BF16)
            stack_heads(qst, q, kmasks, group)
            stack_heads(dst, dmx[r, :], vmasks, group)
            for p in range(heads // 2):
                v = qkv[r, pl.ds(lanes.starts[2] + p * LANES, 2 * LANES)]
                sc[:, pl.ds(p * 2 * group, 2 * group)] = kdot_t(v, dst[p])

            def soft(j, c2):
                at = pl.ds(pl.multiple_of(j * LANES, LANES), LANES)
                p = prob[g, :, at].astype(F32)
                gp = sc[:, at]
                inner = jnp.sum(gp * p, axis=0, keepdims=True)
                ds[:, at] = (p * (gp - inner)).astype(BF16)
                return c2

            lax.fori_loop(0, heads * group // LANES, soft, 0, unroll=2)
            pieces, dk, dv = [], [], []
            for p in range(heads // 2):
                pair = pl.ds(p * 2 * group, 2 * group)
                dk.append(kdot(ds[:, pair], qst[p]) * factor)
                dv.append(kdot(prob[g, :, pair], dst[p]))
                k = qkv[r, pl.ds(lanes.starts[1] + p * LANES, 2 * LANES)].T
                for h in (2 * p, 2 * p + 1):
                    got = kdot(k, ds[:, pl.ds(h * group, group)])
                    at = lanes.place(1, h)
                    pieces.append(got[at : at + HEAD_DIM])
            pieces.append(jnp.zeros((lanes.width - heads * HEAD_DIM, group), F32))
            dq = jnp.concatenate(pieces, axis=0).T * factor
            parts = [dq[:, i * LANES : (i + 1) * LANES] for i in range(3)]
            low, high = slice(0, LANES), slice(LANES, 2 * LANES)
            parts[2] = parts[2] + dk[0][:, low]
            parts.append(dk[0][:, high] + dk[1][:, low])
            parts.append(dk[1][:, high] + dv[0][:, low])
            parts.append(dv[0][:, high] + dv[1][:, low])
            parts.append(dv[1][:, high])
            for i, part in enumerate(parts):
                gat[r, pl.ds(i * LANES, LANES)] = part.astype(BF16)
            return carry

        lax.fori_loop(0, tokens // group, one, 0)

    def under_qkv(t):
        w = blocks.ring.at[blocks.done % blocks.depth]
        add_up(t, kdot_t(gat[:, pl.ds(0, lanes.qkv)], w[:, pl.ds(0, lanes.qkv)]))
        blocks.drop()
        s3 = lanes.starts[3]
        gat[:, pl.ds(s3, LANES)] = gat[:, pl.ds(s3, LANES)] + mix[:, pl.ds(0, LANES)]
        gat[:, pl.ds(s3 + LANES, 2 * LANES)] = mix[:, pl.ds(LANES, 2 * LANES)]
        sent[t] = saves.put(gat, gat_o.at[t])
        if t == nt - 1:
            marks[0].append(sent[t])
        if t + 1 < nt:
            send_all(load_heads(t + 1))

    for t in range(nt):
        steps.append(functools.partial(attend, t))
        steps.append(functools.partial(under_qkv, t))

    def end():
        def rows(r):
            g = gr[r, :] + norm_back(acc[r, :], x_ref[r, :].astype(F32), 0, 1, 1)
            if loss:
                tbuf[r, :] = g.astype(BF16)
            else:
                gout_ref[r, :] = g.astype(BF16)

        row_loop(tokens, 32, rows)
        if loss:
            reorder(gout_ref, tbuf, perm)

    steps.append(end)
    return steps


def heads_scratch(tokens, group, lanes):
    vmem = pltpu.VMEM
    return [
        vmem((lanes.heads // 2, 2 * group, 2 * LANES), BF16),
        vmem((lanes.heads // 2, 2 * group, 2 * LANES), BF16),
        vmem((group, lanes.heads * group), F32),
        vmem((group, lanes.heads * group), BF16),
        vmem((tokens // group, group, lanes.heads * group), BF16),
    ]


def backward_scratch(tokens, width, cols, lanes):
    vmem = pltpu.VMEM
    return [
        vmem((tokens, width), F32),
        vmem((tokens, width), F32),
        vmem((tokens, width), BF16),
        vmem((tokens, width), BF16),
        vmem((tokens, cols), BF16),
        vmem((tokens, cols), BF16),
        vmem((tokens, lanes.width), BF16),
        vmem((tokens, lanes.qkv), BF16),
        vmem((tokens, cols), BF16),
        vmem((tokens, lanes.width), BF16),
        vmem((tokens, width), BF16),
        vmem((tokens, width), BF16),
        DMA((9,)),
        vmem((tokens, width), BF16),
        vmem((tokens, tokens), BF16),
    ]


STAGES = 7
KEPT = 6
SLOTS = 3
Y_A, X_A, X_B, Y_B, Y_C, X_C, X_D, Y_D = KINDS = tuple(range(8))


class Reduce:
    def __init__(self, x_refs, g_refs, o_ref, scratch, chunks, before, split_at, nz, rows, width):
        (
            self.acc, self.stg, self.prb, self.gbuf, self.xraw, self.xt,
            self.ya, self.xa, self.xb, self.yb, self.yc, self.xc, self.xd, self.yd, self.zab, self.zcd,
            self.gsem, self.xsem, self.osem, self.s_p, self.r_p, self.s_xy, self.r_xy, self.s_z, self.r_z,
        ) = scratch
        self.x_refs, self.g_refs, self.o_ref = x_refs, g_refs, o_ref
        self.chunks, self.before, self.split_at = chunks, before, split_at
        self.nz, self.rows, self.width = nz, rows, width
        self.unit = rows // 9
        self.ab = 7 * self.unit
        self.count = len(chunks)
        self.at = position()
        self.peers = neighbours(nz)
        self.order = []
        for _, _, used in chunks:
            for q in used:
                if q not in self.order:
                    self.order.append(q)
        self.turned_so_far = 0

    def add_in(self, dst, src):
        lead = dst.shape[:-2]
        total = 1
        for v in lead:
            total *= v
        if total == 1:
            dst[...] = dst[...] + src[...]
            return

        def body(i, carry):
            index = []
            rest = i
            for v in reversed(lead):
                index.append(rest % v)
                rest = rest // v
            index = tuple(reversed(index))
            dst[index] = dst[index] + src[index]
            return carry

        lax.fori_loop(0, total, body, 0)

    def exchange(self, k, kind, mode):
        y, c, x, z = self.at
        x_dev, y_dev = self.peers[:2]
        unit, ab = self.unit, self.ab
        a = (4 if k % 2 == 0 else 3) * unit
        b = ab - a
        ra, rb, rc, rd = pl.ds(0, a), pl.ds(a, b), pl.ds(ab, unit), pl.ds(ab + unit, unit)
        m = k % SLOTS
        part = self.acc.at[k % KEPT]
        src, buf, target, dst = (
            lambda: (part.at[:, 1 - y, :, ra], self.ya.at[m, :, :, pl.ds(0, a)], y_dev, part.at[:, y, :, ra]),
            lambda: (part.at[:, y, 1 - x, ra], self.xa.at[m, :, pl.ds(0, a)], x_dev, part.at[:, y, x, ra]),
            lambda: (part.at[:, :, 1 - x, rb], self.xb.at[m, :, :, pl.ds(0, b)], x_dev, part.at[:, :, x, rb]),
            lambda: (part.at[:, 1 - y, x, rb], self.yb.at[m, :, pl.ds(0, b)], y_dev, part.at[:, y, x, rb]),
            lambda: (part.at[z, 1 - y, :, rc], self.yc.at[m], y_dev, part.at[z, y, :, rc]),
            lambda: (part.at[z, y, 1 - x, rc], self.xc.at[m], x_dev, part.at[z, y, x, rc]),
            lambda: (part.at[z, :, 1 - x, rd], self.xd.at[m], x_dev, part.at[z, :, x, rd]),
            lambda: (part.at[z, 1 - y, x, rd], self.yd.at[m], y_dev, part.at[z, y, x, rd]),
        )[kind]()
        copy = remote(src, buf, self.s_xy.at[k % STAGES, kind], self.r_xy.at[m, kind], target)
        if mode == START:
            copy.start()
        elif mode == SEND:
            copy.wait_send()
        else:
            copy.wait_recv()
            self.add_in(dst, buf)

    def region_z(self, k, t, which):
        y, c, x, z = self.at
        part = self.acc.at[k % KEPT, t]
        if which == 0:
            return part.at[y, x, pl.ds(0, self.ab)]
        return part.at[:, :, pl.ds(self.ab, 2 * self.unit)]

    def along_z(self, k, hop, which, mode):
        z, nz = self.at[3], self.nz
        below, above = self.peers[3:]
        m, n = k % SLOTS, k % STAGES
        landing = (self.zab, self.zcd)[which]
        s_z, r_z = self.s_z, self.r_z
        t_down, t_up = hop - (nz - 1 - z), nz - 1 - (hop - z)
        if mode != RECV:

            @pl.when((t_down >= 0) & (z > 0))
            def _():
                copy = remote(
                    self.region_z(k, jnp.maximum(t_down, 0), which), landing.at[m, hop, 0],
                    s_z.at[n, which, hop, 0], r_z.at[m, which, hop, 0], below,
                )
                copy.start() if mode == START else copy.wait_send()

            @pl.when((hop >= z) & (z < nz - 1))
            def _():
                copy = remote(
                    self.region_z(k, jnp.minimum(t_up, nz - 1), which), landing.at[m, hop, 1],
                    s_z.at[n, which, hop, 1], r_z.at[m, which, hop, 1], above,
                )
                copy.start() if mode == START else copy.wait_send()

            return
        from_above, from_below = t_down + 1, t_up - 1

        @pl.when((from_above >= 0) & (z < nz - 1))
        def _():
            buf = landing.at[m, hop, 0]
            remote(buf, buf, s_z.at[n, which, hop, 0], r_z.at[m, which, hop, 0], below).wait_recv()
            self.add_in(self.region_z(k, jnp.maximum(from_above, 0), which), buf)

        @pl.when((hop >= z - 1) & (z > 0))
        def _():
            buf = landing.at[m, hop, 1]
            remote(buf, buf, s_z.at[n, which, hop, 1], r_z.at[m, which, hop, 1], above).wait_recv()
            self.add_in(self.region_z(k, jnp.minimum(from_below, nz - 1), which), buf)

    def pair(self, k, mode):
        m = k % 2
        copy = remote(self.stg, self.prb.at[m], self.s_p, self.r_p.at[m], self.peers[2])
        if mode == START:
            copy.start()
        elif mode == SEND:
            copy.wait_send()
        else:
            copy.wait_recv()
            self.add_in(self.acc.at[k % KEPT], self.prb.at[m])

    def load_g(self, k):
        layer, col, _ = self.chunks[k]
        return pltpu.make_async_copy(
            self.g_refs[layer].at[:, :, pl.ds(col * self.width, self.width)], self.gbuf, self.gsem
        )

    def turned(self, q):
        i = self.order.index(q)
        if i >= self.turned_so_far:
            load = pltpu.make_async_copy(self.x_refs[q], self.xraw, self.xsem)
            load.start()
            load.wait()
            for j in range(self.xraw.shape[1] // LANES):
                self.xt[i % 2, pl.ds(j * LANES, LANES), :] = self.xraw[:, pl.ds(j * LANES, LANES)].T
            self.turned_so_far += 1
        return i % 2

    def multiply(self, k):
        layer, col, used = self.chunks[k]
        c = self.at[1]
        if col == 0:
            self.before(layer)
            self.load_g(k).start()
        slots = [self.turned(q) for q in used]
        self.load_g(k).wait()
        rows = self.rows

        def fill(dst, core):
            def body(i, carry):
                t, yy = i // 2, i % 2
                at = pl.ds(pl.multiple_of((yy * 4 + core * 2) * rows, 16), 2 * rows)
                g = self.gbuf[t]
                r = jnp.dot(self.xt[slots[0], at, :], g, preferred_element_type=F32)
                if len(slots) == 2:
                    second = jnp.dot(self.xt[slots[1], at, :], g, preferred_element_type=F32)
                    lane = lax.broadcasted_iota(jnp.int32, r.shape, 1)
                    r = jnp.where(lane < self.split_at, r, second)
                r = r.astype(BF16)
                dst[t, yy, 0] = r[:rows]
                dst[t, yy, 1] = r[rows:]
                return carry

            lax.fori_loop(0, self.nz * 2, body, 0)

        fill(self.stg, 1 - c)
        self.pair(k, START)
        if k >= KEPT:
            self.hand_out(k - KEPT).wait()
        fill(self.acc.at[k % KEPT], c)
        if k + 1 < self.count and self.chunks[k + 1][0] == layer:
            self.load_g(k + 1).start()

    def hand_out(self, k):
        y, c, x, z = self.at
        layer, col, _ = self.chunks[k]
        return pltpu.make_async_copy(
            self.acc.at[k % KEPT, z, y, x],
            self.o_ref.at[layer, :, pl.ds(col * self.width, self.width)],
            self.osem.at[k % KEPT],
        )

    def stage(self, k, s):
        move, z = self.exchange, self.along_z
        if s == 0:
            self.multiply(k)
        if s == 1:
            self.pair(k, SEND)
            self.pair(k, RECV)
            move(k, Y_A, START)
            move(k, X_B, START)
            z(k, 0, 1, START)
        if s == 2:
            z(k, 0, 1, RECV)
            z(k, 1, 1, START)
            move(k, Y_A, RECV)
            move(k, X_A, START)
            move(k, X_B, RECV)
            move(k, Y_B, START)
        if s == 3:
            z(k, 1, 1, RECV)
            z(k, 2, 1, START)
            move(k, X_A, RECV)
            move(k, Y_B, RECV)
            z(k, 0, 0, START)
        if s == 4:
            z(k, 0, 0, RECV)
            z(k, 1, 0, START)
            z(k, 2, 1, RECV)
            move(k, Y_C, START)
            move(k, X_D, START)
        if s == 5:
            z(k, 1, 0, RECV)
            z(k, 2, 0, START)
            move(k, Y_C, RECV)
            move(k, X_C, START)
            move(k, X_D, RECV)
            move(k, Y_D, START)
        if s == 6:
            z(k, 2, 0, RECV)
            move(k, X_C, RECV)
            move(k, Y_D, RECV)
            for kind in KINDS:
                move(k, kind, SEND)
            for hop in range(self.nz - 1):
                z(k, hop, 0, SEND)
                z(k, hop, 1, SEND)
            self.hand_out(k).start()

    def slots(self):
        return self.count + STAGES - 1

    def slot(self, i):
        for s in range(STAGES - 1, -1, -1):
            if 0 <= i - s < self.count:
                self.stage(i - s, s)

    def end(self):
        for k in range(max(0, self.count - KEPT), self.count):
            self.hand_out(k).wait()


def reduce_scratch(tokens, cols, rows, nz):
    width = cols // THIRDS
    unit = rows // 9
    hops = nz - 1
    vmem = pltpu.VMEM
    return [
        vmem((KEPT, nz, 2, 2, rows, width), BF16),
        vmem((nz, 2, 2, rows, width), BF16),
        vmem((2, nz, 2, 2, rows, width), BF16),
        vmem((nz, tokens, width), BF16),
        vmem((tokens, cols), BF16),
        vmem((2, cols, tokens), BF16),
        vmem((SLOTS, nz, 2, 4 * unit, width), BF16),
        vmem((SLOTS, nz, 4 * unit, width), BF16),
        vmem((SLOTS, nz, 2, 4 * unit, width), BF16),
        vmem((SLOTS, nz, 4 * unit, width), BF16),
        vmem((SLOTS, 2, unit, width), BF16),
        vmem((SLOTS, unit, width), BF16),
        vmem((SLOTS, 2, unit, width), BF16),
        vmem((SLOTS, unit, width), BF16),
        vmem((SLOTS, hops, 2, 7 * unit, width), BF16),
        vmem((SLOTS, hops, 2, 2, 2, 2 * unit, width), BF16),
        DMA(()),
        DMA(()),
        DMA((KEPT,)),
        DMA(()),
        DMA((2,)),
        DMA((STAGES, 8)),
        DMA((SLOTS, 8)),
        DMA((STAGES, 2, hops, 2)),
        DMA((SLOTS, 2, hops, 2)),
    ]


PER_SLOT = 3


def backward_pass_kernel(*refs, nz, n_seq, group_0, group_1, sub, lanes, rows):
    rest = list(refs)

    def take(n):
        got = rest[:n]
        del rest[:n]
        return got

    final_ref, teach_ref, mask_ref, coef_ref, mod_ref, w_ref, ada_ref = take(7)
    saved = take(10), take(10)
    o_ref, bout_o, lat_o, sums_o, silu_o = take(5)
    made = take(4), take(4)
    (
        ring, wsem, osem, s_t, r_t, s_lat, r_lat, s_m, r_m, local_sem,
        ada, mod_parts, first, every, along, back, silus, bout, err, gout, gin, mg_0, mg_1,
    ) = take(23)
    heads = take(5), take(5)
    shared = take(15)
    y, c, x, z = position()
    tokens, width = gout.shape
    own_frames, patches = lat_o.shape[1:3]
    part = patches // n_seq
    layers = w_ref.shape[0]
    greet(
        [in_plane(d)[0] for d in range(1, 8)]
        + [(y * 2 + c, xx, (z + d) % nz) for d in range(1, nz) for xx in (x, 1 - x)]
    )
    dp, block, me = y * 2 + c, (y * 2 + c) * 2 + x, x * nz + z
    load_ada = pltpu.make_async_copy(ada_ref, ada, local_sem.at[0])
    load_ada.start()

    uses = [(l, t) for t in range(nz) for l in (2, 1)] + [(0, t) for t in range(nz)]
    order = [(3 * b + l, t) for b in (1, 0) for l, t in uses]
    blocks = Blocks(w_ref, ring, wsem, order, set(range(layers)))
    blocks.pump()
    saves = Saves(osem)
    marks = {}, {}

    x_refs, g_refs, chunks = [], [], []
    for b in range(2):
        gba_o, gbb_o, gat_o, gpre_o = made[b]
        x_refs += [saved[b][1], gba_o, saved[b][6], gbb_o]
        g_refs += [gat_o, gpre_o, saved[b][8]]
    cols = g_refs[0].shape[2]
    third = cols // THIRDS
    for b in (1, 0):
        for layer, used in ((2, (3,)), (1, (2,)), (0, (0, 1))):
            for col in range(THIRDS):
                ids = tuple(4 * b + q for q in used)
                if layer == 0 and (col + 1) * third <= 3 * lanes.span:
                    ids = ids[:1]
                chunks.append((3 * b + layer, col, ids))

    def before(layer):
        for copy in marks[layer // 3][layer % 3]:
            saves.wait(copy)

    reduce = Reduce(
        x_refs, g_refs, o_ref, take(25), chunks, before, 3 * lanes.span - 2 * third, nz, rows, third
    )

    moved, kept = [], []
    for d in range(1, 2 * nz):
        target, q = across(d, nz)
        src = gout.reshape(2 * nz, own_frames, part, width).at[q]
        dst = gin.reshape(own_frames, nz, n_seq, part, width).at[:, z, x]
        moved.append(remote(src, dst, s_t.at[d], r_t.at[d], target))
    kept.append(
        pltpu.make_async_copy(
            gout.reshape(2 * nz, own_frames, part, width).at[me],
            gin.reshape(own_frames, nz, n_seq, part, width).at[:, z, x],
            local_sem.at[1],
        )
    )
    halves = bout.reshape(n_seq, bout_o.shape[0], part, width)
    moved.append(
        remote(halves.at[1 - x], bout_o.at[:, x], s_t.at[0], r_t.at[0], device(y, c, 1 - x, z))
    )
    kept.append(pltpu.make_async_copy(halves.at[x], bout_o.at[:, x], local_sem.at[2]))

    frames_of = gout.reshape(own_frames, nz, patches, width)
    own_lat = pltpu.make_async_copy(frames_of.at[:, z], lat_o.at[z], local_sem.at[3])
    lat_out, sums, spread, slices, rows_out = [], [], [], [], []
    for d in range(1, nz):
        target, q = over_z(d, nz)
        lat_out.append(remote(frames_of.at[:, q], lat_o.at[z], s_lat.at[d], r_lat.at[d], target))
        slices.append(remote(along, back.at[d], s_m.at[2, d], r_m.at[2, d], target))
    for d in range(1, 2 * nz):
        target, q = across(d, nz)
        sums.append(remote(mod_parts.at[q % nz], first.at[d], s_m.at[0, d], r_m.at[0, d], target))
    for d in range(1, 4):
        target, q = over_dp(d)
        spread.append(remote(every.at[dp], every.at[dp], s_m.at[1, d], r_m.at[1, d], target))
    for d in range(1, 8):
        target, q = in_plane(d)
        rows_out.append(remote(silus.at[block], silus.at[block], s_m.at[3, d], r_m.at[3, d], target))

    def modulation(step):
        if step == 0:
            span = lanes.span
            mod_parts[...] = jnp.zeros_like(mod_parts)
            total = jnp.sum(err[...], axis=1, keepdims=True)
            for q in range(nz):
                mod_parts[q, 0:6, :] = mg_0[:, q * span : (q + 1) * span]
                mod_parts[q, 6:12, :] = mg_1[:, q * span : (q + 1) * span]
                mod_parts[q, 12:13, :] = jnp.broadcast_to(total, (1, span))
            send_all(sums)
            own_lat.start()
            send_all(lat_out)
        if step == 1:
            finish_all(sums)
            total = mod_parts[z]
            for d in range(1, 2 * nz):
                total = total + first[d]
            every[dp] = total
            send_all(spread)
        if step == 2:
            finish_all(spread)
            load_ada.wait()
            sums_o[...] = every[...]
            total = jnp.zeros(along.shape, F32)
            for b in range(ada.shape[0]):
                for k in range(6):
                    i = 6 * b + k
                    got = jnp.concatenate([every[q, i : i + 1, :] for q in range(4)] * 2, axis=0)
                    high = got.astype(BF16)
                    rest_1 = got - high.astype(F32)
                    middle = rest_1.astype(BF16)
                    lowest = (rest_1 - middle.astype(F32)).astype(BF16)
                    for piece in (high, middle, lowest):
                        total = total + kdot_t(piece, ada[b, k])
            along[...] = total
            send_all(slices)
        if step == 3:
            finish_all(slices)
            total = along[...]
            for d in range(1, nz):
                total = total + back[d]
            silus[block] = total
            send_all(rows_out)
        if step == 4:
            finish_all(rows_out)
            for q in range(8):
                silu_o[q : q + 1, :] = silus[q, pl.ds(dp, 1), :]

    def ins_of(b):
        x_hbm, _, qkv, prob, mix, bra, _, pre, _, brb = saved[b]
        return x_hbm, mod_ref.at[b], qkv, prob, mix, bra, pre, brb

    def scratch_of(b):
        return list(shared[:8]) + list(heads[b][:4]) + [heads[b][4]] + list(shared[8:])

    def leave():
        send_all(moved)
        send_all(kept)

    def enter():
        for copy in kept:
            copy.wait()
        finish_all(moved)
        saves.finish()

    work = backward_steps(
        (final_ref, teach_ref, mask_ref, coef_ref), ins_of(1), [gout, mg_1] + made[1] + [bout, err],
        scratch_of(1), blocks, saves, marks[1], sub=sub, group=group_1, lanes=lanes,
    )
    one = len(work)
    work.append(leave)
    work.append(enter)
    base = len(work)
    work += backward_steps(
        (gin,), ins_of(0), [gout, mg_0] + made[0],
        scratch_of(0), blocks, saves, marks[0], sub=None, group=group_0, lanes=lanes,
    )
    work.append(functools.partial(modulation, 0))
    gelu_done, attn_done = 2 * nz - 1, one - 2
    need = {5: 0, 4: gelu_done, 3: attn_done, 2: base, 1: base + gelu_done, 0: base + attn_done}
    done, later, since = 0, 1, 0
    for slot in range(reduce.slots()):
        if slot < len(chunks):
            while done <= need[chunks[slot][0]]:
                work[done]()
                done += 1
        reduce.slot(slot)
        if done == len(work) and later < 5:
            modulation(later)
            later += 1
        quota = PER_SLOT
        while quota and done < len(work):
            if done == one + 1:
                since += 1
                if since < 3:
                    break
            work[done]()
            done += 1
            quota -= 1
    for step in range(later, 5):
        modulation(step)
    own_lat.wait()
    finish_all(lat_out)
    saves.finish()
    reduce.end()


def backward_pass(final, teacher, mask, coef, mod, w, ada, saved_0, saved_1, rows, nz, n_seq, sub):
    tokens, width = final.shape
    layers, _, _, cols = w.shape
    frames, halves = sub // n_seq, n_seq
    own_frames = frames // nz
    patches = tokens // nz // own_frames
    lanes = Lanes(cols // 4)
    span = ada.shape[3]
    group_0, group_1 = nz * patches, 8 * sub
    vmem = pltpu.VMEM
    sds = jax.ShapeDtypeStruct
    smem = pl.BlockSpec(memory_space=pltpu.SMEM)
    flat, tall = sds((tokens, width), BF16), sds((nz, tokens, cols), BF16)
    small = (16, span)
    rowsb = vmem((tokens, width), BF16)
    outs = pl.pallas_call(
        functools.partial(
            backward_pass_kernel,
            nz=nz, n_seq=n_seq, group_0=group_0, group_1=group_1, sub=sub, lanes=lanes, rows=rows,
        ),
        out_shape=[
            sds((layers, rows, cols), BF16),
            sds((frames, halves, patches // n_seq, width), BF16),
            sds((nz, own_frames, patches, width), BF16),
            sds((4,) + small, F32),
            sds((8, rows), F32),
        ]
        + [flat, flat, tall, tall] * 2,
        in_specs=[ANY, ANY, VM, smem, VM, ANY, ANY] + [ANY] * 20,
        out_specs=[ANY, ANY, ANY, VM, VM] + [ANY] * 8,
        scratch_shapes=[
            vmem((2, width, cols), BF16),
            DMA((2,)),
            DMA((24,)),
            DMA((2 * nz,)),
            DMA((2 * nz,)),
            DMA((nz,)),
            DMA((nz,)),
            DMA((4, 8)),
            DMA((4, 8)),
            DMA((4,)),
            vmem(ada.shape, BF16),
            vmem((nz,) + small, F32),
            vmem((2 * nz,) + small, F32),
            vmem((4,) + small, F32),
            vmem((8, rows), F32),
            vmem((nz, 8, rows), F32),
            vmem((8, 8, rows), F32),
            rowsb,
            vmem((1, width), F32),
            rowsb,
            rowsb,
            vmem((6, width), F32),
            vmem((6, width), F32),
        ]
        + heads_scratch(tokens, group_0, lanes)
        + heads_scratch(tokens, group_1, lanes)
        + backward_scratch(tokens, width, cols, lanes)
        + reduce_scratch(tokens, cols, rows, nz),
        compiler_params=pltpu.CompilerParams(
            collective_id=1, has_side_effects=True, vmem_limit_bytes=63 << 20
        ),
        name="backward_pass",
    )(final, teacher, mask, coef, mod, w, ada, *saved_0, *saved_1)
    return outs[:5]


def normalize(stream):
    center = stream - jnp.mean(stream, axis=-1, keepdims=True)
    inverse = lax.rsqrt(jnp.mean(center * center, axis=-1, keepdims=True) + EPSILON)
    return center * inverse, inverse


def norm_backward(grad_normed, normed, inverse):
    mean_grad = jnp.mean(grad_normed, axis=-1, keepdims=True)
    mean_along = jnp.mean(grad_normed * normed, axis=-1, keepdims=True)
    return inverse * (grad_normed - mean_grad - normed * mean_along)


def gelu_tanh(values):
    return jax.nn.gelu(values, approximate=True)


def dot(a, b):
    return jnp.dot(a, b, preferred_element_type=F32)


def dot_t(a, b):
    return lax.dot_general(a, b, (((1,), (1,)), ((), ())), preferred_element_type=F32)


def attend_forward(heads, factor):
    q, k, v = heads[:, :, :, 0], heads[:, :, :, 1], heads[:, :, :, 2]
    scores = jnp.einsum("tglhe,tgmhe->tghlm", q, k, preferred_element_type=F32) * factor
    peak = jnp.max(scores, axis=-1, keepdims=True)
    expanded = jnp.exp(scores - peak)
    total = jnp.sum(expanded, axis=-1, keepdims=True)
    probs = (expanded / total).astype(BF16)
    mixed = jnp.einsum("tghlm,tgmhe->tglhe", probs, v, preferred_element_type=F32)
    return mixed.astype(BF16), peak + jnp.log(total)


def attend_backward(heads, log_total, grad_mixed, factor):
    q, k, v = heads[:, :, :, 0], heads[:, :, :, 1], heads[:, :, :, 2]
    scores = jnp.einsum("tglhe,tgmhe->tghlm", q, k, preferred_element_type=F32) * factor
    probs = jnp.exp(scores - log_total)
    grad_v = jnp.einsum(
        "tghlm,tglhe->tgmhe", probs.astype(BF16), grad_mixed, preferred_element_type=F32
    )
    grad_probs = jnp.einsum("tglhe,tgmhe->tghlm", grad_mixed, v, preferred_element_type=F32)
    inner = jnp.sum(grad_probs * probs, axis=-1, keepdims=True)
    grad_scores = (probs * (grad_probs - inner)).astype(BF16)
    grad_q = jnp.einsum("tghlm,tgmhe->tglhe", grad_scores, k, preferred_element_type=F32) * factor
    grad_k = jnp.einsum("tghlm,tglhe->tgmhe", grad_scores, q, preferred_element_type=F32) * factor
    return jnp.stack([grad_q, grad_k, grad_v], axis=3).astype(BF16)


def block_forward(stream, modulation, weights, group):
    attn, up, down = weights
    blocks, width, cols = attn.shape
    inner = cols // 4 * 3
    head_count = cols // 4 // HEAD_DIM
    clips, per_clip, _ = stream.shape
    tokens = clips * per_clip
    factor = HEAD_DIM**-0.5

    def column(i):
        return modulation[:, i][:, None, :]

    normed_a, inverse_a = normalize(stream)
    hidden_a = (normed_a * (1.0 + column(1)) + column(0)).astype(BF16).reshape(tokens, width)
    triple = jnp.stack([dot(hidden_a, attn[t, :, :inner]).astype(BF16) for t in range(blocks)])
    heads = triple.reshape(blocks, tokens // group, group, 3, head_count, HEAD_DIM)
    mixed, log_total = attend_forward(heads, factor)
    mixed = mixed.reshape(blocks, tokens, cols // 4)
    branch_a = sum(dot_t(mixed[t], attn[t, :, inner:]) for t in range(blocks)).reshape(stream.shape)
    middle = stream + column(2) * branch_a
    normed_b, inverse_b = normalize(middle)
    hidden_b = (normed_b * (1.0 + column(4)) + column(3)).astype(BF16).reshape(tokens, width)
    pre_act = jnp.stack([dot(hidden_b, up[t]) for t in range(blocks)])
    activated = gelu_tanh(pre_act).astype(BF16)
    branch_b = sum(dot_t(activated[t], down[t]) for t in range(blocks)).reshape(stream.shape)
    output = middle + column(5) * branch_b
    saved = (
        normed_a, inverse_a, hidden_a, heads, log_total, mixed, branch_a,
        normed_b, inverse_b, hidden_b, pre_act, activated, branch_b,
    )
    return output, saved


def block_backward(grad, modulation, weights, saved, group):
    attn, up, down = weights
    blocks, width, cols = attn.shape
    inner = cols // 4 * 3
    head_count = cols // 4 // HEAD_DIM
    (
        normed_a, inverse_a, hidden_a, heads, log_total, mixed, branch_a,
        normed_b, inverse_b, hidden_b, pre_act, activated, branch_b,
    ) = saved
    tokens = hidden_a.shape[0]
    factor = HEAD_DIM**-0.5

    def column(i):
        return modulation[:, i][:, None, :]

    def clip_sum(values):
        return jnp.sum(values, axis=1)

    gate_b = clip_sum(grad * branch_b)
    branch_grad_b = (grad * column(5)).astype(BF16).reshape(tokens, width)
    grad_act = jnp.stack([dot(branch_grad_b, down[t]) for t in range(blocks)])
    grad_pre = jax.vjp(gelu_tanh, pre_act)[1](grad_act)[0].astype(BF16)
    grad_hidden_b = sum(dot_t(grad_pre[t], up[t]) for t in range(blocks)).reshape(grad.shape)
    shift_b = clip_sum(grad_hidden_b)
    scale_b = clip_sum(grad_hidden_b * normed_b)
    grad_middle = grad + norm_backward(grad_hidden_b * (1.0 + column(4)), normed_b, inverse_b)
    gate_a = clip_sum(grad_middle * branch_a)
    branch_grad_a = (grad_middle * column(2)).astype(BF16).reshape(tokens, width)
    grad_mixed = jnp.stack(
        [dot(branch_grad_a, attn[t, :, inner:]).astype(BF16) for t in range(blocks)]
    )
    grad_mixed = grad_mixed.reshape(blocks, tokens // group, group, head_count, HEAD_DIM)
    grad_heads = attend_backward(heads, log_total, grad_mixed, factor)
    grad_triple = grad_heads.reshape(blocks, tokens, inner)
    grad_hidden_a = sum(
        dot_t(grad_triple[t], attn[t, :, :inner]) for t in range(blocks)
    ).reshape(grad.shape)
    shift_a = clip_sum(grad_hidden_a)
    scale_a = clip_sum(grad_hidden_a * normed_a)
    grad_input = grad_middle + norm_backward(
        grad_hidden_a * (1.0 + column(1)), normed_a, inverse_a
    )
    grad_modulation = jnp.stack([shift_a, scale_a, gate_a, shift_b, scale_b, gate_b], axis=1)
    x_list = [hidden_a, branch_grad_a, hidden_b, branch_grad_b]
    g_list = [jnp.concatenate([grad_triple, mixed], axis=2), grad_pre, activated]
    return grad_input, grad_modulation, x_list, g_list


def local_anywhere(
    latents, condition, teacher, valid_mask,
    qkv_weight, out_weight, up_weight, down_weight, ada_weight,
):
    n_dp, n_seq, n_tensor = (lax.axis_size(a) for a in (DP, SEQ, TENSOR))
    clips, frames, patches, width = latents.shape
    rows = ada_weight.shape[1]
    blocks = qkv_weight.shape[0]
    heads_width = qkv_weight.shape[3]
    inner = 3 * heads_width
    dp, seq, tensor = (lax.axis_index(a) for a in (DP, SEQ, TENSOR))
    row_block = dp * n_seq + seq

    shards = pack_shards(qkv_weight, out_weight, up_weight, down_weight)
    full = lax.all_gather(shards, (DP, SEQ), axis=1, tiled=True)
    full = lax.all_gather(full, TENSOR, axis=1)
    weights = [(full[3 * b], full[3 * b + 1], full[3 * b + 2]) for b in range(blocks)]

    cond_float = condition.astype(F32)
    all_cond = lax.all_gather(condition, DP, axis=0, tiled=True).astype(F32)
    all_silu = jax.nn.silu(all_cond).astype(BF16)
    silu_rows = lax.dynamic_slice_in_dim(all_silu, row_block * rows, rows, axis=1)
    partial_mod = jnp.einsum("cd,bdke->cbke", silu_rows, ada_weight, preferred_element_type=F32)
    partial_mod = lax.psum_scatter(partial_mod, DP, scatter_dimension=0, tiled=True)
    partial_mod = lax.psum(partial_mod, SEQ)
    modulation = lax.all_gather(partial_mod, TENSOR, axis=3, tiled=True)

    by_frame = frames % n_tensor == 0
    split_axis = 1 if by_frame else 0

    def to_spatial(v):
        return lax.all_to_all(v, TENSOR, split_axis=split_axis, concat_axis=2, tiled=True)

    def from_spatial(v):
        return lax.all_to_all(v, TENSOR, split_axis=2, concat_axis=split_axis, tiled=True)

    def to_temporal(v):
        return lax.all_to_all(v, SEQ, split_axis=2, concat_axis=1, tiled=True)

    def from_temporal(v):
        return lax.all_to_all(v, SEQ, split_axis=1, concat_axis=2, tiled=True)

    own_clips = clips if by_frame else clips // n_tensor
    first_clip = 0 if by_frame else tensor * own_clips
    spatial_mod = lax.dynamic_slice_in_dim(modulation[:, 0], first_clip, own_clips, axis=0)
    temporal_mod = modulation[:, 1]

    def patch_major(v):
        return v.transpose(0, 2, 1, 3)

    spatial = to_spatial(latents)
    spatial_shape = spatial.shape
    stream = spatial.astype(F32).reshape(own_clips, -1, width)
    stream, saved_0 = block_forward(stream, spatial_mod, weights[0], spatial_shape[2])
    moved = to_temporal(from_spatial(stream.astype(BF16).reshape(spatial_shape)))
    temporal_shape = moved.shape
    stream = patch_major(moved).astype(F32).reshape(clips, -1, width)
    stream, saved_1 = block_forward(stream, temporal_mod, weights[1], temporal_shape[1])

    def to_frames(v):
        return patch_major(
            v.reshape(clips, temporal_shape[2], temporal_shape[1], width)
        )

    block_out = from_temporal(to_frames(stream.astype(BF16)))

    teacher_rows = patch_major(to_temporal(teacher)).astype(F32).reshape(clips, -1, width)
    mask_float = valid_mask.astype(F32)
    own_mask = lax.dynamic_slice_in_dim(
        mask_float, seq * temporal_shape[2], temporal_shape[2], axis=1
    )
    mask_rows = jnp.repeat(own_mask, temporal_shape[1], axis=1)[:, :, None]
    error = stream - teacher_rows
    error_sum = lax.psum(jnp.sum(mask_rows * error * error), (DP, SEQ, TENSOR))
    total_frames = frames * n_seq
    valid_count = lax.psum(jnp.sum(mask_float), (DP, TENSOR)) * total_frames
    loss_value = error_sum / (width * valid_count)
    token_total = clips * frames * patches * n_dp * n_seq * n_tensor
    grad = mask_rows * error * (2.0 * token_total / valid_count)

    grad, mod_grad_1, x_1, g_1 = block_backward(
        grad, temporal_mod, weights[1], saved_1, temporal_shape[1]
    )
    moved = to_spatial(from_temporal(to_frames(grad.astype(BF16))))
    grad = moved.astype(F32).reshape(own_clips, -1, width)
    grad, mod_grad_0, x_0, g_0 = block_backward(
        grad, spatial_mod, weights[0], saved_0, spatial_shape[2]
    )
    grad_latents = from_spatial(grad.astype(BF16).reshape(spatial_shape)).astype(F32)

    x_list, g_list = x_0 + x_1, g_0 + g_1
    terms = []
    for b in range(blocks):
        for layer, q in ((0, 0), (1, 2), (2, 3)):
            term = jnp.einsum(
                "nd,tnk->tdk", x_list[4 * b + q], g_list[3 * b + layer], preferred_element_type=F32
            )
            if layer == 0:
                other = jnp.einsum(
                    "nd,tnk->tdk", x_list[4 * b + 1], g_list[3 * b], preferred_element_type=F32
                )
                term = jnp.where(jnp.arange(term.shape[2]) < inner, term, other)
            term = lax.psum_scatter(
                term.astype(BF16), (DP, SEQ), scatter_dimension=1, tiled=True
            )
            terms.append(lax.psum_scatter(term, TENSOR, scatter_dimension=0, tiled=True)[0])
    summed = jnp.stack(terms)
    grad_qkv, grad_out, grad_up, grad_down = unpack_shards(summed, blocks, heads_width)

    placed_0 = lax.dynamic_update_slice_in_dim(
        jnp.zeros((clips,) + mod_grad_0.shape[1:], F32), mod_grad_0, first_clip, axis=0
    )
    mod_grad = jnp.stack([placed_0, mod_grad_1], axis=1)
    mod_grad = lax.psum_scatter(mod_grad, TENSOR, scatter_dimension=3, tiled=True)
    mod_grad = lax.psum(mod_grad, SEQ)
    mod_grad = lax.all_gather(mod_grad, DP, axis=0, tiled=True)
    grad_ada = jnp.einsum("cd,cbke->bdke", silu_rows.astype(F32), mod_grad, precision=HIGHEST)
    grad_silu = jnp.einsum("cbke,bdke->cd", mod_grad, ada_weight.astype(F32), precision=HIGHEST)
    grad_silu = lax.psum(grad_silu, TENSOR)
    grad_silu = lax.all_gather(grad_silu, (DP, SEQ), axis=1, tiled=True)
    grad_silu = lax.dynamic_slice_in_dim(grad_silu, dp * clips, clips, axis=0)
    grad_condition = jax.vjp(jax.nn.silu, cond_float)[1](grad_silu)[0]
    return (
        block_out, loss_value, grad_latents, grad_condition,
        grad_qkv, grad_out, grad_up, grad_down, grad_ada,
    )


def pack_shards(qkv_weight, out_weight, up_weight, down_weight):
    blocks, rows = qkv_weight.shape[:2]
    shards = []
    for b in range(blocks):
        shards.append(jnp.concatenate([qkv_weight[b].reshape(rows, -1), out_weight[b].T], axis=1))
        shards.append(up_weight[b])
        shards.append(down_weight[b].T)
    return jnp.stack(shards)


def unpack_shards(summed, blocks, heads_width):
    rows = summed.shape[1]
    inner = 3 * heads_width
    summed = summed.reshape(blocks, 3, rows, -1).astype(F32)
    return (
        summed[:, 0, :, :inner].reshape(blocks, rows, 3, heads_width),
        summed[:, 0, :, inner:].transpose(0, 2, 1),
        summed[:, 1],
        summed[:, 2].transpose(0, 2, 1),
    )


def local_grid(
    latents, condition, teacher, valid_mask,
    qkv_weight, out_weight, up_weight, down_weight, ada_weight,
):
    n_dp, n_seq, nz = (lax.axis_size(a) for a in (DP, SEQ, TENSOR))
    _, frames, patches, width = latents.shape
    blocks, rows = ada_weight.shape[:2]
    heads_width = qkv_weight.shape[3]
    seq = lax.axis_index(SEQ)
    all_frames, own_patches, own_frames = frames * n_seq, patches // n_seq, frames // nz
    tokens = frames * patches

    shards = pack_shards(qkv_weight, out_weight, up_weight, down_weight)
    cond_float = condition.astype(F32)
    mask_float = valid_mask.astype(F32)
    count = jnp.broadcast_to(jnp.sum(mask_float), (1, ada_weight.shape[3]))
    ada = ada_weight.transpose(0, 2, 1, 3)
    full, teacher_rows, modulation, silu_rows, counted, final, saved_0, saved_1 = forward_pass(
        shards,
        latents.reshape(nz, own_frames, patches, width),
        teacher.reshape(frames, n_seq, own_patches, width),
        cond_float.reshape(-1, rows),
        count,
        ada,
        nz,
        n_seq,
        all_frames,
    )
    valid_count = counted[0, 0] / n_seq * all_frames
    token_total = tokens * n_dp * n_seq * nz
    scale = (2.0 * token_total / valid_count).reshape(1, 1)
    own_mask = lax.dynamic_slice_in_dim(mask_float, seq * own_patches, own_patches, axis=1)
    mask_rows = jnp.repeat(own_mask.reshape(-1), all_frames).reshape(tokens, 1)

    summed, block_out, grad_latents, mod_all, silu_grad = backward_pass(
        final, teacher_rows.reshape(tokens, width), mask_rows, scale, modulation, full, ada,
        saved_0, saved_1, rows, nz, n_seq, all_frames,
    )
    loss_value = jnp.sum(mod_all[:, 12, 0]) / (width * valid_count)
    grad_ada = jnp.einsum(
        "cd,cbke->bdke",
        silu_rows[:n_dp],
        mod_all[:, : 6 * blocks].reshape(n_dp, blocks, 6, -1),
        precision=HIGHEST,
    )
    grad_condition = jax.vjp(jax.nn.silu, cond_float)[1](silu_grad.reshape(1, width))[0]
    return (
        block_out.reshape(latents.shape),
        loss_value,
        grad_latents.reshape(latents.shape).astype(F32),
        grad_condition,
        *unpack_shards(summed, blocks, heads_width),
        grad_ada,
    )


def local(latents, *rest):
    sizes = tuple(lax.axis_size(a) for a in (DP, SEQ, TENSOR))
    if sizes == (4, 2, 4) and latents.shape[0] == 1:
        return local_grid(latents, *rest)
    return local_anywhere(latents, *rest)


def solution(mesh):
    return jax.shard_map(
        local,
        mesh=mesh,
        in_specs=(
            P(DP, SEQ, TENSOR, None),
            P(DP, None),
            P(DP, SEQ, TENSOR, None),
            P(DP, TENSOR),
            P(None, (DP, SEQ), None, TENSOR),
            P(None, TENSOR, (DP, SEQ)),
            P(None, (DP, SEQ), TENSOR),
            P(None, TENSOR, (DP, SEQ)),
            P(None, (DP, SEQ), None, TENSOR),
        ),
        out_specs=(
            P(DP, SEQ, TENSOR, None),
            P(),
            P(DP, SEQ, TENSOR, None),
            P(DP, None),
            P(None, (DP, SEQ), None, TENSOR),
            P(None, TENSOR, (DP, SEQ)),
            P(None, (DP, SEQ), TENSOR),
            P(None, TENSOR, (DP, SEQ)),
            P(None, (DP, SEQ), None, TENSOR),
        ),
        check_vma=False,
    )
```

```python
import functools

import jax
import jax.numpy as jnp
from jax import lax
from jax.experimental import pallas as pl
from jax.experimental.pallas import tpu as pltpu
from jax.sharding import PartitionSpec as P

DP, SEQ, TENSOR = "dp", "seq", "tensor"
START, SEND, RECV = range(3)
HEAD_DIM = 72
EPSILON = 1e-06
HIGHEST = lax.Precision.HIGHEST
MESH = pl.DeviceIdType.MESH
DMA = pltpu.SemaphoreType.DMA
BF16 = jnp.bfloat16
F32 = jnp.float32
ANY = pl.BlockSpec(memory_space=pl.ANY)
VM = pl.BlockSpec(memory_space=pltpu.VMEM)
LANES = 128
NEGATIVE = -1e30
GELU_C = 0.7978845608028654
GELU_K = 0.044715


def position():
    dp = lax.axis_index(DP)
    return dp // 2, dp % 2, lax.axis_index(SEQ), lax.axis_index(TENSOR)


def device(y, c, x, z):
    return (y * 2 + c, x, z)


def neighbours(nz):
    y, c, x, z = position()
    return (
        device(y, c, 1 - x, z),
        device(1 - y, c, x, z),
        device(y, 1 - c, x, z),
        device(y, c, x, jnp.maximum(z - 1, 0)),
        device(y, c, x, jnp.minimum(z + 1, nz - 1)),
    )


def remote(src, dst, send_sem, recv_sem, target):
    return pltpu.make_async_remote_copy(
        src_ref=src,
        dst_ref=dst,
        send_sem=send_sem,
        recv_sem=recv_sem,
        device_id=target,
        device_id_type=MESH,
    )


def in_plane(d):
    y, c, x, z = position()
    q = (y * 4 + c * 2 + x + d) % 8
    return (q // 2, q % 2, z), q


def across(d, nz):
    y, c, x, z = position()
    q = (x * nz + z + d) % (2 * nz)
    return (y * 2 + c, q // nz, q % nz), q


def over_z(d, nz):
    y, c, x, z = position()
    q = (z + d) % nz
    return device(y, c, x, q), q


def over_dp(d):
    y, c, x, z = position()
    q = (y * 2 + c + d) % 4
    return (q, x, z), q


def greet(peers):
    barrier = pltpu.get_barrier_semaphore()
    for target in peers:
        pl.semaphore_signal(barrier, inc=1, device_id=target, device_id_type=MESH)
    pl.semaphore_wait(barrier, len(peers))


def send_all(copies):
    for copy in copies:
        copy.start()


def finish_all(copies):
    for copy in copies:
        copy.wait_send()
        copy.wait_recv()


def kdot(a, b):
    return jnp.dot(a, b, preferred_element_type=F32)


def kdot_t(a, b):
    return lax.dot_general(a, b, (((1,), (1,)), ((), ())), preferred_element_type=F32)


class Lanes:
    def __init__(self, span):
        self.span = span
        self.heads = span // HEAD_DIM
        self.starts = [i * span // LANES * LANES for i in range(4)]
        self.offsets = [i * span - s for i, s in enumerate(self.starts)]
        self.width = 3 * LANES
        self.qkv = self.starts[2] + self.width

    def place(self, which, h):
        return self.offsets[which] + h * HEAD_DIM - (h // 2) * LANES

    def mask(self, which, h):
        lane = lax.broadcasted_iota(jnp.int32, (1, 2 * LANES), 1) - self.place(which, h)
        return ((lane >= 0) & (lane < HEAD_DIM)).astype(F32).astype(BF16)


def row_loop(total, step, body, unroll=2):
    def go(i, carry):
        body(pl.ds(pl.multiple_of(i * step, step), step))
        return carry

    lax.fori_loop(0, total // step, go, 0, unroll=unroll)


def tiles(total):
    first = -(-total // 2 // LANES) * LANES
    return ((0, first), (first, total - first))


def normed_of(v):
    center = v - jnp.mean(v, axis=-1, keepdims=True)
    inverse = lax.rsqrt(jnp.mean(center * center, axis=-1, keepdims=True) + EPSILON)
    return center * inverse, inverse


def gelu_inner(u):
    return jnp.tanh(GELU_C * (u + GELU_K * u * u * u))


def order_matrix(tokens, group, back):
    per = tokens // group
    row = lax.broadcasted_iota(jnp.int32, (tokens, tokens), 1 if back else 0)
    col = lax.broadcasted_iota(jnp.int32, (tokens, tokens), 0 if back else 1)
    return (col == row % group * per + row // group).astype(F32).astype(BF16)


def reorder(dst, src, order):
    for c0, n in tiles(src.shape[1]):
        dst[:, pl.ds(c0, n)] = kdot(order[...], src[:, pl.ds(c0, n)]).astype(BF16)


class Blocks:
    def __init__(self, w_ref, ring, sem, order, ready):
        self.w_ref, self.ring, self.sem, self.order = w_ref, ring, sem, order
        self.ready = ready
        self.loaded = self.done = 0
        self.depth = ring.shape[0]

    def copy(self, i):
        layer, t = self.order[i]
        s = i % self.depth
        dst = self.ring.at[s]
        if len(self.w_ref.shape) == 7:
            dst = dst.reshape(self.w_ref.shape[2:])
        return pltpu.make_async_copy(self.w_ref.at[layer, t], dst, self.sem.at[s])

    def pump(self):
        while (
            self.loaded < len(self.order)
            and self.loaded < self.done + self.depth
            and self.order[self.loaded][0] in self.ready
        ):
            self.copy(self.loaded).start()
            self.loaded += 1

    def take(self):
        i = self.done
        self.pump()
        self.copy(i).wait()
        return self.ring.at[i % self.depth]

    def drop(self):
        self.done += 1
        self.pump()


class Saves:
    def __init__(self, sem):
        self.sem, self.copies, self.used = sem, [], 0

    def put(self, src, dst):
        copy = pltpu.make_async_copy(src, dst, self.sem.at[self.used])
        copy.start()
        self.copies.append(copy)
        self.used += 1
        return copy

    def wait(self, copy):
        if any(other is copy for other in self.copies):
            copy.wait()
            self.copies = [other for other in self.copies if other is not copy]

    def finish(self):
        for copy in self.copies:
            copy.wait()
        self.copies = []


def stack_heads(dst, value, masks, group):
    for h, mask in enumerate(masks):
        lane = (h // 2) * LANES
        dst[h // 2, pl.ds(h % 2 * group, group), :] = value[:, lane : lane + 2 * LANES] * mask


FORWARD_SAVES = 24


def forward_steps(x_in, mod_ref, out_ref, saved, scratch, blocks, saves, *, sub, group, lanes):
    x_o, hida_o, qkv_o, prob_o, mix_o, bra_o, hidb_o, pre_o, act_o, brb_o = saved
    xbuf, perm, acc, qkv, qst, sc, hida, prob, mix, hidb, pre, act, mid, bra, brb = scratch
    tokens, width = x_in.shape
    nt = act.shape[0]
    cols = act.shape[2]
    heads = lanes.heads
    scale = HEAD_DIM**-0.5 * 1.4426950408889634
    x_ref = x_in if sub is None else xbuf
    steps = []

    def mod(i):
        return mod_ref[i : i + 1, :]

    def begin():
        if sub is not None:
            perm[...] = order_matrix(tokens, sub, False)
            reorder(xbuf, x_in, perm)
            saves.put(xbuf, x_o)

        def rows(r):
            n, _ = normed_of(x_ref[r, :].astype(F32))
            hida[r, :] = (n * (1.0 + mod(1)) + mod(0)).astype(BF16)

        row_loop(tokens, 32, rows)
        saves.put(hida, hida_o)

    steps.append((None, begin))

    kept = {}

    def project(t):
        if t >= 2:
            saves.wait(kept[0, t - 2])
        w = blocks.take()
        for c0, n in tiles(lanes.qkv):
            qkv[t % 2, :, pl.ds(c0, n)] = kdot(hida[...], w[:, pl.ds(c0, n)]).astype(BF16)
        kept[0, t] = saves.put(qkv.at[t % 2], qkv_o.at[t])

    def attend(t):
        now = qkv.at[t % 2]
        masks = [lanes.mask(1, h) for h in range(heads)]

        def one(g, carry):
            r = pl.ds(pl.multiple_of(g * group, group), group)
            q = pltpu.roll(now[r, pl.ds(0, lanes.width)].astype(F32), lanes.offsets[1], 1).astype(BF16)
            stack_heads(qst, q, masks, group)
            for p in range(heads // 2):
                k = now[r, pl.ds(lanes.starts[1] + p * LANES, 2 * LANES)]
                sc[:, pl.ds(p * 2 * group, 2 * group)] = kdot_t(k, qst[p])

            def soft(j, c2):
                at = pl.ds(pl.multiple_of(j * LANES, LANES), LANES)
                s = sc[:, at] * scale
                if sub is not None:
                    row = lax.broadcasted_iota(jnp.int32, s.shape, 0) // sub
                    col = lax.broadcasted_iota(jnp.int32, s.shape, 1) // sub
                    s = jnp.where(row == col, s, NEGATIVE)
                e = jnp.exp2(s - jnp.max(s, axis=0, keepdims=True))
                prob[t, g, :, at] = (e * (1.0 / jnp.sum(e, axis=0, keepdims=True))).astype(BF16)
                return c2

            lax.fori_loop(0, heads * group // LANES, soft, 0, unroll=2)
            pieces = [jnp.zeros((lanes.offsets[3], group), F32)]
            for p in range(heads // 2):
                v = now[r, pl.ds(lanes.starts[2] + p * LANES, 2 * LANES)].T
                for h in (2 * p, 2 * p + 1):
                    got = kdot(v, prob[t, g, :, pl.ds(h * group, group)])
                    at = lanes.place(2, h)
                    pieces.append(got[at : at + HEAD_DIM])
            rest = lanes.width - lanes.offsets[3] - heads * HEAD_DIM
            if rest:
                pieces.append(jnp.zeros((rest, group), F32))
            mix[t, r, :] = jnp.concatenate(pieces, axis=0).T.astype(BF16)
            return carry

        lax.fori_loop(0, tokens // group, one, 0)
        saves.put(prob.at[t], prob_o.at[t])
        saves.put(mix.at[t], mix_o.at[t])

    def bring_out(t):
        w = blocks.ring.at[blocks.done % blocks.depth]
        got = kdot_t(mix[t], w[:, pl.ds(lanes.starts[3], lanes.width)])
        if t == 0:
            acc[...] = got
        else:
            acc[...] += got
        blocks.drop()

    for t in range(nt):
        steps.append((0, functools.partial(project, t)))
        steps.append((0, functools.partial(attend, t)))
        steps.append((0, functools.partial(bring_out, t)))

    def between():
        def rows(r):
            b = acc[r, :]
            m = x_ref[r, :].astype(F32) + mod(2) * b
            mid[r, :] = m
            bra[r, :] = b.astype(BF16)
            n, _ = normed_of(m)
            hidb[r, :] = (n * (1.0 + mod(4)) + mod(3)).astype(BF16)

        row_loop(tokens, 32, rows)
        saves.put(bra, bra_o)
        saves.put(hidb, hidb_o)

    steps.append((0, between))

    def go_up(t):
        if t >= 2:
            saves.wait(kept[1, t - 2])
        w = blocks.take()
        for c0, n in tiles(cols):
            u = kdot(hidb[...], w[:, pl.ds(c0, n)])
            pre[t % 2, :, pl.ds(c0, n)] = u.astype(BF16)
            act[t, :, pl.ds(c0, n)] = (0.5 * u * (1.0 + gelu_inner(u))).astype(BF16)
        kept[1, t] = saves.put(pre.at[t % 2], pre_o.at[t])
        saves.put(act.at[t], act_o.at[t])
        blocks.drop()

    def go_down(t):
        w = blocks.take()
        got = kdot_t(act[t], w[...])
        if t == 0:
            acc[...] = got
        else:
            acc[...] += got
        blocks.drop()

    for t in range(nt):
        steps.append((1, functools.partial(go_up, t)))
    for t in range(nt):
        steps.append((2, functools.partial(go_down, t)))

    def end():
        def rows(r):
            b = acc[r, :]
            brb[r, :] = b.astype(BF16)
            out_ref[r, :] = (mid[r, :] + mod(5) * b).astype(out_ref.dtype)

        row_loop(tokens, 32, rows)
        saves.put(brb, brb_o)

    steps.append((2, end))
    return steps


def forward_scratch(tokens, width, nt, cols, group, sub, lanes):
    side = tokens if sub is not None else 16
    vmem = pltpu.VMEM
    return [
        vmem((side, width), BF16),
        vmem((side, side), BF16),
        vmem((tokens, width), F32),
        vmem((2, tokens, lanes.qkv), BF16),
        vmem((lanes.heads // 2, 2 * group, 2 * LANES), BF16),
        vmem((group, lanes.heads * group), F32),
        vmem((tokens, width), BF16),
        vmem((nt, tokens // group, group, lanes.heads * group), BF16),
        vmem((nt, tokens, lanes.width), BF16),
        vmem((tokens, width), BF16),
        vmem((2, tokens, cols), BF16),
        vmem((nt, tokens, cols), BF16),
        vmem((tokens, width), F32),
        vmem((tokens, width), BF16),
        vmem((tokens, width), BF16),
    ]


def forward_saved(tokens, width, nt, cols, group, sub, lanes):
    sds = jax.ShapeDtypeStruct
    return [
        sds((tokens, width), BF16),
        sds((tokens, width), BF16),
        sds((nt, tokens, lanes.qkv), BF16),
        sds((nt, tokens // group, group, lanes.heads * group), BF16),
        sds((nt, tokens, lanes.width), BF16),
        sds((tokens, width), BF16),
        sds((tokens, width), BF16),
        sds((nt, tokens, cols), BF16),
        sds((nt, tokens, cols), BF16),
        sds((tokens, width), BF16),
    ]


THIRDS = 3
GATHER_STAGES = 6
SPLITS = ((4, 3, 1, 1), (4, 4, 1, 0), (4, 3, 1, 1), (4, 4, 0, 1))


HALVES = 2
GATHER_SPLITS = ((2, 2, 1, 0), (2, 1, 0, 1), (2, 2, 1, 0), (1, 2, 0, 1))


def split_rows(k, unit):
    a, b, c, d = (v * unit for v in SPLITS[k % len(SPLITS)])
    return a, b, c, d


class Gather:
    def __init__(self, w_ref, g_ref, sems, nz):
        self.w, self.g, self.nz = w_ref, g_ref, nz
        (
            self.lsem, self.s_zab, self.r_zab, self.s_xy, self.r_xy,
            self.s_zcd, self.r_zcd, self.s_c, self.r_c,
        ) = sems
        self.layers, self.rows, self.cols = w_ref.shape
        self.unit = self.rows // 9
        self.count = self.layers * HALVES
        self.at = position()
        self.peers = neighbours(nz)

    def cut(self, k):
        at = 5 * self.unit * (k % HALVES)
        parts = []
        for v in GATHER_SPLITS[k % len(GATHER_SPLITS)]:
            parts.append((at, v * self.unit))
            at += v * self.unit
        return k // HALVES, parts

    def own(self, l):
        y, c, x, z = self.at
        return pltpu.make_async_copy(self.w.at[l], self.g.at[l, z, y, c, x], self.lsem.at[l])

    def region_ab(self, k, t):
        y, c, x, z = self.at
        l, (a, b, _, _) = self.cut(k)
        return self.g.at[l, t, y, c, x, pl.ds(a[0], a[1] + b[1])]

    def region_cd(self, k, t):
        y, c, x, z = self.at
        l, (_, _, rc, rd) = self.cut(k)
        return self.g.at[l, t, :, c, :, pl.ds(rc[0], rc[1] + rd[1])]

    def along_z(self, k, hop, which, mode):
        z, nz = self.at[3], self.nz
        below, above = self.peers[3:]
        region = (self.region_ab, self.region_cd)[which]
        ssem, rsem = ((self.s_zab, self.r_zab), (self.s_zcd, self.r_zcd))[which]
        up, down = z - hop, z + hop
        if mode == RECV:

            @pl.when(z - 1 - hop >= 0)
            def _():
                r = region(k, jnp.maximum(z - 1 - hop, 0))
                remote(r, r, ssem.at[k, hop, 1], rsem.at[k, hop, 1], above).wait_recv()

            @pl.when(z + 1 + hop < nz)
            def _():
                r = region(k, jnp.minimum(z + 1 + hop, nz - 1))
                remote(r, r, ssem.at[k, hop, 0], rsem.at[k, hop, 0], below).wait_recv()

            return
        l, (a, b, _, _) = self.cut(k)
        first = self.w.at[l, pl.ds(a[0], a[1] + b[1])] if which == 0 and hop == 0 else None

        @pl.when((up >= 0) & (z < nz - 1))
        def _():
            r = region(k, jnp.maximum(up, 0))
            copy = remote(r if first is None else first, r, ssem.at[k, hop, 1], rsem.at[k, hop, 1], above)
            copy.start() if mode == START else copy.wait_send()

        @pl.when((down < nz) & (z > 0))
        def _():
            r = region(k, jnp.minimum(down, nz - 1))
            copy = remote(r if first is None else first, r, ssem.at[k, hop, 0], rsem.at[k, hop, 0], below)
            copy.start() if mode == START else copy.wait_send()

    def region_xy(self, k, kind, yy, xx):
        y, c, x, z = self.at
        l, cuts = self.cut(k)
        ra, rb, rc, rd = (pl.ds(*v) for v in cuts)
        g = self.g
        return (
            lambda: g.at[l, :, yy, c, xx, ra],
            lambda: g.at[l, :, yy, c, xx, rb],
            lambda: g.at[l, :, yy, c, :, ra],
            lambda: g.at[l, :, :, c, xx, rb],
            lambda: g.at[l, z, yy, c, xx, rc],
            lambda: g.at[l, z, yy, c, xx, rd],
            lambda: g.at[l, z, yy, c, :, rc],
            lambda: g.at[l, z, :, c, xx, rd],
        )[kind]()

    def along_xy(self, k, kind, mode):
        y, c, x, z = self.at
        on_x = (True, False, False, True, True, False, False, True)[kind]
        l, (a, b, rc, rd) = self.cut(k)
        if (a, b, a, b, rc, rd, rc, rd)[kind][1] == 0:
            return
        target = self.peers[0 if on_x else 1]
        s, r = self.s_xy.at[k, kind], self.r_xy.at[k, kind]
        if mode == RECV:
            there = self.region_xy(k, kind, y, 1 - x) if on_x else self.region_xy(k, kind, 1 - y, x)
            remote(there, there, s, r, target).wait_recv()
            return
        here = self.region_xy(k, kind, y, x)
        src = here
        if kind == 4:
            src = self.w.at[l, pl.ds(*rc)]
        if kind == 5:
            src = self.w.at[l, pl.ds(*rd)]
        copy = remote(src, here, s, r, target)
        copy.start() if mode == START else copy.wait_send()

    def to_core(self, k, mode):
        c = self.at[1]
        l, cuts = self.cut(k)
        rows = pl.ds(cuts[0][0], sum(v[1] for v in cuts))
        r = self.g.at[l, :, :, 1 - c if mode == RECV else c, :, rows]
        copy = remote(r, r, self.s_c.at[k], self.r_c.at[k], self.peers[2])
        if mode == START:
            copy.start()
        elif mode == SEND:
            copy.wait_send()
        else:
            copy.wait_recv()

    def stage(self, k, s):
        z, xy = self.along_z, self.along_xy
        if s == 0:
            z(k, 0, 0, START)
            xy(k, 4, START)
            xy(k, 5, START)
        if s == 1:
            z(k, 0, 0, RECV)
            z(k, 1, 0, START)
            if k % HALVES == 0:
                self.own(k // HALVES).wait()
            xy(k, 4, RECV)
            xy(k, 6, START)
            xy(k, 5, RECV)
            xy(k, 7, START)
        if s == 2:
            z(k, 1, 0, RECV)
            z(k, 2, 0, START)
            xy(k, 6, RECV)
            xy(k, 7, RECV)
            z(k, 0, 1, START)
        if s == 3:
            z(k, 2, 0, RECV)
            xy(k, 0, START)
            xy(k, 1, START)
            z(k, 0, 1, RECV)
            z(k, 1, 1, START)
        if s == 4:
            xy(k, 0, RECV)
            xy(k, 2, START)
            xy(k, 1, RECV)
            xy(k, 3, START)
            z(k, 1, 1, RECV)
            z(k, 2, 1, START)
        if s == 5:
            xy(k, 2, RECV)
            xy(k, 3, RECV)
            z(k, 2, 1, RECV)
            self.to_core(k, START)

    def begin(self, ahead):
        self.ahead = ahead
        for l in range(self.layers):
            self.own(l).start()
        for k in range(min(ahead, self.count)):
            self.stage(k, 0)

    def slots(self):
        return self.count + GATHER_STAGES - 1

    def slot(self, i):
        for k in range(self.count):
            s = i - k
            if s == 0 and k + self.ahead < self.count:
                self.stage(k + self.ahead, 0)
            if 1 <= s < GATHER_STAGES:
                self.stage(k, s)

    def arrive(self, layer):
        for k in range(layer * HALVES, (layer + 1) * HALVES):
            self.to_core(k, RECV)

    def end(self):
        for k in range(self.count):
            self.to_core(k, SEND)
            for kind in range(8):
                self.along_xy(k, kind, SEND)
            for hop in range(self.nz - 1):
                self.along_z(k, hop, 0, SEND)
                self.along_z(k, hop, 1, SEND)


def forward_pass_kernel(*refs, nz, n_seq, group_0, group_1, sub, lanes):
    w_ref, lat_ref, teach_ref, cond_ref, count_ref, ada_ref = refs[:6]
    g_ref, teach_o, mod_o, silu_o, count_o, final_ref = refs[6:12]
    saved_0, saved_1 = refs[12:22], refs[22:32]
    rest = refs[32:]
    sems, rest = rest[:9], rest[9:]
    (
        s_lat, r_lat, s_tea, r_tea, s_m, r_m, local_sem, s_t, r_t,
        ada, cond_all, parts, landed, mod_all, x0, x1, out_0, ring, wsem, osem_0, osem_1,
        qst_0, sc_0, prob_0,
    ) = rest[:24]
    shared = rest[24:]
    y, c, x, z = position()
    x_dev = neighbours(nz)[0]
    layers = w_ref.shape[0]
    tokens, width = x0.shape
    _, own_frames, patches, _ = lat_ref.shape
    frame = nz * patches
    part = patches // n_seq
    greet(
        [in_plane(d)[0] for d in range(1, 8)]
        + [(y * 2 + c, xx, (z + d) % nz) for d in range(1, nz) for xx in (x, 1 - x)]
    )
    gather = Gather(w_ref, g_ref, sems, nz)

    dp, block = y * 2 + c, (y * 2 + c) * 2 + x
    me = x * nz + z
    side = [
        pltpu.make_async_copy(teach_ref.at[:, x], teach_o.at[x], local_sem.at[0]),
        pltpu.make_async_copy(ada_ref, ada, local_sem.at[1]),
    ]
    lat_in, own_rows, teach_in = [], [], []
    for i in range(own_frames):
        rows = pl.ds(pl.multiple_of(i * frame + z * patches, 16), patches)
        own_rows.append(pltpu.make_async_copy(lat_ref.at[z, i], x0.at[rows], local_sem.at[2 + i]))
        for d in range(1, nz):
            target, q = over_z(d, nz)
            lat_in.append(remote(lat_ref.at[q, i], x0.at[rows], s_lat.at[i, d], r_lat.at[i, d], target))
    teach_in.append(remote(teach_ref.at[:, 1 - x], teach_o.at[x], s_tea, r_tea, x_dev))

    conds, sums, spread = [], [], []
    for d in range(1, 4):
        target, q = over_dp(d)
        conds.append(remote(cond_ref, cond_all.at[dp], s_m.at[0, d], r_m.at[0, d], target))
    for d in range(1, 8):
        target, q = in_plane(d)
        sums.append(remote(parts.at[q // 2], landed.at[d], s_m.at[1, d], r_m.at[1, d], target))
    for d in range(1, nz):
        target, q = over_z(d, nz)
        spread.append(remote(mod_all.at[z], mod_all.at[z], s_m.at[2, d], r_m.at[2, d], target))

    def modulate(step):
        if step == 0:
            send_all(conds)
            cond_all[dp] = cond_ref[...]
        if step == 1:
            finish_all(conds)
            side[1].wait()
            silu_o[...] = jnp.zeros_like(silu_o)
            for i in range(4):
                row = cond_all[i, pl.ds(block, 1), :]
                silu_o[i : i + 1, :] = (row / (1.0 + jnp.exp(-row))).astype(BF16).astype(F32)
            parts[...] = jnp.zeros_like(parts)
            for b in range(ada.shape[0]):
                for k in range(6):
                    got = kdot(silu_o[...].astype(BF16), ada[b, k])
                    for i in range(4):
                        parts[i, 6 * b + k : 6 * b + k + 1, :] = got[i : i + 1]
            for i in range(4):
                parts[i, 12:13, :] = count_ref[...]
            send_all(sums)
        if step == 2:
            finish_all(sums)
            total = parts[dp]
            for d in range(1, 8):
                total = total + landed[d]
            mod_all[z] = total
            send_all(spread)
        if step == 3:
            finish_all(spread)
            count = mod_all[0, 12:13, :]
            for q in range(1, nz):
                count = count + mod_all[q, 12:13, :]
            count_o[...] = count
            for b in range(ada.shape[0]):
                mod_o[b] = jnp.concatenate(
                    [mod_all[q, 6 * b : 6 * b + 6, :] for q in range(nz)], axis=1
                )

    moved, kept = [], []
    for i in range(own_frames):
        dst = x1.at[pl.ds(pl.multiple_of((me * own_frames + i) * part, 16), part)]
        for d in range(1, 2 * nz):
            target, q = across(d, nz)
            src = out_0.at[
                pl.ds(pl.multiple_of(i * frame + q % nz * patches + q // nz * part, 16), part)
            ]
            moved.append(remote(src, dst, s_t.at[i, d], r_t.at[i, d], target))
        src = out_0.at[pl.ds(pl.multiple_of(i * frame + z * patches + x * part, 16), part)]
        kept.append(pltpu.make_async_copy(src, dst, local_sem.at[2 + own_frames + i]))

    ready = set()
    order = [(l, t) for l in range(layers) for t in range(nz)]
    blocks = Blocks(g_ref, ring, wsem, order, ready)
    saves_0, saves_1 = Saves(osem_0), Saves(osem_1)
    per_block = layers // 2
    common = list(shared)
    scratch_1 = common
    scratch_0 = common[:4] + [qst_0, sc_0] + common[6:7] + [prob_0] + common[8:]

    def start_spatial():
        for copy in own_rows:
            copy.wait()
        finish_all(lat_in)
        saves_0.put(x0, saved_0[0])

    def leave_spatial():
        send_all(moved)
        send_all(kept)

    def start_temporal():
        for copy in kept:
            copy.wait()
        finish_all(moved)
        saves_0.finish()

    work = [(None, start_spatial)]
    for need, step in forward_steps(
        x0, mod_o.at[0], out_0, saved_0, scratch_0, blocks, saves_0,
        sub=None, group=group_0, lanes=lanes,
    ):
        work.append((need, step))
    work.append((None, leave_spatial))
    pause = len(work)
    work.append((None, start_temporal))
    for need, step in forward_steps(
        x1, mod_o.at[1], final_ref, saved_1, scratch_1, blocks, saves_1,
        sub=sub, group=group_1, lanes=lanes,
    ):
        work.append((None if need is None else need + per_block, step))

    send_all(own_rows)
    send_all(lat_in)
    modulate(0)
    gather.begin(2)
    send_all(side)
    send_all(teach_in)
    done, waited = 0, 0
    for slot in range(gather.slots() + 1):
        if slot < gather.slots():
            gather.slot(slot)
        if slot % 2 == 1 and slot < 6:
            modulate((slot + 1) // 2)
        since = slot - GATHER_STAGES - HALVES + 1
        if since >= 0 and since % HALVES == 0:
            layer = since // HALVES
            gather.arrive(layer)
            ready.add(layer)
            blocks.pump()
        quota = 7
        while done < len(work) and quota and slot >= 5:
            need = work[done][0]
            if need is not None and need not in ready:
                break
            if done == pause:
                waited += 1
                if waited < 2 and slot < gather.slots():
                    break
            work[done][1]()
            done += 1
            quota -= 1
    while done < len(work):
        work[done][1]()
        done += 1
    gather.end()
    side[0].wait()
    finish_all(teach_in)
    saves_1.finish()


def forward_pass(shards, latents, teacher, cond, count, ada, nz, n_seq, sub):
    layers, rows, cols = shards.shape
    hops = nz - 1
    chunks = layers * HALVES
    sds = jax.ShapeDtypeStruct
    _, own_frames, patches, width = latents.shape
    tokens = nz * own_frames * patches
    frames, halves, own_patches, _ = teacher.shape
    vmem = pltpu.VMEM
    mod_shape = (16, ada.shape[3])
    lanes = Lanes(cols // 4)
    group_0, group_1 = nz * patches, 8 * sub
    sizes_0 = (tokens, width, nz, cols, group_0, None, lanes)
    sizes_1 = (tokens, width, nz, cols, group_1, sub, lanes)
    scratch_0, scratch_1 = forward_scratch(*sizes_0), forward_scratch(*sizes_1)
    rowsb = vmem((tokens, width), BF16)
    outs = pl.pallas_call(
        functools.partial(
            forward_pass_kernel, nz=nz, n_seq=n_seq, group_0=group_0, group_1=group_1, sub=sub, lanes=lanes
        ),
        out_shape=[
            sds((layers, nz, 2, 2, 2, rows, cols), BF16),
            sds((halves, frames, own_patches, width), BF16),
            sds((2, 6, width), F32),
            sds((8, cond.shape[1]), F32),
            sds((1, ada.shape[3]), F32),
            sds((tokens, width), F32),
        ]
        + forward_saved(*sizes_0)
        + forward_saved(*sizes_1),
        in_specs=[ANY, ANY, ANY, VM, VM, ANY],
        out_specs=[ANY, ANY, VM, VM, VM, VM] + [ANY] * 20,
        scratch_shapes=[
            DMA((layers,)),
            DMA((chunks, hops, 2)),
            DMA((chunks, hops, 2)),
            DMA((chunks, 8)),
            DMA((chunks, 8)),
            DMA((chunks, hops, 2)),
            DMA((chunks, hops, 2)),
            DMA((chunks,)),
            DMA((chunks,)),
            DMA((own_frames, nz)),
            DMA((own_frames, nz)),
            DMA(()),
            DMA(()),
            DMA((3, 8)),
            DMA((3, 8)),
            DMA((2 + 2 * own_frames,)),
            DMA((own_frames, 2 * nz)),
            DMA((own_frames, 2 * nz)),
            vmem(ada.shape, BF16),
            vmem((4,) + cond.shape, F32),
            vmem((4,) + mod_shape, F32),
            vmem((8,) + mod_shape, F32),
            vmem((nz,) + mod_shape, F32),
            rowsb,
            rowsb,
            rowsb,
            vmem((3, width, cols), BF16),
            DMA((3,)),
            DMA((32,)),
            DMA((32,)),
            scratch_0[4],
            scratch_0[5],
            scratch_0[7],
        ]
        + scratch_1,
        compiler_params=pltpu.CompilerParams(
            collective_id=0, has_side_effects=True, vmem_limit_bytes=62 << 20
        ),
        name="forward_pass",
    )(shards, latents, teacher, cond, count, ada)
    full, teach, mod, silu, count, final = outs[:6]
    full = full.reshape(layers, nz, -1, cols)
    return full, teach, mod, silu, count, final, outs[6:16], outs[16:26]


def backward_steps(head, ins, outs, scratch, blocks, saves, marks, *, sub, group, lanes):
    loss = len(head) > 1
    x_hbm, mod_ref, qkv_hbm, prob_hbm, mix_hbm, bra_hbm, pre_hbm, brb_hbm = ins
    gout_ref, mg_ref, gba_o, gbb_o, gat_o, gpre_o = outs[:6]
    (
        gr, acc, gbb, gba, gpre, gat, dmx, qkv, qst, dst, sc, ds, prob, preb, mix,
        x_ref, branch, lsem, tbuf, perm,
    ) = scratch
    tokens, width = gr.shape
    nt, _, cols = pre_hbm.shape
    heads = lanes.heads
    factor = HEAD_DIM**-0.5
    steps = []

    def mod(i):
        return mod_ref[i : i + 1, :]

    def load(src, dst, n):
        return pltpu.make_async_copy(src, dst, lsem.at[n])

    load_x = load(x_hbm, x_ref, 0)
    load_brb = load(brb_hbm, branch, 1)
    load_bra = load(bra_hbm, branch, 2)

    def load_pre(t):
        return load(pre_hbm.at[t], preb, 3)

    def load_heads(t):
        return load(qkv_hbm.at[t], qkv, 4), load(prob_hbm.at[t], prob, 5), load(mix_hbm.at[t], mix, 6)

    def row_sum(v):
        return jnp.sum(v, axis=0, keepdims=True)

    def begin():
        load_brb.start()
        load_pre(0).start()
        send_all(load_heads(0))
        mg_ref[...] = jnp.zeros_like(mg_ref)
        if loss:
            final_hbm, teach_hbm, mask_ref, coef_ref = head
            bout_ref, err_ref = outs[6:]
            load_teach = load(teach_hbm, x_ref, 7)
            load_final = load(final_hbm, gr, 8)
            load_teach.start()
            load_final.start()
            err_ref[...] = jnp.zeros_like(err_ref)
            perm[...] = order_matrix(tokens, sub, False)
            load_teach.wait()
            reorder(tbuf, x_ref, perm)
            load_final.wait()
        load_x.start()
        load_brb.wait()

        def rows(r):
            if loss:
                f = gr[r, :]
                e = f - tbuf[r, :].astype(F32)
                me = mask_ref[r, :] * e
                err_ref[...] += row_sum(me * e)
                gba[r, :] = f.astype(BF16)
                g = me * coef_ref[0, 0]
            else:
                g = head[0][r, :].astype(F32)
            gr[r, :] = g
            mg_ref[5:6, :] += row_sum(g * branch[r, :].astype(F32))
            gbb[r, :] = (g * mod(5)).astype(BF16)

        row_loop(tokens, 32, rows)
        load_bra.start()
        marks[2] = [saves.put(gbb, gbb_o)]
        marks[1], marks[0] = [], []
        if loss:
            perm[...] = order_matrix(tokens, sub, True)
            reorder(bout_ref, gba, perm)

    steps.append(begin)
    kept = {}

    def through_gelu(t):
        if t:
            saves.wait(kept[t - 1])
        w = blocks.take()
        load_pre(t).wait()
        for c0, n in tiles(cols):
            ga = kdot(gbb[...], w[:, pl.ds(c0, n)])
            u = preb[:, pl.ds(c0, n)].astype(F32)
            th = gelu_inner(u)
            slope = 0.5 * (1.0 + th) + 0.5 * u * (1.0 - th * th) * (
                GELU_C * (1.0 + 3.0 * GELU_K * u * u)
            )
            gpre[:, pl.ds(c0, n)] = (ga * slope).astype(BF16)
        kept[t] = saves.put(gpre, gpre_o.at[t])
        if t == nt - 1:
            marks[1].append(kept[t])
        blocks.drop()
        if t + 1 < nt:
            load_pre(t + 1).start()

    def add_up(t, got):
        if t == 0:
            acc[...] = got
        else:
            acc[...] += got

    def under_up(t):
        w = blocks.take()
        add_up(t, kdot_t(gpre[...], w[...]))
        blocks.drop()

    for t in range(nt):
        steps.append(functools.partial(through_gelu, t))
        steps.append(functools.partial(under_up, t))

    def norm_back(gh, base, shift_row, scale_row, scale_i):
        n, inv = normed_of(base)
        mg_ref[shift_row : shift_row + 1, :] += row_sum(gh)
        mg_ref[scale_row : scale_row + 1, :] += row_sum(gh * n)
        dn = gh * (1.0 + mod(scale_i))
        along = jnp.mean(dn * n, axis=-1, keepdims=True)
        return inv * (dn - jnp.mean(dn, axis=-1, keepdims=True) - n * along)

    def between():
        load_x.wait()
        load_bra.wait()

        def rows(r):
            b = branch[r, :].astype(F32)
            middle = x_ref[r, :].astype(F32) + mod(2) * b
            g = gr[r, :] + norm_back(acc[r, :], middle, 3, 4, 4)
            gr[r, :] = g
            mg_ref[2:3, :] += row_sum(g * b)
            gba[r, :] = (g * mod(2)).astype(BF16)

        row_loop(tokens, 32, rows)
        marks[0].append(saves.put(gba, gba_o))

    steps.append(between)
    sent = {}

    def attend(t):
        if t:
            saves.wait(sent[t - 1])
        w = blocks.take()
        d = kdot(gba[...], w[:, pl.ds(lanes.starts[3], lanes.width)])
        back = lanes.width - (lanes.offsets[3] - lanes.offsets[2])
        dmx[...] = pltpu.roll(d, back, 1).astype(BF16)
        for copy in load_heads(t):
            copy.wait()
        kmasks = [lanes.mask(1, h) for h in range(heads)]
        vmasks = [lanes.mask(2, h) for h in range(heads)]

        def one(g, carry):
            r = pl.ds(pl.multiple_of(g * group, group), group)
            q = pltpu.roll(qkv[r, pl.ds(0, lanes.width)].astype(F32), lanes.offsets[1], 1).astype(BF16)
            stack_heads(qst, q, kmasks, group)
            stack_heads(dst, dmx[r, :], vmasks, group)
            for p in range(heads // 2):
                v = qkv[r, pl.ds(lanes.starts[2] + p * LANES, 2 * LANES)]
                sc[:, pl.ds(p * 2 * group, 2 * group)] = kdot_t(v, dst[p])

            def soft(j, c2):
                at = pl.ds(pl.multiple_of(j * LANES, LANES), LANES)
                p = prob[g, :, at].astype(F32)
                gp = sc[:, at]
                inner = jnp.sum(gp * p, axis=0, keepdims=True)
                ds[:, at] = (p * (gp - inner)).astype(BF16)
                return c2

            lax.fori_loop(0, heads * group // LANES, soft, 0, unroll=2)
            pieces, dk, dv = [], [], []
            for p in range(heads // 2):
                pair = pl.ds(p * 2 * group, 2 * group)
                dk.append(kdot(ds[:, pair], qst[p]) * factor)
                dv.append(kdot(prob[g, :, pair], dst[p]))
                k = qkv[r, pl.ds(lanes.starts[1] + p * LANES, 2 * LANES)].T
                for h in (2 * p, 2 * p + 1):
                    got = kdot(k, ds[:, pl.ds(h * group, group)])
                    at = lanes.place(1, h)
                    pieces.append(got[at : at + HEAD_DIM])
            pieces.append(jnp.zeros((lanes.width - heads * HEAD_DIM, group), F32))
            dq = jnp.concatenate(pieces, axis=0).T * factor
            parts = [dq[:, i * LANES : (i + 1) * LANES] for i in range(3)]
            low, high = slice(0, LANES), slice(LANES, 2 * LANES)
            parts[2] = parts[2] + dk[0][:, low]
            parts.append(dk[0][:, high] + dk[1][:, low])
            parts.append(dk[1][:, high] + dv[0][:, low])
            parts.append(dv[0][:, high] + dv[1][:, low])
            parts.append(dv[1][:, high])
            for i, part in enumerate(parts):
                gat[r, pl.ds(i * LANES, LANES)] = part.astype(BF16)
            return carry

        lax.fori_loop(0, tokens // group, one, 0)

    def under_qkv(t):
        w = blocks.ring.at[blocks.done % blocks.depth]
        add_up(t, kdot_t(gat[:, pl.ds(0, lanes.qkv)], w[:, pl.ds(0, lanes.qkv)]))
        blocks.drop()
        s3 = lanes.starts[3]
        gat[:, pl.ds(s3, LANES)] = gat[:, pl.ds(s3, LANES)] + mix[:, pl.ds(0, LANES)]
        gat[:, pl.ds(s3 + LANES, 2 * LANES)] = mix[:, pl.ds(LANES, 2 * LANES)]
        sent[t] = saves.put(gat, gat_o.at[t])
        if t == nt - 1:
            marks[0].append(sent[t])
        if t + 1 < nt:
            send_all(load_heads(t + 1))

    for t in range(nt):
        steps.append(functools.partial(attend, t))
        steps.append(functools.partial(under_qkv, t))

    def end():
        def rows(r):
            g = gr[r, :] + norm_back(acc[r, :], x_ref[r, :].astype(F32), 0, 1, 1)
            if loss:
                tbuf[r, :] = g.astype(BF16)
            else:
                gout_ref[r, :] = g.astype(BF16)

        row_loop(tokens, 32, rows)
        if loss:
            reorder(gout_ref, tbuf, perm)

    steps.append(end)
    return steps


def heads_scratch(tokens, group, lanes):
    vmem = pltpu.VMEM
    return [
        vmem((lanes.heads // 2, 2 * group, 2 * LANES), BF16),
        vmem((lanes.heads // 2, 2 * group, 2 * LANES), BF16),
        vmem((group, lanes.heads * group), F32),
        vmem((group, lanes.heads * group), BF16),
        vmem((tokens // group, group, lanes.heads * group), BF16),
    ]


def backward_scratch(tokens, width, cols, lanes):
    vmem = pltpu.VMEM
    return [
        vmem((tokens, width), F32),
        vmem((tokens, width), F32),
        vmem((tokens, width), BF16),
        vmem((tokens, width), BF16),
        vmem((tokens, cols), BF16),
        vmem((tokens, cols), BF16),
        vmem((tokens, lanes.width), BF16),
        vmem((tokens, lanes.qkv), BF16),
        vmem((tokens, cols), BF16),
        vmem((tokens, lanes.width), BF16),
        vmem((tokens, width), BF16),
        vmem((tokens, width), BF16),
        DMA((9,)),
        vmem((tokens, width), BF16),
        vmem((tokens, tokens), BF16),
    ]


STAGES = 7
KEPT = 6
SLOTS = 3
Y_A, X_A, X_B, Y_B, Y_C, X_C, X_D, Y_D = KINDS = tuple(range(8))


class Reduce:
    def __init__(self, x_refs, g_refs, o_ref, scratch, chunks, before, split_at, nz, rows, width):
        (
            self.acc, self.stg, self.prb, self.gbuf, self.xraw, self.xt,
            self.ya, self.xa, self.xb, self.yb, self.yc, self.xc, self.xd, self.yd, self.zab, self.zcd,
            self.gsem, self.xsem, self.osem, self.s_p, self.r_p, self.s_xy, self.r_xy, self.s_z, self.r_z,
        ) = scratch
        self.x_refs, self.g_refs, self.o_ref = x_refs, g_refs, o_ref
        self.chunks, self.before, self.split_at = chunks, before, split_at
        self.nz, self.rows, self.width = nz, rows, width
        self.unit = rows // 9
        self.count = len(chunks)
        self.at = position()
        self.peers = neighbours(nz)
        self.order = []
        for _, _, used in chunks:
            for q in used:
                if q not in self.order:
                    self.order.append(q)
        self.turned_so_far = 0

    def add_in(self, dst, src):
        lead = dst.shape[:-2]
        total = 1
        for v in lead:
            total *= v
        if total == 1:
            dst[...] = dst[...] + src[...]
            return

        def body(i, carry):
            index = []
            rest = i
            for v in reversed(lead):
                index.append(rest % v)
                rest = rest // v
            index = tuple(reversed(index))
            dst[index] = dst[index] + src[index]
            return carry

        lax.fori_loop(0, total, body, 0)

    def exchange(self, k, kind, mode):
        y, c, x, z = self.at
        x_dev, y_dev = self.peers[:2]
        a, b, nc, nd = split_rows(k, self.unit)
        if (a, a, b, b, nc, nc, nd, nd)[kind] == 0:
            return
        ra, rb, rc, rd = pl.ds(0, a), pl.ds(a, b), pl.ds(a + b, nc), pl.ds(a + b + nc, nd)
        m = k % SLOTS
        part = self.acc.at[k % KEPT]
        src, buf, target, dst = (
            lambda: (part.at[:, 1 - y, :, ra], self.ya.at[m, :, :, pl.ds(0, a)], y_dev, part.at[:, y, :, ra]),
            lambda: (part.at[:, y, 1 - x, ra], self.xa.at[m, :, pl.ds(0, a)], x_dev, part.at[:, y, x, ra]),
            lambda: (part.at[:, :, 1 - x, rb], self.xb.at[m, :, :, pl.ds(0, b)], x_dev, part.at[:, :, x, rb]),
            lambda: (part.at[:, 1 - y, x, rb], self.yb.at[m, :, pl.ds(0, b)], y_dev, part.at[:, y, x, rb]),
            lambda: (part.at[z, 1 - y, :, rc], self.yc.at[m], y_dev, part.at[z, y, :, rc]),
            lambda: (part.at[z, y, 1 - x, rc], self.xc.at[m], x_dev, part.at[z, y, x, rc]),
            lambda: (part.at[z, :, 1 - x, rd], self.xd.at[m], x_dev, part.at[z, :, x, rd]),
            lambda: (part.at[z, 1 - y, x, rd], self.yd.at[m], y_dev, part.at[z, y, x, rd]),
        )[kind]()
        copy = remote(src, buf, self.s_xy.at[k % STAGES, kind], self.r_xy.at[m, kind], target)
        if mode == START:
            copy.start()
        elif mode == SEND:
            copy.wait_send()
        else:
            copy.wait_recv()
            self.add_in(dst, buf)

    def region_z(self, k, t, which):
        y, c, x, z = self.at
        part = self.acc.at[k % KEPT, t]
        a, b, nc, nd = split_rows(k, self.unit)
        if which == 0:
            return part.at[y, x, pl.ds(0, a + b)]
        return part.at[:, :, pl.ds(a + b, nc + nd)]

    def landing(self, k, hop, way, which):
        a, b, nc, nd = split_rows(k, self.unit)
        if which == 0:
            return self.zab.at[k % SLOTS, hop, way, pl.ds(0, a + b)]
        return self.zcd.at[k % SLOTS, hop, way, :, :, pl.ds(0, nc + nd)]

    def along_z(self, k, hop, which, mode):
        z, nz = self.at[3], self.nz
        below, above = self.peers[3:]
        m, n = k % SLOTS, k % STAGES
        s_z, r_z = self.s_z, self.r_z
        t_down, t_up = hop - (nz - 1 - z), nz - 1 - (hop - z)
        if mode != RECV:

            @pl.when((t_down >= 0) & (z > 0))
            def _():
                copy = remote(
                    self.region_z(k, jnp.maximum(t_down, 0), which), self.landing(k, hop, 0, which),
                    s_z.at[n, which, hop, 0], r_z.at[m, which, hop, 0], below,
                )
                copy.start() if mode == START else copy.wait_send()

            @pl.when((hop >= z) & (z < nz - 1))
            def _():
                copy = remote(
                    self.region_z(k, jnp.minimum(t_up, nz - 1), which), self.landing(k, hop, 1, which),
                    s_z.at[n, which, hop, 1], r_z.at[m, which, hop, 1], above,
                )
                copy.start() if mode == START else copy.wait_send()

            return
        from_above, from_below = t_down + 1, t_up - 1

        @pl.when((from_above >= 0) & (z < nz - 1))
        def _():
            buf = self.landing(k, hop, 0, which)
            remote(buf, buf, s_z.at[n, which, hop, 0], r_z.at[m, which, hop, 0], below).wait_recv()
            self.add_in(self.region_z(k, jnp.maximum(from_above, 0), which), buf)

        @pl.when((hop >= z - 1) & (z > 0))
        def _():
            buf = self.landing(k, hop, 1, which)
            remote(buf, buf, s_z.at[n, which, hop, 1], r_z.at[m, which, hop, 1], above).wait_recv()
            self.add_in(self.region_z(k, jnp.minimum(from_below, nz - 1), which), buf)

    def pair(self, k, mode):
        m = k % 2
        copy = remote(self.stg, self.prb.at[m], self.s_p, self.r_p.at[m], self.peers[2])
        if mode == START:
            copy.start()
        elif mode == SEND:
            copy.wait_send()
        else:
            copy.wait_recv()
            self.add_in(self.acc.at[k % KEPT], self.prb.at[m])

    def load_g(self, k):
        layer, col, _ = self.chunks[k]
        return pltpu.make_async_copy(
            self.g_refs[layer].at[:, :, pl.ds(col * self.width, self.width)], self.gbuf, self.gsem
        )

    def turned(self, q):
        i = self.order.index(q)
        if i >= self.turned_so_far:
            load = pltpu.make_async_copy(self.x_refs[q], self.xraw, self.xsem)
            load.start()
            load.wait()
            for j in range(self.xraw.shape[1] // LANES):
                self.xt[i % 2, pl.ds(j * LANES, LANES), :] = self.xraw[:, pl.ds(j * LANES, LANES)].T
            self.turned_so_far += 1
        return i % 2

    def multiply(self, k):
        layer, col, used = self.chunks[k]
        c = self.at[1]
        if col == 0:
            self.before(layer)
            self.load_g(k).start()
        slots = [self.turned(q) for q in used]
        self.load_g(k).wait()
        rows = self.rows

        def fill(dst, core):
            def rows_of(slot):
                return jnp.concatenate(
                    [
                        self.xt[slot, pl.ds(pl.multiple_of((yy * 4 + core * 2) * rows, 16), 2 * rows), :]
                        for yy in range(2)
                    ],
                    axis=0,
                )

            def body(t, carry):
                g = self.gbuf[t]
                r = jnp.dot(rows_of(slots[0]), g, preferred_element_type=F32)
                if len(slots) == 2:
                    second = jnp.dot(rows_of(slots[1]), g, preferred_element_type=F32)
                    lane = lax.broadcasted_iota(jnp.int32, r.shape, 1)
                    r = jnp.where(lane < self.split_at, r, second)
                r = r.astype(BF16)
                for i in range(4):
                    dst[t, i // 2, i % 2] = r[i * rows : (i + 1) * rows]
                return carry

            lax.fori_loop(0, self.nz, body, 0)

        fill(self.stg, 1 - c)
        self.pair(k, START)
        if k >= KEPT:
            self.hand_out(k - KEPT).wait()
        fill(self.acc.at[k % KEPT], c)
        if k + 1 < self.count and self.chunks[k + 1][0] == layer:
            self.load_g(k + 1).start()

    def hand_out(self, k):
        y, c, x, z = self.at
        layer, col, _ = self.chunks[k]
        return pltpu.make_async_copy(
            self.acc.at[k % KEPT, z, y, x],
            self.o_ref.at[layer, :, pl.ds(col * self.width, self.width)],
            self.osem.at[k % KEPT],
        )

    def stage(self, k, s):
        move, z = self.exchange, self.along_z
        if s == 0:
            self.multiply(k)
        if s == 1:
            self.pair(k, SEND)
            self.pair(k, RECV)
            move(k, Y_A, START)
            move(k, X_B, START)
            z(k, 0, 1, START)
        if s == 2:
            z(k, 0, 1, RECV)
            z(k, 1, 1, START)
            move(k, Y_A, RECV)
            move(k, X_A, START)
            move(k, X_B, RECV)
            move(k, Y_B, START)
        if s == 3:
            z(k, 1, 1, RECV)
            z(k, 2, 1, START)
            move(k, X_A, RECV)
            move(k, Y_B, RECV)
            z(k, 0, 0, START)
        if s == 4:
            z(k, 0, 0, RECV)
            z(k, 1, 0, START)
            z(k, 2, 1, RECV)
            move(k, Y_C, START)
            move(k, X_D, START)
        if s == 5:
            z(k, 1, 0, RECV)
            z(k, 2, 0, START)
            move(k, Y_C, RECV)
            move(k, X_C, START)
            move(k, X_D, RECV)
            move(k, Y_D, START)
        if s == 6:
            z(k, 2, 0, RECV)
            move(k, X_C, RECV)
            move(k, Y_D, RECV)
            for kind in KINDS:
                move(k, kind, SEND)
            for hop in range(self.nz - 1):
                z(k, hop, 0, SEND)
                z(k, hop, 1, SEND)
            self.hand_out(k).start()

    def slots(self):
        return self.count + STAGES - 1

    def slot(self, i):
        for s in range(STAGES - 1, -1, -1):
            if 0 <= i - s < self.count:
                self.stage(i - s, s)

    def end(self):
        for k in range(max(0, self.count - KEPT), self.count):
            self.hand_out(k).wait()


def reduce_scratch(tokens, cols, rows, nz):
    width = cols // THIRDS
    unit = rows // 9
    hops = nz - 1
    vmem = pltpu.VMEM
    return [
        vmem((KEPT, nz, 2, 2, rows, width), BF16),
        vmem((nz, 2, 2, rows, width), BF16),
        vmem((2, nz, 2, 2, rows, width), BF16),
        vmem((nz, tokens, width), BF16),
        vmem((tokens, cols), BF16),
        vmem((2, cols, tokens), BF16),
        vmem((SLOTS, nz, 2, 4 * unit, width), BF16),
        vmem((SLOTS, nz, 4 * unit, width), BF16),
        vmem((SLOTS, nz, 2, 4 * unit, width), BF16),
        vmem((SLOTS, nz, 4 * unit, width), BF16),
        vmem((SLOTS, 2, unit, width), BF16),
        vmem((SLOTS, unit, width), BF16),
        vmem((SLOTS, 2, unit, width), BF16),
        vmem((SLOTS, unit, width), BF16),
        vmem((SLOTS, hops, 2, 8 * unit, width), BF16),
        vmem((SLOTS, hops, 2, 2, 2, 2 * unit, width), BF16),
        DMA(()),
        DMA(()),
        DMA((KEPT,)),
        DMA(()),
        DMA((2,)),
        DMA((STAGES, 8)),
        DMA((SLOTS, 8)),
        DMA((STAGES, 2, hops, 2)),
        DMA((SLOTS, 2, hops, 2)),
    ]


PER_SLOT = 2


def backward_pass_kernel(*refs, nz, n_seq, group_0, group_1, sub, lanes, rows):
    rest = list(refs)

    def take(n):
        got = rest[:n]
        del rest[:n]
        return got

    final_ref, teach_ref, mask_ref, coef_ref, mod_ref, w_ref, ada_ref = take(7)
    saved = take(10), take(10)
    o_ref, bout_o, lat_o, sums_o, silu_o = take(5)
    made = take(4), take(4)
    (
        ring, wsem, osem, s_t, r_t, s_lat, r_lat, s_m, r_m, local_sem,
        ada, mod_parts, first, every, along, back, silus, bout, err, gout, gin, mg_0, mg_1,
    ) = take(23)
    heads = take(5), take(5)
    shared = take(15)
    y, c, x, z = position()
    tokens, width = gout.shape
    own_frames, patches = lat_o.shape[1:3]
    part = patches // n_seq
    layers = w_ref.shape[0]
    greet(
        [in_plane(d)[0] for d in range(1, 8)]
        + [(y * 2 + c, xx, (z + d) % nz) for d in range(1, nz) for xx in (x, 1 - x)]
    )
    dp, block, me = y * 2 + c, (y * 2 + c) * 2 + x, x * nz + z
    load_ada = pltpu.make_async_copy(ada_ref, ada, local_sem.at[0])
    load_ada.start()

    uses = [(l, t) for t in range(nz) for l in (2, 1)] + [(0, t) for t in range(nz)]
    order = [(3 * b + l, t) for b in (1, 0) for l, t in uses]
    blocks = Blocks(w_ref, ring, wsem, order, set(range(layers)))
    blocks.pump()
    saves = Saves(osem)
    marks = {}, {}

    x_refs, g_refs, chunks = [], [], []
    for b in range(2):
        gba_o, gbb_o, gat_o, gpre_o = made[b]
        x_refs += [saved[b][1], gba_o, saved[b][6], gbb_o]
        g_refs += [gat_o, gpre_o, saved[b][8]]
    cols = g_refs[0].shape[2]
    third = cols // THIRDS
    for b in (1, 0):
        for layer, used in ((2, (3,)), (1, (2,)), (0, (0, 1))):
            for col in range(THIRDS):
                ids = tuple(4 * b + q for q in used)
                if layer == 0 and (col + 1) * third <= 3 * lanes.span:
                    ids = ids[:1]
                chunks.append((3 * b + layer, col, ids))

    def before(layer):
        for copy in marks[layer // 3][layer % 3]:
            saves.wait(copy)

    reduce = Reduce(
        x_refs, g_refs, o_ref, take(25), chunks, before, 3 * lanes.span - 2 * third, nz, rows, third
    )

    moved, kept = [], []
    for d in range(1, 2 * nz):
        target, q = across(d, nz)
        src = gout.reshape(2 * nz, own_frames, part, width).at[q]
        dst = gin.reshape(own_frames, nz, n_seq, part, width).at[:, z, x]
        moved.append(remote(src, dst, s_t.at[d], r_t.at[d], target))
    kept.append(
        pltpu.make_async_copy(
            gout.reshape(2 * nz, own_frames, part, width).at[me],
            gin.reshape(own_frames, nz, n_seq, part, width).at[:, z, x],
            local_sem.at[1],
        )
    )
    halves = bout.reshape(n_seq, bout_o.shape[0], part, width)
    moved.append(
        remote(halves.at[1 - x], bout_o.at[:, x], s_t.at[0], r_t.at[0], device(y, c, 1 - x, z))
    )
    kept.append(pltpu.make_async_copy(halves.at[x], bout_o.at[:, x], local_sem.at[2]))

    frames_of = gout.reshape(own_frames, nz, patches, width)
    own_lat = pltpu.make_async_copy(frames_of.at[:, z], lat_o.at[z], local_sem.at[3])
    lat_out, sums, spread, slices, rows_out = [], [], [], [], []
    for d in range(1, nz):
        target, q = over_z(d, nz)
        lat_out.append(remote(frames_of.at[:, q], lat_o.at[z], s_lat.at[d], r_lat.at[d], target))
        slices.append(remote(along, back.at[d], s_m.at[2, d], r_m.at[2, d], target))
    for d in range(1, 2 * nz):
        target, q = across(d, nz)
        sums.append(remote(mod_parts.at[q % nz], first.at[d], s_m.at[0, d], r_m.at[0, d], target))
    for d in range(1, 4):
        target, q = over_dp(d)
        spread.append(remote(every.at[dp], every.at[dp], s_m.at[1, d], r_m.at[1, d], target))
    for d in range(1, 8):
        target, q = in_plane(d)
        rows_out.append(remote(silus.at[block], silus.at[block], s_m.at[3, d], r_m.at[3, d], target))

    def modulation(step):
        if step == 0:
            span = lanes.span
            mod_parts[...] = jnp.zeros_like(mod_parts)
            total = jnp.sum(err[...], axis=1, keepdims=True)
            for q in range(nz):
                mod_parts[q, 0:6, :] = mg_0[:, q * span : (q + 1) * span]
                mod_parts[q, 6:12, :] = mg_1[:, q * span : (q + 1) * span]
                mod_parts[q, 12:13, :] = jnp.broadcast_to(total, (1, span))
            send_all(sums)
            own_lat.start()
            send_all(lat_out)
        if step == 1:
            finish_all(sums)
            total = mod_parts[z]
            for d in range(1, 2 * nz):
                total = total + first[d]
            every[dp] = total
            send_all(spread)
        if step == 2:
            finish_all(spread)
            load_ada.wait()
            sums_o[...] = every[...]
            total = jnp.zeros(along.shape, F32)
            for b in range(ada.shape[0]):
                for k in range(6):
                    i = 6 * b + k
                    got = jnp.concatenate([every[q, i : i + 1, :] for q in range(4)] * 2, axis=0)
                    high = got.astype(BF16)
                    rest_1 = got - high.astype(F32)
                    middle = rest_1.astype(BF16)
                    lowest = (rest_1 - middle.astype(F32)).astype(BF16)
                    for piece in (high, middle, lowest):
                        total = total + kdot_t(piece, ada[b, k])
            along[...] = total
            send_all(slices)
        if step == 3:
            finish_all(slices)
            total = along[...]
            for d in range(1, nz):
                total = total + back[d]
            silus[block] = total
            send_all(rows_out)
        if step == 4:
            finish_all(rows_out)
            for q in range(8):
                silu_o[q : q + 1, :] = silus[q, pl.ds(dp, 1), :]

    def ins_of(b):
        x_hbm, _, qkv, prob, mix, bra, _, pre, _, brb = saved[b]
        return x_hbm, mod_ref.at[b], qkv, prob, mix, bra, pre, brb

    def scratch_of(b):
        return list(shared[:8]) + list(heads[b][:4]) + [heads[b][4]] + list(shared[8:])

    def leave():
        send_all(moved)
        send_all(kept)

    def enter():
        for copy in kept:
            copy.wait()
        finish_all(moved)
        saves.finish()

    work = backward_steps(
        (final_ref, teach_ref, mask_ref, coef_ref), ins_of(1), [gout, mg_1] + made[1] + [bout, err],
        scratch_of(1), blocks, saves, marks[1], sub=sub, group=group_1, lanes=lanes,
    )
    one = len(work)
    work.append(leave)
    work.append(enter)
    base = len(work)
    work += backward_steps(
        (gin,), ins_of(0), [gout, mg_0] + made[0],
        scratch_of(0), blocks, saves, marks[0], sub=None, group=group_0, lanes=lanes,
    )
    work.append(functools.partial(modulation, 0))
    gelu_done, attn_done = 2 * nz - 1, one - 2
    need = {5: 0, 4: gelu_done, 3: attn_done, 2: base, 1: base + gelu_done, 0: base + attn_done}
    done, later, since = 0, 1, 0
    for slot in range(reduce.slots()):
        if slot < len(chunks):
            while done <= need[chunks[slot][0]]:
                work[done]()
                done += 1
        reduce.slot(slot)
        if done == len(work) and later < 5:
            modulation(later)
            later += 1
        quota = PER_SLOT
        while quota and done < len(work):
            if done == one + 1:
                since += 1
                if since < 3:
                    break
            work[done]()
            done += 1
            quota -= 1
    for step in range(later, 5):
        modulation(step)
    own_lat.wait()
    finish_all(lat_out)
    saves.finish()
    reduce.end()


def backward_pass(final, teacher, mask, coef, mod, w, ada, saved_0, saved_1, rows, nz, n_seq, sub):
    tokens, width = final.shape
    layers, _, _, cols = w.shape
    frames, halves = sub // n_seq, n_seq
    own_frames = frames // nz
    patches = tokens // nz // own_frames
    lanes = Lanes(cols // 4)
    span = ada.shape[3]
    group_0, group_1 = nz * patches, 8 * sub
    vmem = pltpu.VMEM
    sds = jax.ShapeDtypeStruct
    smem = pl.BlockSpec(memory_space=pltpu.SMEM)
    flat, tall = sds((tokens, width), BF16), sds((nz, tokens, cols), BF16)
    small = (16, span)
    rowsb = vmem((tokens, width), BF16)
    outs = pl.pallas_call(
        functools.partial(
            backward_pass_kernel,
            nz=nz, n_seq=n_seq, group_0=group_0, group_1=group_1, sub=sub, lanes=lanes, rows=rows,
        ),
        out_shape=[
            sds((layers, rows, cols), BF16),
            sds((frames, halves, patches // n_seq, width), BF16),
            sds((nz, own_frames, patches, width), BF16),
            sds((4,) + small, F32),
            sds((8, rows), F32),
        ]
        + [flat, flat, tall, tall] * 2,
        in_specs=[ANY, ANY, VM, smem, VM, ANY, ANY] + [ANY] * 20,
        out_specs=[ANY, ANY, ANY, VM, VM] + [ANY] * 8,
        scratch_shapes=[
            vmem((2, width, cols), BF16),
            DMA((2,)),
            DMA((24,)),
            DMA((2 * nz,)),
            DMA((2 * nz,)),
            DMA((nz,)),
            DMA((nz,)),
            DMA((4, 8)),
            DMA((4, 8)),
            DMA((4,)),
            vmem(ada.shape, BF16),
            vmem((nz,) + small, F32),
            vmem((2 * nz,) + small, F32),
            vmem((4,) + small, F32),
            vmem((8, rows), F32),
            vmem((nz, 8, rows), F32),
            vmem((8, 8, rows), F32),
            rowsb,
            vmem((1, width), F32),
            rowsb,
            rowsb,
            vmem((6, width), F32),
            vmem((6, width), F32),
        ]
        + heads_scratch(tokens, group_0, lanes)
        + heads_scratch(tokens, group_1, lanes)
        + backward_scratch(tokens, width, cols, lanes)
        + reduce_scratch(tokens, cols, rows, nz),
        compiler_params=pltpu.CompilerParams(
            collective_id=1, has_side_effects=True, vmem_limit_bytes=63 << 20
        ),
        name="backward_pass",
    )(final, teacher, mask, coef, mod, w, ada, *saved_0, *saved_1)
    return outs[:5]


def normalize(stream):
    center = stream - jnp.mean(stream, axis=-1, keepdims=True)
    inverse = lax.rsqrt(jnp.mean(center * center, axis=-1, keepdims=True) + EPSILON)
    return center * inverse, inverse


def norm_backward(grad_normed, normed, inverse):
    mean_grad = jnp.mean(grad_normed, axis=-1, keepdims=True)
    mean_along = jnp.mean(grad_normed * normed, axis=-1, keepdims=True)
    return inverse * (grad_normed - mean_grad - normed * mean_along)


def gelu_tanh(values):
    return jax.nn.gelu(values, approximate=True)


def dot(a, b):
    return jnp.dot(a, b, preferred_element_type=F32)


def dot_t(a, b):
    return lax.dot_general(a, b, (((1,), (1,)), ((), ())), preferred_element_type=F32)


def attend_forward(heads, factor):
    q, k, v = heads[:, :, :, 0], heads[:, :, :, 1], heads[:, :, :, 2]
    scores = jnp.einsum("tglhe,tgmhe->tghlm", q, k, preferred_element_type=F32) * factor
    peak = jnp.max(scores, axis=-1, keepdims=True)
    expanded = jnp.exp(scores - peak)
    total = jnp.sum(expanded, axis=-1, keepdims=True)
    probs = (expanded / total).astype(BF16)
    mixed = jnp.einsum("tghlm,tgmhe->tglhe", probs, v, preferred_element_type=F32)
    return mixed.astype(BF16), peak + jnp.log(total)


def attend_backward(heads, log_total, grad_mixed, factor):
    q, k, v = heads[:, :, :, 0], heads[:, :, :, 1], heads[:, :, :, 2]
    scores = jnp.einsum("tglhe,tgmhe->tghlm", q, k, preferred_element_type=F32) * factor
    probs = jnp.exp(scores - log_total)
    grad_v = jnp.einsum(
        "tghlm,tglhe->tgmhe", probs.astype(BF16), grad_mixed, preferred_element_type=F32
    )
    grad_probs = jnp.einsum("tglhe,tgmhe->tghlm", grad_mixed, v, preferred_element_type=F32)
    inner = jnp.sum(grad_probs * probs, axis=-1, keepdims=True)
    grad_scores = (probs * (grad_probs - inner)).astype(BF16)
    grad_q = jnp.einsum("tghlm,tgmhe->tglhe", grad_scores, k, preferred_element_type=F32) * factor
    grad_k = jnp.einsum("tghlm,tglhe->tgmhe", grad_scores, q, preferred_element_type=F32) * factor
    return jnp.stack([grad_q, grad_k, grad_v], axis=3).astype(BF16)


def block_forward(stream, modulation, weights, group):
    attn, up, down = weights
    blocks, width, cols = attn.shape
    inner = cols // 4 * 3
    head_count = cols // 4 // HEAD_DIM
    clips, per_clip, _ = stream.shape
    tokens = clips * per_clip
    factor = HEAD_DIM**-0.5

    def column(i):
        return modulation[:, i][:, None, :]

    normed_a, inverse_a = normalize(stream)
    hidden_a = (normed_a * (1.0 + column(1)) + column(0)).astype(BF16).reshape(tokens, width)
    triple = jnp.stack([dot(hidden_a, attn[t, :, :inner]).astype(BF16) for t in range(blocks)])
    heads = triple.reshape(blocks, tokens // group, group, 3, head_count, HEAD_DIM)
    mixed, log_total = attend_forward(heads, factor)
    mixed = mixed.reshape(blocks, tokens, cols // 4)
    branch_a = sum(dot_t(mixed[t], attn[t, :, inner:]) for t in range(blocks)).reshape(stream.shape)
    middle = stream + column(2) * branch_a
    normed_b, inverse_b = normalize(middle)
    hidden_b = (normed_b * (1.0 + column(4)) + column(3)).astype(BF16).reshape(tokens, width)
    pre_act = jnp.stack([dot(hidden_b, up[t]) for t in range(blocks)])
    activated = gelu_tanh(pre_act).astype(BF16)
    branch_b = sum(dot_t(activated[t], down[t]) for t in range(blocks)).reshape(stream.shape)
    output = middle + column(5) * branch_b
    saved = (
        normed_a, inverse_a, hidden_a, heads, log_total, mixed, branch_a,
        normed_b, inverse_b, hidden_b, pre_act, activated, branch_b,
    )
    return output, saved


def block_backward(grad, modulation, weights, saved, group):
    attn, up, down = weights
    blocks, width, cols = attn.shape
    inner = cols // 4 * 3
    head_count = cols // 4 // HEAD_DIM
    (
        normed_a, inverse_a, hidden_a, heads, log_total, mixed, branch_a,
        normed_b, inverse_b, hidden_b, pre_act, activated, branch_b,
    ) = saved
    tokens = hidden_a.shape[0]
    factor = HEAD_DIM**-0.5

    def column(i):
        return modulation[:, i][:, None, :]

    def clip_sum(values):
        return jnp.sum(values, axis=1)

    gate_b = clip_sum(grad * branch_b)
    branch_grad_b = (grad * column(5)).astype(BF16).reshape(tokens, width)
    grad_act = jnp.stack([dot(branch_grad_b, down[t]) for t in range(blocks)])
    grad_pre = jax.vjp(gelu_tanh, pre_act)[1](grad_act)[0].astype(BF16)
    grad_hidden_b = sum(dot_t(grad_pre[t], up[t]) for t in range(blocks)).reshape(grad.shape)
    shift_b = clip_sum(grad_hidden_b)
    scale_b = clip_sum(grad_hidden_b * normed_b)
    grad_middle = grad + norm_backward(grad_hidden_b * (1.0 + column(4)), normed_b, inverse_b)
    gate_a = clip_sum(grad_middle * branch_a)
    branch_grad_a = (grad_middle * column(2)).astype(BF16).reshape(tokens, width)
    grad_mixed = jnp.stack(
        [dot(branch_grad_a, attn[t, :, inner:]).astype(BF16) for t in range(blocks)]
    )
    grad_mixed = grad_mixed.reshape(blocks, tokens // group, group, head_count, HEAD_DIM)
    grad_heads = attend_backward(heads, log_total, grad_mixed, factor)
    grad_triple = grad_heads.reshape(blocks, tokens, inner)
    grad_hidden_a = sum(
        dot_t(grad_triple[t], attn[t, :, :inner]) for t in range(blocks)
    ).reshape(grad.shape)
    shift_a = clip_sum(grad_hidden_a)
    scale_a = clip_sum(grad_hidden_a * normed_a)
    grad_input = grad_middle + norm_backward(
        grad_hidden_a * (1.0 + column(1)), normed_a, inverse_a
    )
    grad_modulation = jnp.stack([shift_a, scale_a, gate_a, shift_b, scale_b, gate_b], axis=1)
    x_list = [hidden_a, branch_grad_a, hidden_b, branch_grad_b]
    g_list = [jnp.concatenate([grad_triple, mixed], axis=2), grad_pre, activated]
    return grad_input, grad_modulation, x_list, g_list


def local_anywhere(
    latents, condition, teacher, valid_mask,
    qkv_weight, out_weight, up_weight, down_weight, ada_weight,
):
    n_dp, n_seq, n_tensor = (lax.axis_size(a) for a in (DP, SEQ, TENSOR))
    clips, frames, patches, width = latents.shape
    rows = ada_weight.shape[1]
    blocks = qkv_weight.shape[0]
    heads_width = qkv_weight.shape[3]
    inner = 3 * heads_width
    dp, seq, tensor = (lax.axis_index(a) for a in (DP, SEQ, TENSOR))
    row_block = dp * n_seq + seq

    shards = pack_shards(qkv_weight, out_weight, up_weight, down_weight)
    full = lax.all_gather(shards, (DP, SEQ), axis=1, tiled=True)
    full = lax.all_gather(full, TENSOR, axis=1)
    weights = [(full[3 * b], full[3 * b + 1], full[3 * b + 2]) for b in range(blocks)]

    cond_float = condition.astype(F32)
    all_cond = lax.all_gather(condition, DP, axis=0, tiled=True).astype(F32)
    all_silu = jax.nn.silu(all_cond).astype(BF16)
    silu_rows = lax.dynamic_slice_in_dim(all_silu, row_block * rows, rows, axis=1)
    partial_mod = jnp.einsum("cd,bdke->cbke", silu_rows, ada_weight, preferred_element_type=F32)
    partial_mod = lax.psum_scatter(partial_mod, DP, scatter_dimension=0, tiled=True)
    partial_mod = lax.psum(partial_mod, SEQ)
    modulation = lax.all_gather(partial_mod, TENSOR, axis=3, tiled=True)

    by_frame = frames % n_tensor == 0
    split_axis = 1 if by_frame else 0

    def to_spatial(v):
        return lax.all_to_all(v, TENSOR, split_axis=split_axis, concat_axis=2, tiled=True)

    def from_spatial(v):
        return lax.all_to_all(v, TENSOR, split_axis=2, concat_axis=split_axis, tiled=True)

    def to_temporal(v):
        return lax.all_to_all(v, SEQ, split_axis=2, concat_axis=1, tiled=True)

    def from_temporal(v):
        return lax.all_to_all(v, SEQ, split_axis=1, concat_axis=2, tiled=True)

    own_clips = clips if by_frame else clips // n_tensor
    first_clip = 0 if by_frame else tensor * own_clips
    spatial_mod = lax.dynamic_slice_in_dim(modulation[:, 0], first_clip, own_clips, axis=0)
    temporal_mod = modulation[:, 1]

    def patch_major(v):
        return v.transpose(0, 2, 1, 3)

    spatial = to_spatial(latents)
    spatial_shape = spatial.shape
    stream = spatial.astype(F32).reshape(own_clips, -1, width)
    stream, saved_0 = block_forward(stream, spatial_mod, weights[0], spatial_shape[2])
    moved = to_temporal(from_spatial(stream.astype(BF16).reshape(spatial_shape)))
    temporal_shape = moved.shape
    stream = patch_major(moved).astype(F32).reshape(clips, -1, width)
    stream, saved_1 = block_forward(stream, temporal_mod, weights[1], temporal_shape[1])

    def to_frames(v):
        return patch_major(
            v.reshape(clips, temporal_shape[2], temporal_shape[1], width)
        )

    block_out = from_temporal(to_frames(stream.astype(BF16)))

    teacher_rows = patch_major(to_temporal(teacher)).astype(F32).reshape(clips, -1, width)
    mask_float = valid_mask.astype(F32)
    own_mask = lax.dynamic_slice_in_dim(
        mask_float, seq * temporal_shape[2], temporal_shape[2], axis=1
    )
    mask_rows = jnp.repeat(own_mask, temporal_shape[1], axis=1)[:, :, None]
    error = stream - teacher_rows
    error_sum = lax.psum(jnp.sum(mask_rows * error * error), (DP, SEQ, TENSOR))
    total_frames = frames * n_seq
    valid_count = lax.psum(jnp.sum(mask_float), (DP, TENSOR)) * total_frames
    loss_value = error_sum / (width * valid_count)
    token_total = clips * frames * patches * n_dp * n_seq * n_tensor
    grad = mask_rows * error * (2.0 * token_total / valid_count)

    grad, mod_grad_1, x_1, g_1 = block_backward(
        grad, temporal_mod, weights[1], saved_1, temporal_shape[1]
    )
    moved = to_spatial(from_temporal(to_frames(grad.astype(BF16))))
    grad = moved.astype(F32).reshape(own_clips, -1, width)
    grad, mod_grad_0, x_0, g_0 = block_backward(
        grad, spatial_mod, weights[0], saved_0, spatial_shape[2]
    )
    grad_latents = from_spatial(grad.astype(BF16).reshape(spatial_shape)).astype(F32)

    x_list, g_list = x_0 + x_1, g_0 + g_1
    terms = []
    for b in range(blocks):
        for layer, q in ((0, 0), (1, 2), (2, 3)):
            term = jnp.einsum(
                "nd,tnk->tdk", x_list[4 * b + q], g_list[3 * b + layer], preferred_element_type=F32
            )
            if layer == 0:
                other = jnp.einsum(
                    "nd,tnk->tdk", x_list[4 * b + 1], g_list[3 * b], preferred_element_type=F32
                )
                term = jnp.where(jnp.arange(term.shape[2]) < inner, term, other)
            term = lax.psum_scatter(
                term.astype(BF16), (DP, SEQ), scatter_dimension=1, tiled=True
            )
            terms.append(lax.psum_scatter(term, TENSOR, scatter_dimension=0, tiled=True)[0])
    summed = jnp.stack(terms)
    grad_qkv, grad_out, grad_up, grad_down = unpack_shards(summed, blocks, heads_width)

    placed_0 = lax.dynamic_update_slice_in_dim(
        jnp.zeros((clips,) + mod_grad_0.shape[1:], F32), mod_grad_0, first_clip, axis=0
    )
    mod_grad = jnp.stack([placed_0, mod_grad_1], axis=1)
    mod_grad = lax.psum_scatter(mod_grad, TENSOR, scatter_dimension=3, tiled=True)
    mod_grad = lax.psum(mod_grad, SEQ)
    mod_grad = lax.all_gather(mod_grad, DP, axis=0, tiled=True)
    grad_ada = jnp.einsum("cd,cbke->bdke", silu_rows.astype(F32), mod_grad, precision=HIGHEST)
    grad_silu = jnp.einsum("cbke,bdke->cd", mod_grad, ada_weight.astype(F32), precision=HIGHEST)
    grad_silu = lax.psum(grad_silu, TENSOR)
    grad_silu = lax.all_gather(grad_silu, (DP, SEQ), axis=1, tiled=True)
    grad_silu = lax.dynamic_slice_in_dim(grad_silu, dp * clips, clips, axis=0)
    grad_condition = jax.vjp(jax.nn.silu, cond_float)[1](grad_silu)[0]
    return (
        block_out, loss_value, grad_latents, grad_condition,
        grad_qkv, grad_out, grad_up, grad_down, grad_ada,
    )


def pack_shards(qkv_weight, out_weight, up_weight, down_weight):
    blocks, rows = qkv_weight.shape[:2]
    shards = []
    for b in range(blocks):
        shards.append(jnp.concatenate([qkv_weight[b].reshape(rows, -1), out_weight[b].T], axis=1))
        shards.append(up_weight[b])
        shards.append(down_weight[b].T)
    return jnp.stack(shards)


def unpack_shards(summed, blocks, heads_width):
    rows = summed.shape[1]
    inner = 3 * heads_width
    summed = summed.reshape(blocks, 3, rows, -1).astype(F32)
    return (
        summed[:, 0, :, :inner].reshape(blocks, rows, 3, heads_width),
        summed[:, 0, :, inner:].transpose(0, 2, 1),
        summed[:, 1],
        summed[:, 2].transpose(0, 2, 1),
    )


def local_grid(
    latents, condition, teacher, valid_mask,
    qkv_weight, out_weight, up_weight, down_weight, ada_weight,
):
    n_dp, n_seq, nz = (lax.axis_size(a) for a in (DP, SEQ, TENSOR))
    _, frames, patches, width = latents.shape
    blocks, rows = ada_weight.shape[:2]
    heads_width = qkv_weight.shape[3]
    seq = lax.axis_index(SEQ)
    all_frames, own_patches, own_frames = frames * n_seq, patches // n_seq, frames // nz
    tokens = frames * patches

    shards = pack_shards(qkv_weight, out_weight, up_weight, down_weight)
    cond_float = condition.astype(F32)
    mask_float = valid_mask.astype(F32)
    count = jnp.broadcast_to(jnp.sum(mask_float), (1, ada_weight.shape[3]))
    ada = ada_weight.transpose(0, 2, 1, 3)
    full, teacher_rows, modulation, silu_rows, counted, final, saved_0, saved_1 = forward_pass(
        shards,
        latents.reshape(nz, own_frames, patches, width),
        teacher.reshape(frames, n_seq, own_patches, width),
        cond_float.reshape(-1, rows),
        count,
        ada,
        nz,
        n_seq,
        all_frames,
    )
    valid_count = counted[0, 0] / n_seq * all_frames
    token_total = tokens * n_dp * n_seq * nz
    scale = (2.0 * token_total / valid_count).reshape(1, 1)
    own_mask = lax.dynamic_slice_in_dim(mask_float, seq * own_patches, own_patches, axis=1)
    mask_rows = jnp.repeat(own_mask.reshape(-1), all_frames).reshape(tokens, 1)

    summed, block_out, grad_latents, mod_all, silu_grad = backward_pass(
        final, teacher_rows.reshape(tokens, width), mask_rows, scale, modulation, full, ada,
        saved_0, saved_1, rows, nz, n_seq, all_frames,
    )
    loss_value = jnp.sum(mod_all[:, 12, 0]) / (width * valid_count)
    grad_ada = jnp.einsum(
        "cd,cbke->bdke",
        silu_rows[:n_dp],
        mod_all[:, : 6 * blocks].reshape(n_dp, blocks, 6, -1),
        precision=HIGHEST,
    )
    grad_condition = jax.vjp(jax.nn.silu, cond_float)[1](silu_grad.reshape(1, width))[0]
    return (
        block_out.reshape(latents.shape),
        loss_value,
        grad_latents.reshape(latents.shape).astype(F32),
        grad_condition,
        *unpack_shards(summed, blocks, heads_width),
        grad_ada,
    )


def local(latents, *rest):
    sizes = tuple(lax.axis_size(a) for a in (DP, SEQ, TENSOR))
    if sizes == (4, 2, 4) and latents.shape[0] == 1:
        return local_grid(latents, *rest)
    return local_anywhere(latents, *rest)


def solution(mesh):
    return jax.shard_map(
        local,
        mesh=mesh,
        in_specs=(
            P(DP, SEQ, TENSOR, None),
            P(DP, None),
            P(DP, SEQ, TENSOR, None),
            P(DP, TENSOR),
            P(None, (DP, SEQ), None, TENSOR),
            P(None, TENSOR, (DP, SEQ)),
            P(None, (DP, SEQ), TENSOR),
            P(None, TENSOR, (DP, SEQ)),
            P(None, (DP, SEQ), None, TENSOR),
        ),
        out_specs=(
            P(DP, SEQ, TENSOR, None),
            P(),
            P(DP, SEQ, TENSOR, None),
            P(DP, None),
            P(None, (DP, SEQ), None, TENSOR),
            P(None, TENSOR, (DP, SEQ)),
            P(None, (DP, SEQ), TENSOR),
            P(None, TENSOR, (DP, SEQ)),
            P(None, (DP, SEQ), None, TENSOR),
        ),
        check_vma=False,
    )
```

```python
import functools

import jax
import jax.numpy as jnp
from jax import lax
from jax.experimental import pallas as pl
from jax.experimental.pallas import tpu as pltpu
from jax.sharding import PartitionSpec as P

DP, SEQ, TENSOR = "dp", "seq", "tensor"
START, SEND, RECV = range(3)
HEAD_DIM = 72
EPSILON = 1e-06
HIGHEST = lax.Precision.HIGHEST
MESH = pl.DeviceIdType.MESH
DMA = pltpu.SemaphoreType.DMA
BF16 = jnp.bfloat16
F32 = jnp.float32
ANY = pl.BlockSpec(memory_space=pl.ANY)
VM = pl.BlockSpec(memory_space=pltpu.VMEM)
LANES = 128
NEGATIVE = -1e30
GELU_C = 0.7978845608028654
GELU_K = 0.044715


def position():
    dp = lax.axis_index(DP)
    return dp // 2, dp % 2, lax.axis_index(SEQ), lax.axis_index(TENSOR)


def device(y, c, x, z):
    return (y * 2 + c, x, z)


def neighbours(nz):
    y, c, x, z = position()
    return (
        device(y, c, 1 - x, z),
        device(1 - y, c, x, z),
        device(y, 1 - c, x, z),
        device(y, c, x, jnp.maximum(z - 1, 0)),
        device(y, c, x, jnp.minimum(z + 1, nz - 1)),
    )


def remote(src, dst, send_sem, recv_sem, target):
    return pltpu.make_async_remote_copy(
        src_ref=src,
        dst_ref=dst,
        send_sem=send_sem,
        recv_sem=recv_sem,
        device_id=target,
        device_id_type=MESH,
    )


def in_plane(d):
    y, c, x, z = position()
    q = (y * 4 + c * 2 + x + d) % 8
    return (q // 2, q % 2, z), q


def across(d, nz):
    y, c, x, z = position()
    q = (x * nz + z + d) % (2 * nz)
    return (y * 2 + c, q // nz, q % nz), q


def over_z(d, nz):
    y, c, x, z = position()
    q = (z + d) % nz
    return device(y, c, x, q), q


def over_dp(d):
    y, c, x, z = position()
    q = (y * 2 + c + d) % 4
    return (q, x, z), q


def greet(peers):
    barrier = pltpu.get_barrier_semaphore()
    for target in peers:
        pl.semaphore_signal(barrier, inc=1, device_id=target, device_id_type=MESH)
    pl.semaphore_wait(barrier, len(peers))


def send_all(copies):
    for copy in copies:
        copy.start()


def finish_all(copies):
    for copy in copies:
        copy.wait_send()
        copy.wait_recv()


def kdot(a, b):
    return jnp.dot(a, b, preferred_element_type=F32)


def kdot_t(a, b):
    return lax.dot_general(a, b, (((1,), (1,)), ((), ())), preferred_element_type=F32)


class Lanes:
    def __init__(self, span):
        self.span = span
        self.heads = span // HEAD_DIM
        self.starts = [i * span // LANES * LANES for i in range(4)]
        self.offsets = [i * span - s for i, s in enumerate(self.starts)]
        self.width = 3 * LANES
        self.qkv = self.starts[2] + self.width

    def place(self, which, h):
        return self.offsets[which] + h * HEAD_DIM - (h // 2) * LANES

    def mask(self, which, h):
        lane = lax.broadcasted_iota(jnp.int32, (1, 2 * LANES), 1) - self.place(which, h)
        return ((lane >= 0) & (lane < HEAD_DIM)).astype(F32).astype(BF16)


def row_loop(total, step, body, unroll=2):
    def go(i, carry):
        body(pl.ds(pl.multiple_of(i * step, step), step))
        return carry

    lax.fori_loop(0, total // step, go, 0, unroll=unroll)


def tiles(total):
    first = -(-total // 2 // LANES) * LANES
    return ((0, first), (first, total - first))


def normed_of(v):
    center = v - jnp.mean(v, axis=-1, keepdims=True)
    inverse = lax.rsqrt(jnp.mean(center * center, axis=-1, keepdims=True) + EPSILON)
    return center * inverse, inverse


def gelu_inner(u):
    return jnp.tanh(GELU_C * (u + GELU_K * u * u * u))


def order_matrix(tokens, group, back):
    per = tokens // group
    row = lax.broadcasted_iota(jnp.int32, (tokens, tokens), 1 if back else 0)
    col = lax.broadcasted_iota(jnp.int32, (tokens, tokens), 0 if back else 1)
    return (col == row % group * per + row // group).astype(F32).astype(BF16)


def reorder(dst, src, order):
    for c0, n in tiles(src.shape[1]):
        dst[:, pl.ds(c0, n)] = kdot(order[...], src[:, pl.ds(c0, n)]).astype(BF16)


class Blocks:
    def __init__(self, w_ref, ring, sem, order, ready):
        self.w_ref, self.ring, self.sem, self.order = w_ref, ring, sem, order
        self.ready = ready
        self.loaded = self.done = 0
        self.depth = ring.shape[0]

    def copy(self, i):
        layer, t = self.order[i]
        s = i % self.depth
        dst = self.ring.at[s]
        if len(self.w_ref.shape) == 7:
            dst = dst.reshape(self.w_ref.shape[2:])
        return pltpu.make_async_copy(self.w_ref.at[layer, t], dst, self.sem.at[s])

    def pump(self):
        while (
            self.loaded < len(self.order)
            and self.loaded < self.done + self.depth
            and self.order[self.loaded][0] in self.ready
        ):
            self.copy(self.loaded).start()
            self.loaded += 1

    def take(self):
        i = self.done
        self.pump()
        self.copy(i).wait()
        return self.ring.at[i % self.depth]

    def drop(self):
        self.done += 1
        self.pump()


class Saves:
    def __init__(self, sem):
        self.sem, self.copies, self.used = sem, [], 0

    def put(self, src, dst):
        copy = pltpu.make_async_copy(src, dst, self.sem.at[self.used])
        copy.start()
        self.copies.append(copy)
        self.used += 1
        return copy

    def wait(self, copy):
        if any(other is copy for other in self.copies):
            copy.wait()
            self.copies = [other for other in self.copies if other is not copy]

    def finish(self):
        for copy in self.copies:
            copy.wait()
        self.copies = []


def stack_heads(dst, value, masks, group):
    for h, mask in enumerate(masks):
        lane = (h // 2) * LANES
        dst[h // 2, pl.ds(h % 2 * group, group), :] = value[:, lane : lane + 2 * LANES] * mask


FORWARD_SAVES = 24


def forward_steps(x_in, mod_ref, out_ref, saved, scratch, blocks, saves, *, sub, group, lanes):
    x_o, hida_o, qkv_o, prob_o, mix_o, bra_o, hidb_o, pre_o, act_o, brb_o = saved
    xbuf, perm, acc, qkv, qst, sc, hida, prob, mix, hidb, pre, act, mid, bra, brb = scratch
    tokens, width = x_in.shape
    nt = act.shape[0]
    cols = act.shape[2]
    heads = lanes.heads
    scale = HEAD_DIM**-0.5 * 1.4426950408889634
    x_ref = x_in if sub is None else xbuf
    steps = []

    def mod(i):
        return mod_ref[i : i + 1, :]

    def begin():
        if sub is not None:
            perm[...] = order_matrix(tokens, sub, False)
            reorder(xbuf, x_in, perm)
            saves.put(xbuf, x_o)

        def rows(r):
            n, _ = normed_of(x_ref[r, :].astype(F32))
            hida[r, :] = (n * (1.0 + mod(1)) + mod(0)).astype(BF16)

        row_loop(tokens, 32, rows)
        saves.put(hida, hida_o)

    steps.append((None, begin))

    kept = {}

    def project(t):
        if t >= 2:
            saves.wait(kept[0, t - 2])
        w = blocks.take()
        for c0, n in tiles(lanes.qkv):
            qkv[t % 2, :, pl.ds(c0, n)] = kdot(hida[...], w[:, pl.ds(c0, n)]).astype(BF16)
        kept[0, t] = saves.put(qkv.at[t % 2], qkv_o.at[t])

    def attend(t):
        now = qkv.at[t % 2]
        masks = [lanes.mask(1, h) for h in range(heads)]

        def one(g, carry):
            r = pl.ds(pl.multiple_of(g * group, group), group)
            q = pltpu.roll(now[r, pl.ds(0, lanes.width)].astype(F32), lanes.offsets[1], 1).astype(BF16)
            stack_heads(qst, q, masks, group)
            for p in range(heads // 2):
                k = now[r, pl.ds(lanes.starts[1] + p * LANES, 2 * LANES)]
                sc[:, pl.ds(p * 2 * group, 2 * group)] = kdot_t(k, qst[p])

            def soft(j, c2):
                at = pl.ds(pl.multiple_of(j * LANES, LANES), LANES)
                s = sc[:, at] * scale
                if sub is not None:
                    row = lax.broadcasted_iota(jnp.int32, s.shape, 0) // sub
                    col = lax.broadcasted_iota(jnp.int32, s.shape, 1) // sub
                    s = jnp.where(row == col, s, NEGATIVE)
                e = jnp.exp2(s - jnp.max(s, axis=0, keepdims=True))
                prob[t, g, :, at] = (e * (1.0 / jnp.sum(e, axis=0, keepdims=True))).astype(BF16)
                return c2

            lax.fori_loop(0, heads * group // LANES, soft, 0, unroll=2)
            pieces = [jnp.zeros((lanes.offsets[3], group), F32)]
            for p in range(heads // 2):
                v = now[r, pl.ds(lanes.starts[2] + p * LANES, 2 * LANES)].T
                for h in (2 * p, 2 * p + 1):
                    got = kdot(v, prob[t, g, :, pl.ds(h * group, group)])
                    at = lanes.place(2, h)
                    pieces.append(got[at : at + HEAD_DIM])
            rest = lanes.width - lanes.offsets[3] - heads * HEAD_DIM
            if rest:
                pieces.append(jnp.zeros((rest, group), F32))
            mix[t, r, :] = jnp.concatenate(pieces, axis=0).T.astype(BF16)
            return carry

        lax.fori_loop(0, tokens // group, one, 0)
        saves.put(prob.at[t], prob_o.at[t])
        saves.put(mix.at[t], mix_o.at[t])

    def bring_out(t):
        w = blocks.ring.at[blocks.done % blocks.depth]
        got = kdot_t(mix[t], w[:, pl.ds(lanes.starts[3], lanes.width)])
        if t == 0:
            acc[...] = got
        else:
            acc[...] += got
        blocks.drop()

    for t in range(nt):
        steps.append((0, functools.partial(project, t)))
        steps.append((0, functools.partial(attend, t)))
        steps.append((0, functools.partial(bring_out, t)))

    def between():
        def rows(r):
            b = acc[r, :]
            m = x_ref[r, :].astype(F32) + mod(2) * b
            mid[r, :] = m
            bra[r, :] = b.astype(BF16)
            n, _ = normed_of(m)
            hidb[r, :] = (n * (1.0 + mod(4)) + mod(3)).astype(BF16)

        row_loop(tokens, 32, rows)
        saves.put(bra, bra_o)
        saves.put(hidb, hidb_o)

    steps.append((0, between))

    def go_up(t):
        if t >= 2:
            saves.wait(kept[1, t - 2])
        w = blocks.take()
        for c0, n in tiles(cols):
            u = kdot(hidb[...], w[:, pl.ds(c0, n)])
            pre[t % 2, :, pl.ds(c0, n)] = u.astype(BF16)
            act[t, :, pl.ds(c0, n)] = (0.5 * u * (1.0 + gelu_inner(u))).astype(BF16)
        kept[1, t] = saves.put(pre.at[t % 2], pre_o.at[t])
        saves.put(act.at[t], act_o.at[t])
        blocks.drop()

    def go_down(t):
        w = blocks.take()
        got = kdot_t(act[t], w[...])
        if t == 0:
            acc[...] = got
        else:
            acc[...] += got
        blocks.drop()

    for t in range(nt):
        steps.append((1, functools.partial(go_up, t)))
    for t in range(nt):
        steps.append((2, functools.partial(go_down, t)))

    def end():
        def rows(r):
            b = acc[r, :]
            brb[r, :] = b.astype(BF16)
            out_ref[r, :] = (mid[r, :] + mod(5) * b).astype(out_ref.dtype)

        row_loop(tokens, 32, rows)
        saves.put(brb, brb_o)

    steps.append((2, end))
    return steps


def forward_scratch(tokens, width, nt, cols, group, sub, lanes):
    side = tokens if sub is not None else 16
    vmem = pltpu.VMEM
    return [
        vmem((side, width), BF16),
        vmem((side, side), BF16),
        vmem((tokens, width), F32),
        vmem((2, tokens, lanes.qkv), BF16),
        vmem((lanes.heads // 2, 2 * group, 2 * LANES), BF16),
        vmem((group, lanes.heads * group), F32),
        vmem((tokens, width), BF16),
        vmem((nt, tokens // group, group, lanes.heads * group), BF16),
        vmem((nt, tokens, lanes.width), BF16),
        vmem((tokens, width), BF16),
        vmem((2, tokens, cols), BF16),
        vmem((nt, tokens, cols), BF16),
        vmem((tokens, width), F32),
        vmem((tokens, width), BF16),
        vmem((tokens, width), BF16),
    ]


def forward_saved(tokens, width, nt, cols, group, sub, lanes):
    sds = jax.ShapeDtypeStruct
    return [
        sds((tokens, width), BF16),
        sds((tokens, width), BF16),
        sds((nt, tokens, lanes.qkv), BF16),
        sds((nt, tokens // group, group, lanes.heads * group), BF16),
        sds((nt, tokens, lanes.width), BF16),
        sds((tokens, width), BF16),
        sds((tokens, width), BF16),
        sds((nt, tokens, cols), BF16),
        sds((nt, tokens, cols), BF16),
        sds((tokens, width), BF16),
    ]


THIRDS = 3
GATHER_STAGES = 6
SPLITS = ((4, 3, 1, 1), (4, 4, 1, 0), (4, 3, 1, 1), (4, 4, 0, 1))


HALVES = 2
GATHER_SPLITS = ((2, 2, 1, 0), (2, 1, 0, 1), (2, 2, 1, 0), (1, 2, 0, 1))


def split_rows(k, unit):
    a, b, c, d = (v * unit for v in SPLITS[k % len(SPLITS)])
    return a, b, c, d


class Gather:
    def __init__(self, w_ref, g_ref, sems, nz):
        self.w, self.g, self.nz = w_ref, g_ref, nz
        (
            self.lsem, self.s_zab, self.r_zab, self.s_xy, self.r_xy,
            self.s_zcd, self.r_zcd, self.s_c, self.r_c,
        ) = sems
        self.layers, self.rows, self.cols = w_ref.shape
        self.unit = self.rows // 9
        self.count = self.layers * HALVES
        self.at = position()
        self.peers = neighbours(nz)

    def cut(self, k):
        at = 5 * self.unit * (k % HALVES)
        parts = []
        for v in GATHER_SPLITS[k % len(GATHER_SPLITS)]:
            parts.append((at, v * self.unit))
            at += v * self.unit
        return k // HALVES, parts

    def own(self, l):
        y, c, x, z = self.at
        return pltpu.make_async_copy(self.w.at[l], self.g.at[l, z, y, c, x], self.lsem.at[l])

    def region_ab(self, k, t):
        y, c, x, z = self.at
        l, (a, b, _, _) = self.cut(k)
        return self.g.at[l, t, y, c, x, pl.ds(a[0], a[1] + b[1])]

    def region_cd(self, k, t):
        y, c, x, z = self.at
        l, (_, _, rc, rd) = self.cut(k)
        return self.g.at[l, t, :, c, :, pl.ds(rc[0], rc[1] + rd[1])]

    def along_z(self, k, hop, which, mode):
        z, nz = self.at[3], self.nz
        below, above = self.peers[3:]
        region = (self.region_ab, self.region_cd)[which]
        ssem, rsem = ((self.s_zab, self.r_zab), (self.s_zcd, self.r_zcd))[which]
        up, down = z - hop, z + hop
        if mode == RECV:

            @pl.when(z - 1 - hop >= 0)
            def _():
                r = region(k, jnp.maximum(z - 1 - hop, 0))
                remote(r, r, ssem.at[k, hop, 1], rsem.at[k, hop, 1], above).wait_recv()

            @pl.when(z + 1 + hop < nz)
            def _():
                r = region(k, jnp.minimum(z + 1 + hop, nz - 1))
                remote(r, r, ssem.at[k, hop, 0], rsem.at[k, hop, 0], below).wait_recv()

            return
        l, (a, b, _, _) = self.cut(k)
        first = self.w.at[l, pl.ds(a[0], a[1] + b[1])] if which == 0 and hop == 0 else None

        @pl.when((up >= 0) & (z < nz - 1))
        def _():
            r = region(k, jnp.maximum(up, 0))
            copy = remote(r if first is None else first, r, ssem.at[k, hop, 1], rsem.at[k, hop, 1], above)
            copy.start() if mode == START else copy.wait_send()

        @pl.when((down < nz) & (z > 0))
        def _():
            r = region(k, jnp.minimum(down, nz - 1))
            copy = remote(r if first is None else first, r, ssem.at[k, hop, 0], rsem.at[k, hop, 0], below)
            copy.start() if mode == START else copy.wait_send()

    def region_xy(self, k, kind, yy, xx):
        y, c, x, z = self.at
        l, cuts = self.cut(k)
        ra, rb, rc, rd = (pl.ds(*v) for v in cuts)
        g = self.g
        return (
            lambda: g.at[l, :, yy, c, xx, ra],
            lambda: g.at[l, :, yy, c, xx, rb],
            lambda: g.at[l, :, yy, c, :, ra],
            lambda: g.at[l, :, :, c, xx, rb],
            lambda: g.at[l, z, yy, c, xx, rc],
            lambda: g.at[l, z, yy, c, xx, rd],
            lambda: g.at[l, z, yy, c, :, rc],
            lambda: g.at[l, z, :, c, xx, rd],
        )[kind]()

    def along_xy(self, k, kind, mode):
        y, c, x, z = self.at
        on_x = (True, False, False, True, True, False, False, True)[kind]
        l, (a, b, rc, rd) = self.cut(k)
        if (a, b, a, b, rc, rd, rc, rd)[kind][1] == 0:
            return
        target = self.peers[0 if on_x else 1]
        s, r = self.s_xy.at[k, kind], self.r_xy.at[k, kind]
        if mode == RECV:
            there = self.region_xy(k, kind, y, 1 - x) if on_x else self.region_xy(k, kind, 1 - y, x)
            remote(there, there, s, r, target).wait_recv()
            return
        here = self.region_xy(k, kind, y, x)
        src = here
        if kind == 4:
            src = self.w.at[l, pl.ds(*rc)]
        if kind == 5:
            src = self.w.at[l, pl.ds(*rd)]
        copy = remote(src, here, s, r, target)
        copy.start() if mode == START else copy.wait_send()

    def to_core(self, k, mode):
        c = self.at[1]
        l, cuts = self.cut(k)
        rows = pl.ds(cuts[0][0], sum(v[1] for v in cuts))
        r = self.g.at[l, :, :, 1 - c if mode == RECV else c, :, rows]
        copy = remote(r, r, self.s_c.at[k], self.r_c.at[k], self.peers[2])
        if mode == START:
            copy.start()
        elif mode == SEND:
            copy.wait_send()
        else:
            copy.wait_recv()

    def stage(self, k, s):
        z, xy = self.along_z, self.along_xy
        if s == 0:
            z(k, 0, 0, START)
            xy(k, 4, START)
            xy(k, 5, START)
        if s == 1:
            z(k, 0, 0, RECV)
            z(k, 1, 0, START)
            if k % HALVES == 0:
                self.own(k // HALVES).wait()
            xy(k, 4, RECV)
            xy(k, 6, START)
            xy(k, 5, RECV)
            xy(k, 7, START)
        if s == 2:
            z(k, 1, 0, RECV)
            z(k, 2, 0, START)
            xy(k, 6, RECV)
            xy(k, 7, RECV)
            z(k, 0, 1, START)
        if s == 3:
            z(k, 2, 0, RECV)
            xy(k, 0, START)
            xy(k, 1, START)
            z(k, 0, 1, RECV)
            z(k, 1, 1, START)
        if s == 4:
            xy(k, 0, RECV)
            xy(k, 2, START)
            xy(k, 1, RECV)
            xy(k, 3, START)
            z(k, 1, 1, RECV)
            z(k, 2, 1, START)
        if s == 5:
            xy(k, 2, RECV)
            xy(k, 3, RECV)
            z(k, 2, 1, RECV)
            self.to_core(k, START)

    def begin(self, ahead):
        self.ahead = ahead
        for l in range(self.layers):
            self.own(l).start()
        for k in range(min(ahead, self.count)):
            self.stage(k, 0)

    def slots(self):
        return self.count + GATHER_STAGES - 1

    def slot(self, i):
        for k in reversed(range(self.count)):
            s = i - k
            if s == 0 and k + self.ahead < self.count:
                self.stage(k + self.ahead, 0)
            if 1 <= s < GATHER_STAGES:
                self.stage(k, s)

    def arrive(self, layer):
        for k in range(layer * HALVES, (layer + 1) * HALVES):
            self.to_core(k, RECV)

    def end(self):
        for k in range(self.count):
            self.to_core(k, SEND)
            for kind in range(8):
                self.along_xy(k, kind, SEND)
            for hop in range(self.nz - 1):
                self.along_z(k, hop, 0, SEND)
                self.along_z(k, hop, 1, SEND)


def forward_pass_kernel(*refs, nz, n_seq, group_0, group_1, sub, lanes):
    w_ref, lat_ref, teach_ref, cond_ref, count_ref, ada_ref = refs[:6]
    g_ref, teach_o, mod_o, silu_o, count_o, final_ref = refs[6:12]
    saved_0, saved_1 = refs[12:22], refs[22:32]
    rest = refs[32:]
    sems, rest = rest[:9], rest[9:]
    (
        s_lat, r_lat, s_tea, r_tea, s_m, r_m, local_sem, s_t, r_t,
        ada, cond_all, parts, landed, mod_all, x0, x1, out_0, ring, wsem, osem_0, osem_1,
        qst_0, sc_0, prob_0,
    ) = rest[:24]
    shared = rest[24:]
    y, c, x, z = position()
    x_dev = neighbours(nz)[0]
    layers = w_ref.shape[0]
    tokens, width = x0.shape
    _, own_frames, patches, _ = lat_ref.shape
    frame = nz * patches
    part = patches // n_seq
    greet(
        [in_plane(d)[0] for d in range(1, 8)]
        + [(y * 2 + c, xx, (z + d) % nz) for d in range(1, nz) for xx in (x, 1 - x)]
    )
    gather = Gather(w_ref, g_ref, sems, nz)

    dp, block = y * 2 + c, (y * 2 + c) * 2 + x
    me = x * nz + z
    side = [
        pltpu.make_async_copy(teach_ref.at[:, x], teach_o.at[x], local_sem.at[0]),
        pltpu.make_async_copy(ada_ref, ada, local_sem.at[1]),
    ]
    lat_in, own_rows, teach_in = [], [], []
    for i in range(own_frames):
        rows = pl.ds(pl.multiple_of(i * frame + z * patches, 16), patches)
        own_rows.append(pltpu.make_async_copy(lat_ref.at[z, i], x0.at[rows], local_sem.at[2 + i]))
        for d in range(1, nz):
            target, q = over_z(d, nz)
            lat_in.append(remote(lat_ref.at[q, i], x0.at[rows], s_lat.at[i, d], r_lat.at[i, d], target))
    teach_in.append(remote(teach_ref.at[:, 1 - x], teach_o.at[x], s_tea, r_tea, x_dev))

    conds, sums, spread = [], [], []
    for d in range(1, 4):
        target, q = over_dp(d)
        conds.append(remote(cond_ref, cond_all.at[dp], s_m.at[0, d], r_m.at[0, d], target))
    for d in range(1, 8):
        target, q = in_plane(d)
        sums.append(remote(parts.at[q // 2], landed.at[d], s_m.at[1, d], r_m.at[1, d], target))
    for d in range(1, nz):
        target, q = over_z(d, nz)
        spread.append(remote(mod_all.at[z], mod_all.at[z], s_m.at[2, d], r_m.at[2, d], target))

    def modulate(step):
        if step == 0:
            send_all(conds)
            cond_all[dp] = cond_ref[...]
        if step == 1:
            finish_all(conds)
            side[1].wait()
            silu_o[...] = jnp.zeros_like(silu_o)
            for i in range(4):
                row = cond_all[i, pl.ds(block, 1), :]
                silu_o[i : i + 1, :] = (row / (1.0 + jnp.exp(-row))).astype(BF16).astype(F32)
            parts[...] = jnp.zeros_like(parts)
            for b in range(ada.shape[0]):
                for k in range(6):
                    got = kdot(silu_o[...].astype(BF16), ada[b, k])
                    for i in range(4):
                        parts[i, 6 * b + k : 6 * b + k + 1, :] = got[i : i + 1]
            for i in range(4):
                parts[i, 12:13, :] = count_ref[...]
            send_all(sums)
        if step == 2:
            finish_all(sums)
            total = parts[dp]
            for d in range(1, 8):
                total = total + landed[d]
            mod_all[z] = total
            send_all(spread)
        if step == 3:
            finish_all(spread)
            count = mod_all[0, 12:13, :]
            for q in range(1, nz):
                count = count + mod_all[q, 12:13, :]
            count_o[...] = count
            for b in range(ada.shape[0]):
                mod_o[b] = jnp.concatenate(
                    [mod_all[q, 6 * b : 6 * b + 6, :] for q in range(nz)], axis=1
                )

    moved, kept = [], []
    for i in range(own_frames):
        dst = x1.at[pl.ds(pl.multiple_of((me * own_frames + i) * part, 16), part)]
        for d in range(1, 2 * nz):
            target, q = across(d, nz)
            src = out_0.at[
                pl.ds(pl.multiple_of(i * frame + q % nz * patches + q // nz * part, 16), part)
            ]
            moved.append(remote(src, dst, s_t.at[i, d], r_t.at[i, d], target))
        src = out_0.at[pl.ds(pl.multiple_of(i * frame + z * patches + x * part, 16), part)]
        kept.append(pltpu.make_async_copy(src, dst, local_sem.at[2 + own_frames + i]))

    ready = set()
    order = [(l, t) for l in range(layers) for t in range(nz)]
    blocks = Blocks(g_ref, ring, wsem, order, ready)
    saves_0, saves_1 = Saves(osem_0), Saves(osem_1)
    per_block = layers // 2
    common = list(shared)
    scratch_1 = common
    scratch_0 = common[:4] + [qst_0, sc_0] + common[6:7] + [prob_0] + common[8:]

    def start_spatial():
        for copy in own_rows:
            copy.wait()
        finish_all(lat_in)
        saves_0.put(x0, saved_0[0])

    def leave_spatial():
        send_all(moved)
        send_all(kept)

    def start_temporal():
        for copy in kept:
            copy.wait()
        finish_all(moved)
        saves_0.finish()

    work = [(None, start_spatial)]
    for need, step in forward_steps(
        x0, mod_o.at[0], out_0, saved_0, scratch_0, blocks, saves_0,
        sub=None, group=group_0, lanes=lanes,
    ):
        work.append((need, step))
    work.append((None, leave_spatial))
    pause = len(work)
    work.append((None, start_temporal))
    for need, step in forward_steps(
        x1, mod_o.at[1], final_ref, saved_1, scratch_1, blocks, saves_1,
        sub=sub, group=group_1, lanes=lanes,
    ):
        work.append((None if need is None else need + per_block, step))

    send_all(own_rows)
    send_all(lat_in)
    modulate(0)
    gather.begin(2)
    send_all(side)
    send_all(teach_in)
    done, waited = 0, 0
    for slot in range(gather.slots() + 1):
        if slot < gather.slots():
            gather.slot(slot)
        if slot % 2 == 1 and slot < 6:
            modulate((slot + 1) // 2)
        since = slot - GATHER_STAGES - HALVES + 1
        if since >= 0 and since % HALVES == 0:
            layer = since // HALVES
            gather.arrive(layer)
            ready.add(layer)
            blocks.pump()
        quota = 7
        while done < len(work) and quota and slot >= 5:
            need = work[done][0]
            if need is not None and need not in ready:
                break
            if done == pause:
                waited += 1
                if waited < 2 and slot < gather.slots():
                    break
            work[done][1]()
            done += 1
            quota -= 1
    while done < len(work):
        work[done][1]()
        done += 1
    gather.end()
    side[0].wait()
    finish_all(teach_in)
    saves_1.finish()


def forward_pass(shards, latents, teacher, cond, count, ada, nz, n_seq, sub):
    layers, rows, cols = shards.shape
    hops = nz - 1
    chunks = layers * HALVES
    sds = jax.ShapeDtypeStruct
    _, own_frames, patches, width = latents.shape
    tokens = nz * own_frames * patches
    frames, halves, own_patches, _ = teacher.shape
    vmem = pltpu.VMEM
    mod_shape = (16, ada.shape[3])
    lanes = Lanes(cols // 4)
    group_0, group_1 = nz * patches, 8 * sub
    sizes_0 = (tokens, width, nz, cols, group_0, None, lanes)
    sizes_1 = (tokens, width, nz, cols, group_1, sub, lanes)
    scratch_0, scratch_1 = forward_scratch(*sizes_0), forward_scratch(*sizes_1)
    rowsb = vmem((tokens, width), BF16)
    outs = pl.pallas_call(
        functools.partial(
            forward_pass_kernel, nz=nz, n_seq=n_seq, group_0=group_0, group_1=group_1, sub=sub, lanes=lanes
        ),
        out_shape=[
            sds((layers, nz, 2, 2, 2, rows, cols), BF16),
            sds((halves, frames, own_patches, width), BF16),
            sds((2, 6, width), F32),
            sds((8, cond.shape[1]), F32),
            sds((1, ada.shape[3]), F32),
            sds((tokens, width), F32),
        ]
        + forward_saved(*sizes_0)
        + forward_saved(*sizes_1),
        in_specs=[ANY, ANY, ANY, VM, VM, ANY],
        out_specs=[ANY, ANY, VM, VM, VM, VM] + [ANY] * 20,
        scratch_shapes=[
            DMA((layers,)),
            DMA((chunks, hops, 2)),
            DMA((chunks, hops, 2)),
            DMA((chunks, 8)),
            DMA((chunks, 8)),
            DMA((chunks, hops, 2)),
            DMA((chunks, hops, 2)),
            DMA((chunks,)),
            DMA((chunks,)),
            DMA((own_frames, nz)),
            DMA((own_frames, nz)),
            DMA(()),
            DMA(()),
            DMA((3, 8)),
            DMA((3, 8)),
            DMA((2 + 2 * own_frames,)),
            DMA((own_frames, 2 * nz)),
            DMA((own_frames, 2 * nz)),
            vmem(ada.shape, BF16),
            vmem((4,) + cond.shape, F32),
            vmem((4,) + mod_shape, F32),
            vmem((8,) + mod_shape, F32),
            vmem((nz,) + mod_shape, F32),
            rowsb,
            rowsb,
            rowsb,
            vmem((3, width, cols), BF16),
            DMA((3,)),
            DMA((32,)),
            DMA((32,)),
            scratch_0[4],
            scratch_0[5],
            scratch_0[7],
        ]
        + scratch_1,
        compiler_params=pltpu.CompilerParams(
            collective_id=0, has_side_effects=True, vmem_limit_bytes=62 << 20
        ),
        name="forward_pass",
    )(shards, latents, teacher, cond, count, ada)
    full, teach, mod, silu, count, final = outs[:6]
    full = full.reshape(layers, nz, -1, cols)
    return full, teach, mod, silu, count, final, outs[6:16], outs[16:26]


def backward_steps(head, ins, outs, scratch, blocks, saves, marks, *, sub, group, lanes):
    loss = len(head) > 1
    x_hbm, mod_ref, qkv_hbm, prob_hbm, mix_hbm, bra_hbm, pre_hbm, brb_hbm = ins
    gout_ref, mg_ref, gba_o, gbb_o, gat_o, gpre_o = outs[:6]
    (
        gr, acc, gbb, gba, gpre, gat, dmx, qkv, qst, dst, sc, ds, prob, preb, mix,
        x_ref, branch, lsem, tbuf, perm,
    ) = scratch
    tokens, width = gr.shape
    nt, _, cols = pre_hbm.shape
    heads = lanes.heads
    factor = HEAD_DIM**-0.5
    steps = []

    def mod(i):
        return mod_ref[i : i + 1, :]

    def load(src, dst, n):
        return pltpu.make_async_copy(src, dst, lsem.at[n])

    load_x = load(x_hbm, x_ref, 0)
    load_brb = load(brb_hbm, branch, 1)
    load_bra = load(bra_hbm, branch, 2)

    def load_pre(t):
        return load(pre_hbm.at[t], preb, 3)

    def load_heads(t):
        return load(qkv_hbm.at[t], qkv, 4), load(prob_hbm.at[t], prob, 5), load(mix_hbm.at[t], mix, 6)

    def row_sum(v):
        return jnp.sum(v, axis=0, keepdims=True)

    def begin():
        load_brb.start()
        load_pre(0).start()
        send_all(load_heads(0))
        mg_ref[...] = jnp.zeros_like(mg_ref)
        if loss:
            final_hbm, teach_hbm, mask_ref, coef_ref = head
            bout_ref, err_ref = outs[6:]
            load_teach = load(teach_hbm, x_ref, 7)
            load_final = load(final_hbm, gr, 8)
            load_teach.start()
            load_final.start()
            err_ref[...] = jnp.zeros_like(err_ref)
            perm[...] = order_matrix(tokens, sub, False)
            load_teach.wait()
            reorder(tbuf, x_ref, perm)
            load_final.wait()
        load_x.start()
        load_brb.wait()

        def rows(r):
            if loss:
                f = gr[r, :]
                e = f - tbuf[r, :].astype(F32)
                me = mask_ref[r, :] * e
                err_ref[...] += row_sum(me * e)
                gba[r, :] = f.astype(BF16)
                g = me * coef_ref[0, 0]
            else:
                g = head[0][r, :].astype(F32)
            gr[r, :] = g
            mg_ref[5:6, :] += row_sum(g * branch[r, :].astype(F32))
            gbb[r, :] = (g * mod(5)).astype(BF16)

        row_loop(tokens, 32, rows)
        load_bra.start()
        marks[2] = [saves.put(gbb, gbb_o)]
        marks[1], marks[0] = [], []
        if loss:
            perm[...] = order_matrix(tokens, sub, True)
            reorder(bout_ref, gba, perm)

    steps.append(begin)
    kept = {}

    def through_gelu(t):
        if t:
            saves.wait(kept[t - 1])
        w = blocks.take()
        load_pre(t).wait()
        for c0, n in tiles(cols):
            ga = kdot(gbb[...], w[:, pl.ds(c0, n)])
            u = preb[:, pl.ds(c0, n)].astype(F32)
            th = gelu_inner(u)
            slope = 0.5 * (1.0 + th) + 0.5 * u * (1.0 - th * th) * (
                GELU_C * (1.0 + 3.0 * GELU_K * u * u)
            )
            gpre[:, pl.ds(c0, n)] = (ga * slope).astype(BF16)
        kept[t] = saves.put(gpre, gpre_o.at[t])
        if t == nt - 1:
            marks[1].append(kept[t])
        blocks.drop()
        if t + 1 < nt:
            load_pre(t + 1).start()

    def add_up(t, got):
        if t == 0:
            acc[...] = got
        else:
            acc[...] += got

    def under_up(t):
        w = blocks.take()
        add_up(t, kdot_t(gpre[...], w[...]))
        blocks.drop()

    for t in range(nt):
        steps.append(functools.partial(through_gelu, t))
        steps.append(functools.partial(under_up, t))

    def norm_back(gh, base, shift_row, scale_row, scale_i):
        n, inv = normed_of(base)
        mg_ref[shift_row : shift_row + 1, :] += row_sum(gh)
        mg_ref[scale_row : scale_row + 1, :] += row_sum(gh * n)
        dn = gh * (1.0 + mod(scale_i))
        along = jnp.mean(dn * n, axis=-1, keepdims=True)
        return inv * (dn - jnp.mean(dn, axis=-1, keepdims=True) - n * along)

    def between():
        load_x.wait()
        load_bra.wait()

        def rows(r):
            b = branch[r, :].astype(F32)
            middle = x_ref[r, :].astype(F32) + mod(2) * b
            g = gr[r, :] + norm_back(acc[r, :], middle, 3, 4, 4)
            gr[r, :] = g
            mg_ref[2:3, :] += row_sum(g * b)
            gba[r, :] = (g * mod(2)).astype(BF16)

        row_loop(tokens, 32, rows)
        marks[0].append(saves.put(gba, gba_o))

    steps.append(between)
    sent = {}

    def attend(t):
        if t:
            saves.wait(sent[t - 1])
        w = blocks.take()
        d = kdot(gba[...], w[:, pl.ds(lanes.starts[3], lanes.width)])
        back = lanes.width - (lanes.offsets[3] - lanes.offsets[2])
        dmx[...] = pltpu.roll(d, back, 1).astype(BF16)
        for copy in load_heads(t):
            copy.wait()
        kmasks = [lanes.mask(1, h) for h in range(heads)]
        vmasks = [lanes.mask(2, h) for h in range(heads)]

        def one(g, carry):
            r = pl.ds(pl.multiple_of(g * group, group), group)
            q = pltpu.roll(qkv[r, pl.ds(0, lanes.width)].astype(F32), lanes.offsets[1], 1).astype(BF16)
            stack_heads(qst, q, kmasks, group)
            stack_heads(dst, dmx[r, :], vmasks, group)
            for p in range(heads // 2):
                v = qkv[r, pl.ds(lanes.starts[2] + p * LANES, 2 * LANES)]
                sc[:, pl.ds(p * 2 * group, 2 * group)] = kdot_t(v, dst[p])

            def soft(j, c2):
                at = pl.ds(pl.multiple_of(j * LANES, LANES), LANES)
                p = prob[g, :, at].astype(F32)
                gp = sc[:, at]
                inner = jnp.sum(gp * p, axis=0, keepdims=True)
                ds[:, at] = (p * (gp - inner)).astype(BF16)
                return c2

            lax.fori_loop(0, heads * group // LANES, soft, 0, unroll=2)
            pieces, dk, dv = [], [], []
            for p in range(heads // 2):
                pair = pl.ds(p * 2 * group, 2 * group)
                dk.append(kdot(ds[:, pair], qst[p]) * factor)
                dv.append(kdot(prob[g, :, pair], dst[p]))
                k = qkv[r, pl.ds(lanes.starts[1] + p * LANES, 2 * LANES)].T
                for h in (2 * p, 2 * p + 1):
                    got = kdot(k, ds[:, pl.ds(h * group, group)])
                    at = lanes.place(1, h)
                    pieces.append(got[at : at + HEAD_DIM])
            pieces.append(jnp.zeros((lanes.width - heads * HEAD_DIM, group), F32))
            dq = jnp.concatenate(pieces, axis=0).T * factor
            parts = [dq[:, i * LANES : (i + 1) * LANES] for i in range(3)]
            low, high = slice(0, LANES), slice(LANES, 2 * LANES)
            parts[2] = parts[2] + dk[0][:, low]
            parts.append(dk[0][:, high] + dk[1][:, low])
            parts.append(dk[1][:, high] + dv[0][:, low])
            parts.append(dv[0][:, high] + dv[1][:, low])
            parts.append(dv[1][:, high])
            for i, part in enumerate(parts):
                gat[r, pl.ds(i * LANES, LANES)] = part.astype(BF16)
            return carry

        lax.fori_loop(0, tokens // group, one, 0)

    def under_qkv(t):
        w = blocks.ring.at[blocks.done % blocks.depth]
        add_up(t, kdot_t(gat[:, pl.ds(0, lanes.qkv)], w[:, pl.ds(0, lanes.qkv)]))
        blocks.drop()
        s3 = lanes.starts[3]
        gat[:, pl.ds(s3, LANES)] = gat[:, pl.ds(s3, LANES)] + mix[:, pl.ds(0, LANES)]
        gat[:, pl.ds(s3 + LANES, 2 * LANES)] = mix[:, pl.ds(LANES, 2 * LANES)]
        sent[t] = saves.put(gat, gat_o.at[t])
        if t == nt - 1:
            marks[0].append(sent[t])
        if t + 1 < nt:
            send_all(load_heads(t + 1))

    for t in range(nt):
        steps.append(functools.partial(attend, t))
        steps.append(functools.partial(under_qkv, t))

    def end():
        def rows(r):
            g = gr[r, :] + norm_back(acc[r, :], x_ref[r, :].astype(F32), 0, 1, 1)
            if loss:
                tbuf[r, :] = g.astype(BF16)
            else:
                gout_ref[r, :] = g.astype(BF16)

        row_loop(tokens, 32, rows)
        if loss:
            reorder(gout_ref, tbuf, perm)

    steps.append(end)
    return steps


def heads_scratch(tokens, group, lanes):
    vmem = pltpu.VMEM
    return [
        vmem((lanes.heads // 2, 2 * group, 2 * LANES), BF16),
        vmem((lanes.heads // 2, 2 * group, 2 * LANES), BF16),
        vmem((group, lanes.heads * group), F32),
        vmem((group, lanes.heads * group), BF16),
        vmem((tokens // group, group, lanes.heads * group), BF16),
    ]


def backward_scratch(tokens, width, cols, lanes):
    vmem = pltpu.VMEM
    return [
        vmem((tokens, width), F32),
        vmem((tokens, width), F32),
        vmem((tokens, width), BF16),
        vmem((tokens, width), BF16),
        vmem((tokens, cols), BF16),
        vmem((tokens, cols), BF16),
        vmem((tokens, lanes.width), BF16),
        vmem((tokens, lanes.qkv), BF16),
        vmem((tokens, cols), BF16),
        vmem((tokens, lanes.width), BF16),
        vmem((tokens, width), BF16),
        vmem((tokens, width), BF16),
        DMA((9,)),
        vmem((tokens, width), BF16),
        vmem((tokens, tokens), BF16),
    ]


STAGES = 7
KEPT = 6
SLOTS = 3
Y_A, X_A, X_B, Y_B, Y_C, X_C, X_D, Y_D = KINDS = tuple(range(8))


class Reduce:
    def __init__(self, x_refs, g_refs, o_ref, scratch, chunks, before, split_at, nz, rows, width):
        (
            self.acc, self.stg, self.prb, self.gbuf, self.xraw, self.xt,
            self.ya, self.xa, self.xb, self.yb, self.yc, self.xc, self.xd, self.yd, self.zab, self.zcd,
            self.gsem, self.xsem, self.osem, self.s_p, self.r_p, self.s_xy, self.r_xy, self.s_z, self.r_z,
        ) = scratch
        self.x_refs, self.g_refs, self.o_ref = x_refs, g_refs, o_ref
        self.chunks, self.before, self.split_at = chunks, before, split_at
        self.nz, self.rows, self.width = nz, rows, width
        self.unit = rows // 9
        self.count = len(chunks)
        self.at = position()
        self.peers = neighbours(nz)
        self.order = []
        for _, _, used in chunks:
            for q in used:
                if q not in self.order:
                    self.order.append(q)
        self.turned_so_far = 0

    def add_in(self, dst, src):
        lead = dst.shape[:-2]
        total = 1
        for v in lead:
            total *= v
        if total == 1:
            dst[...] = dst[...] + src[...]
            return

        def body(i, carry):
            index = []
            rest = i
            for v in reversed(lead):
                index.append(rest % v)
                rest = rest // v
            index = tuple(reversed(index))
            dst[index] = dst[index] + src[index]
            return carry

        lax.fori_loop(0, total, body, 0)

    def exchange(self, k, kind, mode):
        y, c, x, z = self.at
        x_dev, y_dev = self.peers[:2]
        a, b, nc, nd = split_rows(k, self.unit)
        if (a, a, b, b, nc, nc, nd, nd)[kind] == 0:
            return
        ra, rb, rc, rd = pl.ds(0, a), pl.ds(a, b), pl.ds(a + b, nc), pl.ds(a + b + nc, nd)
        m = k % SLOTS
        part = self.acc.at[k % KEPT]
        src, buf, target, dst = (
            lambda: (part.at[:, 1 - y, :, ra], self.ya.at[m, :, :, pl.ds(0, a)], y_dev, part.at[:, y, :, ra]),
            lambda: (part.at[:, y, 1 - x, ra], self.xa.at[m, :, pl.ds(0, a)], x_dev, part.at[:, y, x, ra]),
            lambda: (part.at[:, :, 1 - x, rb], self.xb.at[m, :, :, pl.ds(0, b)], x_dev, part.at[:, :, x, rb]),
            lambda: (part.at[:, 1 - y, x, rb], self.yb.at[m, :, pl.ds(0, b)], y_dev, part.at[:, y, x, rb]),
            lambda: (part.at[z, 1 - y, :, rc], self.yc.at[m], y_dev, part.at[z, y, :, rc]),
            lambda: (part.at[z, y, 1 - x, rc], self.xc.at[m], x_dev, part.at[z, y, x, rc]),
            lambda: (part.at[z, :, 1 - x, rd], self.xd.at[m], x_dev, part.at[z, :, x, rd]),
            lambda: (part.at[z, 1 - y, x, rd], self.yd.at[m], y_dev, part.at[z, y, x, rd]),
        )[kind]()
        copy = remote(src, buf, self.s_xy.at[k % STAGES, kind], self.r_xy.at[m, kind], target)
        if mode == START:
            copy.start()
        elif mode == SEND:
            copy.wait_send()
        else:
            copy.wait_recv()
            self.add_in(dst, buf)

    def region_z(self, k, t, which):
        y, c, x, z = self.at
        part = self.acc.at[k % KEPT, t]
        a, b, nc, nd = split_rows(k, self.unit)
        if which == 0:
            return part.at[y, x, pl.ds(0, a + b)]
        return part.at[:, :, pl.ds(a + b, nc + nd)]

    def landing(self, k, hop, way, which):
        a, b, nc, nd = split_rows(k, self.unit)
        if which == 0:
            return self.zab.at[k % SLOTS, hop, way, pl.ds(0, a + b)]
        return self.zcd.at[k % SLOTS, hop, way, :, :, pl.ds(0, nc + nd)]

    def along_z(self, k, hop, which, mode):
        z, nz = self.at[3], self.nz
        below, above = self.peers[3:]
        m, n = k % SLOTS, k % STAGES
        s_z, r_z = self.s_z, self.r_z
        t_down, t_up = hop - (nz - 1 - z), nz - 1 - (hop - z)
        if mode != RECV:

            @pl.when((t_down >= 0) & (z > 0))
            def _():
                copy = remote(
                    self.region_z(k, jnp.maximum(t_down, 0), which), self.landing(k, hop, 0, which),
                    s_z.at[n, which, hop, 0], r_z.at[m, which, hop, 0], below,
                )
                copy.start() if mode == START else copy.wait_send()

            @pl.when((hop >= z) & (z < nz - 1))
            def _():
                copy = remote(
                    self.region_z(k, jnp.minimum(t_up, nz - 1), which), self.landing(k, hop, 1, which),
                    s_z.at[n, which, hop, 1], r_z.at[m, which, hop, 1], above,
                )
                copy.start() if mode == START else copy.wait_send()

            return
        from_above, from_below = t_down + 1, t_up - 1

        @pl.when((from_above >= 0) & (z < nz - 1))
        def _():
            buf = self.landing(k, hop, 0, which)
            remote(buf, buf, s_z.at[n, which, hop, 0], r_z.at[m, which, hop, 0], below).wait_recv()
            self.add_in(self.region_z(k, jnp.maximum(from_above, 0), which), buf)

        @pl.when((hop >= z - 1) & (z > 0))
        def _():
            buf = self.landing(k, hop, 1, which)
            remote(buf, buf, s_z.at[n, which, hop, 1], r_z.at[m, which, hop, 1], above).wait_recv()
            self.add_in(self.region_z(k, jnp.minimum(from_below, nz - 1), which), buf)

    def pair(self, k, mode):
        m = k % 2
        copy = remote(self.stg, self.prb.at[m], self.s_p, self.r_p.at[m], self.peers[2])
        if mode == START:
            copy.start()
        elif mode == SEND:
            copy.wait_send()
        else:
            copy.wait_recv()
            self.add_in(self.acc.at[k % KEPT], self.prb.at[m])

    def load_g(self, k):
        layer, col, _ = self.chunks[k]
        return pltpu.make_async_copy(
            self.g_refs[layer].at[:, :, pl.ds(col * self.width, self.width)], self.gbuf, self.gsem
        )

    def turned(self, q):
        i = self.order.index(q)
        if i >= self.turned_so_far:
            load = pltpu.make_async_copy(self.x_refs[q], self.xraw, self.xsem)
            load.start()
            load.wait()
            for j in range(self.xraw.shape[1] // LANES):
                self.xt[i % 2, pl.ds(j * LANES, LANES), :] = self.xraw[:, pl.ds(j * LANES, LANES)].T
            self.turned_so_far += 1
        return i % 2

    def multiply(self, k):
        layer, col, used = self.chunks[k]
        c = self.at[1]
        if col == 0:
            self.before(layer)
            self.load_g(k).start()
        slots = [self.turned(q) for q in used]
        self.load_g(k).wait()
        rows = self.rows

        def fill(dst, core):
            def rows_of(slot):
                return jnp.concatenate(
                    [
                        self.xt[slot, pl.ds(pl.multiple_of((yy * 4 + core * 2) * rows, 16), 2 * rows), :]
                        for yy in range(2)
                    ],
                    axis=0,
                )

            def body(t, carry):
                g = self.gbuf[t]
                r = jnp.dot(rows_of(slots[-1]), g, preferred_element_type=F32)
                if len(slots) == 2:
                    n = -(-self.split_at // LANES) * LANES
                    other = jnp.dot(rows_of(slots[0]), g[:, :n], preferred_element_type=F32)
                    lane = lax.broadcasted_iota(jnp.int32, other.shape, 1)
                    other = jnp.where(lane < self.split_at, other, r[:, :n])
                    r = jnp.concatenate([other, r[:, n:]], axis=1)
                r = r.astype(BF16)
                for i in range(4):
                    dst[t, i // 2, i % 2] = r[i * rows : (i + 1) * rows]
                return carry

            lax.fori_loop(0, self.nz, body, 0)

        fill(self.stg, 1 - c)
        self.pair(k, START)
        if k >= KEPT:
            self.hand_out(k - KEPT).wait()
        fill(self.acc.at[k % KEPT], c)
        if k + 1 < self.count and self.chunks[k + 1][0] == layer:
            self.load_g(k + 1).start()

    def hand_out(self, k):
        y, c, x, z = self.at
        layer, col, _ = self.chunks[k]
        return pltpu.make_async_copy(
            self.acc.at[k % KEPT, z, y, x],
            self.o_ref.at[layer, :, pl.ds(col * self.width, self.width)],
            self.osem.at[k % KEPT],
        )

    def stage(self, k, s):
        move, z = self.exchange, self.along_z
        if s == 0:
            self.multiply(k)
        if s == 1:
            self.pair(k, SEND)
            self.pair(k, RECV)
            move(k, Y_A, START)
            move(k, X_B, START)
            z(k, 0, 1, START)
        if s == 2:
            z(k, 0, 1, RECV)
            z(k, 1, 1, START)
            move(k, Y_A, RECV)
            move(k, X_A, START)
            move(k, X_B, RECV)
            move(k, Y_B, START)
        if s == 3:
            z(k, 1, 1, RECV)
            z(k, 2, 1, START)
            move(k, X_A, RECV)
            move(k, Y_B, RECV)
            z(k, 0, 0, START)
        if s == 4:
            z(k, 0, 0, RECV)
            z(k, 1, 0, START)
            z(k, 2, 1, RECV)
            move(k, Y_C, START)
            move(k, X_D, START)
        if s == 5:
            z(k, 1, 0, RECV)
            z(k, 2, 0, START)
            move(k, Y_C, RECV)
            move(k, X_C, START)
            move(k, X_D, RECV)
            move(k, Y_D, START)
        if s == 6:
            z(k, 2, 0, RECV)
            move(k, X_C, RECV)
            move(k, Y_D, RECV)
            for kind in KINDS:
                move(k, kind, SEND)
            for hop in range(self.nz - 1):
                z(k, hop, 0, SEND)
                z(k, hop, 1, SEND)
            self.hand_out(k).start()

    def slots(self):
        return self.count + STAGES - 1

    def slot(self, i):
        for s in range(STAGES - 1, -1, -1):
            if 0 <= i - s < self.count:
                self.stage(i - s, s)

    def end(self):
        for k in range(max(0, self.count - KEPT), self.count):
            self.hand_out(k).wait()


def reduce_scratch(tokens, cols, rows, nz):
    width = cols // THIRDS
    unit = rows // 9
    hops = nz - 1
    vmem = pltpu.VMEM
    return [
        vmem((KEPT, nz, 2, 2, rows, width), BF16),
        vmem((nz, 2, 2, rows, width), BF16),
        vmem((2, nz, 2, 2, rows, width), BF16),
        vmem((nz, tokens, width), BF16),
        vmem((tokens, cols), BF16),
        vmem((2, cols, tokens), BF16),
        vmem((SLOTS, nz, 2, 4 * unit, width), BF16),
        vmem((SLOTS, nz, 4 * unit, width), BF16),
        vmem((SLOTS, nz, 2, 4 * unit, width), BF16),
        vmem((SLOTS, nz, 4 * unit, width), BF16),
        vmem((SLOTS, 2, unit, width), BF16),
        vmem((SLOTS, unit, width), BF16),
        vmem((SLOTS, 2, unit, width), BF16),
        vmem((SLOTS, unit, width), BF16),
        vmem((SLOTS, hops, 2, 8 * unit, width), BF16),
        vmem((SLOTS, hops, 2, 2, 2, 2 * unit, width), BF16),
        DMA(()),
        DMA(()),
        DMA((KEPT,)),
        DMA(()),
        DMA((2,)),
        DMA((STAGES, 8)),
        DMA((SLOTS, 8)),
        DMA((STAGES, 2, hops, 2)),
        DMA((SLOTS, 2, hops, 2)),
    ]


PER_SLOT = 2


def backward_pass_kernel(*refs, nz, n_seq, group_0, group_1, sub, lanes, rows):
    rest = list(refs)

    def take(n):
        got = rest[:n]
        del rest[:n]
        return got

    final_ref, teach_ref, mask_ref, coef_ref, mod_ref, w_ref, ada_ref = take(7)
    saved = take(10), take(10)
    o_ref, bout_o, lat_o, sums_o, silu_o = take(5)
    made = take(4), take(4)
    (
        ring, wsem, osem, s_t, r_t, s_lat, r_lat, s_m, r_m, local_sem,
        ada, mod_parts, first, every, along, back, silus, bout, err, gout, gin, mg_0, mg_1,
    ) = take(23)
    heads = take(5), take(5)
    shared = take(15)
    y, c, x, z = position()
    tokens, width = gout.shape
    own_frames, patches = lat_o.shape[1:3]
    part = patches // n_seq
    layers = w_ref.shape[0]
    greet(
        [in_plane(d)[0] for d in range(1, 8)]
        + [(y * 2 + c, xx, (z + d) % nz) for d in range(1, nz) for xx in (x, 1 - x)]
    )
    dp, block, me = y * 2 + c, (y * 2 + c) * 2 + x, x * nz + z
    load_ada = pltpu.make_async_copy(ada_ref, ada, local_sem.at[0])
    load_ada.start()

    uses = [(l, t) for t in range(nz) for l in (2, 1)] + [(0, t) for t in range(nz)]
    order = [(3 * b + l, t) for b in (1, 0) for l, t in uses]
    blocks = Blocks(w_ref, ring, wsem, order, set(range(layers)))
    blocks.pump()
    saves = Saves(osem)
    marks = {}, {}

    x_refs, g_refs, chunks = [], [], []
    for b in range(2):
        gba_o, gbb_o, gat_o, gpre_o = made[b]
        x_refs += [saved[b][1], gba_o, saved[b][6], gbb_o]
        g_refs += [gat_o, gpre_o, saved[b][8]]
    cols = g_refs[0].shape[2]
    third = cols // THIRDS
    for b in (1, 0):
        for layer, used in ((2, (3,)), (1, (2,)), (0, (0, 1))):
            for col in range(THIRDS):
                ids = tuple(4 * b + q for q in used)
                if layer == 0 and (col + 1) * third <= 3 * lanes.span:
                    ids = ids[:1]
                chunks.append((3 * b + layer, col, ids))

    def before(layer):
        for copy in marks[layer // 3][layer % 3]:
            saves.wait(copy)

    reduce = Reduce(
        x_refs, g_refs, o_ref, take(25), chunks, before, 3 * lanes.span - 2 * third, nz, rows, third
    )

    moved, kept = [], []
    for d in range(1, 2 * nz):
        target, q = across(d, nz)
        src = gout.reshape(2 * nz, own_frames, part, width).at[q]
        dst = gin.reshape(own_frames, nz, n_seq, part, width).at[:, z, x]
        moved.append(remote(src, dst, s_t.at[d], r_t.at[d], target))
    kept.append(
        pltpu.make_async_copy(
            gout.reshape(2 * nz, own_frames, part, width).at[me],
            gin.reshape(own_frames, nz, n_seq, part, width).at[:, z, x],
            local_sem.at[1],
        )
    )
    halves = bout.reshape(n_seq, bout_o.shape[0], part, width)
    moved.append(
        remote(halves.at[1 - x], bout_o.at[:, x], s_t.at[0], r_t.at[0], device(y, c, 1 - x, z))
    )
    kept.append(pltpu.make_async_copy(halves.at[x], bout_o.at[:, x], local_sem.at[2]))

    frames_of = gout.reshape(own_frames, nz, patches, width)
    own_lat = pltpu.make_async_copy(frames_of.at[:, z], lat_o.at[z], local_sem.at[3])
    lat_out, sums, spread, slices, rows_out = [], [], [], [], []
    for d in range(1, nz):
        target, q = over_z(d, nz)
        lat_out.append(remote(frames_of.at[:, q], lat_o.at[z], s_lat.at[d], r_lat.at[d], target))
        slices.append(remote(along, back.at[d], s_m.at[2, d], r_m.at[2, d], target))
    for d in range(1, 2 * nz):
        target, q = across(d, nz)
        sums.append(remote(mod_parts.at[q % nz], first.at[d], s_m.at[0, d], r_m.at[0, d], target))
    for d in range(1, 4):
        target, q = over_dp(d)
        spread.append(remote(every.at[dp], every.at[dp], s_m.at[1, d], r_m.at[1, d], target))
    for d in range(1, 8):
        target, q = in_plane(d)
        rows_out.append(remote(silus.at[block], silus.at[block], s_m.at[3, d], r_m.at[3, d], target))

    def modulation(step):
        if step == 0:
            span = lanes.span
            mod_parts[...] = jnp.zeros_like(mod_parts)
            total = jnp.sum(err[...], axis=1, keepdims=True)
            for q in range(nz):
                mod_parts[q, 0:6, :] = mg_0[:, q * span : (q + 1) * span]
                mod_parts[q, 6:12, :] = mg_1[:, q * span : (q + 1) * span]
                mod_parts[q, 12:13, :] = jnp.broadcast_to(total, (1, span))
            send_all(sums)
            own_lat.start()
            send_all(lat_out)
        if step == 1:
            finish_all(sums)
            total = mod_parts[z]
            for d in range(1, 2 * nz):
                total = total + first[d]
            every[dp] = total
            send_all(spread)
        if step == 2:
            finish_all(spread)
            load_ada.wait()
            sums_o[...] = every[...]
            total = jnp.zeros(along.shape, F32)
            for b in range(ada.shape[0]):
                for k in range(6):
                    i = 6 * b + k
                    got = jnp.concatenate([every[q, i : i + 1, :] for q in range(4)] * 2, axis=0)
                    high = got.astype(BF16)
                    rest_1 = got - high.astype(F32)
                    middle = rest_1.astype(BF16)
                    lowest = (rest_1 - middle.astype(F32)).astype(BF16)
                    for piece in (high, middle, lowest):
                        total = total + kdot_t(piece, ada[b, k])
            along[...] = total
            send_all(slices)
        if step == 3:
            finish_all(slices)
            total = along[...]
            for d in range(1, nz):
                total = total + back[d]
            silus[block] = total
            send_all(rows_out)
        if step == 4:
            finish_all(rows_out)
            for q in range(8):
                silu_o[q : q + 1, :] = silus[q, pl.ds(dp, 1), :]

    def ins_of(b):
        x_hbm, _, qkv, prob, mix, bra, _, pre, _, brb = saved[b]
        return x_hbm, mod_ref.at[b], qkv, prob, mix, bra, pre, brb

    def scratch_of(b):
        return list(shared[:8]) + list(heads[b][:4]) + [heads[b][4]] + list(shared[8:])

    def leave():
        send_all(moved)
        send_all(kept)

    def enter():
        for copy in kept:
            copy.wait()
        finish_all(moved)
        saves.finish()

    work = backward_steps(
        (final_ref, teach_ref, mask_ref, coef_ref), ins_of(1), [gout, mg_1] + made[1] + [bout, err],
        scratch_of(1), blocks, saves, marks[1], sub=sub, group=group_1, lanes=lanes,
    )
    one = len(work)
    work.append(leave)
    work.append(enter)
    base = len(work)
    work += backward_steps(
        (gin,), ins_of(0), [gout, mg_0] + made[0],
        scratch_of(0), blocks, saves, marks[0], sub=None, group=group_0, lanes=lanes,
    )
    work.append(functools.partial(modulation, 0))
    gelu_done, attn_done = 2 * nz - 1, one - 2
    need = {5: 0, 4: gelu_done, 3: attn_done, 2: base, 1: base + gelu_done, 0: base + attn_done}
    done, later, since = 0, 1, 0
    for slot in range(reduce.slots()):
        if slot < len(chunks):
            while done <= need[chunks[slot][0]]:
                work[done]()
                done += 1
        reduce.slot(slot)
        if done == len(work) and later < 5:
            modulation(later)
            later += 1
        quota = PER_SLOT
        while quota and done < len(work):
            if done == one + 1:
                since += 1
                if since < 3:
                    break
            work[done]()
            done += 1
            quota -= 1
    for step in range(later, 5):
        modulation(step)
    own_lat.wait()
    finish_all(lat_out)
    saves.finish()
    reduce.end()


def backward_pass(final, teacher, mask, coef, mod, w, ada, saved_0, saved_1, rows, nz, n_seq, sub):
    tokens, width = final.shape
    layers, _, _, cols = w.shape
    frames, halves = sub // n_seq, n_seq
    own_frames = frames // nz
    patches = tokens // nz // own_frames
    lanes = Lanes(cols // 4)
    span = ada.shape[3]
    group_0, group_1 = nz * patches, 8 * sub
    vmem = pltpu.VMEM
    sds = jax.ShapeDtypeStruct
    smem = pl.BlockSpec(memory_space=pltpu.SMEM)
    flat, tall = sds((tokens, width), BF16), sds((nz, tokens, cols), BF16)
    small = (16, span)
    rowsb = vmem((tokens, width), BF16)
    outs = pl.pallas_call(
        functools.partial(
            backward_pass_kernel,
            nz=nz, n_seq=n_seq, group_0=group_0, group_1=group_1, sub=sub, lanes=lanes, rows=rows,
        ),
        out_shape=[
            sds((layers, rows, cols), BF16),
            sds((frames, halves, patches // n_seq, width), BF16),
            sds((nz, own_frames, patches, width), BF16),
            sds((4,) + small, F32),
            sds((8, rows), F32),
        ]
        + [flat, flat, tall, tall] * 2,
        in_specs=[ANY, ANY, VM, smem, VM, ANY, ANY] + [ANY] * 20,
        out_specs=[ANY, ANY, ANY, VM, VM] + [ANY] * 8,
        scratch_shapes=[
            vmem((2, width, cols), BF16),
            DMA((2,)),
            DMA((24,)),
            DMA((2 * nz,)),
            DMA((2 * nz,)),
            DMA((nz,)),
            DMA((nz,)),
            DMA((4, 8)),
            DMA((4, 8)),
            DMA((4,)),
            vmem(ada.shape, BF16),
            vmem((nz,) + small, F32),
            vmem((2 * nz,) + small, F32),
            vmem((4,) + small, F32),
            vmem((8, rows), F32),
            vmem((nz, 8, rows), F32),
            vmem((8, 8, rows), F32),
            rowsb,
            vmem((1, width), F32),
            rowsb,
            rowsb,
            vmem((6, width), F32),
            vmem((6, width), F32),
        ]
        + heads_scratch(tokens, group_0, lanes)
        + heads_scratch(tokens, group_1, lanes)
        + backward_scratch(tokens, width, cols, lanes)
        + reduce_scratch(tokens, cols, rows, nz),
        compiler_params=pltpu.CompilerParams(
            collective_id=1, has_side_effects=True, vmem_limit_bytes=63 << 20
        ),
        name="backward_pass",
    )(final, teacher, mask, coef, mod, w, ada, *saved_0, *saved_1)
    return outs[:5]


def normalize(stream):
    center = stream - jnp.mean(stream, axis=-1, keepdims=True)
    inverse = lax.rsqrt(jnp.mean(center * center, axis=-1, keepdims=True) + EPSILON)
    return center * inverse, inverse


def norm_backward(grad_normed, normed, inverse):
    mean_grad = jnp.mean(grad_normed, axis=-1, keepdims=True)
    mean_along = jnp.mean(grad_normed * normed, axis=-1, keepdims=True)
    return inverse * (grad_normed - mean_grad - normed * mean_along)


def gelu_tanh(values):
    return jax.nn.gelu(values, approximate=True)


def dot(a, b):
    return jnp.dot(a, b, preferred_element_type=F32)


def dot_t(a, b):
    return lax.dot_general(a, b, (((1,), (1,)), ((), ())), preferred_element_type=F32)


def attend_forward(heads, factor):
    q, k, v = heads[:, :, :, 0], heads[:, :, :, 1], heads[:, :, :, 2]
    scores = jnp.einsum("tglhe,tgmhe->tghlm", q, k, preferred_element_type=F32) * factor
    peak = jnp.max(scores, axis=-1, keepdims=True)
    expanded = jnp.exp(scores - peak)
    total = jnp.sum(expanded, axis=-1, keepdims=True)
    probs = (expanded / total).astype(BF16)
    mixed = jnp.einsum("tghlm,tgmhe->tglhe", probs, v, preferred_element_type=F32)
    return mixed.astype(BF16), peak + jnp.log(total)


def attend_backward(heads, log_total, grad_mixed, factor):
    q, k, v = heads[:, :, :, 0], heads[:, :, :, 1], heads[:, :, :, 2]
    scores = jnp.einsum("tglhe,tgmhe->tghlm", q, k, preferred_element_type=F32) * factor
    probs = jnp.exp(scores - log_total)
    grad_v = jnp.einsum(
        "tghlm,tglhe->tgmhe", probs.astype(BF16), grad_mixed, preferred_element_type=F32
    )
    grad_probs = jnp.einsum("tglhe,tgmhe->tghlm", grad_mixed, v, preferred_element_type=F32)
    inner = jnp.sum(grad_probs * probs, axis=-1, keepdims=True)
    grad_scores = (probs * (grad_probs - inner)).astype(BF16)
    grad_q = jnp.einsum("tghlm,tgmhe->tglhe", grad_scores, k, preferred_element_type=F32) * factor
    grad_k = jnp.einsum("tghlm,tglhe->tgmhe", grad_scores, q, preferred_element_type=F32) * factor
    return jnp.stack([grad_q, grad_k, grad_v], axis=3).astype(BF16)


def block_forward(stream, modulation, weights, group):
    attn, up, down = weights
    blocks, width, cols = attn.shape
    inner = cols // 4 * 3
    head_count = cols // 4 // HEAD_DIM
    clips, per_clip, _ = stream.shape
    tokens = clips * per_clip
    factor = HEAD_DIM**-0.5

    def column(i):
        return modulation[:, i][:, None, :]

    normed_a, inverse_a = normalize(stream)
    hidden_a = (normed_a * (1.0 + column(1)) + column(0)).astype(BF16).reshape(tokens, width)
    triple = jnp.stack([dot(hidden_a, attn[t, :, :inner]).astype(BF16) for t in range(blocks)])
    heads = triple.reshape(blocks, tokens // group, group, 3, head_count, HEAD_DIM)
    mixed, log_total = attend_forward(heads, factor)
    mixed = mixed.reshape(blocks, tokens, cols // 4)
    branch_a = sum(dot_t(mixed[t], attn[t, :, inner:]) for t in range(blocks)).reshape(stream.shape)
    middle = stream + column(2) * branch_a
    normed_b, inverse_b = normalize(middle)
    hidden_b = (normed_b * (1.0 + column(4)) + column(3)).astype(BF16).reshape(tokens, width)
    pre_act = jnp.stack([dot(hidden_b, up[t]) for t in range(blocks)])
    activated = gelu_tanh(pre_act).astype(BF16)
    branch_b = sum(dot_t(activated[t], down[t]) for t in range(blocks)).reshape(stream.shape)
    output = middle + column(5) * branch_b
    saved = (
        normed_a, inverse_a, hidden_a, heads, log_total, mixed, branch_a,
        normed_b, inverse_b, hidden_b, pre_act, activated, branch_b,
    )
    return output, saved


def block_backward(grad, modulation, weights, saved, group):
    attn, up, down = weights
    blocks, width, cols = attn.shape
    inner = cols // 4 * 3
    head_count = cols // 4 // HEAD_DIM
    (
        normed_a, inverse_a, hidden_a, heads, log_total, mixed, branch_a,
        normed_b, inverse_b, hidden_b, pre_act, activated, branch_b,
    ) = saved
    tokens = hidden_a.shape[0]
    factor = HEAD_DIM**-0.5

    def column(i):
        return modulation[:, i][:, None, :]

    def clip_sum(values):
        return jnp.sum(values, axis=1)

    gate_b = clip_sum(grad * branch_b)
    branch_grad_b = (grad * column(5)).astype(BF16).reshape(tokens, width)
    grad_act = jnp.stack([dot(branch_grad_b, down[t]) for t in range(blocks)])
    grad_pre = jax.vjp(gelu_tanh, pre_act)[1](grad_act)[0].astype(BF16)
    grad_hidden_b = sum(dot_t(grad_pre[t], up[t]) for t in range(blocks)).reshape(grad.shape)
    shift_b = clip_sum(grad_hidden_b)
    scale_b = clip_sum(grad_hidden_b * normed_b)
    grad_middle = grad + norm_backward(grad_hidden_b * (1.0 + column(4)), normed_b, inverse_b)
    gate_a = clip_sum(grad_middle * branch_a)
    branch_grad_a = (grad_middle * column(2)).astype(BF16).reshape(tokens, width)
    grad_mixed = jnp.stack(
        [dot(branch_grad_a, attn[t, :, inner:]).astype(BF16) for t in range(blocks)]
    )
    grad_mixed = grad_mixed.reshape(blocks, tokens // group, group, head_count, HEAD_DIM)
    grad_heads = attend_backward(heads, log_total, grad_mixed, factor)
    grad_triple = grad_heads.reshape(blocks, tokens, inner)
    grad_hidden_a = sum(
        dot_t(grad_triple[t], attn[t, :, :inner]) for t in range(blocks)
    ).reshape(grad.shape)
    shift_a = clip_sum(grad_hidden_a)
    scale_a = clip_sum(grad_hidden_a * normed_a)
    grad_input = grad_middle + norm_backward(
        grad_hidden_a * (1.0 + column(1)), normed_a, inverse_a
    )
    grad_modulation = jnp.stack([shift_a, scale_a, gate_a, shift_b, scale_b, gate_b], axis=1)
    x_list = [hidden_a, branch_grad_a, hidden_b, branch_grad_b]
    g_list = [jnp.concatenate([grad_triple, mixed], axis=2), grad_pre, activated]
    return grad_input, grad_modulation, x_list, g_list


def local_anywhere(
    latents, condition, teacher, valid_mask,
    qkv_weight, out_weight, up_weight, down_weight, ada_weight,
):
    n_dp, n_seq, n_tensor = (lax.axis_size(a) for a in (DP, SEQ, TENSOR))
    clips, frames, patches, width = latents.shape
    rows = ada_weight.shape[1]
    blocks = qkv_weight.shape[0]
    heads_width = qkv_weight.shape[3]
    inner = 3 * heads_width
    dp, seq, tensor = (lax.axis_index(a) for a in (DP, SEQ, TENSOR))
    row_block = dp * n_seq + seq

    shards = pack_shards(qkv_weight, out_weight, up_weight, down_weight)
    full = lax.all_gather(shards, (DP, SEQ), axis=1, tiled=True)
    full = lax.all_gather(full, TENSOR, axis=1)
    weights = [(full[3 * b], full[3 * b + 1], full[3 * b + 2]) for b in range(blocks)]

    cond_float = condition.astype(F32)
    all_cond = lax.all_gather(condition, DP, axis=0, tiled=True).astype(F32)
    all_silu = jax.nn.silu(all_cond).astype(BF16)
    silu_rows = lax.dynamic_slice_in_dim(all_silu, row_block * rows, rows, axis=1)
    partial_mod = jnp.einsum("cd,bdke->cbke", silu_rows, ada_weight, preferred_element_type=F32)
    partial_mod = lax.psum_scatter(partial_mod, DP, scatter_dimension=0, tiled=True)
    partial_mod = lax.psum(partial_mod, SEQ)
    modulation = lax.all_gather(partial_mod, TENSOR, axis=3, tiled=True)

    by_frame = frames % n_tensor == 0
    split_axis = 1 if by_frame else 0

    def to_spatial(v):
        return lax.all_to_all(v, TENSOR, split_axis=split_axis, concat_axis=2, tiled=True)

    def from_spatial(v):
        return lax.all_to_all(v, TENSOR, split_axis=2, concat_axis=split_axis, tiled=True)

    def to_temporal(v):
        return lax.all_to_all(v, SEQ, split_axis=2, concat_axis=1, tiled=True)

    def from_temporal(v):
        return lax.all_to_all(v, SEQ, split_axis=1, concat_axis=2, tiled=True)

    own_clips = clips if by_frame else clips // n_tensor
    first_clip = 0 if by_frame else tensor * own_clips
    spatial_mod = lax.dynamic_slice_in_dim(modulation[:, 0], first_clip, own_clips, axis=0)
    temporal_mod = modulation[:, 1]

    def patch_major(v):
        return v.transpose(0, 2, 1, 3)

    spatial = to_spatial(latents)
    spatial_shape = spatial.shape
    stream = spatial.astype(F32).reshape(own_clips, -1, width)
    stream, saved_0 = block_forward(stream, spatial_mod, weights[0], spatial_shape[2])
    moved = to_temporal(from_spatial(stream.astype(BF16).reshape(spatial_shape)))
    temporal_shape = moved.shape
    stream = patch_major(moved).astype(F32).reshape(clips, -1, width)
    stream, saved_1 = block_forward(stream, temporal_mod, weights[1], temporal_shape[1])

    def to_frames(v):
        return patch_major(
            v.reshape(clips, temporal_shape[2], temporal_shape[1], width)
        )

    block_out = from_temporal(to_frames(stream.astype(BF16)))

    teacher_rows = patch_major(to_temporal(teacher)).astype(F32).reshape(clips, -1, width)
    mask_float = valid_mask.astype(F32)
    own_mask = lax.dynamic_slice_in_dim(
        mask_float, seq * temporal_shape[2], temporal_shape[2], axis=1
    )
    mask_rows = jnp.repeat(own_mask, temporal_shape[1], axis=1)[:, :, None]
    error = stream - teacher_rows
    error_sum = lax.psum(jnp.sum(mask_rows * error * error), (DP, SEQ, TENSOR))
    total_frames = frames * n_seq
    valid_count = lax.psum(jnp.sum(mask_float), (DP, TENSOR)) * total_frames
    loss_value = error_sum / (width * valid_count)
    token_total = clips * frames * patches * n_dp * n_seq * n_tensor
    grad = mask_rows * error * (2.0 * token_total / valid_count)

    grad, mod_grad_1, x_1, g_1 = block_backward(
        grad, temporal_mod, weights[1], saved_1, temporal_shape[1]
    )
    moved = to_spatial(from_temporal(to_frames(grad.astype(BF16))))
    grad = moved.astype(F32).reshape(own_clips, -1, width)
    grad, mod_grad_0, x_0, g_0 = block_backward(
        grad, spatial_mod, weights[0], saved_0, spatial_shape[2]
    )
    grad_latents = from_spatial(grad.astype(BF16).reshape(spatial_shape)).astype(F32)

    x_list, g_list = x_0 + x_1, g_0 + g_1
    terms = []
    for b in range(blocks):
        for layer, q in ((0, 0), (1, 2), (2, 3)):
            term = jnp.einsum(
                "nd,tnk->tdk", x_list[4 * b + q], g_list[3 * b + layer], preferred_element_type=F32
            )
            if layer == 0:
                other = jnp.einsum(
                    "nd,tnk->tdk", x_list[4 * b + 1], g_list[3 * b], preferred_element_type=F32
                )
                term = jnp.where(jnp.arange(term.shape[2]) < inner, term, other)
            term = lax.psum_scatter(
                term.astype(BF16), (DP, SEQ), scatter_dimension=1, tiled=True
            )
            terms.append(lax.psum_scatter(term, TENSOR, scatter_dimension=0, tiled=True)[0])
    summed = jnp.stack(terms)
    grad_qkv, grad_out, grad_up, grad_down = unpack_shards(summed, blocks, heads_width)

    placed_0 = lax.dynamic_update_slice_in_dim(
        jnp.zeros((clips,) + mod_grad_0.shape[1:], F32), mod_grad_0, first_clip, axis=0
    )
    mod_grad = jnp.stack([placed_0, mod_grad_1], axis=1)
    mod_grad = lax.psum_scatter(mod_grad, TENSOR, scatter_dimension=3, tiled=True)
    mod_grad = lax.psum(mod_grad, SEQ)
    mod_grad = lax.all_gather(mod_grad, DP, axis=0, tiled=True)
    grad_ada = jnp.einsum("cd,cbke->bdke", silu_rows.astype(F32), mod_grad, precision=HIGHEST)
    grad_silu = jnp.einsum("cbke,bdke->cd", mod_grad, ada_weight.astype(F32), precision=HIGHEST)
    grad_silu = lax.psum(grad_silu, TENSOR)
    grad_silu = lax.all_gather(grad_silu, (DP, SEQ), axis=1, tiled=True)
    grad_silu = lax.dynamic_slice_in_dim(grad_silu, dp * clips, clips, axis=0)
    grad_condition = jax.vjp(jax.nn.silu, cond_float)[1](grad_silu)[0]
    return (
        block_out, loss_value, grad_latents, grad_condition,
        grad_qkv, grad_out, grad_up, grad_down, grad_ada,
    )


def pack_shards(qkv_weight, out_weight, up_weight, down_weight):
    blocks, rows = qkv_weight.shape[:2]
    shards = []
    for b in range(blocks):
        shards.append(jnp.concatenate([qkv_weight[b].reshape(rows, -1), out_weight[b].T], axis=1))
        shards.append(up_weight[b])
        shards.append(down_weight[b].T)
    return jnp.stack(shards)


def unpack_shards(summed, blocks, heads_width):
    rows = summed.shape[1]
    inner = 3 * heads_width
    summed = summed.reshape(blocks, 3, rows, -1).astype(F32)
    return (
        summed[:, 0, :, :inner].reshape(blocks, rows, 3, heads_width),
        summed[:, 0, :, inner:].transpose(0, 2, 1),
        summed[:, 1],
        summed[:, 2].transpose(0, 2, 1),
    )


def local_grid(
    latents, condition, teacher, valid_mask,
    qkv_weight, out_weight, up_weight, down_weight, ada_weight,
):
    n_dp, n_seq, nz = (lax.axis_size(a) for a in (DP, SEQ, TENSOR))
    _, frames, patches, width = latents.shape
    blocks, rows = ada_weight.shape[:2]
    heads_width = qkv_weight.shape[3]
    seq = lax.axis_index(SEQ)
    all_frames, own_patches, own_frames = frames * n_seq, patches // n_seq, frames // nz
    tokens = frames * patches

    shards = pack_shards(qkv_weight, out_weight, up_weight, down_weight)
    cond_float = condition.astype(F32)
    mask_float = valid_mask.astype(F32)
    count = jnp.broadcast_to(jnp.sum(mask_float), (1, ada_weight.shape[3]))
    ada = ada_weight.transpose(0, 2, 1, 3)
    full, teacher_rows, modulation, silu_rows, counted, final, saved_0, saved_1 = forward_pass(
        shards,
        latents.reshape(nz, own_frames, patches, width),
        teacher.reshape(frames, n_seq, own_patches, width),
        cond_float.reshape(-1, rows),
        count,
        ada,
        nz,
        n_seq,
        all_frames,
    )
    valid_count = counted[0, 0] / n_seq * all_frames
    token_total = tokens * n_dp * n_seq * nz
    scale = (2.0 * token_total / valid_count).reshape(1, 1)
    own_mask = lax.dynamic_slice_in_dim(mask_float, seq * own_patches, own_patches, axis=1)
    mask_rows = jnp.repeat(own_mask.reshape(-1), all_frames).reshape(tokens, 1)

    summed, block_out, grad_latents, mod_all, silu_grad = backward_pass(
        final, teacher_rows.reshape(tokens, width), mask_rows, scale, modulation, full, ada,
        saved_0, saved_1, rows, nz, n_seq, all_frames,
    )
    loss_value = jnp.sum(mod_all[:, 12, 0]) / (width * valid_count)
    grad_ada = jnp.einsum(
        "cd,cbke->bdke",
        silu_rows[:n_dp],
        mod_all[:, : 6 * blocks].reshape(n_dp, blocks, 6, -1),
        precision=HIGHEST,
    )
    grad_condition = jax.vjp(jax.nn.silu, cond_float)[1](silu_grad.reshape(1, width))[0]
    return (
        block_out.reshape(latents.shape),
        loss_value,
        grad_latents.reshape(latents.shape).astype(F32),
        grad_condition,
        *unpack_shards(summed, blocks, heads_width),
        grad_ada,
    )


def local(latents, *rest):
    sizes = tuple(lax.axis_size(a) for a in (DP, SEQ, TENSOR))
    if sizes == (4, 2, 4) and latents.shape[0] == 1:
        return local_grid(latents, *rest)
    return local_anywhere(latents, *rest)


def solution(mesh):
    return jax.shard_map(
        local,
        mesh=mesh,
        in_specs=(
            P(DP, SEQ, TENSOR, None),
            P(DP, None),
            P(DP, SEQ, TENSOR, None),
            P(DP, TENSOR),
            P(None, (DP, SEQ), None, TENSOR),
            P(None, TENSOR, (DP, SEQ)),
            P(None, (DP, SEQ), TENSOR),
            P(None, TENSOR, (DP, SEQ)),
            P(None, (DP, SEQ), None, TENSOR),
        ),
        out_specs=(
            P(DP, SEQ, TENSOR, None),
            P(),
            P(DP, SEQ, TENSOR, None),
            P(DP, None),
            P(None, (DP, SEQ), None, TENSOR),
            P(None, TENSOR, (DP, SEQ)),
            P(None, (DP, SEQ), TENSOR),
            P(None, TENSOR, (DP, SEQ)),
            P(None, (DP, SEQ), None, TENSOR),
        ),
        check_vma=False,
    )
```
